32 devices in a mesh: pipe: 4 (over x, core), dp: 8 (over z, y).
Axes of the slice: x: 2, y: 2, z: 4, core: 2. Of those that a mesh axis runs over, the one named last changes fastest.
Arguments:
- inputs: bfloat16 [2, 2, 256, 1024], P(None, None, 'dp'), may hold values from -6 to 6
- cotangent: bfloat16 [2, 2, 256, 1024], P(None, None, 'dp'), may hold values from -0.375 to 0.375
- reduce_weight: bfloat16 [2, 4, 1024, 256], P(None, 'pipe'), may hold values from -0.1875 to 0.1875
- expand_weight: bfloat16 [2, 4, 1024, 256], P(None, 'pipe'), may hold values from -0.375 to 0.375
Outputs:
- gradients: float32 [4, 2, 1024, 256], P('pipe', None, 'dp')
The draws below stay inside these ranges and needn't reach their ends.
All inputs are finite; a program needn't handle non-finite values.
Results may differ from the reference program's by a relative error of at most 0.023.
Values may be sent and summed in bfloat16 or wider, within the bound.
No kernel may reach another device: no remote copies, remote signals or barrier semaphores. Data moves between devices by JAX's collectives and lax.ppermute only.
A program may use at most 64 MiB of HBM per device.

```python
import jax
import jax.numpy as jnp
from jax import lax

C = 1024
B = 256
MICRO = 2
SECTIONS = 4
ROWS = 256


def spiked(array, stream_key, source, target, parts, factor):
    def block_of(dim):
        return (jnp.arange(array.shape[dim]) // (array.shape[dim] // parts)).reshape((-1,) + (1,) * (array.ndim - 1 - dim))

    first = jax.random.permutation(stream_key, parts)[block_of(target)]
    far = (block_of(target) + parts // 2) % parts
    return jnp.where((block_of(source) == first) | (block_of(source) == far), factor * array, array)


def shard_levels(key, dims, cuts, least, top_value):
    factor_of, own = 1.0, jax.random.fold_in(key, 6)
    for position, blocks in cuts:
        draws = jnp.exp(jax.random.uniform(jax.random.fold_in(own, position), (blocks,), jnp.float32, least / len(cuts), top_value / len(cuts)))
        factor_of = factor_of * jnp.repeat(draws, dims[position] // blocks).reshape([-1 if axis == position else 1 for axis in range(len(dims))])
    return factor_of


def bell_draw(own_key, extent, spread, reach, shards=(), dtype=jnp.bfloat16):
    factor_of = shard_levels(own_key, extent, shards, -0.22, 0.18) if shards else 1.0
    drawn = jax.random.normal(own_key, extent, jnp.float32) * spread * factor_of
    return jnp.minimum(jnp.maximum(drawn, -reach), reach).astype(dtype)


def noise_with(key, shape, scale, limit, cuts, heavy, held_as=jnp.bfloat16):
    entries = scale * jax.random.normal(key, shape, jnp.float32)
    if cuts:
        entries = entries * shard_levels(key, shape, cuts, -0.22, 0.18)
    return jnp.clip(spiked(entries, jax.random.fold_in(key, 3), *heavy), -limit, limit).astype(held_as)


def setup_inputs(seed: int = 0) -> dict:
    splits = jax.random.split(jax.random.key(seed), 5)
    return {
        "inputs": bell_draw(splits[0], (2, MICRO, ROWS, C), 1.0, 6.0, ((2, 8),)),
        "cotangent": noise_with(splits[1], (2, MICRO, ROWS, C), (1.0 / (MICRO * ROWS) ** 0.5), 0.375, ((2, 8),), (2, 3, 8, 2.0)),
        "reduce_weight": bell_draw(splits[2], (2, SECTIONS, C, B), C ** -0.5, 0.1875, ((1, 4),)),
        "expand_weight": bell_draw(splits[3], (2, SECTIONS, C, B), B ** -0.5, 0.375, ((1, 4),)),
    }


EPSILON = 1e-06

def contract(first_op, second_op, first_dim, second_dim):
    return lax.dot_general(first_op, second_op, (((first_dim,), (second_dim,)), ((), ())), preferred_element_type=jnp.float32)

def smooth_slope(values):
    sigma = jax.nn.sigmoid(values)
    return sigma * (1.0 + values * (1.0 - sigma))

def section_forward(trunk_rows, reduce_mat, expand_mat):
    widened = trunk_rows.astype(jnp.float32)
    norm_scale = lax.rsqrt(lax.optimization_barrier(jnp.mean(widened * widened, axis=-1, keepdims=True)) + EPSILON)
    lifted = jax.nn.silu(widened * norm_scale).astype(jnp.bfloat16)
    inner_sum = jnp.dot(lifted, reduce_mat, preferred_element_type=jnp.float32)
    active = jax.nn.silu(inner_sum).astype(jnp.bfloat16)
    output = (widened + contract(active, expand_mat, 1, 1)).astype(jnp.bfloat16)
    return (output, lifted, inner_sum, active)

def back_path(trunk_rows, inner_sum, reduce_mat, expand_mat, upstream):
    widened = trunk_rows.astype(jnp.float32)
    norm_scale = lax.rsqrt(lax.optimization_barrier(jnp.mean(widened * widened, axis=-1, keepdims=True)) + EPSILON)
    normed = widened * norm_scale
    back_active = jnp.dot(upstream, expand_mat, preferred_element_type=jnp.float32)
    back_inner = (back_active * smooth_slope(inner_sum)).astype(jnp.bfloat16)
    back_lifted = contract(back_inner, reduce_mat, 1, 1)
    back_normed = back_lifted * smooth_slope(normed)
    projection = lax.optimization_barrier(jnp.mean(back_normed * widened, axis=-1, keepdims=True))
    back_trunk = upstream.astype(jnp.float32) + norm_scale * back_normed - widened * norm_scale ** 3 * projection
    return (back_trunk.astype(jnp.bfloat16), back_inner)

def reference(inputs, cotangent, reduce_weight, expand_weight):
    grads_reduce = [jnp.zeros((C, B), jnp.float32) for section_at in range(SECTIONS)]
    grads_expand = [jnp.zeros((C, B), jnp.float32) for section_at in range(SECTIONS)]
    for direction in range(2):
        for batch_at in range(MICRO):
            trunk_rows = inputs[direction, batch_at]
            history = []
            for section_at in range(SECTIONS):
                holder = section_at if direction == 0 else SECTIONS - 1 - section_at
                reduce_mat = reduce_weight[direction, holder]
                expand_mat = expand_weight[direction, holder]
                output, lifted, inner_sum, active = section_forward(trunk_rows, reduce_mat, expand_mat)
                history.append((trunk_rows, lifted, inner_sum, active, reduce_mat, expand_mat))
                trunk_rows = output
            upstream = cotangent[direction, batch_at]
            for section_at in reversed(range(SECTIONS)):
                trunk_in, lifted, inner_sum, active, reduce_mat, expand_mat = history[section_at]
                back_trunk, back_inner = back_path(trunk_in, inner_sum, reduce_mat, expand_mat, upstream)
                grads_reduce[section_at] = grads_reduce[section_at] + contract(lifted, back_inner, 0, 0)
                grads_expand[section_at] = grads_expand[section_at] + contract(upstream, active, 0, 0)
                upstream = back_trunk
    return jnp.stack([jnp.stack([grads_reduce[section_at], grads_expand[section_at]]) for section_at in range(SECTIONS)])
```

```python
import functools

import jax
import jax.numpy as jnp
from jax import lax
from jax.experimental import pallas as pl
from jax.experimental.pallas import tpu as pltpu
from jax.sharding import PartitionSpec as P

EPSILON = 1e-06
AXES = ("pipe", "dp")
HBM = pl.BlockSpec(memory_space=pl.ANY)
VMEM = pl.BlockSpec(memory_space=pltpu.VMEM)


def contract(first_op, second_op, first_dim, second_dim):
    return lax.dot_general(
        first_op,
        second_op,
        (((first_dim,), (second_dim,)), ((), ())),
        preferred_element_type=jnp.float32,
    )


def smooth_slope(values):
    sigma = jax.nn.sigmoid(values)
    return sigma * (1.0 + values * (1.0 - sigma))


def norm_of(widened):
    return lax.rsqrt(jnp.mean(widened * widened, axis=-1, keepdims=True) + EPSILON)


def where_am_i(step):
    position = lax.axis_index("pipe")
    stage, core = lax.div(position, 2), lax.rem(position, 2)
    way = jnp.where(stage == step, 0, 1)
    return stage, core, way


def weight_copies(own, other, held, sems, core, way):
    copies = []
    for order in range(2):
        is_own = lax.rem(way + order, 2) == core
        for kind in range(2):
            mine = pltpu.make_async_copy(own[kind].at[way], held[kind].at[order], sems.at[kind, order])
            theirs = pltpu.make_async_copy(
                other[kind].at[way], held[kind].at[order], sems.at[kind, order]
            )
            copies.append((is_own, mine, theirs))
    return copies


def start_all(copies):
    for is_own, mine, theirs in copies:
        pl.when(is_own)(mine.start)
        pl.when(jnp.logical_not(is_own))(theirs.start)


def stage_body(step, first, forward, backward, last, *refs):
    refs = list(refs)
    stage, core, way = where_am_i(step)
    own, other = (refs.pop(0), refs.pop(0)), (refs.pop(0), refs.pop(0))
    enter = refs.pop(0) if forward else None
    upstream_in = refs.pop(0) if backward else None
    if not forward:
        trunks, inners = refs.pop(0), refs.pop(0)
    if forward:
        flows = refs.pop(0)
    if forward and not backward:
        leave = refs.pop(0)
    if backward:
        back_flows = refs.pop(0)
    if backward and not last:
        back_leave = refs.pop(0)
    if forward:
        trunks, inners = refs.pop(0), refs.pop(0)
    held = (refs.pop(0), refs.pop(0))
    sems = refs.pop(0)
    channels = trunks.shape[2]

    copies = weight_copies(own, other, held, sems, core, way)
    start_all(copies if forward else copies[2:] + copies[:2])
    if forward:
        rows = enter[way, core] if first else enter[...]
        for order in range(2):
            slot = lax.rem(order + core, 2)
            widened = rows.astype(jnp.float32)
            normed = widened * norm_of(widened)
            lifted = jax.nn.silu(normed).astype(jnp.bfloat16)
            trunks[order] = rows
            flows[slot, :, :channels] = lifted
            copies[2 * order][1].wait()
            inner_sum = jnp.dot(lifted, held[0][order], preferred_element_type=jnp.float32)
            active = jax.nn.silu(inner_sum).astype(jnp.bfloat16)
            inners[order] = inner_sum
            flows[slot, :, channels:] = active
            copies[2 * order + 1][1].wait()
            rows = (widened + contract(active, held[1][order], 1, 1)).astype(jnp.bfloat16)
        if not backward:
            leave[...] = rows
    if backward:
        upstream = upstream_in[way, core] if forward else upstream_in[...]
        for order in (1, 0):
            slot = lax.rem(order + core, 2)
            back_flows[slot, :, :channels] = upstream
            if not forward:
                copies[2 * order + 1][1].wait()
            back_active = jnp.dot(upstream, held[1][order], preferred_element_type=jnp.float32)
            back_inner = (back_active * smooth_slope(inners[order])).astype(jnp.bfloat16)
            back_flows[slot, :, channels:] = back_inner
            if not forward:
                copies[2 * order][1].wait()
            if last and order == 0:
                break
            back_lifted = contract(back_inner, held[0][order], 1, 1)
            widened = trunks[order].astype(jnp.float32)
            norm_scale = norm_of(widened)
            back_normed = back_lifted * smooth_slope(widened * norm_scale)
            projection = jnp.mean(back_normed * widened, axis=-1, keepdims=True)
            upstream = (
                upstream.astype(jnp.float32)
                + norm_scale * back_normed
                - widened * norm_scale**3 * projection
            ).astype(jnp.bfloat16)
        if not last:
            back_leave[...] = upstream


def run_stage(weights, step, first, forward, backward, last, rows, sizes, *arrays):
    channels, inner = sizes
    packed = jax.ShapeDtypeStruct((2, rows, channels + inner), jnp.bfloat16)
    line = jax.ShapeDtypeStruct((rows, channels), jnp.bfloat16)
    kept = [((2, rows, channels), jnp.bfloat16), ((2, rows, inner), jnp.float32)]
    outs, scratch = [], []
    if forward:
        outs.append(packed)
    if forward and not backward:
        outs.append(line)
    if backward:
        outs.append(packed)
    if backward and not last:
        outs.append(line)
    if forward and not backward:
        outs += [jax.ShapeDtypeStruct(*shape) for shape in kept]
    if forward and backward:
        scratch += [pltpu.VMEM(*shape) for shape in kept]
    scratch += [pltpu.VMEM((2, channels, inner), jnp.bfloat16)] * 2
    scratch += [pltpu.SemaphoreType.DMA((2, 2))]
    passes = 4 * (int(forward) + int(backward))
    return pl.pallas_call(
        functools.partial(stage_body, step, first, forward, backward, last),
        out_shape=outs,
        in_specs=[HBM] * 4 + [VMEM] * len(arrays),
        out_specs=[VMEM] * len(outs),
        scratch_shapes=scratch,
        cost_estimate=pl.CostEstimate(
            flops=2 * passes * rows * channels * inner,
            bytes_accessed=8 * channels * inner,
            transcendentals=passes * rows * channels,
        ),
    )(*weights, *arrays)


def parity(value, mask):
    total, bit = 0, 0
    while mask >> bit:
        if mask >> bit & 1:
            total = total + lax.rem(lax.div(value, 1 << bit), 2)
        bit += 1
    return lax.rem(total, 2)


def halving_plan(size):
    depth = size.bit_length() - 1
    masks = [6 if bit == 2 else 1 << bit for bit in range(depth)]
    plans = []
    for core in range(2):
        order = masks[core:] + masks[:core]
        splits = []
        for at, mask in enumerate(order):
            odd = lambda value: bin(value).count("1") & 1
            splits.append(
                next(
                    a
                    for a in range(1, size)
                    if odd(a & mask) and not any(odd(a & later) for later in order[at + 1 :])
                )
            )
        table = [0] * size
        for chunk in range(size):
            place = 0
            for split in splits:
                place = 2 * place + (bin(chunk & split).count("1") & 1)
            table[place] = chunk
        plans.append((order, splits, table))
    return plans


def side_of(plans, at):
    core, shard = lax.rem(lax.axis_index("pipe"), 2), lax.axis_index("dp")
    return jnp.where(core == 0, parity(shard, plans[0][1][at]), parity(shard, plans[1][1][at]))


def gradient_body(plans, stages, *refs):
    flows, back_flows = refs[:stages], refs[stages : 2 * stages]
    away = refs[2 * stages : 2 * stages + 6]
    send, keep, left, right, full = refs[2 * stages + 6 :]
    stage, core, _ = where_am_i(0)
    rows, channels = flows[0].shape[1], left.shape[2]
    chunk = send.shape[2]
    for step in range(stages):

        @pl.when(stage == step)
        def _():
            left[0, :rows] = flows[step][0, :, :channels]
            right[1, :rows] = flows[step][0, :, channels:]
            left[1, :rows] = back_flows[step][0, :, :channels]
            right[0, :rows] = back_flows[step][0, :, channels:]

    parts = [(away[0], away[1]), (away[2].at[0], away[3].at[0]), (away[4], away[5])]
    for at, (flow, back_flow) in enumerate(parts):
        place = pl.ds((at + 1) * rows, rows)
        left[0, place] = flow[:, :channels]
        right[1, place] = flow[:, channels:]
        left[1, place] = back_flow[:, :channels]
        right[0, place] = back_flow[:, channels:]
    for which in range(2):
        full[which] = contract(left[which], right[which], 0, 0)
    side = side_of(plans, 0)
    half = send.shape[0]
    flip = [plan[2][half] for plan in plans]
    for at in range(half):
        spots = []
        for target_side in (1 - side, side):
            near = plans[0][2][at] ^ (flip[0] * target_side)
            far = plans[1][2][at] ^ (flip[1] * target_side)
            spots.append(pl.multiple_of(jnp.where(core == 0, near, far) * chunk, chunk))
        for which in range(2):
            send[at, which] = full[which, pl.ds(spots[0], chunk)].astype(jnp.bfloat16)
            keep[at, which] = full[which, pl.ds(spots[1], chunk)]


def halve_body(plans, at, keep_in, came, send, keep):
    half = keep.shape[0]
    side = side_of(plans, at)
    for spot in range(half):
        mine, theirs = side * half + spot, (1 - side) * half + spot
        send[spot] = (keep_in[theirs] + came[theirs].astype(jnp.float32)).astype(jnp.bfloat16)
        keep[spot] = keep_in[mine] + came[mine].astype(jnp.float32)


def shards(inputs, cotangent, reduce_weight, expand_weight):
    stages = lax.axis_size("pipe") // 2
    replicas = lax.axis_size("dp")
    stage, core, _ = where_am_i(0)
    channels, inner = reduce_weight.shape[2:]
    rows = inputs.shape[1] * inputs.shape[2] // 2
    sizes = (channels, inner)
    entering = inputs.reshape(2, 2, rows, channels)
    ending = cotangent.reshape(2, 2, rows, channels)
    own = [reduce_weight[:, 0], expand_weight[:, 0]]

    core_pairs = [(p, p ^ 1) for p in range(2 * stages)]
    mirror_pairs = [(p, 2 * (stages - 1 - p // 2) + p % 2) for p in range(2 * stages)]

    def hop(shard, step):
        pairs = []
        for c in range(2):
            pairs.append((2 * step + c, 2 * step + 2 + c))
            pairs.append((2 * (stages - 1 - step) + c, 2 * (stages - 2 - step) + c))
        return lax.ppermute(shard, "pipe", pairs)

    def swap_cores(shard):
        return lax.ppermute(shard, "pipe", core_pairs)

    def pick(parts, at):
        chosen = parts[0]
        for step in range(1, stages):
            chosen = jnp.where(at == step, parts[step], chosen)
        return chosen

    weights = own + [swap_cores(weight) for weight in own]
    flows, trunks, inners = [], [], []
    enter = entering
    for step in range(stages - 1):
        flow, leave, trunk, inner_sum = run_stage(
            weights, step, step == 0, True, False, False, rows, sizes, enter
        )
        flows.append(flow)
        trunks.append(trunk)
        inners.append(inner_sum)
        enter = hop(leave, step)
    flow, back_flow, leave = run_stage(
        weights, stages - 1, stages == 1, True, True, False, rows, sizes, enter, ending
    )
    flows.append(flow)
    back_flows = [back_flow]
    upstream = hop(leave, 0)
    far_flow = lax.ppermute(pick(flows, stages - 1 - stage), "pipe", mirror_pairs)
    for step in range(stages - 2, -1, -1):
        outs = run_stage(
            weights,
            step,
            False,
            False,
            True,
            step == 0,
            rows,
            sizes,
            upstream,
            trunks[step],
            inners[step],
        )
        back_flows.insert(0, outs[0])
        if step:
            upstream = hop(outs[1], stages - 1 - step)
    far_back = lax.ppermute(pick(back_flows, stages - 1 - stage), "pipe", mirror_pairs)
    away = [
        swap_cores(pick(flows, stage)[1]),
        swap_cores(pick(back_flows, stage)[1]),
        far_flow,
        far_back,
        swap_cores(far_flow[1]),
        swap_cores(far_back[1]),
    ]

    plans = halving_plan(replicas)
    chunk = channels // replicas
    half = replicas // 2
    send, keep = pl.pallas_call(
        functools.partial(gradient_body, plans, stages),
        out_shape=[
            jax.ShapeDtypeStruct((half, 2, chunk, inner), jnp.bfloat16),
            jax.ShapeDtypeStruct((half, 2, chunk, inner), jnp.float32),
        ],
        in_specs=[VMEM] * (2 * stages + 6),
        out_specs=[VMEM] * 2,
        scratch_shapes=[
            pltpu.VMEM((2, 4 * rows, channels), jnp.bfloat16),
            pltpu.VMEM((2, 4 * rows, inner), jnp.bfloat16),
            pltpu.VMEM((2, channels, inner), jnp.float32),
        ],
    )(*flows, *back_flows, *away)
    for at in range(replicas.bit_length() - 1):
        pairs = []
        for p in range(2 * stages):
            for q in range(replicas):
                pairs.append((p * replicas + q, p * replicas + (q ^ plans[p % 2][0][at])))
        came = lax.ppermute(send, AXES, pairs)
        if half == 1:
            return keep + came.astype(jnp.float32)
        half //= 2
        send, keep = pl.pallas_call(
            functools.partial(halve_body, plans, at + 1),
            out_shape=[
                jax.ShapeDtypeStruct((half, 2, chunk, inner), jnp.bfloat16),
                jax.ShapeDtypeStruct((half, 2, chunk, inner), jnp.float32),
            ],
            in_specs=[VMEM] * 2,
            out_specs=[VMEM] * 2,
        )(keep, came)


def solution(mesh):
    return jax.shard_map(
        shards,
        mesh=mesh,
        in_specs=(
            P(None, None, "dp", None),
            P(None, None, "dp", None),
            P(None, "pipe", None, None),
            P(None, "pipe", None, None),
        ),
        out_specs=P("pipe", None, "dp", None),
        check_vma=False,
    )
```

```python
import functools

import jax
import jax.numpy as jnp
from jax import lax
from jax.experimental import pallas as pl
from jax.experimental.pallas import tpu as pltpu
from jax.sharding import PartitionSpec as P

EPSILON = 1e-06
AXES = ("pipe", "dp")
HBM = pl.BlockSpec(memory_space=pl.ANY)
VMEM = pl.BlockSpec(memory_space=pltpu.VMEM)
PARAMS = pltpu.CompilerParams(vmem_limit_bytes=16 << 20)


def contract(first_op, second_op, first_dim, second_dim):
    return lax.dot_general(
        first_op,
        second_op,
        (((first_dim,), (second_dim,)), ((), ())),
        preferred_element_type=jnp.float32,
    )


def smooth_slope(values):
    sigma = jax.nn.sigmoid(values)
    return sigma * (1.0 + values * (1.0 - sigma))


def norm_of(widened):
    return lax.rsqrt(jnp.mean(widened * widened, axis=-1, keepdims=True) + EPSILON)


def where_am_i(step):
    position = lax.axis_index("pipe")
    stage, core = lax.div(position, 2), lax.rem(position, 2)
    way = jnp.where(stage == step, 0, 1)
    return stage, core, way


def weight_copies(own, other, held, sems, core, way):
    copies = []
    for order in range(2):
        is_own = lax.rem(way + order, 2) == core
        for kind in range(2):
            mine = pltpu.make_async_copy(own[kind].at[way], held[kind].at[order], sems.at[kind, order])
            theirs = pltpu.make_async_copy(
                other[kind].at[way], held[kind].at[order], sems.at[kind, order]
            )
            copies.append((is_own, mine, theirs))
    return copies


def start_all(copies):
    for is_own, mine, theirs in copies:
        pl.when(is_own)(mine.start)
        pl.when(jnp.logical_not(is_own))(theirs.start)


def stage_body(step, first, forward, backward, last, *refs):
    refs = list(refs)
    stage, core, way = where_am_i(step)
    own, other = (refs.pop(0), refs.pop(0)), (refs.pop(0), refs.pop(0))
    enter = refs.pop(0) if forward else None
    upstream_in = refs.pop(0) if backward else None
    if not forward:
        trunks, inners = refs.pop(0), refs.pop(0)
    if forward:
        flows = refs.pop(0)
    if forward and not backward:
        leave = refs.pop(0)
    if backward:
        back_flows = refs.pop(0)
    if backward and not last:
        back_leave = refs.pop(0)
    if forward:
        trunks, inners = refs.pop(0), refs.pop(0)
    held = (refs.pop(0), refs.pop(0))
    sems = refs.pop(0)
    channels = trunks.shape[2]

    copies = weight_copies(own, other, held, sems, core, way)
    start_all(copies if forward else copies[2:] + copies[:2])
    if forward:
        rows = enter[way, core] if first else enter[...]
        for order in range(2):
            slot = lax.rem(order + core, 2)
            widened = rows.astype(jnp.float32)
            normed = widened * norm_of(widened)
            lifted = jax.nn.silu(normed).astype(jnp.bfloat16)
            trunks[order] = rows
            flows[slot, :, :channels] = lifted
            copies[2 * order][1].wait()
            inner_sum = jnp.dot(lifted, held[0][order], preferred_element_type=jnp.float32)
            active = jax.nn.silu(inner_sum).astype(jnp.bfloat16)
            inners[order] = inner_sum
            flows[slot, :, channels:] = active
            copies[2 * order + 1][1].wait()
            rows = (widened + contract(active, held[1][order], 1, 1)).astype(jnp.bfloat16)
        if not backward:
            leave[...] = rows
    if backward:
        upstream = upstream_in[way, core] if forward else upstream_in[...]
        for order in (1, 0):
            slot = lax.rem(order + core, 2)
            back_flows[slot, :, :channels] = upstream
            if not forward:
                copies[2 * order + 1][1].wait()
            back_active = jnp.dot(upstream, held[1][order], preferred_element_type=jnp.float32)
            back_inner = (back_active * smooth_slope(inners[order])).astype(jnp.bfloat16)
            back_flows[slot, :, channels:] = back_inner
            if not forward:
                copies[2 * order][1].wait()
            if last and order == 0:
                break
            back_lifted = contract(back_inner, held[0][order], 1, 1)
            widened = trunks[order].astype(jnp.float32)
            norm_scale = norm_of(widened)
            back_normed = back_lifted * smooth_slope(widened * norm_scale)
            projection = jnp.mean(back_normed * widened, axis=-1, keepdims=True)
            upstream = (
                upstream.astype(jnp.float32)
                + norm_scale * back_normed
                - widened * norm_scale**3 * projection
            ).astype(jnp.bfloat16)
        if not last:
            back_leave[...] = upstream


def run_stage(weights, step, first, forward, backward, last, rows, sizes, *arrays):
    channels, inner = sizes
    packed = jax.ShapeDtypeStruct((2, rows, channels + inner), jnp.bfloat16)
    line = jax.ShapeDtypeStruct((rows, channels), jnp.bfloat16)
    kept = [((2, rows, channels), jnp.bfloat16), ((2, rows, inner), jnp.float32)]
    outs, scratch = [], []
    if forward:
        outs.append(packed)
    if forward and not backward:
        outs.append(line)
    if backward:
        outs.append(packed)
    if backward and not last:
        outs.append(line)
    if forward and not backward:
        outs += [jax.ShapeDtypeStruct(*shape) for shape in kept]
    if forward and backward:
        scratch += [pltpu.VMEM(*shape) for shape in kept]
    scratch += [pltpu.VMEM((2, channels, inner), jnp.bfloat16)] * 2
    scratch += [pltpu.SemaphoreType.DMA((2, 2))]
    passes = 4 * (int(forward) + int(backward))
    return pl.pallas_call(
        functools.partial(stage_body, step, first, forward, backward, last),
        out_shape=outs,
        in_specs=[HBM] * 4 + [VMEM] * len(arrays),
        out_specs=[VMEM] * len(outs),
        scratch_shapes=scratch,
        compiler_params=PARAMS,
        cost_estimate=pl.CostEstimate(
            flops=2 * passes * rows * channels * inner,
            bytes_accessed=8 * channels * inner,
            transcendentals=passes * rows * channels,
        ),
    )(*weights, *arrays)


def parity(value, mask):
    total, bit = 0, 0
    while mask >> bit:
        if mask >> bit & 1:
            total = total + lax.rem(lax.div(value, 1 << bit), 2)
        bit += 1
    return lax.rem(total, 2)


def halving_plan(size):
    depth = size.bit_length() - 1
    masks = [6 if bit == 2 else 1 << bit for bit in range(depth)]
    plans = []
    for core in range(2):
        order = masks[core:] + masks[:core]
        splits = []
        for at, mask in enumerate(order):
            odd = lambda value: bin(value).count("1") & 1
            splits.append(
                next(
                    a
                    for a in range(1, size)
                    if odd(a & mask) and not any(odd(a & later) for later in order[at + 1 :])
                )
            )
        table = [0] * size
        for chunk in range(size):
            place = 0
            for split in splits:
                place = 2 * place + (bin(chunk & split).count("1") & 1)
            table[place] = chunk
        plans.append((order, splits, table))
    return plans


def side_of(plans, at):
    core, shard = lax.rem(lax.axis_index("pipe"), 2), lax.axis_index("dp")
    return jnp.where(core == 0, parity(shard, plans[0][1][at]), parity(shard, plans[1][1][at]))


def gradient_body(plans, stages, *refs):
    flows, back_flows = refs[:stages], refs[stages : 2 * stages]
    away = refs[2 * stages : 2 * stages + 6]
    send, keep, left, right, full = refs[2 * stages + 6 :]
    stage, core, _ = where_am_i(0)
    rows, channels = flows[0].shape[1], left.shape[2]
    chunk = send.shape[2]
    for step in range(stages):

        @pl.when(stage == step)
        def _():
            left[0, :rows] = flows[step][0, :, :channels]
            right[1, :rows] = flows[step][0, :, channels:]
            left[1, :rows] = back_flows[step][0, :, :channels]
            right[0, :rows] = back_flows[step][0, :, channels:]

    parts = [(away[0], away[1]), (away[2].at[0], away[3].at[0]), (away[4], away[5])]
    for at, (flow, back_flow) in enumerate(parts):
        place = pl.ds((at + 1) * rows, rows)
        left[0, place] = flow[:, :channels]
        right[1, place] = flow[:, channels:]
        left[1, place] = back_flow[:, :channels]
        right[0, place] = back_flow[:, channels:]
    for which in range(2):
        full[which] = contract(left[which], right[which], 0, 0)
    side = side_of(plans, 0)
    half = send.shape[0]
    flip = [plan[2][half] for plan in plans]
    for at in range(half):
        spots = []
        for target_side in (1 - side, side):
            near = plans[0][2][at] ^ (flip[0] * target_side)
            far = plans[1][2][at] ^ (flip[1] * target_side)
            spots.append(pl.multiple_of(jnp.where(core == 0, near, far) * chunk, chunk))
        for which in range(2):
            send[at, which] = full[which, pl.ds(spots[0], chunk)].astype(jnp.bfloat16)
            keep[at, which] = full[which, pl.ds(spots[1], chunk)]


def halve_body(plans, at, keep_in, came, send, keep):
    half = keep.shape[0]
    side = side_of(plans, at)
    for spot in range(half):
        mine, theirs = side * half + spot, (1 - side) * half + spot
        send[spot] = (keep_in[theirs] + came[theirs].astype(jnp.float32)).astype(jnp.bfloat16)
        keep[spot] = keep_in[mine] + came[mine].astype(jnp.float32)


def shards(inputs, cotangent, reduce_weight, expand_weight):
    stages = lax.axis_size("pipe") // 2
    replicas = lax.axis_size("dp")
    stage, core, _ = where_am_i(0)
    channels, inner = reduce_weight.shape[2:]
    rows = inputs.shape[1] * inputs.shape[2] // 2
    sizes = (channels, inner)
    entering = inputs.reshape(2, 2, rows, channels)
    ending = cotangent.reshape(2, 2, rows, channels)
    own = [reduce_weight[:, 0], expand_weight[:, 0]]

    core_pairs = [(p, p ^ 1) for p in range(2 * stages)]
    mirror_pairs = [(p, 2 * (stages - 1 - p // 2) + p % 2) for p in range(2 * stages)]

    def hop(shard, step):
        pairs = []
        for c in range(2):
            pairs.append((2 * step + c, 2 * step + 2 + c))
            pairs.append((2 * (stages - 1 - step) + c, 2 * (stages - 2 - step) + c))
        return lax.ppermute(shard, "pipe", pairs)

    def swap_cores(shard):
        return lax.ppermute(shard, "pipe", core_pairs)

    def pick(parts, at):
        chosen = parts[0]
        for step in range(1, stages):
            chosen = jnp.where(at == step, parts[step], chosen)
        return chosen

    weights = own + [swap_cores(weight) for weight in own]
    flows, trunks, inners = [], [], []
    enter = entering
    for step in range(stages - 1):
        flow, leave, trunk, inner_sum = run_stage(
            weights, step, step == 0, True, False, False, rows, sizes, enter
        )
        flows.append(flow)
        trunks.append(trunk)
        inners.append(inner_sum)
        enter = hop(leave, step)
    flow, back_flow, leave = run_stage(
        weights, stages - 1, stages == 1, True, True, False, rows, sizes, enter, ending
    )
    flows.append(flow)
    back_flows = [back_flow]
    upstream = hop(leave, 0)
    far_flow = lax.ppermute(pick(flows, stages - 1 - stage), "pipe", mirror_pairs)
    for step in range(stages - 2, -1, -1):
        outs = run_stage(
            weights,
            step,
            False,
            False,
            True,
            step == 0,
            rows,
            sizes,
            upstream,
            trunks[step],
            inners[step],
        )
        back_flows.insert(0, outs[0])
        if step:
            upstream = hop(outs[1], stages - 1 - step)
    far_back = lax.ppermute(pick(back_flows, stages - 1 - stage), "pipe", mirror_pairs)
    away = [
        swap_cores(pick(flows, stage)[1]),
        swap_cores(pick(back_flows, stage)[1]),
        far_flow,
        far_back,
        swap_cores(far_flow[1]),
        swap_cores(far_back[1]),
    ]

    plans = halving_plan(replicas)
    chunk = channels // replicas
    half = replicas // 2
    send, keep = pl.pallas_call(
        functools.partial(gradient_body, plans, stages),
        out_shape=[
            jax.ShapeDtypeStruct((half, 2, chunk, inner), jnp.bfloat16),
            jax.ShapeDtypeStruct((half, 2, chunk, inner), jnp.float32),
        ],
        in_specs=[VMEM] * (2 * stages + 6),
        out_specs=[VMEM] * 2,
        scratch_shapes=[
            pltpu.VMEM((2, 4 * rows, channels), jnp.bfloat16),
            pltpu.VMEM((2, 4 * rows, inner), jnp.bfloat16),
            pltpu.VMEM((2, channels, inner), jnp.float32),
        ],
        compiler_params=PARAMS,
    )(*flows, *back_flows, *away)
    for at in range(replicas.bit_length() - 1):
        pairs = []
        for p in range(2 * stages):
            for q in range(replicas):
                pairs.append((p * replicas + q, p * replicas + (q ^ plans[p % 2][0][at])))
        came = lax.ppermute(send, AXES, pairs)
        if half == 1:
            return keep + came.astype(jnp.float32)
        half //= 2
        send, keep = pl.pallas_call(
            functools.partial(halve_body, plans, at + 1),
            out_shape=[
                jax.ShapeDtypeStruct((half, 2, chunk, inner), jnp.bfloat16),
                jax.ShapeDtypeStruct((half, 2, chunk, inner), jnp.float32),
            ],
            in_specs=[VMEM] * 2,
            out_specs=[VMEM] * 2,
            compiler_params=PARAMS,
        )(keep, came)


def solution(mesh):
    return jax.shard_map(
        shards,
        mesh=mesh,
        in_specs=(
            P(None, None, "dp", None),
            P(None, None, "dp", None),
            P(None, "pipe", None, None),
            P(None, "pipe", None, None),
        ),
        out_specs=P("pipe", None, "dp", None),
        check_vma=False,
    )
```

```python
import functools

import jax
import jax.numpy as jnp
from jax import lax
from jax.experimental import pallas as pl
from jax.experimental.pallas import tpu as pltpu
from jax.sharding import PartitionSpec as P

EPSILON = 1e-06
AXES = ("pipe", "dp")
HBM = pl.BlockSpec(memory_space=pltpu.HBM)
ANY = pl.BlockSpec(memory_space=pl.ANY)
VMEM = pl.BlockSpec(memory_space=pltpu.VMEM)
PARAMS = pltpu.CompilerParams(vmem_limit_bytes=16 << 20)


def contract(first_op, second_op, first_dim, second_dim):
    return lax.dot_general(
        first_op,
        second_op,
        (((first_dim,), (second_dim,)), ((), ())),
        preferred_element_type=jnp.float32,
    )


def smooth_slope(values):
    sigma = jax.nn.sigmoid(values)
    return sigma * (1.0 + values * (1.0 - sigma))


def norm_of(widened):
    return lax.rsqrt(jnp.mean(widened * widened, axis=-1, keepdims=True) + EPSILON)


def where_am_i(step):
    position = lax.axis_index("pipe")
    stage, core = lax.div(position, 2), lax.rem(position, 2)
    way = jnp.where(stage == step, 0, 1)
    return stage, core, way


def prologue_body(steps, *refs):
    reduce_all, expand_all, inputs, cotangent = refs[:4]
    outs, sems = refs[4:-1], refs[-1]
    _, core, way = where_am_i(0)
    _, _, turn = where_am_i(steps - 1)
    sources = (
        reduce_all.at[way],
        expand_all.at[way],
        inputs.at[way, core],
        reduce_all.at[turn],
        expand_all.at[turn],
        cotangent.at[turn, core],
    )
    copies = [
        pltpu.make_async_copy(source, out, sems.at[at])
        for at, (source, out) in enumerate(zip(sources, outs))
    ]
    for copy in copies:
        copy.start()
    for copy in copies:
        copy.wait()


def weight_copies(own, other, held, sems, core, way):
    copies = []
    for order in range(2):
        is_own = lax.rem(way + order, 2) == core
        for kind in range(2):
            mine = pltpu.make_async_copy(own[kind].at[way], held[kind].at[order], sems.at[kind, order])
            theirs = pltpu.make_async_copy(
                other[kind].at[way], held[kind].at[order], sems.at[kind, order]
            )
            copies.append((is_own, mine, theirs))
    return copies


def start_all(copies):
    for is_own, mine, theirs in copies:
        pl.when(is_own)(mine.start)
        pl.when(jnp.logical_not(is_own))(theirs.start)


def stage_body(step, forward, backward, last, near, *refs):
    refs = list(refs)
    _, core, way = where_am_i(step)
    own, other = (refs.pop(0), refs.pop(0)), (refs.pop(0), refs.pop(0))
    enter = refs.pop(0) if forward else None
    upstream_in = refs.pop(0) if backward else None
    if not forward:
        trunks, inners = refs.pop(0), refs.pop(0)
    if forward:
        flows = refs.pop(0)
    if forward and not backward:
        leave = refs.pop(0)
    if backward:
        upstreams, back_inners = refs.pop(0), refs.pop(0)
    if backward and not last:
        back_leave = refs.pop(0)
    if forward:
        trunks, inners = refs.pop(0), refs.pop(0)
    channels = trunks.shape[2]

    def run(reduce_mats, expand_mats, wait):
        if forward:
            rows = enter[...]
            for order in range(2):
                slot = lax.rem(order + core, 2)
                widened = rows.astype(jnp.float32)
                normed = widened * norm_of(widened)
                lifted = jax.nn.silu(normed).astype(jnp.bfloat16)
                trunks[order] = rows
                flows[slot, :, :channels] = lifted
                wait(0, order)
                inner_sum = jnp.dot(
                    lifted, reduce_mats[order][...], preferred_element_type=jnp.float32
                )
                active = jax.nn.silu(inner_sum).astype(jnp.bfloat16)
                inners[order] = inner_sum
                flows[slot, :, channels:] = active
                wait(1, order)
                rows = (widened + contract(active, expand_mats[order][...], 1, 1)).astype(jnp.bfloat16)
            if not backward:
                leave[...] = rows
        if backward:
            upstream = upstream_in[...]
            for order in (1, 0):
                slot = lax.rem(order + core, 2)
                upstreams[slot] = upstream
                if not forward:
                    wait(1, order)
                back_active = jnp.dot(
                    upstream, expand_mats[order][...], preferred_element_type=jnp.float32
                )
                back_inner = (back_active * smooth_slope(inners[order])).astype(jnp.bfloat16)
                back_inners[slot] = back_inner
                if not forward:
                    wait(0, order)
                if last and order == 0:
                    break
                back_lifted = contract(back_inner, reduce_mats[order][...], 1, 1)
                widened = trunks[order].astype(jnp.float32)
                norm_scale = norm_of(widened)
                back_normed = back_lifted * smooth_slope(widened * norm_scale)
                projection = jnp.mean(back_normed * widened, axis=-1, keepdims=True)
                upstream = (
                    upstream.astype(jnp.float32)
                    + norm_scale * back_normed
                    - widened * norm_scale**3 * projection
                ).astype(jnp.bfloat16)
            if not last:
                back_leave[...] = upstream

    if near:
        idle = lambda kind, order: None

        @pl.when(way == core)
        def _():
            run((own[0], other[0]), (own[1], other[1]), idle)

        @pl.when(way != core)
        def _():
            run((other[0], own[0]), (other[1], own[1]), idle)

    else:
        held = (refs.pop(0), refs.pop(0))
        copies = weight_copies(own, other, held, refs.pop(0), core, way)
        start_all(copies if forward else copies[2:] + copies[:2])
        run(
            [held[0].at[order] for order in range(2)],
            [held[1].at[order] for order in range(2)],
            lambda kind, order: copies[2 * order + kind][1].wait(),
        )


def run_stage(weights, step, forward, backward, near, rows, sizes, *arrays):
    channels, inner = sizes
    last = backward and step == 0 and not forward
    shape = lambda dtype, *dims: jax.ShapeDtypeStruct(dims, dtype)
    line = shape(jnp.bfloat16, rows, channels)
    kept = [((2, rows, channels), jnp.bfloat16), ((2, rows, inner), jnp.float32)]
    outs, scratch = [], []
    if forward:
        outs.append(shape(jnp.bfloat16, 2, rows, channels + inner))
    if forward and not backward:
        outs.append(line)
    if backward:
        outs.append(shape(jnp.bfloat16, 2, rows, channels))
        outs.append(shape(jnp.bfloat16, 2, rows, inner))
    if backward and not last:
        outs.append(line)
    if forward and not backward:
        outs += [jax.ShapeDtypeStruct(*one) for one in kept]
    if forward and backward:
        scratch += [pltpu.VMEM(*one) for one in kept]
    if not near:
        scratch += [pltpu.VMEM((2, channels, inner), jnp.bfloat16)] * 2
        scratch += [pltpu.SemaphoreType.DMA((2, 2))]
    passes = 4 * (int(forward) + int(backward))
    return pl.pallas_call(
        functools.partial(stage_body, step, forward, backward, last, near),
        out_shape=outs,
        in_specs=[VMEM if near else ANY] * 4 + [VMEM] * len(arrays),
        out_specs=[VMEM] * len(outs),
        scratch_shapes=scratch,
        compiler_params=PARAMS,
        cost_estimate=pl.CostEstimate(
            flops=2 * passes * rows * channels * inner,
            bytes_accessed=8 * channels * inner,
            transcendentals=passes * rows * channels,
        ),
    )(*weights, *arrays)


def parity(value, mask):
    total, bit = 0, 0
    while mask >> bit:
        if mask >> bit & 1:
            total = total + lax.rem(lax.div(value, 1 << bit), 2)
        bit += 1
    return lax.rem(total, 2)


def halving_plan(size, turn):
    depth = size.bit_length() - 1
    order = [6 if bit == 2 else 1 << bit for bit in range(depth)]
    order = order[turn:] + order[:turn]
    odd = lambda value: bin(value).count("1") & 1
    splits = []
    for at, mask in enumerate(order):
        fits = lambda a: odd(a & mask) and not any(odd(a & m) for m in order[at + 1 :])
        splits.append(next(a for a in range(1, size) if fits(a)))
    table = [0] * size
    for chunk in range(size):
        place = 0
        for split in splits:
            place = 2 * place + odd(chunk & split)
        table[place] = chunk
    return order, splits, table


def side_of(plans, at):
    core, shard = lax.rem(lax.axis_index("pipe"), 2), lax.axis_index("dp")
    return jnp.where(core == 0, parity(shard, plans[0][1][at]), parity(shard, plans[1][1][at]))


def gradient_body(plans, pick_left, pick_right, count, *refs):
    arrays, (send, keep, left, right, full) = refs[:count], refs[count:]
    stage, core, _ = where_am_i(0)
    rows = left.shape[0] // 4
    chunk = send.shape[1]
    for target, pick in ((left, pick_left), (right, pick_right)):
        near, away = pick(arrays)
        for step, part in enumerate(near):

            @pl.when(stage == step)
            def _():
                target[:rows] = part[...]

        for at, part in enumerate(away):
            target[(at + 1) * rows : (at + 2) * rows] = part[...]
    full[...] = contract(left[...], right[...], 0, 0)
    side = side_of(plans, 0)
    half = send.shape[0]
    flip = [plan[2][half] for plan in plans]
    for at in range(half):
        spots = []
        for target_side in (1 - side, side):
            first = plans[0][2][at] ^ (flip[0] * target_side)
            second = plans[1][2][at] ^ (flip[1] * target_side)
            spots.append(pl.multiple_of(jnp.where(core == 0, first, second) * chunk, chunk))
        send[at] = full[pl.ds(spots[0], chunk)].astype(jnp.bfloat16)
        keep[at] = full[pl.ds(spots[1], chunk)]


def halve_body(plans, at, keep_in, came, send, keep):
    half = keep.shape[0]
    side = side_of(plans, at)
    for spot in range(half):
        mine, theirs = side * half + spot, (1 - side) * half + spot
        send[spot] = (keep_in[theirs] + came[theirs].astype(jnp.float32)).astype(jnp.bfloat16)
        keep[spot] = keep_in[mine] + came[mine].astype(jnp.float32)


def finish_body(keep_reduce, came_reduce, keep_expand, came_expand, out):
    out[0, 0] = keep_reduce[0] + came_reduce[0].astype(jnp.float32)
    out[0, 1] = keep_expand[0] + came_expand[0].astype(jnp.float32)


def shards(inputs, cotangent, reduce_weight, expand_weight):
    stages = lax.axis_size("pipe") // 2
    replicas = lax.axis_size("dp")
    stage, core, _ = where_am_i(0)
    channels, inner = reduce_weight.shape[2:]
    rows = inputs.shape[1] * inputs.shape[2] // 2
    sizes = (channels, inner)
    entering = inputs.reshape(2, 2, rows, channels)
    ending = cotangent.reshape(2, 2, rows, channels)
    own = [reduce_weight[:, 0], expand_weight[:, 0]]

    core_pairs = [(p, p ^ 1) for p in range(2 * stages)]
    mirror_pairs = [(p, 2 * (stages - 1 - p // 2) + p % 2) for p in range(2 * stages)]

    def hop(shard, step):
        pairs = []
        for c in range(2):
            pairs.append((2 * step + c, 2 * step + 2 + c))
            pairs.append((2 * (stages - 1 - step) + c, 2 * (stages - 2 - step) + c))
        return lax.ppermute(shard, "pipe", pairs)

    def swap_cores(shard):
        return lax.ppermute(shard, "pipe", core_pairs)

    def mirror(shard):
        return lax.ppermute(shard, "pipe", mirror_pairs)

    def pick(parts, at):
        chosen = parts[0]
        for step in range(1, stages):
            chosen = jnp.where(at == step, parts[step], chosen)
        return chosen

    mat = jax.ShapeDtypeStruct((channels, inner), jnp.bfloat16)
    line = jax.ShapeDtypeStruct((rows, channels), jnp.bfloat16)
    held_hbm = [pltpu.with_memory_space_constraint(a, pltpu.HBM) for a in (*own, entering, ending)]
    *near, enter, turn_reduce, turn_expand, ending = pl.pallas_call(
        functools.partial(prologue_body, stages),
        out_shape=[mat, mat, line] * 2,
        in_specs=[HBM] * 4,
        out_specs=[VMEM] * 6,
        scratch_shapes=[pltpu.SemaphoreType.DMA((6,))],
        compiler_params=PARAMS,
    )(*held_hbm)
    near += [swap_cores(weight) for weight in near]
    turn = [turn_reduce, turn_expand]
    turn += [swap_cores(weight) for weight in turn]
    if stages > 2:
        weights = own + [swap_cores(weight) for weight in own]
    flows, trunks, inners = [], [], []
    for step in range(stages - 1):
        flow, leave, trunk, inner_sum = run_stage(
            weights if step else near, step, True, False, step == 0, rows, sizes, enter
        )
        flows.append(flow)
        trunks.append(trunk)
        inners.append(inner_sum)
        enter = hop(leave, step)
    flow, upstreams, back_inners, leave = run_stage(
        turn, stages - 1, True, True, True, rows, sizes, enter, ending
    )
    flows.append(flow)
    upstreams, back_inners = [upstreams], [back_inners]
    upstream = hop(leave, 0)
    far_flow = mirror(pick(flows, stages - 1 - stage))
    for step in range(stages - 2, -1, -1):
        outs = run_stage(
            weights if step else near,
            step,
            False,
            True,
            step == 0,
            rows,
            sizes,
            upstream,
            trunks[step],
            inners[step],
        )
        upstreams.insert(0, outs[0])
        back_inners.insert(0, outs[1])
        if step:
            upstream = hop(outs[2], stages - 1 - step)
    far_up = mirror(pick(upstreams, stages - 1 - stage))
    far_inner = mirror(pick(back_inners, stages - 1 - stage))

    side_flow = swap_cores(pick(flows, stage)[1])
    side_up = swap_cores(pick(upstreams, stage)[1])
    side_inner = swap_cores(pick(back_inners, stage)[1])
    cross_flow = swap_cores(far_flow[1])
    cross_up = swap_cores(far_up[1])
    cross_inner = swap_cores(far_inner[1])

    wide, narrow = slice(0, channels), slice(channels, channels + inner)

    def of_flows(columns):
        def pick_parts(arrays):
            near = [flow.at[0, :, columns] for flow in arrays[:stages]]
            side, far, cross = arrays[stages : stages + 3]
            return near, [side.at[:, columns], far.at[0, :, columns], cross.at[:, columns]]

        return pick_parts

    def of_backs(arrays):
        near = [back.at[0] for back in arrays[stages + 3 : 2 * stages + 3]]
        side, far, cross = arrays[2 * stages + 3 : 2 * stages + 6]
        return near, [side, far.at[0], cross]

    plans = [halving_plan(replicas, turn) for turn in range(2)]
    chunk = channels // replicas

    def sums(count):
        return [
            jax.ShapeDtypeStruct((count, chunk, inner), jnp.bfloat16),
            jax.ShapeDtypeStruct((count, chunk, inner), jnp.float32),
        ]

    fore = flows + [side_flow, far_flow, cross_flow]
    streams = []
    for pick_left, pick_right, backs, plan in (
        (of_backs, of_flows(narrow), upstreams + [side_up, far_up, cross_up], plans),
        (of_flows(wide), of_backs, back_inners + [side_inner, far_inner, cross_inner], plans[::-1]),
    ):
        arrays = fore + backs
        send, keep = pl.pallas_call(
            functools.partial(gradient_body, plan, pick_left, pick_right, len(arrays)),
            out_shape=sums(replicas // 2),
            in_specs=[VMEM] * len(arrays),
            out_specs=[VMEM] * 2,
            scratch_shapes=[
                pltpu.VMEM((4 * rows, channels), jnp.bfloat16),
                pltpu.VMEM((4 * rows, inner), jnp.bfloat16),
                pltpu.VMEM((channels, inner), jnp.float32),
            ],
            compiler_params=PARAMS,
        )(*arrays)
        streams.append((plan, send, keep))
    for at in range(replicas.bit_length() - 1):
        half = replicas >> (at + 2)
        arrived = []
        for plan, send, keep in streams:
            pairs = []
            for p in range(2 * stages):
                for q in range(replicas):
                    pairs.append((p * replicas + q, p * replicas + (q ^ plan[p % 2][0][at])))
            arrived.append((plan, keep, lax.ppermute(send, AXES, pairs)))
        if half == 0:
            break
        streams = []
        for plan, keep, came in arrived:
            send, keep = pl.pallas_call(
                functools.partial(halve_body, plan, at + 1),
                out_shape=sums(half),
                in_specs=[VMEM] * 2,
                out_specs=[VMEM] * 2,
                compiler_params=PARAMS,
            )(keep, came)
            streams.append((plan, send, keep))
    (_, keep_expand, came_expand), (_, keep_reduce, came_reduce) = arrived
    return pl.pallas_call(
        finish_body,
        out_shape=jax.ShapeDtypeStruct((1, 2, chunk, inner), jnp.float32),
        in_specs=[VMEM] * 4,
        out_specs=VMEM,
        compiler_params=PARAMS,
    )(keep_reduce, came_reduce, keep_expand, came_expand)


def solution(mesh):
    return jax.shard_map(
        shards,
        mesh=mesh,
        in_specs=(
            P(None, None, "dp", None),
            P(None, None, "dp", None),
            P(None, "pipe", None, None),
            P(None, "pipe", None, None),
        ),
        out_specs=P("pipe", None, "dp", None),
        check_vma=False,
    )
```

```python
import functools

import jax
import jax.numpy as jnp
from jax import lax
from jax.experimental import pallas as pl
from jax.experimental.pallas import tpu as pltpu
from jax.sharding import PartitionSpec as P

EPSILON = 1e-06
AXES = ("pipe", "dp")
HBM = pl.BlockSpec(memory_space=pltpu.HBM)
ANY = pl.BlockSpec(memory_space=pl.ANY)
VMEM = pl.BlockSpec(memory_space=pltpu.VMEM)
PARAMS = pltpu.CompilerParams(vmem_limit_bytes=16 << 20)


def contract(first_op, second_op, first_dim, second_dim):
    return lax.dot_general(
        first_op,
        second_op,
        (((first_dim,), (second_dim,)), ((), ())),
        preferred_element_type=jnp.float32,
    )


def smooth_slope(values):
    sigma = jax.nn.sigmoid(values)
    return sigma * (1.0 + values * (1.0 - sigma))


def norm_of(widened):
    return lax.rsqrt(jnp.mean(widened * widened, axis=-1, keepdims=True) + EPSILON)


def where_am_i(step):
    position = lax.axis_index("pipe")
    stage, core = lax.div(position, 2), lax.rem(position, 2)
    way = jnp.where(stage == step, 0, 1)
    return stage, core, way


def prologue_body(steps, *refs):
    reduce_all, expand_all, inputs = refs[:3]
    outs, sems = refs[3:-1], refs[-1]
    _, core, way = where_am_i(0)
    _, _, turn = where_am_i(steps - 1)
    sources = (
        reduce_all.at[way],
        expand_all.at[way],
        inputs.at[way, core],
        reduce_all.at[turn],
        expand_all.at[turn],
    )
    copies = [
        pltpu.make_async_copy(source, out, sems.at[at])
        for at, (source, out) in enumerate(zip(sources, outs))
    ]
    for copy in copies:
        copy.start()
    for copy in copies:
        copy.wait()


def weight_copies(own, other, held, sems, core, way):
    copies = []
    for order in range(2):
        is_own = lax.rem(way + order, 2) == core
        for kind in range(2):
            mine = pltpu.make_async_copy(own[kind].at[way], held[kind].at[order], sems.at[kind, order])
            theirs = pltpu.make_async_copy(
                other[kind].at[way], held[kind].at[order], sems.at[kind, order]
            )
            copies.append((is_own, mine, theirs))
    return copies


def start_all(copies):
    for is_own, mine, theirs in copies:
        pl.when(is_own)(mine.start)
        pl.when(jnp.logical_not(is_own))(theirs.start)


def stage_body(step, forward, backward, last, near, *refs):
    refs = list(refs)
    _, core, way = where_am_i(step)
    own, other = (refs.pop(0), refs.pop(0)), (refs.pop(0), refs.pop(0))
    enter = refs.pop(0) if forward else None
    upstream_in = refs.pop(0) if backward else None
    if not forward:
        trunks, inners = refs.pop(0), refs.pop(0)
    if forward:
        flows = refs.pop(0)
    if forward and not backward:
        leave = refs.pop(0)
    if backward:
        upstreams, back_inners = refs.pop(0), refs.pop(0)
    if backward and not last:
        back_leave = refs.pop(0)
    if forward:
        trunks, inners = refs.pop(0), refs.pop(0)
    channels = trunks.shape[2]
    if forward and backward:
        ending, ending_sem = refs.pop(0), refs.pop(0)
        bring = pltpu.make_async_copy(upstream_in.at[way, core], ending, ending_sem)
        bring.start()

    def run(reduce_mats, expand_mats, wait):
        if forward:
            rows = enter[...]
            for order in range(2):
                slot = lax.rem(order + core, 2)
                widened = rows.astype(jnp.float32)
                normed = widened * norm_of(widened)
                lifted = jax.nn.silu(normed).astype(jnp.bfloat16)
                trunks[order] = rows
                flows[slot, :, :channels] = lifted
                wait(0, order)
                inner_sum = jnp.dot(
                    lifted, reduce_mats[order][...], preferred_element_type=jnp.float32
                )
                active = jax.nn.silu(inner_sum).astype(jnp.bfloat16)
                inners[order] = inner_sum
                flows[slot, :, channels:] = active
                wait(1, order)
                rows = (widened + contract(active, expand_mats[order][...], 1, 1)).astype(jnp.bfloat16)
            if not backward:
                leave[...] = rows
        if backward:
            if forward:
                bring.wait()
            upstream = ending[...] if forward else upstream_in[...]
            for order in (1, 0):
                slot = lax.rem(order + core, 2)
                upstreams[slot] = upstream
                if not forward:
                    wait(1, order)
                back_active = jnp.dot(
                    upstream, expand_mats[order][...], preferred_element_type=jnp.float32
                )
                back_inner = (back_active * smooth_slope(inners[order])).astype(jnp.bfloat16)
                back_inners[slot] = back_inner
                if not forward:
                    wait(0, order)
                if last and order == 0:
                    break
                back_lifted = contract(back_inner, reduce_mats[order][...], 1, 1)
                widened = trunks[order].astype(jnp.float32)
                norm_scale = norm_of(widened)
                back_normed = back_lifted * smooth_slope(widened * norm_scale)
                projection = jnp.mean(back_normed * widened, axis=-1, keepdims=True)
                upstream = (
                    upstream.astype(jnp.float32)
                    + norm_scale * back_normed
                    - widened * norm_scale**3 * projection
                ).astype(jnp.bfloat16)
            if not last:
                back_leave[...] = upstream

    if near:
        idle = lambda kind, order: None

        @pl.when(way == core)
        def _():
            run((own[0], other[0]), (own[1], other[1]), idle)

        @pl.when(way != core)
        def _():
            run((other[0], own[0]), (other[1], own[1]), idle)

    else:
        held = (refs.pop(0), refs.pop(0))
        copies = weight_copies(own, other, held, refs.pop(0), core, way)
        start_all(copies if forward else copies[2:] + copies[:2])
        run(
            [held[0].at[order] for order in range(2)],
            [held[1].at[order] for order in range(2)],
            lambda kind, order: copies[2 * order + kind][1].wait(),
        )


def run_stage(weights, step, forward, backward, near, rows, sizes, *arrays):
    channels, inner = sizes
    last = backward and step == 0 and not forward
    shape = lambda dtype, *dims: jax.ShapeDtypeStruct(dims, dtype)
    line = shape(jnp.bfloat16, rows, channels)
    kept = [((2, rows, channels), jnp.bfloat16), ((2, rows, inner), jnp.float32)]
    outs, scratch = [], []
    if forward:
        outs.append(shape(jnp.bfloat16, 2, rows, channels + inner))
    if forward and not backward:
        outs.append(line)
    if backward:
        outs.append(shape(jnp.bfloat16, 2, rows, channels))
        outs.append(shape(jnp.bfloat16, 2, rows, inner))
    if backward and not last:
        outs.append(line)
    if forward and not backward:
        outs += [jax.ShapeDtypeStruct(*one) for one in kept]
    if forward and backward:
        scratch += [pltpu.VMEM(*one) for one in kept]
        scratch += [pltpu.VMEM((rows, channels), jnp.bfloat16), pltpu.SemaphoreType.DMA]
    if not near:
        scratch += [pltpu.VMEM((2, channels, inner), jnp.bfloat16)] * 2
        scratch += [pltpu.SemaphoreType.DMA((2, 2))]
    passes = 4 * (int(forward) + int(backward))
    return pl.pallas_call(
        functools.partial(stage_body, step, forward, backward, last, near),
        out_shape=outs,
        in_specs=[VMEM if near else ANY] * 4
        + ([VMEM, HBM] if forward and backward else [VMEM] * len(arrays)),
        out_specs=[VMEM] * len(outs),
        scratch_shapes=scratch,
        compiler_params=PARAMS,
        cost_estimate=pl.CostEstimate(
            flops=2 * passes * rows * channels * inner,
            bytes_accessed=8 * channels * inner,
            transcendentals=passes * rows * channels,
        ),
    )(*weights, *arrays)


def parity(value, mask):
    total, bit = 0, 0
    while mask >> bit:
        if mask >> bit & 1:
            total = total + lax.rem(lax.div(value, 1 << bit), 2)
        bit += 1
    return lax.rem(total, 2)


def halving_plan(size, turn):
    order = [1 << bit for bit in range(size.bit_length() - 1)]
    if turn and len(order) > 1:
        order[:2] = order[1::-1]
    table = [0] * size
    for chunk in range(size):
        place = 0
        for mask in order:
            place = 2 * place + int(chunk & mask != 0)
        table[place] = chunk
    return order, order, table


def side_of(plans, at):
    core, shard = lax.rem(lax.axis_index("pipe"), 2), lax.axis_index("dp")
    return jnp.where(core == 0, parity(shard, plans[0][1][at]), parity(shard, plans[1][1][at]))


def gradient_body(plans, pick_left, pick_right, count, *refs):
    arrays, (send, keep, left, right, full) = refs[:count], refs[count:]
    stage, core, _ = where_am_i(0)
    rows = left.shape[0] // 4
    chunk = send.shape[1]
    for target, pick in ((left, pick_left), (right, pick_right)):
        near, away = pick(arrays)
        for step, part in enumerate(near):

            @pl.when(stage == step)
            def _():
                target[:rows] = part[...]

        for at, part in enumerate(away):
            target[(at + 1) * rows : (at + 2) * rows] = part[...]
    full[...] = contract(left[...], right[...], 0, 0)
    side = side_of(plans, 0)
    half = send.shape[0]
    flip = [plan[2][half] for plan in plans]
    for at in range(half):
        spots = []
        for target_side in (1 - side, side):
            first = plans[0][2][at] ^ (flip[0] * target_side)
            second = plans[1][2][at] ^ (flip[1] * target_side)
            spots.append(pl.multiple_of(jnp.where(core == 0, first, second) * chunk, chunk))
        send[at] = full[pl.ds(spots[0], chunk)].astype(jnp.bfloat16)
        keep[at] = full[pl.ds(spots[1], chunk)]


def halve_body(plans, at, keep_in, came, send, keep):
    half = keep.shape[0]
    side = side_of(plans, at)
    for spot in range(half):
        mine, theirs = side * half + spot, (1 - side) * half + spot
        send[spot] = (keep_in[theirs] + came[theirs].astype(jnp.float32)).astype(jnp.bfloat16)
        keep[spot] = keep_in[mine] + came[mine].astype(jnp.float32)


def bit_of(value, bit):
    return lax.rem(lax.div(value, 1 << bit), 2)


def first_sides():
    core, shard = lax.rem(lax.axis_index("pipe"), 2), lax.axis_index("dp")
    low, high = bit_of(shard, 0), bit_of(shard, 1)
    return core, jnp.where(core == 0, low, high), jnp.where(core == 0, high, low)


def split_columns(wide, keep, send, chunk):
    core, side, _ = first_sides()
    for place in range(wide.shape[1] // (2 * chunk)):
        for target, at in ((keep, side), (send, 1 - side)):
            block = jnp.where(core == 0, 2 * place + at, place // 2 * 4 + 2 * at + place % 2)
            source = pl.ds(pl.multiple_of(block * chunk, chunk), chunk)
            target[:, place * chunk : (place + 1) * chunk] = wide[:, source]


def gather_rows(target, near, away):
    stage, _, _ = where_am_i(0)
    rows = target.shape[0] // 4
    for step, part in enumerate(near):

        @pl.when(stage == step)
        def _():
            target[:rows] = part[...]

    for at, part in enumerate(away):
        target[(at + 1) * rows : (at + 2) * rows] = part[...]


def early_body(stages, chunk, *refs):
    arrays, (keep_left, keep_right, send, wide) = refs[: stages + 3], refs[stages + 3 :]
    channels = wide.shape[1]
    flows, (side, far, cross) = arrays[:stages], arrays[stages:]
    for target, columns in ((wide, slice(0, channels)), (keep_right, slice(channels, None))):
        near = [flow.at[0, :, columns] for flow in flows]
        gather_rows(target, near, [side.at[:, columns], far.at[0, :, columns], cross.at[:, columns]])
    split_columns(wide, keep_left, send, chunk)
    send[:, channels // 2 :] = keep_right[...]


def late_body(stages, chunk, *refs):
    arrays, outs = refs[: stages + 3], refs[stages + 3 :]
    side, far, cross = arrays[stages:]
    gather_rows(outs[-1], [back.at[0] for back in arrays[:stages]], [side, far.at[0], cross])
    if chunk:
        split_columns(outs[2], outs[0], outs[1], chunk)


def half_gradient_body(left, left_came, right, right_came, send, keep, full):
    full[...] = contract(left[...], right[...], 0, 0) + contract(left_came[...], right_came[...], 0, 0)
    _, _, side = first_sides()
    chunk = send.shape[1]
    for place in range(send.shape[0]):
        theirs = pl.ds(pl.multiple_of((2 * place + 1 - side) * chunk, chunk), chunk)
        mine = pl.ds(pl.multiple_of((2 * place + side) * chunk, chunk), chunk)
        send[place] = full[theirs].astype(jnp.bfloat16)
        keep[place] = full[mine]


def next_body(bit, keep_in, came, send, keep):
    side = bit_of(lax.axis_index("dp"), bit)
    for place in range(keep.shape[0]):
        theirs, mine = 2 * place + 1 - side, 2 * place + side
        send[place] = (keep_in[theirs] + came[theirs].astype(jnp.float32)).astype(jnp.bfloat16)
        keep[place] = keep_in[mine] + came[mine].astype(jnp.float32)


def finish_body(keep_reduce, came_reduce, keep_expand, came_expand, out):
    out[0, 0] = keep_reduce[0] + came_reduce[0].astype(jnp.float32)
    out[0, 1] = keep_expand[0] + came_expand[0].astype(jnp.float32)


def shards(inputs, cotangent, reduce_weight, expand_weight):
    stages = lax.axis_size("pipe") // 2
    replicas = lax.axis_size("dp")
    stage, core, _ = where_am_i(0)
    channels, inner = reduce_weight.shape[2:]
    rows = inputs.shape[1] * inputs.shape[2] // 2
    sizes = (channels, inner)
    entering = inputs.reshape(2, 2, rows, channels)
    ending = cotangent.reshape(2, 2, rows, channels)
    own = [reduce_weight[:, 0], expand_weight[:, 0]]

    core_pairs = [(p, p ^ 1) for p in range(2 * stages)]
    mirror_pairs = [(p, 2 * (stages - 1 - p // 2) + p % 2) for p in range(2 * stages)]

    def hop(shard, step):
        pairs = []
        for c in range(2):
            pairs.append((2 * step + c, 2 * step + 2 + c))
            pairs.append((2 * (stages - 1 - step) + c, 2 * (stages - 2 - step) + c))
        return lax.ppermute(shard, "pipe", pairs)

    def swap_cores(shard):
        return lax.ppermute(shard, "pipe", core_pairs)

    def mirror(shard):
        return lax.ppermute(shard, "pipe", mirror_pairs)

    def pick(parts, at):
        chosen = parts[0]
        for step in range(1, stages):
            chosen = jnp.where(at == step, parts[step], chosen)
        return chosen

    mat = jax.ShapeDtypeStruct((channels, inner), jnp.bfloat16)
    line = jax.ShapeDtypeStruct((rows, channels), jnp.bfloat16)
    held_hbm = [pltpu.with_memory_space_constraint(a, pltpu.HBM) for a in (*own, entering, ending)]
    *held_hbm, ending = held_hbm
    *near, enter, turn_reduce, turn_expand = pl.pallas_call(
        functools.partial(prologue_body, stages),
        out_shape=[mat, mat, line, mat, mat],
        in_specs=[HBM] * 3,
        out_specs=[VMEM] * 5,
        scratch_shapes=[pltpu.SemaphoreType.DMA((5,))],
        compiler_params=PARAMS,
    )(*held_hbm)
    near += [swap_cores(weight) for weight in near]
    turn = [turn_reduce, turn_expand]
    turn += [swap_cores(weight) for weight in turn]
    if stages > 2:
        weights = own + [swap_cores(weight) for weight in own]
    flows, trunks, inners = [], [], []
    for step in range(stages - 1):
        flow, leave, trunk, inner_sum = run_stage(
            weights if step else near, step, True, False, step == 0, rows, sizes, enter
        )
        flows.append(flow)
        trunks.append(trunk)
        inners.append(inner_sum)
        enter = hop(leave, step)
    flow, upstreams, back_inners, leave = run_stage(
        turn, stages - 1, True, True, True, rows, sizes, enter, ending
    )
    flows.append(flow)
    upstreams, back_inners = [upstreams], [back_inners]
    upstream = hop(leave, 0)
    far_flow = mirror(pick(flows, stages - 1 - stage))
    for step in range(stages - 2, -1, -1):
        outs = run_stage(
            weights if step else near,
            step,
            False,
            True,
            step == 0,
            rows,
            sizes,
            upstream,
            trunks[step],
            inners[step],
        )
        upstreams.insert(0, outs[0])
        back_inners.insert(0, outs[1])
        if step:
            upstream = hop(outs[2], stages - 1 - step)
    far_up = mirror(pick(upstreams, stages - 1 - stage))
    far_inner = mirror(pick(back_inners, stages - 1 - stage))

    side_flow = swap_cores(pick(flows, stage)[1])
    side_up = swap_cores(pick(upstreams, stage)[1])
    side_inner = swap_cores(pick(back_inners, stage)[1])
    cross_flow = swap_cores(far_flow[1])
    cross_up = swap_cores(far_up[1])
    cross_inner = swap_cores(far_inner[1])

    chunk = channels // replicas
    fore = flows + [side_flow, far_flow, cross_flow]
    ups = upstreams + [side_up, far_up, cross_up]
    backs = back_inners + [side_inner, far_inner, cross_inner]
    halve = halve_rows if chunk % 128 == 0 and replicas >= 4 else halve_sums
    parts = halve(stages, replicas, chunk, sizes, rows, fore, ups, backs)
    return pl.pallas_call(
        finish_body,
        out_shape=jax.ShapeDtypeStruct((1, 2, chunk, inner), jnp.float32),
        in_specs=[VMEM] * 4,
        out_specs=VMEM,
        compiler_params=PARAMS,
    )(*parts)


def sums(count, chunk, inner):
    return [
        jax.ShapeDtypeStruct((count, chunk, inner), jnp.bfloat16),
        jax.ShapeDtypeStruct((count, chunk, inner), jnp.float32),
    ]


def exchange(shard, stages, replicas, first, second):
    pairs = []
    for p in range(2 * stages):
        for q in range(replicas):
            pairs.append((p * replicas + q, p * replicas + (q ^ (second if p % 2 else first))))
    return lax.ppermute(shard, AXES, pairs)


def halve_rows(stages, replicas, chunk, sizes, rows, fore, ups, backs):
    channels, inner = sizes
    shape = lambda *dims: jax.ShapeDtypeStruct(dims, jnp.bfloat16)
    half = shape(4 * rows, channels // 2)
    narrow = shape(4 * rows, inner)
    left, right, send = pl.pallas_call(
        functools.partial(early_body, stages, chunk),
        out_shape=[half, narrow, shape(4 * rows, channels // 2 + inner)],
        in_specs=[VMEM] * len(fore),
        out_specs=[VMEM] * 3,
        scratch_shapes=[pltpu.VMEM((4 * rows, channels), jnp.bfloat16)],
        compiler_params=PARAMS,
    )(*fore)
    came = exchange(send, stages, replicas, 1, 2)
    came_left, came_right = came[:, : channels // 2], came[:, channels // 2 :]
    back = pl.pallas_call(
        functools.partial(late_body, stages, 0),
        out_shape=narrow,
        in_specs=[VMEM] * len(backs),
        out_specs=VMEM,
        compiler_params=PARAMS,
    )(*backs)
    came_back = exchange(back, stages, replicas, 1, 2)
    up, up_send = pl.pallas_call(
        functools.partial(late_body, stages, chunk),
        out_shape=[half, half],
        in_specs=[VMEM] * len(ups),
        out_specs=[VMEM] * 2,
        scratch_shapes=[pltpu.VMEM((4 * rows, channels), jnp.bfloat16)],
        compiler_params=PARAMS,
    )(*ups)
    came_up = exchange(up_send, stages, replicas, 1, 2)
    parts = []
    for operands in ((left, came_left, back, came_back), (up, came_up, right, came_right)):
        count = replicas // 4
        send, keep = pl.pallas_call(
            half_gradient_body,
            out_shape=sums(count, chunk, inner),
            in_specs=[VMEM] * 4,
            out_specs=[VMEM] * 2,
            scratch_shapes=[pltpu.VMEM((channels // 2, inner), jnp.float32)],
            compiler_params=PARAMS,
        )(*operands)
        came = exchange(send, stages, replicas, 2, 1)
        for bit in range(2, replicas.bit_length() - 1):
            count //= 2
            send, keep = pl.pallas_call(
                functools.partial(next_body, bit),
                out_shape=sums(count, chunk, inner),
                in_specs=[VMEM] * 2,
                out_specs=[VMEM] * 2,
                compiler_params=PARAMS,
            )(keep, came)
            came = exchange(send, stages, replicas, 1 << bit, 1 << bit)
        parts += [keep, came]
    return parts


def halve_sums(stages, replicas, chunk, sizes, rows, fore, ups, backs):
    channels, inner = sizes
    wide, narrow = slice(0, channels), slice(channels, channels + inner)

    def of_flows(columns):
        def pick_parts(arrays):
            near = [flow.at[0, :, columns] for flow in arrays[:stages]]
            side, far, cross = arrays[stages : stages + 3]
            return near, [side.at[:, columns], far.at[0, :, columns], cross.at[:, columns]]

        return pick_parts

    def of_backs(arrays):
        near = [back.at[0] for back in arrays[stages + 3 : 2 * stages + 3]]
        side, far, cross = arrays[2 * stages + 3 : 2 * stages + 6]
        return near, [side, far.at[0], cross]

    plans = [halving_plan(replicas, turn) for turn in range(2)]
    streams = []
    for pick_left, pick_right, late, plan in (
        (of_backs, of_flows(narrow), ups, plans),
        (of_flows(wide), of_backs, backs, plans[::-1]),
    ):
        arrays = fore + late
        send, keep = pl.pallas_call(
            functools.partial(gradient_body, plan, pick_left, pick_right, len(arrays)),
            out_shape=sums(replicas // 2, chunk, inner),
            in_specs=[VMEM] * len(arrays),
            out_specs=[VMEM] * 2,
            scratch_shapes=[
                pltpu.VMEM((4 * rows, channels), jnp.bfloat16),
                pltpu.VMEM((4 * rows, inner), jnp.bfloat16),
                pltpu.VMEM((channels, inner), jnp.float32),
            ],
            compiler_params=PARAMS,
        )(*arrays)
        streams.append((plan, send, keep))
    for at in range(replicas.bit_length() - 1):
        half = replicas >> (at + 2)
        arrived = []
        for plan, send, keep in streams:
            pairs = []
            for p in range(2 * stages):
                for q in range(replicas):
                    pairs.append((p * replicas + q, p * replicas + (q ^ plan[p % 2][0][at])))
            arrived.append((plan, keep, lax.ppermute(send, AXES, pairs)))
        if half == 0:
            break
        streams = []
        for plan, keep, came in arrived:
            send, keep = pl.pallas_call(
                functools.partial(halve_body, plan, at + 1),
                out_shape=sums(half, chunk, inner),
                in_specs=[VMEM] * 2,
                out_specs=[VMEM] * 2,
                compiler_params=PARAMS,
            )(keep, came)
            streams.append((plan, send, keep))
    (_, keep_expand, came_expand), (_, keep_reduce, came_reduce) = arrived
    return keep_reduce, came_reduce, keep_expand, came_expand


def solution(mesh):
    return jax.shard_map(
        shards,
        mesh=mesh,
        in_specs=(
            P(None, None, "dp", None),
            P(None, None, "dp", None),
            P(None, "pipe", None, None),
            P(None, "pipe", None, None),
        ),
        out_specs=P("pipe", None, "dp", None),
        check_vma=False,
    )
```

```python
import functools

import jax
import jax.numpy as jnp
from jax import lax
from jax.experimental import pallas as pl
from jax.experimental.pallas import tpu as pltpu
from jax.sharding import PartitionSpec as P


EPSILON = 1e-06
AXES = ("pipe", "dp")
HBM = pl.BlockSpec(memory_space=pltpu.HBM)
ANY = pl.BlockSpec(memory_space=pl.ANY)
VMEM = pl.BlockSpec(memory_space=pltpu.VMEM)
PARAMS = pltpu.CompilerParams(vmem_limit_bytes=16 << 20)


def contract(first_op, second_op, first_dim, second_dim):
    return lax.dot_general(
        first_op,
        second_op,
        (((first_dim,), (second_dim,)), ((), ())),
        preferred_element_type=jnp.float32,
    )


def smooth_slope(values):
    sigma = jax.nn.sigmoid(values)
    return sigma * (1.0 + values * (1.0 - sigma))


def norm_of(widened):
    return lax.rsqrt(jnp.mean(widened * widened, axis=-1, keepdims=True) + EPSILON)


def where_am_i(step):
    position = lax.axis_index("pipe")
    stage, core = lax.div(position, 2), lax.rem(position, 2)
    way = jnp.where(stage == step, 0, 1)
    return stage, core, way


def bring_all(sources, outs, sems):
    copies = [
        pltpu.make_async_copy(source, out, sems.at[at])
        for at, (source, out) in enumerate(zip(sources, outs))
    ]
    for copy in copies:
        copy.start()
    return copies


def load_body(step, reduce_all, expand_all, *refs):
    _, core, way = where_am_i(step)
    sources, outs = [reduce_all.at[way], expand_all.at[way]], refs[:-1]
    if step == 0:
        sources.append(refs[0].at[way, core])
        outs = outs[1:]
    for copy in bring_all(sources, outs, refs[-1]):
        copy.wait()


def load(step, own, *more):
    channels, inner = own[0].shape[1:]
    mat = jax.ShapeDtypeStruct((channels, inner), jnp.bfloat16)
    outs = [mat, mat] + [jax.ShapeDtypeStruct(a.shape[2:], a.dtype) for a in more]
    return pl.pallas_call(
        functools.partial(load_body, step),
        out_shape=outs,
        in_specs=[HBM] * (2 + len(more)),
        out_specs=[VMEM] * len(outs),
        scratch_shapes=[pltpu.SemaphoreType.DMA((len(outs),))],
        compiler_params=PARAMS,
    )(*own, *more)


def meanwhile_body(step, mirrored, expand_own, expand_other, inputs, cotangent, leave, *refs):
    outs, sems = refs[:-1], refs[-1]
    stage, core, way = where_am_i(step)
    ending, back_active = outs[:2]
    sources = [cotangent.at[way, core]]
    if mirrored:
        sources += [cotangent.at[1, core], inputs.at[1, core]]
    copies = bring_all(sources, [outs[0]] + list(outs[2:]), sems)
    copies[0].wait()

    @pl.when(way == core)
    def _():
        back_active[...] = jnp.dot(
            ending[...], expand_other[...], preferred_element_type=jnp.float32
        )

    @pl.when(way != core)
    def _():
        back_active[...] = jnp.dot(ending[...], expand_own[...], preferred_element_type=jnp.float32)

    for copy in copies[1:]:
        copy.wait()
    if mirrored:
        rows = outs[3]

        @pl.when(stage != 0)
        def _():
            rows[...] = leave[...]

        widened = rows[...].astype(jnp.float32)
        rows[...] = jax.nn.silu(widened * norm_of(widened)).astype(jnp.bfloat16)


def weight_copies(own, other, held, sems, core, way):
    copies = []
    for order in range(2):
        is_own = lax.rem(way + order, 2) == core
        for kind in range(2):
            mine = pltpu.make_async_copy(own[kind].at[way], held[kind].at[order], sems.at[kind, order])
            theirs = pltpu.make_async_copy(
                other[kind].at[way], held[kind].at[order], sems.at[kind, order]
            )
            copies.append((is_own, mine, theirs))
    return copies


def start_all(copies):
    for is_own, mine, theirs in copies:
        pl.when(is_own)(mine.start)
        pl.when(jnp.logical_not(is_own))(theirs.start)


def stage_body(step, forward, backward, last, near, *refs):
    refs = list(refs)
    _, core, way = where_am_i(step)
    own, other = (refs.pop(0), refs.pop(0)), (refs.pop(0), refs.pop(0))
    enter = refs.pop(0) if forward else None
    upstream_in = refs.pop(0) if backward else None
    first_active = refs.pop(0) if forward and backward else None
    if not forward:
        trunks, inners = refs.pop(0), refs.pop(0)
    if forward:
        flows = refs.pop(0)
    if forward and not backward:
        leave = refs.pop(0)
    if backward:
        upstreams, back_inners = refs.pop(0), refs.pop(0)
    if backward and not last:
        back_leave = refs.pop(0)
    if forward:
        trunks, inners = refs.pop(0), refs.pop(0)
    channels = trunks.shape[2]

    def run(reduce_mats, expand_mats, wait):
        if forward:
            rows = enter[...]
            for order in range(2):
                slot = lax.rem(order + core, 2)
                widened = rows.astype(jnp.float32)
                normed = widened * norm_of(widened)
                lifted = jax.nn.silu(normed).astype(jnp.bfloat16)
                trunks[order] = rows
                flows[slot, :, :channels] = lifted
                wait(0, order)
                inner_sum = jnp.dot(
                    lifted, reduce_mats[order][...], preferred_element_type=jnp.float32
                )
                active = jax.nn.silu(inner_sum).astype(jnp.bfloat16)
                inners[order] = inner_sum
                flows[slot, :, channels:] = active
                wait(1, order)
                rows = (widened + contract(active, expand_mats[order][...], 1, 1)).astype(jnp.bfloat16)
            if not backward:
                leave[...] = rows
        if backward:
            upstream = upstream_in[...]
            for order in (1, 0):
                slot = lax.rem(order + core, 2)
                upstreams[slot] = upstream
                if not forward:
                    wait(1, order)
                if forward and order:
                    back_active = first_active[...]
                else:
                    back_active = jnp.dot(
                        upstream, expand_mats[order][...], preferred_element_type=jnp.float32
                    )
                back_inner = (back_active * smooth_slope(inners[order])).astype(jnp.bfloat16)
                back_inners[slot] = back_inner
                if not forward:
                    wait(0, order)
                if last and order == 0:
                    break
                back_lifted = contract(back_inner, reduce_mats[order][...], 1, 1)
                widened = trunks[order].astype(jnp.float32)
                norm_scale = norm_of(widened)
                back_normed = back_lifted * smooth_slope(widened * norm_scale)
                projection = jnp.mean(back_normed * widened, axis=-1, keepdims=True)
                upstream = (
                    upstream.astype(jnp.float32)
                    + norm_scale * back_normed
                    - widened * norm_scale**3 * projection
                ).astype(jnp.bfloat16)
            if not last:
                back_leave[...] = upstream

    if near:
        idle = lambda kind, order: None

        @pl.when(way == core)
        def _():
            run((own[0], other[0]), (own[1], other[1]), idle)

        @pl.when(way != core)
        def _():
            run((other[0], own[0]), (other[1], own[1]), idle)

    else:
        held = (refs.pop(0), refs.pop(0))
        copies = weight_copies(own, other, held, refs.pop(0), core, way)
        start_all(copies if forward else copies[2:] + copies[:2])
        run(
            [held[0].at[order] for order in range(2)],
            [held[1].at[order] for order in range(2)],
            lambda kind, order: copies[2 * order + kind][1].wait(),
        )


def run_stage(weights, step, forward, backward, near, rows, sizes, *arrays):
    channels, inner = sizes
    last = backward and step == 0 and not forward
    shape = lambda dtype, *dims: jax.ShapeDtypeStruct(dims, dtype)
    line = shape(jnp.bfloat16, rows, channels)
    kept = [((2, rows, channels), jnp.bfloat16), ((2, rows, inner), jnp.float32)]
    outs, scratch = [], []
    if forward:
        outs.append(shape(jnp.bfloat16, 2, rows, channels + inner))
    if forward and not backward:
        outs.append(line)
    if backward:
        outs.append(shape(jnp.bfloat16, 2, rows, channels))
        outs.append(shape(jnp.bfloat16, 2, rows, inner))
    if backward and not last:
        outs.append(line)
    if forward and not backward:
        outs += [jax.ShapeDtypeStruct(*one) for one in kept]
    if forward and backward:
        scratch += [pltpu.VMEM(*one) for one in kept]
    if not near:
        scratch += [pltpu.VMEM((2, channels, inner), jnp.bfloat16)] * 2
        scratch += [pltpu.SemaphoreType.DMA((2, 2))]
    passes = 4 * (int(forward) + int(backward))
    return pl.pallas_call(
        functools.partial(stage_body, step, forward, backward, last, near),
        out_shape=outs,
        in_specs=[VMEM if near else ANY] * 4 + [VMEM] * len(arrays),
        out_specs=[VMEM] * len(outs),
        scratch_shapes=scratch,
        compiler_params=PARAMS,
        cost_estimate=pl.CostEstimate(
            flops=2 * passes * rows * channels * inner,
            bytes_accessed=8 * channels * inner,
            transcendentals=passes * rows * channels,
        ),
    )(*weights, *arrays)


def parity(value, mask):
    total, bit = 0, 0
    while mask >> bit:
        if mask >> bit & 1:
            total = total + lax.rem(lax.div(value, 1 << bit), 2)
        bit += 1
    return lax.rem(total, 2)


def halving_plan(size, turn):
    order = [1 << bit for bit in range(size.bit_length() - 1)]
    if turn and len(order) > 1:
        order[:2] = order[1::-1]
    table = [0] * size
    for chunk in range(size):
        place = 0
        for mask in order:
            place = 2 * place + int(chunk & mask != 0)
        table[place] = chunk
    return order, order, table


def side_of(plans, at):
    core, shard = lax.rem(lax.axis_index("pipe"), 2), lax.axis_index("dp")
    return jnp.where(core == 0, parity(shard, plans[0][1][at]), parity(shard, plans[1][1][at]))


def gradient_body(plans, pick_left, pick_right, count, *refs):
    arrays, (send, keep, left, right, full) = refs[:count], refs[count:]
    stage, core, _ = where_am_i(0)
    rows = left.shape[0] // 4
    chunk = send.shape[1]
    for target, pick in ((left, pick_left), (right, pick_right)):
        near, away = pick(arrays)
        for step, part in enumerate(near):

            @pl.when(stage == step)
            def _():
                target[:rows] = part[...]

        for at, part in enumerate(away):
            target[(at + 1) * rows : (at + 2) * rows] = part[...]
    full[...] = contract(left[...], right[...], 0, 0)
    side = side_of(plans, 0)
    half = send.shape[0]
    flip = [plan[2][half] for plan in plans]
    for at in range(half):
        spots = []
        for target_side in (1 - side, side):
            first = plans[0][2][at] ^ (flip[0] * target_side)
            second = plans[1][2][at] ^ (flip[1] * target_side)
            spots.append(pl.multiple_of(jnp.where(core == 0, first, second) * chunk, chunk))
        send[at] = full[pl.ds(spots[0], chunk)].astype(jnp.bfloat16)
        keep[at] = full[pl.ds(spots[1], chunk)]


def halve_body(plans, at, keep_in, came, send, keep):
    half = keep.shape[0]
    side = side_of(plans, at)
    for spot in range(half):
        mine, theirs = side * half + spot, (1 - side) * half + spot
        send[spot] = (keep_in[theirs] + came[theirs].astype(jnp.float32)).astype(jnp.bfloat16)
        keep[spot] = keep_in[mine] + came[mine].astype(jnp.float32)


def bit_of(value, bit):
    return lax.rem(lax.div(value, 1 << bit), 2)


def first_sides():
    core, shard = lax.rem(lax.axis_index("pipe"), 2), lax.axis_index("dp")
    low, high = bit_of(shard, 0), bit_of(shard, 1)
    return core, jnp.where(core == 0, low, high), jnp.where(core == 0, high, low)


def split_columns(wide, keep, send, chunk):
    core, side, _ = first_sides()
    for place in range(wide.shape[1] // (2 * chunk)):
        for target, at in ((keep, side), (send, 1 - side)):
            block = jnp.where(core == 0, 2 * place + at, place // 2 * 4 + 2 * at + place % 2)
            source = pl.ds(pl.multiple_of(block * chunk, chunk), chunk)
            target[:, place * chunk : (place + 1) * chunk] = wide[:, source]


def gather_rows(target, near, away):
    stage, _, _ = where_am_i(0)
    rows = target.shape[0] // 4
    for step, part in enumerate(near):

        @pl.when(stage == step)
        def _():
            target[:rows] = part[...]

    for at, part in enumerate(away):
        target[(at + 1) * rows : (at + 2) * rows] = part[...]


def early_body(stages, chunk, *refs):
    arrays, (keep_left, keep_right, send, wide) = refs[: stages + 3], refs[stages + 3 :]
    channels = wide.shape[1]
    flows, (side, far, cross) = arrays[:stages], arrays[stages:]
    for target, columns in ((wide, slice(0, channels)), (keep_right, slice(channels, None))):
        near = [flow.at[0, :, columns] for flow in flows]
        gather_rows(target, near, [side.at[:, columns], far.at[:, columns], cross.at[:, columns]])
    split_columns(wide, keep_left, send, chunk)
    send[:, channels // 2 :] = keep_right[...]


def late_body(stages, chunk, *refs):
    arrays, outs = refs[: stages + 3], refs[stages + 3 :]
    side, far, cross = arrays[stages:]
    gather_rows(outs[-1], [back.at[0] for back in arrays[:stages]], [side, far, cross])
    if chunk:
        split_columns(outs[2], outs[0], outs[1], chunk)


def half_gradient_body(left, left_came, right, right_came, send, keep, full):
    full[...] = contract(left[...], right[...], 0, 0) + contract(left_came[...], right_came[...], 0, 0)
    _, _, side = first_sides()
    chunk = send.shape[1]
    for place in range(send.shape[0]):
        theirs = pl.ds(pl.multiple_of((2 * place + 1 - side) * chunk, chunk), chunk)
        mine = pl.ds(pl.multiple_of((2 * place + side) * chunk, chunk), chunk)
        send[place] = full[theirs].astype(jnp.bfloat16)
        keep[place] = full[mine]


def next_body(bit, keep_in, came, send, keep):
    side = bit_of(lax.axis_index("dp"), bit)
    for place in range(keep.shape[0]):
        theirs, mine = 2 * place + 1 - side, 2 * place + side
        send[place] = (keep_in[theirs] + came[theirs].astype(jnp.float32)).astype(jnp.bfloat16)
        keep[place] = keep_in[mine] + came[mine].astype(jnp.float32)


def finish_body(keep_reduce, came_reduce, keep_expand, came_expand, out):
    out[0, 0] = keep_reduce[0] + came_reduce[0].astype(jnp.float32)
    out[0, 1] = keep_expand[0] + came_expand[0].astype(jnp.float32)


def shards(inputs, cotangent, reduce_weight, expand_weight):
    stages = lax.axis_size("pipe") // 2
    replicas = lax.axis_size("dp")
    stage, core, _ = where_am_i(0)
    channels, inner = reduce_weight.shape[2:]
    rows = inputs.shape[1] * inputs.shape[2] // 2
    sizes = (channels, inner)
    entering = inputs.reshape(2, 2, rows, channels)
    ending = cotangent.reshape(2, 2, rows, channels)
    own = [reduce_weight[:, 0], expand_weight[:, 0]]

    core_pairs = [(p, p ^ 1) for p in range(2 * stages)]
    mirror_pairs = [(p, 2 * (stages - 1 - p // 2) + p % 2) for p in range(2 * stages)]

    def hop(shard, step):
        pairs = []
        for c in range(2):
            pairs.append((2 * step + c, 2 * step + 2 + c))
            pairs.append((2 * (stages - 1 - step) + c, 2 * (stages - 2 - step) + c))
        return lax.ppermute(shard, "pipe", pairs)

    def swap_cores(shard):
        return lax.ppermute(shard, "pipe", core_pairs)

    def mirror(shard):
        return lax.ppermute(shard, "pipe", mirror_pairs)

    def pick(parts, at):
        chosen = parts[0]
        for step in range(1, stages):
            chosen = jnp.where(at == step, parts[step], chosen)
        return chosen

    in_hbm = lambda array: pltpu.with_memory_space_constraint(array, pltpu.HBM)
    own, entering, ending = [in_hbm(one) for one in own], in_hbm(entering), in_hbm(ending)
    *near, enter = load(0, own, entering)
    near += [swap_cores(weight) for weight in near]
    turn = list(load(stages - 1, own))
    turn += [swap_cores(weight) for weight in turn]
    if stages > 2:
        weights = own + [swap_cores(weight) for weight in own]
    flows, trunks, inners = [], [], []
    for step in range(stages - 1):
        flow, leave, trunk, inner_sum = run_stage(
            weights if step else near, step, True, False, step == 0, rows, sizes, enter
        )
        flows.append(flow)
        trunks.append(trunk)
        inners.append(inner_sum)
        enter = hop(leave, step)
    mirrored = stages == 2
    line = jax.ShapeDtypeStruct((rows, channels), jnp.bfloat16)
    outs = [line, jax.ShapeDtypeStruct((rows, inner), jnp.float32)] + [line, line] * mirrored
    ending, first_active, *known = pl.pallas_call(
        functools.partial(meanwhile_body, stages - 1, mirrored),
        out_shape=outs,
        in_specs=[VMEM, VMEM, HBM, HBM, VMEM],
        out_specs=[VMEM] * len(outs),
        scratch_shapes=[pltpu.SemaphoreType.DMA((3,))],
        compiler_params=PARAMS,
    )(turn[1], turn[3], entering, ending, leave)
    flow, upstreams, back_inners, leave = run_stage(
        turn, stages - 1, True, True, True, rows, sizes, enter, ending, first_active
    )
    flows.append(flow)
    upstreams, back_inners = [upstreams], [back_inners]
    upstream = hop(leave, 0)
    away = stages - 1 - stage
    side_flow = swap_cores(pick(flows, stage)[1])
    near_core = lambda first, second: jnp.where(core == 0, first, second)
    going = pick(flows, away)
    if mirrored:
        lifted = near_core(going[1, :, :channels], going[0, :, :channels])
        going = jnp.concatenate([lifted, going[0, :, channels:], going[1, :, channels:]], axis=1)
    far_flow = mirror(going)
    if mirrored:
        lifted, actives = far_flow[:, :channels], far_flow[:, channels:]
        far_flow = jnp.concatenate([near_core(known[1], lifted), actives[:, :inner]], axis=1)
        cross_flow = jnp.concatenate([near_core(lifted, known[1]), actives[:, inner:]], axis=1)
    else:
        far_flow, cross_flow = far_flow[0], far_flow[1]
    cross_flow = swap_cores(cross_flow)
    for step in range(stages - 2, -1, -1):
        outs = run_stage(
            weights if step else near,
            step,
            False,
            True,
            step == 0,
            rows,
            sizes,
            upstream,
            trunks[step],
            inners[step],
        )
        upstreams.insert(0, outs[0])
        back_inners.insert(0, outs[1])
        if step:
            upstream = hop(outs[2], stages - 1 - step)
    going = pick(upstreams, away)
    far_up = mirror(near_core(going[0], going[1]) if mirrored else going)
    far_inner = mirror(pick(back_inners, away))
    side_up = swap_cores(pick(upstreams, stage)[1])
    side_inner = swap_cores(pick(back_inners, stage)[1])
    if mirrored:
        top = jnp.where(stage == 0, leave, known[0])
        far_up, cross_up = near_core(far_up, top), near_core(top, far_up)
    else:
        far_up, cross_up = far_up[0], far_up[1]
    cross_up = swap_cores(cross_up)
    cross_inner = swap_cores(far_inner[1])
    far_inner = far_inner[0]

    chunk = channels // replicas
    fore = flows + [side_flow, far_flow, cross_flow]
    ups = upstreams + [side_up, far_up, cross_up]
    backs = back_inners + [side_inner, far_inner, cross_inner]
    halve = halve_rows if chunk % 128 == 0 and replicas >= 4 else halve_sums
    parts = halve(stages, replicas, chunk, sizes, rows, fore, ups, backs)
    return pl.pallas_call(
        finish_body,
        out_shape=jax.ShapeDtypeStruct((1, 2, chunk, inner), jnp.float32),
        in_specs=[VMEM] * 4,
        out_specs=VMEM,
        compiler_params=PARAMS,
    )(*parts)


def sums(count, chunk, inner):
    return [
        jax.ShapeDtypeStruct((count, chunk, inner), jnp.bfloat16),
        jax.ShapeDtypeStruct((count, chunk, inner), jnp.float32),
    ]


def exchange(shard, stages, replicas, first, second):
    pairs = []
    for p in range(2 * stages):
        for q in range(replicas):
            pairs.append((p * replicas + q, p * replicas + (q ^ (second if p % 2 else first))))
    return lax.ppermute(shard, AXES, pairs)


def halve_rows(stages, replicas, chunk, sizes, rows, fore, ups, backs):
    channels, inner = sizes
    shape = lambda *dims: jax.ShapeDtypeStruct(dims, jnp.bfloat16)
    half = shape(4 * rows, channels // 2)
    narrow = shape(4 * rows, inner)
    left, right, send = pl.pallas_call(
        functools.partial(early_body, stages, chunk),
        out_shape=[half, narrow, shape(4 * rows, channels // 2 + inner)],
        in_specs=[VMEM] * len(fore),
        out_specs=[VMEM] * 3,
        scratch_shapes=[pltpu.VMEM((4 * rows, channels), jnp.bfloat16)],
        compiler_params=PARAMS,
    )(*fore)
    came = exchange(send, stages, replicas, 1, 2)
    came_left, came_right = came[:, : channels // 2], came[:, channels // 2 :]
    back = pl.pallas_call(
        functools.partial(late_body, stages, 0),
        out_shape=narrow,
        in_specs=[VMEM] * len(backs),
        out_specs=VMEM,
        compiler_params=PARAMS,
    )(*backs)
    came_back = exchange(back, stages, replicas, 1, 2)
    up, up_send = pl.pallas_call(
        functools.partial(late_body, stages, chunk),
        out_shape=[half, half],
        in_specs=[VMEM] * len(ups),
        out_specs=[VMEM] * 2,
        scratch_shapes=[pltpu.VMEM((4 * rows, channels), jnp.bfloat16)],
        compiler_params=PARAMS,
    )(*ups)
    came_up = exchange(up_send, stages, replicas, 1, 2)
    parts = []
    for operands in ((left, came_left, back, came_back), (up, came_up, right, came_right)):
        count = replicas // 4
        send, keep = pl.pallas_call(
            half_gradient_body,
            out_shape=sums(count, chunk, inner),
            in_specs=[VMEM] * 4,
            out_specs=[VMEM] * 2,
            scratch_shapes=[pltpu.VMEM((channels // 2, inner), jnp.float32)],
            compiler_params=PARAMS,
        )(*operands)
        came = exchange(send, stages, replicas, 2, 1)
        for bit in range(2, replicas.bit_length() - 1):
            count //= 2
            send, keep = pl.pallas_call(
                functools.partial(next_body, bit),
                out_shape=sums(count, chunk, inner),
                in_specs=[VMEM] * 2,
                out_specs=[VMEM] * 2,
                compiler_params=PARAMS,
            )(keep, came)
            came = exchange(send, stages, replicas, 1 << bit, 1 << bit)
        parts += [keep, came]
    return parts


def halve_sums(stages, replicas, chunk, sizes, rows, fore, ups, backs):
    channels, inner = sizes
    wide, narrow = slice(0, channels), slice(channels, channels + inner)

    def of_flows(columns):
        def pick_parts(arrays):
            near = [flow.at[0, :, columns] for flow in arrays[:stages]]
            side, far, cross = arrays[stages : stages + 3]
            return near, [side.at[:, columns], far.at[:, columns], cross.at[:, columns]]

        return pick_parts

    def of_backs(arrays):
        near = [back.at[0] for back in arrays[stages + 3 : 2 * stages + 3]]
        side, far, cross = arrays[2 * stages + 3 : 2 * stages + 6]
        return near, [side, far, cross]

    plans = [halving_plan(replicas, turn) for turn in range(2)]
    streams = []
    for pick_left, pick_right, late, plan in (
        (of_backs, of_flows(narrow), ups, plans),
        (of_flows(wide), of_backs, backs, plans[::-1]),
    ):
        arrays = fore + late
        send, keep = pl.pallas_call(
            functools.partial(gradient_body, plan, pick_left, pick_right, len(arrays)),
            out_shape=sums(replicas // 2, chunk, inner),
            in_specs=[VMEM] * len(arrays),
            out_specs=[VMEM] * 2,
            scratch_shapes=[
                pltpu.VMEM((4 * rows, channels), jnp.bfloat16),
                pltpu.VMEM((4 * rows, inner), jnp.bfloat16),
                pltpu.VMEM((channels, inner), jnp.float32),
            ],
            compiler_params=PARAMS,
        )(*arrays)
        streams.append((plan, send, keep))
    for at in range(replicas.bit_length() - 1):
        half = replicas >> (at + 2)
        arrived = []
        for plan, send, keep in streams:
            pairs = []
            for p in range(2 * stages):
                for q in range(replicas):
                    pairs.append((p * replicas + q, p * replicas + (q ^ plan[p % 2][0][at])))
            arrived.append((plan, keep, lax.ppermute(send, AXES, pairs)))
        if half == 0:
            break
        streams = []
        for plan, keep, came in arrived:
            send, keep = pl.pallas_call(
                functools.partial(halve_body, plan, at + 1),
                out_shape=sums(half, chunk, inner),
                in_specs=[VMEM] * 2,
                out_specs=[VMEM] * 2,
                compiler_params=PARAMS,
            )(keep, came)
            streams.append((plan, send, keep))
    (_, keep_expand, came_expand), (_, keep_reduce, came_reduce) = arrived
    return keep_reduce, came_reduce, keep_expand, came_expand


def solution(mesh):
    return jax.shard_map(
        shards,
        mesh=mesh,
        in_specs=(
            P(None, None, "dp", None),
            P(None, None, "dp", None),
            P(None, "pipe", None, None),
            P(None, "pipe", None, None),
        ),
        out_specs=P("pipe", None, "dp", None),
        check_vma=False,
    )
```

```python
import functools

import jax
import jax.numpy as jnp
from jax import lax
from jax.experimental import pallas as pl
from jax.experimental.pallas import tpu as pltpu
from jax.sharding import PartitionSpec as P


EPSILON = 1e-06
AXES = ("pipe", "dp")
HBM = pl.BlockSpec(memory_space=pltpu.HBM)
ANY = pl.BlockSpec(memory_space=pl.ANY)
VMEM = pl.BlockSpec(memory_space=pltpu.VMEM)
PARAMS = pltpu.CompilerParams(vmem_limit_bytes=16 << 20)


def contract(first_op, second_op, first_dim, second_dim):
    return lax.dot_general(
        first_op,
        second_op,
        (((first_dim,), (second_dim,)), ((), ())),
        preferred_element_type=jnp.float32,
    )


def smooth_slope(values):
    sigma = jax.nn.sigmoid(values)
    return sigma * (1.0 + values * (1.0 - sigma))


def norm_of(widened):
    return lax.rsqrt(jnp.mean(widened * widened, axis=-1, keepdims=True) + EPSILON)


def where_am_i(step):
    position = lax.axis_index("pipe")
    stage, core = lax.div(position, 2), lax.rem(position, 2)
    way = jnp.where(stage == step, 0, 1)
    return stage, core, way


def bring_all(sources, outs, sems):
    copies = [
        pltpu.make_async_copy(source, out, sems.at[at])
        for at, (source, out) in enumerate(zip(sources, outs))
    ]
    for copy in copies:
        copy.start()
    return copies


def load_body(step, reduce_all, expand_all, *refs):
    _, core, way = where_am_i(step)
    sources, outs = [reduce_all.at[way], expand_all.at[way]], refs[:-1]
    if step == 0:
        sources.append(refs[0].at[way, core])
        outs = outs[1:]
    for copy in bring_all(sources, outs, refs[-1]):
        copy.wait()


def load(step, own, *more):
    channels, inner = own[0].shape[1:]
    mat = jax.ShapeDtypeStruct((channels, inner), jnp.bfloat16)
    outs = [mat, mat] + [jax.ShapeDtypeStruct(a.shape[2:], a.dtype) for a in more]
    return pl.pallas_call(
        functools.partial(load_body, step),
        out_shape=outs,
        in_specs=[HBM] * (2 + len(more)),
        out_specs=[VMEM] * len(outs),
        scratch_shapes=[pltpu.SemaphoreType.DMA((len(outs),))],
        compiler_params=PARAMS,
    )(*own, *more)


def meanwhile_body(step, mirrored, expand_own, expand_other, inputs, cotangent, leave, *refs):
    outs, sems = refs[:-1], refs[-1]
    stage, core, way = where_am_i(step)
    ending, back_active = outs[:2]
    sources = [cotangent.at[way, core]]
    if mirrored:
        sources += [cotangent.at[1, core], inputs.at[1, core]]
    copies = bring_all(sources, [outs[0]] + list(outs[2:]), sems)
    copies[0].wait()

    @pl.when(way == core)
    def _():
        back_active[...] = jnp.dot(
            ending[...], expand_other[...], preferred_element_type=jnp.float32
        )

    @pl.when(way != core)
    def _():
        back_active[...] = jnp.dot(ending[...], expand_own[...], preferred_element_type=jnp.float32)

    for copy in copies[1:]:
        copy.wait()
    if mirrored:
        rows = outs[3]

        @pl.when(stage != 0)
        def _():
            rows[...] = leave[...]

        widened = rows[...].astype(jnp.float32)
        rows[...] = jax.nn.silu(widened * norm_of(widened)).astype(jnp.bfloat16)


def weight_copies(own, other, held, sems, core, way):
    copies = []
    for order in range(2):
        is_own = lax.rem(way + order, 2) == core
        for kind in range(2):
            mine = pltpu.make_async_copy(own[kind].at[way], held[kind].at[order], sems.at[kind, order])
            theirs = pltpu.make_async_copy(
                other[kind].at[way], held[kind].at[order], sems.at[kind, order]
            )
            copies.append((is_own, mine, theirs))
    return copies


def start_all(copies):
    for is_own, mine, theirs in copies:
        pl.when(is_own)(mine.start)
        pl.when(jnp.logical_not(is_own))(theirs.start)


def stage_body(step, forward, backward, last, near, *refs):
    refs = list(refs)
    _, core, way = where_am_i(step)
    own, other = (refs.pop(0), refs.pop(0)), (refs.pop(0), refs.pop(0))
    enter = refs.pop(0) if forward else None
    upstream_in = refs.pop(0) if backward else None
    first_active = refs.pop(0) if forward and backward else None
    if not forward:
        trunks, inners = refs.pop(0), refs.pop(0)
    if forward:
        flows = refs.pop(0)
    if forward and not backward:
        leave = refs.pop(0)
    if backward:
        upstreams, back_inners = refs.pop(0), refs.pop(0)
    if backward and not last:
        back_leave = refs.pop(0)
    if forward:
        trunks, inners = refs.pop(0), refs.pop(0)
    channels = trunks.shape[2]

    def run(reduce_mats, expand_mats, wait):
        if forward:
            rows = enter[...]
            for order in range(2):
                slot = lax.rem(order + core, 2)
                widened = rows.astype(jnp.float32)
                normed = widened * norm_of(widened)
                lifted = jax.nn.silu(normed).astype(jnp.bfloat16)
                trunks[order] = rows
                flows[slot, :, :channels] = lifted
                wait(0, order)
                inner_sum = jnp.dot(
                    lifted, reduce_mats[order][...], preferred_element_type=jnp.float32
                )
                active = jax.nn.silu(inner_sum).astype(jnp.bfloat16)
                inners[order] = inner_sum
                flows[slot, :, channels:] = active
                wait(1, order)
                rows = (widened + contract(active, expand_mats[order][...], 1, 1)).astype(jnp.bfloat16)
            if not backward:
                leave[...] = rows
        if backward:
            upstream = upstream_in[...]
            for order in (1, 0):
                slot = lax.rem(order + core, 2)
                upstreams[slot] = upstream
                if not forward:
                    wait(1, order)
                if forward and order:
                    back_active = first_active[...]
                else:
                    back_active = jnp.dot(
                        upstream, expand_mats[order][...], preferred_element_type=jnp.float32
                    )
                back_inner = (back_active * smooth_slope(inners[order])).astype(jnp.bfloat16)
                back_inners[slot] = back_inner
                if not forward:
                    wait(0, order)
                if last and order == 0:
                    break
                back_lifted = contract(back_inner, reduce_mats[order][...], 1, 1)
                widened = trunks[order].astype(jnp.float32)
                norm_scale = norm_of(widened)
                back_normed = back_lifted * smooth_slope(widened * norm_scale)
                projection = jnp.mean(back_normed * widened, axis=-1, keepdims=True)
                upstream = (
                    upstream.astype(jnp.float32)
                    + norm_scale * back_normed
                    - widened * norm_scale**3 * projection
                ).astype(jnp.bfloat16)
            if not last:
                back_leave[...] = upstream

    if near:
        idle = lambda kind, order: None

        @pl.when(way == core)
        def _():
            run((own[0], other[0]), (own[1], other[1]), idle)

        @pl.when(way != core)
        def _():
            run((other[0], own[0]), (other[1], own[1]), idle)

    else:
        held = (refs.pop(0), refs.pop(0))
        copies = weight_copies(own, other, held, refs.pop(0), core, way)
        start_all(copies if forward else copies[2:] + copies[:2])
        run(
            [held[0].at[order] for order in range(2)],
            [held[1].at[order] for order in range(2)],
            lambda kind, order: copies[2 * order + kind][1].wait(),
        )


def run_stage(weights, step, forward, backward, near, rows, sizes, *arrays):
    channels, inner = sizes
    last = backward and step == 0 and not forward
    shape = lambda dtype, *dims: jax.ShapeDtypeStruct(dims, dtype)
    line = shape(jnp.bfloat16, rows, channels)
    kept = [((2, rows, channels), jnp.bfloat16), ((2, rows, inner), jnp.float32)]
    outs, scratch = [], []
    if forward:
        outs.append(shape(jnp.bfloat16, 2, rows, channels + inner))
    if forward and not backward:
        outs.append(line)
    if backward:
        outs.append(shape(jnp.bfloat16, 2, rows, channels))
        outs.append(shape(jnp.bfloat16, 2, rows, inner))
    if backward and not last:
        outs.append(line)
    if forward and not backward:
        outs += [jax.ShapeDtypeStruct(*one) for one in kept]
    if forward and backward:
        scratch += [pltpu.VMEM(*one) for one in kept]
    if not near:
        scratch += [pltpu.VMEM((2, channels, inner), jnp.bfloat16)] * 2
        scratch += [pltpu.SemaphoreType.DMA((2, 2))]
    passes = 4 * (int(forward) + int(backward))
    return pl.pallas_call(
        functools.partial(stage_body, step, forward, backward, last, near),
        out_shape=outs,
        in_specs=[VMEM if near else ANY] * 4 + [VMEM] * len(arrays),
        out_specs=[VMEM] * len(outs),
        scratch_shapes=scratch,
        compiler_params=PARAMS,
        cost_estimate=pl.CostEstimate(
            flops=2 * passes * rows * channels * inner,
            bytes_accessed=8 * channels * inner,
            transcendentals=passes * rows * channels,
        ),
    )(*weights, *arrays)


def parity(value, mask):
    total, bit = 0, 0
    while mask >> bit:
        if mask >> bit & 1:
            total = total + lax.rem(lax.div(value, 1 << bit), 2)
        bit += 1
    return lax.rem(total, 2)


def halving_plan(size, turn):
    order = [1 << bit for bit in range(size.bit_length() - 1)]
    if turn and len(order) > 1:
        order[:2] = order[1::-1]
    table = [0] * size
    for chunk in range(size):
        place = 0
        for mask in order:
            place = 2 * place + int(chunk & mask != 0)
        table[place] = chunk
    return order, order, table


def side_of(plans, at):
    core, shard = lax.rem(lax.axis_index("pipe"), 2), lax.axis_index("dp")
    return jnp.where(core == 0, parity(shard, plans[0][1][at]), parity(shard, plans[1][1][at]))


def gradient_body(plans, pick_left, pick_right, count, *refs):
    arrays, (send, keep, left, right, full) = refs[:count], refs[count:]
    stage, core, _ = where_am_i(0)
    rows = left.shape[0] // 4
    chunk = send.shape[1]
    for target, pick in ((left, pick_left), (right, pick_right)):
        near, away = pick(arrays)
        for step, part in enumerate(near):

            @pl.when(stage == step)
            def _():
                target[:rows] = part[...]

        for at, part in enumerate(away):
            target[(at + 1) * rows : (at + 2) * rows] = part[...]
    full[...] = contract(left[...], right[...], 0, 0)
    side = side_of(plans, 0)
    half = send.shape[0]
    flip = [plan[2][half] for plan in plans]
    for at in range(half):
        spots = []
        for target_side in (1 - side, side):
            first = plans[0][2][at] ^ (flip[0] * target_side)
            second = plans[1][2][at] ^ (flip[1] * target_side)
            spots.append(pl.multiple_of(jnp.where(core == 0, first, second) * chunk, chunk))
        send[at] = full[pl.ds(spots[0], chunk)].astype(jnp.bfloat16)
        keep[at] = full[pl.ds(spots[1], chunk)]


def halve_body(plans, at, keep_in, came, send, keep):
    half = keep.shape[0]
    side = side_of(plans, at)
    for spot in range(half):
        mine, theirs = side * half + spot, (1 - side) * half + spot
        send[spot] = (keep_in[theirs] + came[theirs].astype(jnp.float32)).astype(jnp.bfloat16)
        keep[spot] = keep_in[mine] + came[mine].astype(jnp.float32)


def bit_of(value, bit):
    return lax.rem(lax.div(value, 1 << bit), 2)


def first_sides():
    core, shard = lax.rem(lax.axis_index("pipe"), 2), lax.axis_index("dp")
    low, high = bit_of(shard, 0), bit_of(shard, 1)
    return core, jnp.where(core == 0, low, high), jnp.where(core == 0, high, low)


def split_columns(wide, keep, send, chunk):
    core, side, _ = first_sides()
    for place in range(wide.shape[1] // (2 * chunk)):
        for target, at in ((keep, side), (send, 1 - side)):
            block = jnp.where(core == 0, 2 * place + at, place // 2 * 4 + 2 * at + place % 2)
            source = pl.ds(pl.multiple_of(block * chunk, chunk), chunk)
            target[:, place * chunk : (place + 1) * chunk] = wide[:, source]


def gather_rows(target, near, away):
    stage, _, _ = where_am_i(0)
    rows = target.shape[0] // 4
    for step, part in enumerate(near):

        @pl.when(stage == step)
        def _():
            target[:rows] = part[...]

    for at, part in enumerate(away):
        target[(at + 1) * rows : (at + 2) * rows] = part[...]


def early_body(stages, chunk, *refs):
    arrays, (keep_left, keep_right, send, wide) = refs[: stages + 3], refs[stages + 3 :]
    channels = wide.shape[1]
    flows, (side, far, cross) = arrays[:stages], arrays[stages:]
    for target, columns in ((wide, slice(0, channels)), (keep_right, slice(channels, None))):
        near = [flow.at[0, :, columns] for flow in flows]
        gather_rows(target, near, [side.at[:, columns], far.at[:, columns], cross.at[:, columns]])
    split_columns(wide, keep_left, send, chunk)
    send[:, channels // 2 :] = keep_right[...]


def late_body(stages, chunk, *refs):
    arrays, outs = refs[: stages + 3], refs[stages + 3 :]
    side, far, cross = arrays[stages:]
    gather_rows(outs[-1], [back.at[0] for back in arrays[:stages]], [side, far, cross])
    if chunk:
        split_columns(outs[2], outs[0], outs[1], chunk)


def half_gradient_body(left, left_came, right, right_came, send, keep, full):
    full[...] = contract(left[...], right[...], 0, 0) + contract(left_came[...], right_came[...], 0, 0)
    _, _, side = first_sides()
    chunk = send.shape[1]
    for place in range(send.shape[0]):
        theirs = pl.ds(pl.multiple_of((2 * place + 1 - side) * chunk, chunk), chunk)
        mine = pl.ds(pl.multiple_of((2 * place + side) * chunk, chunk), chunk)
        send[place] = full[theirs].astype(jnp.bfloat16)
        keep[place] = full[mine]


def next_body(bit, keep_in, came, send, keep):
    side = bit_of(lax.axis_index("dp"), bit)
    for place in range(keep.shape[0]):
        theirs, mine = 2 * place + 1 - side, 2 * place + side
        send[place] = (keep_in[theirs] + came[theirs].astype(jnp.float32)).astype(jnp.bfloat16)
        keep[place] = keep_in[mine] + came[mine].astype(jnp.float32)


def finish_body(keep_reduce, came_reduce, keep_expand, came_expand, out):
    out[0, 0] = keep_reduce[0] + came_reduce[0].astype(jnp.float32)
    out[0, 1] = keep_expand[0] + came_expand[0].astype(jnp.float32)


def shards(inputs, cotangent, reduce_weight, expand_weight):
    stages = lax.axis_size("pipe") // 2
    replicas = lax.axis_size("dp")
    stage, core, _ = where_am_i(0)
    channels, inner = reduce_weight.shape[2:]
    rows = inputs.shape[1] * inputs.shape[2] // 2
    sizes = (channels, inner)
    entering = inputs.reshape(2, 2, rows, channels)
    ending = cotangent.reshape(2, 2, rows, channels)
    own = [reduce_weight[:, 0], expand_weight[:, 0]]

    core_pairs = [(p, p ^ 1) for p in range(2 * stages)]
    mirror_pairs = [(p, 2 * (stages - 1 - p // 2) + p % 2) for p in range(2 * stages)]

    def hop(shard, step):
        pairs = []
        for c in range(2):
            pairs.append((2 * step + c, 2 * step + 2 + c))
            pairs.append((2 * (stages - 1 - step) + c, 2 * (stages - 2 - step) + c))
        return lax.ppermute(shard, "pipe", pairs)

    def swap_cores(shard):
        return lax.ppermute(shard, "pipe", core_pairs)

    def mirror(shard):
        return lax.ppermute(shard, "pipe", mirror_pairs)

    at_stage = [stage == step for step in range(stages)]
    first_core = core == 0
    at_stage, first_core, entering = lax.optimization_barrier((at_stage, first_core, entering))

    def pick(parts, mirrored_stage=False):
        tests = at_stage[::-1] if mirrored_stage else at_stage
        chosen = parts[0]
        for test, part in zip(tests[1:], parts[1:]):
            chosen = jnp.where(test, part, chosen)
        return chosen

    in_hbm = lambda array: pltpu.with_memory_space_constraint(array, pltpu.HBM)
    own, entering, ending = [in_hbm(one) for one in own], in_hbm(entering), in_hbm(ending)
    *near, enter = load(0, own, entering)
    near += [swap_cores(weight) for weight in near]
    turn = list(load(stages - 1, own))
    turn += [swap_cores(weight) for weight in turn]
    if stages > 2:
        weights = own + [swap_cores(weight) for weight in own]
    flows, trunks, inners = [], [], []
    for step in range(stages - 1):
        flow, leave, trunk, inner_sum = run_stage(
            weights if step else near, step, True, False, step == 0, rows, sizes, enter
        )
        flows.append(flow)
        trunks.append(trunk)
        inners.append(inner_sum)
        enter = hop(leave, step)
    mirrored = stages == 2
    line = jax.ShapeDtypeStruct((rows, channels), jnp.bfloat16)
    outs = [line, jax.ShapeDtypeStruct((rows, inner), jnp.float32)] + [line, line] * mirrored
    ending, first_active, *known = pl.pallas_call(
        functools.partial(meanwhile_body, stages - 1, mirrored),
        out_shape=outs,
        in_specs=[VMEM, VMEM, HBM, HBM, VMEM],
        out_specs=[VMEM] * len(outs),
        scratch_shapes=[pltpu.SemaphoreType.DMA((3,))],
        compiler_params=PARAMS,
    )(turn[1], turn[3], entering, ending, leave)
    flow, upstreams, back_inners, leave = run_stage(
        turn, stages - 1, True, True, True, rows, sizes, enter, ending, first_active
    )
    flows.append(flow)
    upstreams, back_inners = [upstreams], [back_inners]
    upstream = hop(leave, 0)
    side_flow = swap_cores(pick(flows)[1])
    near_core = lambda first, second: jnp.where(first_core, first, second)
    going = pick(flows, True)
    if mirrored:
        lifted = near_core(going[1, :, :channels], going[0, :, :channels])
        going = jnp.concatenate([lifted, going[0, :, channels:], going[1, :, channels:]], axis=1)
    far_flow = mirror(going)
    if mirrored:
        lifted, actives = far_flow[:, :channels], far_flow[:, channels:]
        far_flow = jnp.concatenate([near_core(known[1], lifted), actives[:, :inner]], axis=1)
        cross_flow = jnp.concatenate([near_core(lifted, known[1]), actives[:, inner:]], axis=1)
    else:
        far_flow, cross_flow = far_flow[0], far_flow[1]
    cross_flow = swap_cores(cross_flow)
    for step in range(stages - 2, -1, -1):
        outs = run_stage(
            weights if step else near,
            step,
            False,
            True,
            step == 0,
            rows,
            sizes,
            upstream,
            trunks[step],
            inners[step],
        )
        upstreams.insert(0, outs[0])
        back_inners.insert(0, outs[1])
        if step:
            upstream = hop(outs[2], stages - 1 - step)
    going = pick(upstreams, True)
    far_up = mirror(near_core(going[0], going[1]) if mirrored else going)
    far_inner = mirror(pick(back_inners, True))
    side_up = swap_cores(pick(upstreams)[1])
    side_inner = swap_cores(pick(back_inners)[1])
    if mirrored:
        top = jnp.where(at_stage[0], leave, known[0])
        far_up, cross_up = near_core(far_up, top), near_core(top, far_up)
    else:
        far_up, cross_up = far_up[0], far_up[1]
    cross_up = swap_cores(cross_up)
    cross_inner = swap_cores(far_inner[1])
    far_inner = far_inner[0]

    chunk = channels // replicas
    fore = flows + [side_flow, far_flow, cross_flow]
    ups = upstreams + [side_up, far_up, cross_up]
    backs = back_inners + [side_inner, far_inner, cross_inner]
    halve = halve_rows if chunk % 128 == 0 and replicas >= 4 else halve_sums
    parts = halve(stages, replicas, chunk, sizes, rows, fore, ups, backs)
    return pl.pallas_call(
        finish_body,
        out_shape=jax.ShapeDtypeStruct((1, 2, chunk, inner), jnp.float32),
        in_specs=[VMEM] * 4,
        out_specs=VMEM,
        compiler_params=PARAMS,
    )(*parts)


def sums(count, chunk, inner):
    return [
        jax.ShapeDtypeStruct((count, chunk, inner), jnp.bfloat16),
        jax.ShapeDtypeStruct((count, chunk, inner), jnp.float32),
    ]


def exchange(shard, stages, replicas, first, second):
    pairs = []
    for p in range(2 * stages):
        for q in range(replicas):
            pairs.append((p * replicas + q, p * replicas + (q ^ (second if p % 2 else first))))
    return lax.ppermute(shard, AXES, pairs)


def halve_rows(stages, replicas, chunk, sizes, rows, fore, ups, backs):
    channels, inner = sizes
    shape = lambda *dims: jax.ShapeDtypeStruct(dims, jnp.bfloat16)
    half = shape(4 * rows, channels // 2)
    narrow = shape(4 * rows, inner)
    left, right, send = pl.pallas_call(
        functools.partial(early_body, stages, chunk),
        out_shape=[half, narrow, shape(4 * rows, channels // 2 + inner)],
        in_specs=[VMEM] * len(fore),
        out_specs=[VMEM] * 3,
        scratch_shapes=[pltpu.VMEM((4 * rows, channels), jnp.bfloat16)],
        compiler_params=PARAMS,
    )(*fore)
    came = exchange(send, stages, replicas, 1, 2)
    came_left, came_right = came[:, : channels // 2], came[:, channels // 2 :]
    back = pl.pallas_call(
        functools.partial(late_body, stages, 0),
        out_shape=narrow,
        in_specs=[VMEM] * len(backs),
        out_specs=VMEM,
        compiler_params=PARAMS,
    )(*backs)
    came_back = exchange(back, stages, replicas, 1, 2)
    up, up_send = pl.pallas_call(
        functools.partial(late_body, stages, chunk),
        out_shape=[half, half],
        in_specs=[VMEM] * len(ups),
        out_specs=[VMEM] * 2,
        scratch_shapes=[pltpu.VMEM((4 * rows, channels), jnp.bfloat16)],
        compiler_params=PARAMS,
    )(*ups)
    came_up = exchange(up_send, stages, replicas, 1, 2)
    parts = []
    streams = ((left, came_left, back, came_back), (up, came_up, right, came_right))
    for operands in streams:
        count = replicas // 4
        send, keep = pl.pallas_call(
            half_gradient_body,
            out_shape=sums(count, chunk, inner),
            in_specs=[VMEM] * 4,
            out_specs=[VMEM] * 2,
            scratch_shapes=[pltpu.VMEM((channels // 2, inner), jnp.float32)],
            compiler_params=PARAMS,
        )(*operands)
        came = exchange(send, stages, replicas, 2, 1)
        for bit in range(2, replicas.bit_length() - 1):
            count //= 2
            send, keep = pl.pallas_call(
                functools.partial(next_body, bit),
                out_shape=sums(count, chunk, inner),
                in_specs=[VMEM] * 2,
                out_specs=[VMEM] * 2,
                compiler_params=PARAMS,
            )(keep, came)
            came = exchange(send, stages, replicas, 1 << bit, 1 << bit)
        parts += [keep, came]
    return parts


def halve_sums(stages, replicas, chunk, sizes, rows, fore, ups, backs):
    channels, inner = sizes
    wide, narrow = slice(0, channels), slice(channels, channels + inner)

    def of_flows(columns):
        def pick_parts(arrays):
            near = [flow.at[0, :, columns] for flow in arrays[:stages]]
            side, far, cross = arrays[stages : stages + 3]
            return near, [side.at[:, columns], far.at[:, columns], cross.at[:, columns]]

        return pick_parts

    def of_backs(arrays):
        near = [back.at[0] for back in arrays[stages + 3 : 2 * stages + 3]]
        side, far, cross = arrays[2 * stages + 3 : 2 * stages + 6]
        return near, [side, far, cross]

    plans = [halving_plan(replicas, turn) for turn in range(2)]
    streams = []
    for pick_left, pick_right, late, plan in (
        (of_backs, of_flows(narrow), ups, plans),
        (of_flows(wide), of_backs, backs, plans[::-1]),
    ):
        arrays = fore + late
        send, keep = pl.pallas_call(
            functools.partial(gradient_body, plan, pick_left, pick_right, len(arrays)),
            out_shape=sums(replicas // 2, chunk, inner),
            in_specs=[VMEM] * len(arrays),
            out_specs=[VMEM] * 2,
            scratch_shapes=[
                pltpu.VMEM((4 * rows, channels), jnp.bfloat16),
                pltpu.VMEM((4 * rows, inner), jnp.bfloat16),
                pltpu.VMEM((channels, inner), jnp.float32),
            ],
            compiler_params=PARAMS,
        )(*arrays)
        streams.append((plan, send, keep))
    for at in range(replicas.bit_length() - 1):
        half = replicas >> (at + 2)
        arrived = []
        for plan, send, keep in streams:
            pairs = []
            for p in range(2 * stages):
                for q in range(replicas):
                    pairs.append((p * replicas + q, p * replicas + (q ^ plan[p % 2][0][at])))
            arrived.append((plan, keep, lax.ppermute(send, AXES, pairs)))
        if half == 0:
            break
        streams = []
        for plan, keep, came in arrived:
            send, keep = pl.pallas_call(
                functools.partial(halve_body, plan, at + 1),
                out_shape=sums(half, chunk, inner),
                in_specs=[VMEM] * 2,
                out_specs=[VMEM] * 2,
                compiler_params=PARAMS,
            )(keep, came)
            streams.append((plan, send, keep))
    (_, keep_expand, came_expand), (_, keep_reduce, came_reduce) = arrived
    return keep_reduce, came_reduce, keep_expand, came_expand


def solution(mesh):
    return jax.shard_map(
        shards,
        mesh=mesh,
        in_specs=(
            P(None, None, "dp", None),
            P(None, None, "dp", None),
            P(None, "pipe", None, None),
            P(None, "pipe", None, None),
        ),
        out_specs=P("pipe", None, "dp", None),
        check_vma=False,
    )
```

```python
import functools

import jax
import jax.numpy as jnp
from jax import lax
from jax.experimental import pallas as pl
from jax.experimental.pallas import tpu as pltpu
from jax.sharding import PartitionSpec as P


EPSILON = 1e-06
AXES = ("pipe", "dp")
HBM = pl.BlockSpec(memory_space=pltpu.HBM)
ANY = pl.BlockSpec(memory_space=pl.ANY)
VMEM = pl.BlockSpec(memory_space=pltpu.VMEM)
PARAMS = pltpu.CompilerParams(vmem_limit_bytes=16 << 20)


def contract(first_op, second_op, first_dim, second_dim):
    return lax.dot_general(
        first_op,
        second_op,
        (((first_dim,), (second_dim,)), ((), ())),
        preferred_element_type=jnp.float32,
    )


def smooth_slope(values):
    sigma = jax.nn.sigmoid(values)
    return sigma * (1.0 + values * (1.0 - sigma))


def norm_of(widened):
    return lax.rsqrt(jnp.mean(widened * widened, axis=-1, keepdims=True) + EPSILON)


def where_am_i(step):
    position = lax.axis_index("pipe")
    stage, core = lax.div(position, 2), lax.rem(position, 2)
    way = jnp.where(stage == step, 0, 1)
    return stage, core, way


def bring_all(sources, outs, sems):
    copies = [
        pltpu.make_async_copy(source, out, sems.at[at])
        for at, (source, out) in enumerate(zip(sources, outs))
    ]
    for copy in copies:
        copy.start()
    return copies


def load_body(step, reduce_all, expand_all, *refs):
    _, core, way = where_am_i(step)
    sources, outs = [reduce_all.at[way], expand_all.at[way]], refs[:-1]
    if step == 0:
        sources.append(refs[0].at[way, core])
        outs = outs[1:]
    for copy in bring_all(sources, outs, refs[-1]):
        copy.wait()


def load(step, own, *more):
    channels, inner = own[0].shape[1:]
    mat = jax.ShapeDtypeStruct((channels, inner), jnp.bfloat16)
    outs = [mat, mat] + [jax.ShapeDtypeStruct(a.shape[2:], a.dtype) for a in more]
    return pl.pallas_call(
        functools.partial(load_body, step),
        out_shape=outs,
        in_specs=[HBM] * (2 + len(more)),
        out_specs=[VMEM] * len(outs),
        scratch_shapes=[pltpu.SemaphoreType.DMA((len(outs),))],
        compiler_params=PARAMS,
    )(*own, *more)


def meanwhile_body(step, mirrored, expand_own, expand_other, inputs, cotangent, leave, *refs):
    outs, sems = refs[:-1], refs[-1]
    stage, core, way = where_am_i(step)
    ending, back_active = outs[:2]
    sources = [cotangent.at[way, core]]
    if mirrored:
        sources += [cotangent.at[1, core], inputs.at[1, core]]
    copies = bring_all(sources, [outs[0]] + list(outs[2:]), sems)
    copies[0].wait()

    @pl.when(way == core)
    def _():
        back_active[...] = jnp.dot(
            ending[...], expand_other[...], preferred_element_type=jnp.float32
        )

    @pl.when(way != core)
    def _():
        back_active[...] = jnp.dot(ending[...], expand_own[...], preferred_element_type=jnp.float32)

    for copy in copies[1:]:
        copy.wait()
    if mirrored:
        rows = outs[3]

        @pl.when(stage != 0)
        def _():
            rows[...] = leave[...]

        widened = rows[...].astype(jnp.float32)
        rows[...] = jax.nn.silu(widened * norm_of(widened)).astype(jnp.bfloat16)


def weight_copies(own, other, held, sems, core, way):
    copies = []
    for order in range(2):
        is_own = lax.rem(way + order, 2) == core
        for kind in range(2):
            mine = pltpu.make_async_copy(own[kind].at[way], held[kind].at[order], sems.at[kind, order])
            theirs = pltpu.make_async_copy(
                other[kind].at[way], held[kind].at[order], sems.at[kind, order]
            )
            copies.append((is_own, mine, theirs))
    return copies


def start_all(copies):
    for is_own, mine, theirs in copies:
        pl.when(is_own)(mine.start)
        pl.when(jnp.logical_not(is_own))(theirs.start)


def stage_body(step, forward, backward, last, near, *refs):
    refs = list(refs)
    _, core, way = where_am_i(step)
    own, other = (refs.pop(0), refs.pop(0)), (refs.pop(0), refs.pop(0))
    enter = refs.pop(0) if forward else None
    upstream_in = refs.pop(0) if backward else None
    first_active = refs.pop(0) if forward and backward else None
    if not forward:
        trunks, inners = refs.pop(0), refs.pop(0)
    if forward:
        flows = refs.pop(0)
    if forward and not backward:
        leave = refs.pop(0)
    if backward:
        upstreams, back_inners = refs.pop(0), refs.pop(0)
    if backward and not last:
        back_leave = refs.pop(0)
    if forward:
        trunks, inners = refs.pop(0), refs.pop(0)
    channels = trunks.shape[2]

    def run(reduce_mats, expand_mats, wait):
        if forward:
            rows = enter[...]
            for order in range(2):
                slot = lax.rem(order + core, 2)
                widened = rows.astype(jnp.float32)
                normed = widened * norm_of(widened)
                lifted = jax.nn.silu(normed).astype(jnp.bfloat16)
                trunks[order] = rows
                flows[slot, :, :channels] = lifted
                wait(0, order)
                inner_sum = jnp.dot(
                    lifted, reduce_mats[order][...], preferred_element_type=jnp.float32
                )
                active = jax.nn.silu(inner_sum).astype(jnp.bfloat16)
                inners[order] = inner_sum
                flows[slot, :, channels:] = active
                wait(1, order)
                rows = (widened + contract(active, expand_mats[order][...], 1, 1)).astype(jnp.bfloat16)
            if not backward:
                leave[...] = rows
        if backward:
            upstream = upstream_in[...]
            for order in (1, 0):
                slot = lax.rem(order + core, 2)
                upstreams[slot] = upstream
                if not forward:
                    wait(1, order)
                if forward and order:
                    back_active = first_active[...]
                else:
                    back_active = jnp.dot(
                        upstream, expand_mats[order][...], preferred_element_type=jnp.float32
                    )
                back_inner = (back_active * smooth_slope(inners[order])).astype(jnp.bfloat16)
                back_inners[slot] = back_inner
                if not forward:
                    wait(0, order)
                if last and order == 0:
                    break
                back_lifted = contract(back_inner, reduce_mats[order][...], 1, 1)
                widened = trunks[order].astype(jnp.float32)
                norm_scale = norm_of(widened)
                back_normed = back_lifted * smooth_slope(widened * norm_scale)
                projection = jnp.mean(back_normed * widened, axis=-1, keepdims=True)
                upstream = (
                    upstream.astype(jnp.float32)
                    + norm_scale * back_normed
                    - widened * norm_scale**3 * projection
                ).astype(jnp.bfloat16)
            if not last:
                back_leave[...] = upstream

    if near:
        idle = lambda kind, order: None

        @pl.when(way == core)
        def _():
            run((own[0], other[0]), (own[1], other[1]), idle)

        @pl.when(way != core)
        def _():
            run((other[0], own[0]), (other[1], own[1]), idle)

    else:
        held = (refs.pop(0), refs.pop(0))
        copies = weight_copies(own, other, held, refs.pop(0), core, way)
        start_all(copies if forward else copies[2:] + copies[:2])
        run(
            [held[0].at[order] for order in range(2)],
            [held[1].at[order] for order in range(2)],
            lambda kind, order: copies[2 * order + kind][1].wait(),
        )


def run_stage(weights, step, forward, backward, near, rows, sizes, *arrays):
    channels, inner = sizes
    last = backward and step == 0 and not forward
    shape = lambda dtype, *dims: jax.ShapeDtypeStruct(dims, dtype)
    line = shape(jnp.bfloat16, rows, channels)
    kept = [((2, rows, channels), jnp.bfloat16), ((2, rows, inner), jnp.float32)]
    outs, scratch = [], []
    if forward:
        outs.append(shape(jnp.bfloat16, 2, rows, channels + inner))
    if forward and not backward:
        outs.append(line)
    if backward:
        outs.append(shape(jnp.bfloat16, 2, rows, channels))
        outs.append(shape(jnp.bfloat16, 2, rows, inner))
    if backward and not last:
        outs.append(line)
    if forward and not backward:
        outs += [jax.ShapeDtypeStruct(*one) for one in kept]
    if forward and backward:
        scratch += [pltpu.VMEM(*one) for one in kept]
    if not near:
        scratch += [pltpu.VMEM((2, channels, inner), jnp.bfloat16)] * 2
        scratch += [pltpu.SemaphoreType.DMA((2, 2))]
    passes = 4 * (int(forward) + int(backward))
    return pl.pallas_call(
        functools.partial(stage_body, step, forward, backward, last, near),
        out_shape=outs,
        in_specs=[VMEM if near else ANY] * 4 + [VMEM] * len(arrays),
        out_specs=[VMEM] * len(outs),
        scratch_shapes=scratch,
        compiler_params=PARAMS,
        cost_estimate=pl.CostEstimate(
            flops=2 * passes * rows * channels * inner,
            bytes_accessed=8 * channels * inner,
            transcendentals=passes * rows * channels,
        ),
    )(*weights, *arrays)


def parity(value, mask):
    total, bit = 0, 0
    while mask >> bit:
        if mask >> bit & 1:
            total = total + lax.rem(lax.div(value, 1 << bit), 2)
        bit += 1
    return lax.rem(total, 2)


def halving_plan(size, turn):
    order = [1 << bit for bit in range(size.bit_length() - 1)]
    if turn and len(order) > 1:
        order[:2] = order[1::-1]
    table = [0] * size
    for chunk in range(size):
        place = 0
        for mask in order:
            place = 2 * place + int(chunk & mask != 0)
        table[place] = chunk
    return order, order, table


def side_of(plans, at):
    core, shard = lax.rem(lax.axis_index("pipe"), 2), lax.axis_index("dp")
    return jnp.where(core == 0, parity(shard, plans[0][1][at]), parity(shard, plans[1][1][at]))


def gradient_body(plans, pick_left, pick_right, count, *refs):
    arrays, (send, keep, left, right, full) = refs[:count], refs[count:]
    stage, core, _ = where_am_i(0)
    rows = left.shape[0] // 4
    chunk = send.shape[1]
    for target, pick in ((left, pick_left), (right, pick_right)):
        near, away = pick(arrays)
        for step, part in enumerate(near):

            @pl.when(stage == step)
            def _():
                target[:rows] = part[...]

        for at, part in enumerate(away):
            target[(at + 1) * rows : (at + 2) * rows] = part[...]
    full[...] = contract(left[...], right[...], 0, 0)
    side = side_of(plans, 0)
    half = send.shape[0]
    flip = [plan[2][half] for plan in plans]
    for at in range(half):
        spots = []
        for target_side in (1 - side, side):
            first = plans[0][2][at] ^ (flip[0] * target_side)
            second = plans[1][2][at] ^ (flip[1] * target_side)
            spots.append(pl.multiple_of(jnp.where(core == 0, first, second) * chunk, chunk))
        send[at] = full[pl.ds(spots[0], chunk)].astype(jnp.bfloat16)
        keep[at] = full[pl.ds(spots[1], chunk)]


def halve_body(plans, at, keep_in, came, send, keep):
    half = keep.shape[0]
    side = side_of(plans, at)
    for spot in range(half):
        mine, theirs = side * half + spot, (1 - side) * half + spot
        send[spot] = (keep_in[theirs] + came[theirs].astype(jnp.float32)).astype(jnp.bfloat16)
        keep[spot] = keep_in[mine] + came[mine].astype(jnp.float32)


def bit_of(value, bit):
    return lax.rem(lax.div(value, 1 << bit), 2)


def first_sides():
    core, shard = lax.rem(lax.axis_index("pipe"), 2), lax.axis_index("dp")
    low, high = bit_of(shard, 0), bit_of(shard, 1)
    return core, jnp.where(core == 0, low, high), jnp.where(core == 0, high, low)


def split_columns(wide, keep, send, chunk):
    core, side, _ = first_sides()
    for place in range(wide.shape[1] // (2 * chunk)):
        for target, at in ((keep, side), (send, 1 - side)):
            block = jnp.where(core == 0, 2 * place + at, place // 2 * 4 + 2 * at + place % 2)
            source = pl.ds(pl.multiple_of(block * chunk, chunk), chunk)
            target[:, place * chunk : (place + 1) * chunk] = wide[:, source]


def gather_rows(target, near, away):
    stage, _, _ = where_am_i(0)
    rows = target.shape[0] // 4
    for step, part in enumerate(near):

        @pl.when(stage == step)
        def _():
            target[:rows] = part[...]

    for at, part in enumerate(away):
        target[(at + 1) * rows : (at + 2) * rows] = part[...]


def flow_rows(arrays, stages, columns):
    near = [flow.at[0, :, columns] for flow in arrays[:stages]]
    return near, [part.at[:, columns] for part in arrays[stages : stages + 3]]


def back_rows(arrays, stages):
    return [back.at[0] for back in arrays[:stages]], arrays[stages : stages + 3]


def early_body(stages, channels, *refs):
    gather_rows(refs[-1], *flow_rows(refs, stages, slice(channels, None)))


def late_up_body(stages, chunk, *refs):
    keep, send, wide = refs[stages + 3 :]
    gather_rows(wide, *back_rows(refs, stages))
    split_columns(wide, keep, send, chunk)


def late_inner_body(stages, chunk, *refs):
    left, right, send, wide = refs[2 * stages + 6 :]
    channels = wide.shape[1]
    gather_rows(wide, *flow_rows(refs, stages, slice(0, channels)))
    split_columns(wide, left, send, chunk)
    gather_rows(right, *back_rows(refs[stages + 3 :], stages))
    send[:, channels // 2 :] = right[...]


def half_gradient_body(left, right, *refs):
    came, (send, keep, full) = refs[:-3], refs[-3:]
    columns = left.shape[1]
    if len(came) == 1:
        came = (came[0].at[:, :columns], came[0].at[:, columns:])
    full[...] = contract(left[...], right[...], 0, 0) + contract(came[0][...], came[1][...], 0, 0)
    _, _, side = first_sides()
    chunk = send.shape[1]
    for place in range(send.shape[0]):
        theirs = pl.ds(pl.multiple_of((2 * place + 1 - side) * chunk, chunk), chunk)
        mine = pl.ds(pl.multiple_of((2 * place + side) * chunk, chunk), chunk)
        send[place] = full[theirs].astype(jnp.bfloat16)
        keep[place] = full[mine]


def next_body(bit, keep_in, came, send, keep):
    side = bit_of(lax.axis_index("dp"), bit)
    for place in range(keep.shape[0]):
        theirs, mine = 2 * place + 1 - side, 2 * place + side
        send[place] = (keep_in[theirs] + came[theirs].astype(jnp.float32)).astype(jnp.bfloat16)
        keep[place] = keep_in[mine] + came[mine].astype(jnp.float32)


def finish_body(keep_reduce, came_reduce, keep_expand, came_expand, out):
    out[0, 0] = keep_reduce[0] + came_reduce[0].astype(jnp.float32)
    out[0, 1] = keep_expand[0] + came_expand[0].astype(jnp.float32)


def shards(inputs, cotangent, reduce_weight, expand_weight):
    stages = lax.axis_size("pipe") // 2
    replicas = lax.axis_size("dp")
    stage, core, _ = where_am_i(0)
    channels, inner = reduce_weight.shape[2:]
    rows = inputs.shape[1] * inputs.shape[2] // 2
    sizes = (channels, inner)
    entering = inputs.reshape(2, 2, rows, channels)
    ending = cotangent.reshape(2, 2, rows, channels)
    own = [reduce_weight[:, 0], expand_weight[:, 0]]

    core_pairs = [(p, p ^ 1) for p in range(2 * stages)]
    mirror_pairs = [(p, 2 * (stages - 1 - p // 2) + p % 2) for p in range(2 * stages)]

    def hop(shard, step):
        pairs = []
        for c in range(2):
            pairs.append((2 * step + c, 2 * step + 2 + c))
            pairs.append((2 * (stages - 1 - step) + c, 2 * (stages - 2 - step) + c))
        return lax.ppermute(shard, "pipe", pairs)

    def swap_cores(shard):
        return lax.ppermute(shard, "pipe", core_pairs)

    def mirror(shard):
        return lax.ppermute(shard, "pipe", mirror_pairs)

    at_stage = [stage == step for step in range(stages)]
    first_core = core == 0
    at_stage, first_core, entering = lax.optimization_barrier((at_stage, first_core, entering))

    def pick(parts, mirrored_stage=False):
        tests = at_stage[::-1] if mirrored_stage else at_stage
        chosen = parts[0]
        for test, part in zip(tests[1:], parts[1:]):
            chosen = jnp.where(test, part, chosen)
        return chosen

    in_hbm = lambda array: pltpu.with_memory_space_constraint(array, pltpu.HBM)
    own, entering, ending = [in_hbm(one) for one in own], in_hbm(entering), in_hbm(ending)
    *near, enter = load(0, own, entering)
    near += [swap_cores(weight) for weight in near]
    turn = list(load(stages - 1, own))
    turn += [swap_cores(weight) for weight in turn]
    if stages > 2:
        weights = own + [swap_cores(weight) for weight in own]
    flows, trunks, inners = [], [], []
    for step in range(stages - 1):
        flow, leave, trunk, inner_sum = run_stage(
            weights if step else near, step, True, False, step == 0, rows, sizes, enter
        )
        flows.append(flow)
        trunks.append(trunk)
        inners.append(inner_sum)
        enter = hop(leave, step)
    mirrored = stages == 2
    line = jax.ShapeDtypeStruct((rows, channels), jnp.bfloat16)
    outs = [line, jax.ShapeDtypeStruct((rows, inner), jnp.float32)] + [line, line] * mirrored
    ending, first_active, *known = pl.pallas_call(
        functools.partial(meanwhile_body, stages - 1, mirrored),
        out_shape=outs,
        in_specs=[VMEM, VMEM, HBM, HBM, VMEM],
        out_specs=[VMEM] * len(outs),
        scratch_shapes=[pltpu.SemaphoreType.DMA((3,))],
        compiler_params=PARAMS,
    )(turn[1], turn[3], entering, ending, leave)
    flow, upstreams, back_inners, leave = run_stage(
        turn, stages - 1, True, True, True, rows, sizes, enter, ending, first_active
    )
    flows.append(flow)
    upstreams, back_inners = [upstreams], [back_inners]
    upstream = hop(leave, 0)
    side_flow = swap_cores(pick(flows)[1])
    near_core = lambda first, second: jnp.where(first_core, first, second)
    going = pick(flows, True)
    if mirrored:
        lifted = near_core(going[1, :, :channels], going[0, :, :channels])
        going = jnp.concatenate([lifted, going[0, :, channels:], going[1, :, channels:]], axis=1)
    far_flow = mirror(going)
    if mirrored:
        lifted, actives = far_flow[:, :channels], far_flow[:, channels:]
        far_flow = jnp.concatenate([near_core(known[1], lifted), actives[:, :inner]], axis=1)
        cross_flow = jnp.concatenate([near_core(lifted, known[1]), actives[:, inner:]], axis=1)
    else:
        far_flow, cross_flow = far_flow[0], far_flow[1]
    cross_flow = swap_cores(cross_flow)
    for step in range(stages - 2, -1, -1):
        outs = run_stage(
            weights if step else near,
            step,
            False,
            True,
            step == 0,
            rows,
            sizes,
            upstream,
            trunks[step],
            inners[step],
        )
        upstreams.insert(0, outs[0])
        back_inners.insert(0, outs[1])
        if step:
            upstream = hop(outs[2], stages - 1 - step)
    going = pick(upstreams, True)
    far_up = mirror(near_core(going[0], going[1]) if mirrored else going)
    far_inner = mirror(pick(back_inners, True))
    side_up = swap_cores(pick(upstreams)[1])
    side_inner = swap_cores(pick(back_inners)[1])
    if mirrored:
        top = jnp.where(at_stage[0], leave, known[0])
        far_up, cross_up = near_core(far_up, top), near_core(top, far_up)
    else:
        far_up, cross_up = far_up[0], far_up[1]
    cross_up = swap_cores(cross_up)
    cross_inner = swap_cores(far_inner[1])
    far_inner = far_inner[0]

    chunk = channels // replicas
    fore = flows + [side_flow, far_flow, cross_flow]
    ups = upstreams + [side_up, far_up, cross_up]
    backs = back_inners + [side_inner, far_inner, cross_inner]
    halve = halve_rows if chunk % 128 == 0 and replicas >= 4 else halve_sums
    parts = halve(stages, replicas, chunk, sizes, rows, fore, ups, backs)
    return pl.pallas_call(
        finish_body,
        out_shape=jax.ShapeDtypeStruct((1, 2, chunk, inner), jnp.float32),
        in_specs=[VMEM] * 4,
        out_specs=VMEM,
        compiler_params=PARAMS,
    )(*parts)


def sums(count, chunk, inner):
    return [
        jax.ShapeDtypeStruct((count, chunk, inner), jnp.bfloat16),
        jax.ShapeDtypeStruct((count, chunk, inner), jnp.float32),
    ]


def exchange(shard, stages, replicas, first, second):
    pairs = []
    for p in range(2 * stages):
        for q in range(replicas):
            pairs.append((p * replicas + q, p * replicas + (q ^ (second if p % 2 else first))))
    return lax.ppermute(shard, AXES, pairs)


def halve_rows(stages, replicas, chunk, sizes, rows, fore, ups, backs):
    channels, inner = sizes
    shape = lambda *dims: jax.ShapeDtypeStruct(dims, jnp.bfloat16)
    half = shape(4 * rows, channels // 2)
    narrow = shape(4 * rows, inner)
    active = pl.pallas_call(
        functools.partial(early_body, stages, channels),
        out_shape=narrow,
        in_specs=[VMEM] * len(fore),
        out_specs=VMEM,
        compiler_params=PARAMS,
    )(*fore)
    came_active = exchange(active, stages, replicas, 1, 2)
    up, up_send = pl.pallas_call(
        functools.partial(late_up_body, stages, chunk),
        out_shape=[half, half],
        in_specs=[VMEM] * len(ups),
        out_specs=[VMEM] * 2,
        scratch_shapes=[pltpu.VMEM((4 * rows, channels), jnp.bfloat16)],
        compiler_params=PARAMS,
    )(*ups)
    came_up = exchange(up_send, stages, replicas, 1, 2)
    lifted, back, send = pl.pallas_call(
        functools.partial(late_inner_body, stages, chunk),
        out_shape=[half, narrow, shape(4 * rows, channels // 2 + inner)],
        in_specs=[VMEM] * (len(fore) + len(backs)),
        out_specs=[VMEM] * 3,
        scratch_shapes=[pltpu.VMEM((4 * rows, channels), jnp.bfloat16)],
        compiler_params=PARAMS,
    )(*fore, *backs)
    came_inner = exchange(send, stages, replicas, 1, 2)
    parts = []
    streams = ((lifted, back, came_inner), (up, active, came_up, came_active))
    for operands in streams:
        count = replicas // 4
        send, keep = pl.pallas_call(
            half_gradient_body,
            out_shape=sums(count, chunk, inner),
            in_specs=[VMEM] * len(operands),
            out_specs=[VMEM] * 2,
            scratch_shapes=[pltpu.VMEM((channels // 2, inner), jnp.float32)],
            compiler_params=PARAMS,
        )(*operands)
        came = exchange(send, stages, replicas, 2, 1)
        for bit in range(2, replicas.bit_length() - 1):
            count //= 2
            send, keep = pl.pallas_call(
                functools.partial(next_body, bit),
                out_shape=sums(count, chunk, inner),
                in_specs=[VMEM] * 2,
                out_specs=[VMEM] * 2,
                compiler_params=PARAMS,
            )(keep, came)
            came = exchange(send, stages, replicas, 1 << bit, 1 << bit)
        parts += [keep, came]
    return parts


def halve_sums(stages, replicas, chunk, sizes, rows, fore, ups, backs):
    channels, inner = sizes
    wide, narrow = slice(0, channels), slice(channels, channels + inner)

    def of_flows(columns):
        def pick_parts(arrays):
            near = [flow.at[0, :, columns] for flow in arrays[:stages]]
            side, far, cross = arrays[stages : stages + 3]
            return near, [side.at[:, columns], far.at[:, columns], cross.at[:, columns]]

        return pick_parts

    def of_backs(arrays):
        near = [back.at[0] for back in arrays[stages + 3 : 2 * stages + 3]]
        side, far, cross = arrays[2 * stages + 3 : 2 * stages + 6]
        return near, [side, far, cross]

    plans = [halving_plan(replicas, turn) for turn in range(2)]
    streams = []
    for pick_left, pick_right, late, plan in (
        (of_backs, of_flows(narrow), ups, plans),
        (of_flows(wide), of_backs, backs, plans[::-1]),
    ):
        arrays = fore + late
        send, keep = pl.pallas_call(
            functools.partial(gradient_body, plan, pick_left, pick_right, len(arrays)),
            out_shape=sums(replicas // 2, chunk, inner),
            in_specs=[VMEM] * len(arrays),
            out_specs=[VMEM] * 2,
            scratch_shapes=[
                pltpu.VMEM((4 * rows, channels), jnp.bfloat16),
                pltpu.VMEM((4 * rows, inner), jnp.bfloat16),
                pltpu.VMEM((channels, inner), jnp.float32),
            ],
            compiler_params=PARAMS,
        )(*arrays)
        streams.append((plan, send, keep))
    for at in range(replicas.bit_length() - 1):
        half = replicas >> (at + 2)
        arrived = []
        for plan, send, keep in streams:
            pairs = []
            for p in range(2 * stages):
                for q in range(replicas):
                    pairs.append((p * replicas + q, p * replicas + (q ^ plan[p % 2][0][at])))
            arrived.append((plan, keep, lax.ppermute(send, AXES, pairs)))
        if half == 0:
            break
        streams = []
        for plan, keep, came in arrived:
            send, keep = pl.pallas_call(
                functools.partial(halve_body, plan, at + 1),
                out_shape=sums(half, chunk, inner),
                in_specs=[VMEM] * 2,
                out_specs=[VMEM] * 2,
                compiler_params=PARAMS,
            )(keep, came)
            streams.append((plan, send, keep))
    (_, keep_expand, came_expand), (_, keep_reduce, came_reduce) = arrived
    return keep_reduce, came_reduce, keep_expand, came_expand


def solution(mesh):
    return jax.shard_map(
        shards,
        mesh=mesh,
        in_specs=(
            P(None, None, "dp", None),
            P(None, None, "dp", None),
            P(None, "pipe", None, None),
            P(None, "pipe", None, None),
        ),
        out_specs=P("pipe", None, "dp", None),
        check_vma=False,
    )
```

```python
import functools

import jax
import jax.numpy as jnp
from jax import lax
from jax.experimental import pallas as pl
from jax.experimental.pallas import tpu as pltpu
from jax.sharding import PartitionSpec as P


EPSILON = 1e-06
AXES = ("pipe", "dp")
HBM = pl.BlockSpec(memory_space=pltpu.HBM)
ANY = pl.BlockSpec(memory_space=pl.ANY)
VMEM = pl.BlockSpec(memory_space=pltpu.VMEM)
PARAMS = pltpu.CompilerParams(vmem_limit_bytes=16 << 20)


def contract(first_op, second_op, first_dim, second_dim):
    return lax.dot_general(
        first_op,
        second_op,
        (((first_dim,), (second_dim,)), ((), ())),
        preferred_element_type=jnp.float32,
    )


def smooth_slope(values):
    sigma = jax.nn.sigmoid(values)
    return sigma * (1.0 + values * (1.0 - sigma))


def norm_of(widened):
    return lax.rsqrt(jnp.mean(widened * widened, axis=-1, keepdims=True) + EPSILON)


def where_am_i(step):
    position = lax.axis_index("pipe")
    stage, core = lax.div(position, 2), lax.rem(position, 2)
    way = jnp.where(stage == step, 0, 1)
    return stage, core, way


def bring_all(sources, outs, sems):
    copies = [
        pltpu.make_async_copy(source, out, sems.at[at])
        for at, (source, out) in enumerate(zip(sources, outs))
    ]
    for copy in copies:
        copy.start()
    return copies


def load_body(step, reduce_all, expand_all, *refs):
    _, core, way = where_am_i(step)
    sources, outs = [reduce_all.at[way], expand_all.at[way]], refs[:-1]
    if step == 0:
        sources.append(refs[0].at[way, core])
        outs = outs[1:]
    for copy in bring_all(sources, outs, refs[-1]):
        copy.wait()


def load(step, own, *more):
    channels, inner = own[0].shape[1:]
    mat = jax.ShapeDtypeStruct((channels, inner), jnp.bfloat16)
    outs = [mat, mat] + [jax.ShapeDtypeStruct(a.shape[2:], a.dtype) for a in more]
    return pl.pallas_call(
        functools.partial(load_body, step),
        out_shape=outs,
        in_specs=[HBM] * (2 + len(more)),
        out_specs=[VMEM] * len(outs),
        scratch_shapes=[pltpu.SemaphoreType.DMA((len(outs),))],
        compiler_params=PARAMS,
    )(*own, *more)


def meanwhile_body(step, mirrored, expand_own, expand_other, inputs, cotangent, leave, *refs):
    outs, sems = refs[:-1], refs[-1]
    stage, core, way = where_am_i(step)
    ending, back_active = outs[:2]
    sources = [cotangent.at[way, core]]
    if mirrored:
        sources += [cotangent.at[1, core], inputs.at[1, core]]
    copies = bring_all(sources, [outs[0]] + list(outs[2:]), sems)
    copies[0].wait()

    @pl.when(way == core)
    def _():
        back_active[...] = jnp.dot(
            ending[...], expand_other[...], preferred_element_type=jnp.float32
        )

    @pl.when(way != core)
    def _():
        back_active[...] = jnp.dot(ending[...], expand_own[...], preferred_element_type=jnp.float32)

    for copy in copies[1:]:
        copy.wait()
    if mirrored:
        rows = outs[3]

        @pl.when(stage != 0)
        def _():
            rows[...] = leave[...]

        widened = rows[...].astype(jnp.float32)
        rows[...] = jax.nn.silu(widened * norm_of(widened)).astype(jnp.bfloat16)


def weight_copies(own, other, held, sems, core, way):
    copies = []
    for order in range(2):
        is_own = lax.rem(way + order, 2) == core
        for kind in range(2):
            mine = pltpu.make_async_copy(own[kind].at[way], held[kind].at[order], sems.at[kind, order])
            theirs = pltpu.make_async_copy(
                other[kind].at[way], held[kind].at[order], sems.at[kind, order]
            )
            copies.append((is_own, mine, theirs))
    return copies


def start_all(copies):
    for is_own, mine, theirs in copies:
        pl.when(is_own)(mine.start)
        pl.when(jnp.logical_not(is_own))(theirs.start)


def stage_body(step, forward, backward, last, near, *refs):
    refs = list(refs)
    _, core, way = where_am_i(step)
    own, other = (refs.pop(0), refs.pop(0)), (refs.pop(0), refs.pop(0))
    enter = refs.pop(0) if forward else None
    upstream_in = refs.pop(0) if backward else None
    first_active = refs.pop(0) if forward and backward else None
    if not forward:
        trunks, inners = refs.pop(0), refs.pop(0)
    if forward:
        flows = refs.pop(0)
    if forward and not backward:
        leave = refs.pop(0)
    if backward:
        upstreams, back_inners = refs.pop(0), refs.pop(0)
    if backward and not last:
        back_leave = refs.pop(0)
    if forward:
        trunks, inners = refs.pop(0), refs.pop(0)
    channels = trunks.shape[2]

    def run(reduce_mats, expand_mats, wait):
        if forward:
            rows = enter[...]
            for order in range(2):
                slot = lax.rem(order + core, 2)
                widened = rows.astype(jnp.float32)
                normed = widened * norm_of(widened)
                lifted = jax.nn.silu(normed).astype(jnp.bfloat16)
                trunks[order] = rows
                flows[slot, :, :channels] = lifted
                wait(0, order)
                inner_sum = jnp.dot(
                    lifted, reduce_mats[order][...], preferred_element_type=jnp.float32
                )
                active = jax.nn.silu(inner_sum).astype(jnp.bfloat16)
                inners[order] = inner_sum
                flows[slot, :, channels:] = active
                wait(1, order)
                rows = (widened + contract(active, expand_mats[order][...], 1, 1)).astype(jnp.bfloat16)
            if not backward:
                leave[...] = rows
        if backward:
            upstream = upstream_in[...]
            for order in (1, 0):
                slot = lax.rem(order + core, 2)
                upstreams[slot] = upstream
                if not forward:
                    wait(1, order)
                if forward and order:
                    back_active = first_active[...]
                else:
                    back_active = jnp.dot(
                        upstream, expand_mats[order][...], preferred_element_type=jnp.float32
                    )
                back_inner = (back_active * smooth_slope(inners[order])).astype(jnp.bfloat16)
                back_inners[slot] = back_inner
                if not forward:
                    wait(0, order)
                if last and order == 0:
                    break
                back_lifted = contract(back_inner, reduce_mats[order][...], 1, 1)
                widened = trunks[order].astype(jnp.float32)
                norm_scale = norm_of(widened)
                back_normed = back_lifted * smooth_slope(widened * norm_scale)
                projection = jnp.mean(back_normed * widened, axis=-1, keepdims=True)
                upstream = (
                    upstream.astype(jnp.float32)
                    + norm_scale * back_normed
                    - widened * norm_scale**3 * projection
                ).astype(jnp.bfloat16)
            if not last:
                back_leave[...] = upstream

    if near:
        idle = lambda kind, order: None

        @pl.when(way == core)
        def _():
            run((own[0], other[0]), (own[1], other[1]), idle)

        @pl.when(way != core)
        def _():
            run((other[0], own[0]), (other[1], own[1]), idle)

    else:
        held = (refs.pop(0), refs.pop(0))
        copies = weight_copies(own, other, held, refs.pop(0), core, way)
        start_all(copies if forward else copies[2:] + copies[:2])
        run(
            [held[0].at[order] for order in range(2)],
            [held[1].at[order] for order in range(2)],
            lambda kind, order: copies[2 * order + kind][1].wait(),
        )


def run_stage(weights, step, forward, backward, near, rows, sizes, *arrays):
    channels, inner = sizes
    last = backward and step == 0 and not forward
    shape = lambda dtype, *dims: jax.ShapeDtypeStruct(dims, dtype)
    line = shape(jnp.bfloat16, rows, channels)
    kept = [((2, rows, channels), jnp.bfloat16), ((2, rows, inner), jnp.float32)]
    outs, scratch = [], []
    if forward:
        outs.append(shape(jnp.bfloat16, 2, rows, channels + inner))
    if forward and not backward:
        outs.append(line)
    if backward:
        outs.append(shape(jnp.bfloat16, 2, rows, channels))
        outs.append(shape(jnp.bfloat16, 2, rows, inner))
    if backward and not last:
        outs.append(line)
    if forward and not backward:
        outs += [jax.ShapeDtypeStruct(*one) for one in kept]
    if forward and backward:
        scratch += [pltpu.VMEM(*one) for one in kept]
    if not near:
        scratch += [pltpu.VMEM((2, channels, inner), jnp.bfloat16)] * 2
        scratch += [pltpu.SemaphoreType.DMA((2, 2))]
    passes = 4 * (int(forward) + int(backward))
    return pl.pallas_call(
        functools.partial(stage_body, step, forward, backward, last, near),
        out_shape=outs,
        in_specs=[VMEM if near else ANY] * 4 + [VMEM] * len(arrays),
        out_specs=[VMEM] * len(outs),
        scratch_shapes=scratch,
        compiler_params=PARAMS,
        cost_estimate=pl.CostEstimate(
            flops=2 * passes * rows * channels * inner,
            bytes_accessed=8 * channels * inner,
            transcendentals=passes * rows * channels,
        ),
    )(*weights, *arrays)


def parity(value, mask):
    total, bit = 0, 0
    while mask >> bit:
        if mask >> bit & 1:
            total = total + lax.rem(lax.div(value, 1 << bit), 2)
        bit += 1
    return lax.rem(total, 2)


def halving_plan(size, turn):
    order = [1 << bit for bit in range(size.bit_length() - 1)]
    if turn and len(order) > 1:
        order[:2] = order[1::-1]
    table = [0] * size
    for chunk in range(size):
        place = 0
        for mask in order:
            place = 2 * place + int(chunk & mask != 0)
        table[place] = chunk
    return order, order, table


def side_of(plans, at):
    core, shard = lax.rem(lax.axis_index("pipe"), 2), lax.axis_index("dp")
    return jnp.where(core == 0, parity(shard, plans[0][1][at]), parity(shard, plans[1][1][at]))


def gradient_body(plans, pick_left, pick_right, count, *refs):
    arrays, (send, keep, left, right, full) = refs[:count], refs[count:]
    stage, core, _ = where_am_i(0)
    rows = left.shape[0] // 4
    chunk = send.shape[1]
    for target, pick in ((left, pick_left), (right, pick_right)):
        near, away = pick(arrays)
        for step, part in enumerate(near):

            @pl.when(stage == step)
            def _():
                target[:rows] = part[...]

        for at, part in enumerate(away):
            target[(at + 1) * rows : (at + 2) * rows] = part[...]
    full[...] = contract(left[...], right[...], 0, 0)
    side = side_of(plans, 0)
    half = send.shape[0]
    flip = [plan[2][half] for plan in plans]
    for at in range(half):
        spots = []
        for target_side in (1 - side, side):
            first = plans[0][2][at] ^ (flip[0] * target_side)
            second = plans[1][2][at] ^ (flip[1] * target_side)
            spots.append(pl.multiple_of(jnp.where(core == 0, first, second) * chunk, chunk))
        send[at] = full[pl.ds(spots[0], chunk)].astype(jnp.bfloat16)
        keep[at] = full[pl.ds(spots[1], chunk)]


def halve_body(plans, at, keep_in, came, send, keep):
    half = keep.shape[0]
    side = side_of(plans, at)
    for spot in range(half):
        mine, theirs = side * half + spot, (1 - side) * half + spot
        send[spot] = (keep_in[theirs] + came[theirs].astype(jnp.float32)).astype(jnp.bfloat16)
        keep[spot] = keep_in[mine] + came[mine].astype(jnp.float32)


def bit_of(value, bit):
    return lax.rem(lax.div(value, 1 << bit), 2)


def first_sides():
    core, shard = lax.rem(lax.axis_index("pipe"), 2), lax.axis_index("dp")
    low, high = bit_of(shard, 0), bit_of(shard, 1)
    return core, jnp.where(core == 0, low, high), jnp.where(core == 0, high, low)


def split_columns(wide, keep, send, chunk):
    core, side, _ = first_sides()
    for place in range(wide.shape[1] // (2 * chunk)):
        for target, at in ((keep, side), (send, 1 - side)):
            block = jnp.where(core == 0, 2 * place + at, place // 2 * 4 + 2 * at + place % 2)
            source = pl.ds(pl.multiple_of(block * chunk, chunk), chunk)
            target[:, place * chunk : (place + 1) * chunk] = wide[:, source]


def gather_rows(target, near, away):
    stage, _, _ = where_am_i(0)
    rows = target.shape[0] // 4
    for step, part in enumerate(near):

        @pl.when(stage == step)
        def _():
            target[:rows] = part[...]

    for at, part in enumerate(away):
        target[(at + 1) * rows : (at + 2) * rows] = part[...]


def flow_rows(arrays, stages, columns):
    near = [flow.at[0, :, columns] for flow in arrays[:stages]]
    return near, [part.at[:, columns] for part in arrays[stages : stages + 3]]


def back_rows(arrays, stages):
    return [back.at[0] for back in arrays[:stages]], arrays[stages : stages + 3]


def late_body(stages, chunk, up, *refs):
    left, right, send, wide = refs[2 * stages + 6 :]
    channels = wide.shape[1]
    backs = back_rows(refs[stages + 3 :], stages)
    if up:
        gather_rows(wide, *backs)
        gather_rows(right, *flow_rows(refs, stages, slice(channels, None)))
    else:
        gather_rows(wide, *flow_rows(refs, stages, slice(0, channels)))
        gather_rows(right, *backs)
    split_columns(wide, left, send, chunk)
    send[:, channels // 2 :] = right[...]


def half_gradient_body(left, right, came, send, keep, full):
    columns = left.shape[1]
    full[...] = contract(left[...], right[...], 0, 0) + contract(
        came[:, :columns], came[:, columns:], 0, 0
    )
    _, _, side = first_sides()
    chunk = send.shape[1]
    for place in range(send.shape[0]):
        theirs = pl.ds(pl.multiple_of((2 * place + 1 - side) * chunk, chunk), chunk)
        mine = pl.ds(pl.multiple_of((2 * place + side) * chunk, chunk), chunk)
        send[place] = full[theirs].astype(jnp.bfloat16)
        keep[place] = full[mine]


def next_body(bit, keep_in, came, send, keep):
    side = bit_of(lax.axis_index("dp"), bit)
    for place in range(keep.shape[0]):
        theirs, mine = 2 * place + 1 - side, 2 * place + side
        send[place] = (keep_in[theirs] + came[theirs].astype(jnp.float32)).astype(jnp.bfloat16)
        keep[place] = keep_in[mine] + came[mine].astype(jnp.float32)


def finish_body(keep_reduce, came_reduce, keep_expand, came_expand, out):
    out[0, 0] = keep_reduce[0] + came_reduce[0].astype(jnp.float32)
    out[0, 1] = keep_expand[0] + came_expand[0].astype(jnp.float32)


def shards(inputs, cotangent, reduce_weight, expand_weight):
    stages = lax.axis_size("pipe") // 2
    replicas = lax.axis_size("dp")
    stage, core, _ = where_am_i(0)
    channels, inner = reduce_weight.shape[2:]
    rows = inputs.shape[1] * inputs.shape[2] // 2
    sizes = (channels, inner)
    entering = inputs.reshape(2, 2, rows, channels)
    ending = cotangent.reshape(2, 2, rows, channels)
    own = [reduce_weight[:, 0], expand_weight[:, 0]]

    core_pairs = [(p, p ^ 1) for p in range(2 * stages)]
    mirror_pairs = [(p, 2 * (stages - 1 - p // 2) + p % 2) for p in range(2 * stages)]

    def hop(shard, step):
        pairs = []
        for c in range(2):
            pairs.append((2 * step + c, 2 * step + 2 + c))
            pairs.append((2 * (stages - 1 - step) + c, 2 * (stages - 2 - step) + c))
        return lax.ppermute(shard, "pipe", pairs)

    def swap_cores(shard):
        return lax.ppermute(shard, "pipe", core_pairs)

    def mirror(shard):
        return lax.ppermute(shard, "pipe", mirror_pairs)

    at_stage = [stage == step for step in range(stages)]
    first_core = core == 0
    at_stage, first_core, entering = lax.optimization_barrier((at_stage, first_core, entering))

    def pick(parts, mirrored_stage=False):
        tests = at_stage[::-1] if mirrored_stage else at_stage
        chosen = parts[0]
        for test, part in zip(tests[1:], parts[1:]):
            chosen = jnp.where(test, part, chosen)
        return chosen

    in_hbm = lambda array: pltpu.with_memory_space_constraint(array, pltpu.HBM)
    own, entering, ending = [in_hbm(one) for one in own], in_hbm(entering), in_hbm(ending)
    *near, enter = load(0, own, entering)
    near += [swap_cores(weight) for weight in near]
    turn = list(load(stages - 1, own))
    turn += [swap_cores(weight) for weight in turn]
    if stages > 2:
        weights = own + [swap_cores(weight) for weight in own]
    flows, trunks, inners = [], [], []
    for step in range(stages - 1):
        flow, leave, trunk, inner_sum = run_stage(
            weights if step else near, step, True, False, step == 0, rows, sizes, enter
        )
        flows.append(flow)
        trunks.append(trunk)
        inners.append(inner_sum)
        enter = hop(leave, step)
    mirrored = stages == 2
    line = jax.ShapeDtypeStruct((rows, channels), jnp.bfloat16)
    outs = [line, jax.ShapeDtypeStruct((rows, inner), jnp.float32)] + [line, line] * mirrored
    ending, first_active, *known = pl.pallas_call(
        functools.partial(meanwhile_body, stages - 1, mirrored),
        out_shape=outs,
        in_specs=[VMEM, VMEM, HBM, HBM, VMEM],
        out_specs=[VMEM] * len(outs),
        scratch_shapes=[pltpu.SemaphoreType.DMA((3,))],
        compiler_params=PARAMS,
    )(turn[1], turn[3], entering, ending, leave)
    flow, upstreams, back_inners, leave = run_stage(
        turn, stages - 1, True, True, True, rows, sizes, enter, ending, first_active
    )
    flows.append(flow)
    upstreams, back_inners = [upstreams], [back_inners]
    upstream = hop(leave, 0)
    side_flow = swap_cores(pick(flows)[1])
    near_core = lambda first, second: jnp.where(first_core, first, second)
    going = pick(flows, True)
    if mirrored:
        lifted = near_core(going[1, :, :channels], going[0, :, :channels])
        going = jnp.concatenate([lifted, going[0, :, channels:], going[1, :, channels:]], axis=1)
    far_flow = mirror(going)
    if mirrored:
        lifted, actives = far_flow[:, :channels], far_flow[:, channels:]
        far_flow = jnp.concatenate([near_core(known[1], lifted), actives[:, :inner]], axis=1)
        cross_flow = jnp.concatenate([near_core(lifted, known[1]), actives[:, inner:]], axis=1)
    else:
        far_flow, cross_flow = far_flow[0], far_flow[1]
    cross_flow = swap_cores(cross_flow)
    for step in range(stages - 2, -1, -1):
        outs = run_stage(
            weights if step else near,
            step,
            False,
            True,
            step == 0,
            rows,
            sizes,
            upstream,
            trunks[step],
            inners[step],
        )
        upstreams.insert(0, outs[0])
        back_inners.insert(0, outs[1])
        if step:
            upstream = hop(outs[2], stages - 1 - step)
    going = pick(upstreams, True)
    far_up = mirror(near_core(going[0], going[1]) if mirrored else going)
    far_inner = mirror(pick(back_inners, True))
    side_up = swap_cores(pick(upstreams)[1])
    side_inner = swap_cores(pick(back_inners)[1])
    if mirrored:
        top = jnp.where(at_stage[0], leave, known[0])
        far_up, cross_up = near_core(far_up, top), near_core(top, far_up)
    else:
        far_up, cross_up = far_up[0], far_up[1]
    cross_up = swap_cores(cross_up)
    far_inner, cross_inner = far_inner[0], far_inner[1]
    cross_inner = swap_cores(cross_inner)

    chunk = channels // replicas
    fore = flows + [side_flow, far_flow, cross_flow]
    ups = upstreams + [side_up, far_up, cross_up]
    backs = back_inners + [side_inner, far_inner, cross_inner]
    halve = halve_rows if chunk % 128 == 0 and replicas >= 4 else halve_sums
    parts = halve(stages, replicas, chunk, sizes, rows, fore, ups, backs)
    return pl.pallas_call(
        finish_body,
        out_shape=jax.ShapeDtypeStruct((1, 2, chunk, inner), jnp.float32),
        in_specs=[VMEM] * 4,
        out_specs=VMEM,
        compiler_params=PARAMS,
    )(*parts)


def sums(count, chunk, inner):
    return [
        jax.ShapeDtypeStruct((count, chunk, inner), jnp.bfloat16),
        jax.ShapeDtypeStruct((count, chunk, inner), jnp.float32),
    ]


def exchange(shard, stages, replicas, first, second):
    pairs = []
    for p in range(2 * stages):
        for q in range(replicas):
            pairs.append((p * replicas + q, p * replicas + (q ^ (second if p % 2 else first))))
    return lax.ppermute(shard, AXES, pairs)


def halve_rows(stages, replicas, chunk, sizes, rows, fore, ups, backs):
    channels, inner = sizes
    shape = lambda *dims: jax.ShapeDtypeStruct(dims, jnp.bfloat16)
    half = shape(4 * rows, channels // 2)
    narrow = shape(4 * rows, inner)
    parts = []
    for name, late in (("inner", backs), ("up", ups)):
        left, right, send = pl.pallas_call(
            functools.partial(late_body, stages, chunk, name == "up"),
            out_shape=[half, narrow, shape(4 * rows, channels // 2 + inner)],
            in_specs=[VMEM] * (len(fore) + len(late)),
            out_specs=[VMEM] * 3,
            scratch_shapes=[pltpu.VMEM((4 * rows, channels), jnp.bfloat16)],
            compiler_params=PARAMS,
        )(*fore, *late)
        came = exchange(send, stages, replicas, 1, 2)
        count = replicas // 4
        send, keep = pl.pallas_call(
            half_gradient_body,
            out_shape=sums(count, chunk, inner),
            in_specs=[VMEM] * 3,
            out_specs=[VMEM] * 2,
            scratch_shapes=[pltpu.VMEM((channels // 2, inner), jnp.float32)],
            compiler_params=PARAMS,
        )(left, right, came)
        came = exchange(send, stages, replicas, 2, 1)
        for bit in range(2, replicas.bit_length() - 1):
            count //= 2
            send, keep = pl.pallas_call(
                functools.partial(next_body, bit),
                out_shape=sums(count, chunk, inner),
                in_specs=[VMEM] * 2,
                out_specs=[VMEM] * 2,
                compiler_params=PARAMS,
            )(keep, came)
            came = exchange(send, stages, replicas, 1 << bit, 1 << bit)
        parts += [keep, came]
    return parts


def halve_sums(stages, replicas, chunk, sizes, rows, fore, ups, backs):
    channels, inner = sizes
    wide, narrow = slice(0, channels), slice(channels, channels + inner)

    def of_flows(columns):
        def pick_parts(arrays):
            near = [flow.at[0, :, columns] for flow in arrays[:stages]]
            side, far, cross = arrays[stages : stages + 3]
            return near, [side.at[:, columns], far.at[:, columns], cross.at[:, columns]]

        return pick_parts

    def of_backs(arrays):
        near = [back.at[0] for back in arrays[stages + 3 : 2 * stages + 3]]
        side, far, cross = arrays[2 * stages + 3 : 2 * stages + 6]
        return near, [side, far, cross]

    plans = [halving_plan(replicas, turn) for turn in range(2)]
    streams = []
    for pick_left, pick_right, late, plan in (
        (of_backs, of_flows(narrow), ups, plans),
        (of_flows(wide), of_backs, backs, plans[::-1]),
    ):
        arrays = fore + late
        send, keep = pl.pallas_call(
            functools.partial(gradient_body, plan, pick_left, pick_right, len(arrays)),
            out_shape=sums(replicas // 2, chunk, inner),
            in_specs=[VMEM] * len(arrays),
            out_specs=[VMEM] * 2,
            scratch_shapes=[
                pltpu.VMEM((4 * rows, channels), jnp.bfloat16),
                pltpu.VMEM((4 * rows, inner), jnp.bfloat16),
                pltpu.VMEM((channels, inner), jnp.float32),
            ],
            compiler_params=PARAMS,
        )(*arrays)
        streams.append((plan, send, keep))
    for at in range(replicas.bit_length() - 1):
        half = replicas >> (at + 2)
        arrived = []
        for plan, send, keep in streams:
            pairs = []
            for p in range(2 * stages):
                for q in range(replicas):
                    pairs.append((p * replicas + q, p * replicas + (q ^ plan[p % 2][0][at])))
            arrived.append((plan, keep, lax.ppermute(send, AXES, pairs)))
        if half == 0:
            break
        streams = []
        for plan, keep, came in arrived:
            send, keep = pl.pallas_call(
                functools.partial(halve_body, plan, at + 1),
                out_shape=sums(half, chunk, inner),
                in_specs=[VMEM] * 2,
                out_specs=[VMEM] * 2,
                compiler_params=PARAMS,
            )(keep, came)
            streams.append((plan, send, keep))
    (_, keep_expand, came_expand), (_, keep_reduce, came_reduce) = arrived
    return keep_reduce, came_reduce, keep_expand, came_expand


def solution(mesh):
    return jax.shard_map(
        shards,
        mesh=mesh,
        in_specs=(
            P(None, None, "dp", None),
            P(None, None, "dp", None),
            P(None, "pipe", None, None),
            P(None, "pipe", None, None),
        ),
        out_specs=P("pipe", None, "dp", None),
        check_vma=False,
    )
```

```python
import functools

import jax
import jax.numpy as jnp
from jax import lax
from jax.experimental import pallas as pl
from jax.experimental.pallas import tpu as pltpu
from jax.sharding import PartitionSpec as P


EPSILON = 1e-06
AXES = ("pipe", "dp")
HBM = pl.BlockSpec(memory_space=pltpu.HBM)
ANY = pl.BlockSpec(memory_space=pl.ANY)
VMEM = pl.BlockSpec(memory_space=pltpu.VMEM)
PARAMS = pltpu.CompilerParams(vmem_limit_bytes=16 << 20)


def contract(first_op, second_op, first_dim, second_dim):
    return lax.dot_general(
        first_op,
        second_op,
        (((first_dim,), (second_dim,)), ((), ())),
        preferred_element_type=jnp.float32,
    )


def smooth_slope(values):
    sigma = jax.nn.sigmoid(values)
    return sigma * (1.0 + values * (1.0 - sigma))


def norm_of(widened):
    return lax.rsqrt(jnp.mean(widened * widened, axis=-1, keepdims=True) + EPSILON)


def where_am_i(step):
    position = lax.axis_index("pipe")
    stage, core = lax.div(position, 2), lax.rem(position, 2)
    way = jnp.where(stage == step, 0, 1)
    return stage, core, way


PIECES = 4


def bring_all(sources, outs, sems):
    copies = []
    for at, (source, out) in enumerate(zip(sources, outs)):
        size = out.shape[0] // PIECES
        for piece in range(PIECES):
            part = pl.ds(piece * size, size)
            copies.append(
                pltpu.make_async_copy(source.at[part], out.at[part], sems.at[at, piece])
            )
    for copy in copies:
        copy.start()
    return copies


def load_body(step, reduce_all, expand_all, *refs):
    _, core, way = where_am_i(step)
    sources, outs = [reduce_all.at[way], expand_all.at[way]], refs[:-1]
    if step == 0:
        sources.append(refs[0].at[way, core])
        outs = outs[1:]
    for copy in bring_all(sources, outs, refs[-1]):
        copy.wait()


def load(step, own, *more):
    channels, inner = own[0].shape[1:]
    mat = jax.ShapeDtypeStruct((channels, inner), jnp.bfloat16)
    outs = [mat, mat] + [jax.ShapeDtypeStruct(a.shape[2:], a.dtype) for a in more]
    return pl.pallas_call(
        functools.partial(load_body, step),
        out_shape=outs,
        in_specs=[HBM] * (2 + len(more)),
        out_specs=[VMEM] * len(outs),
        scratch_shapes=[pltpu.SemaphoreType.DMA((len(outs), PIECES))],
        compiler_params=PARAMS,
    )(*own, *more)


def meanwhile_body(step, mirrored, expand_own, expand_other, inputs, cotangent, leave, *refs):
    outs, sems = refs[:-1], refs[-1]
    stage, core, way = where_am_i(step)
    ending, back_active = outs[:2]
    sources = [cotangent.at[way, core]]
    if mirrored:
        sources += [cotangent.at[1, core], inputs.at[1, core]]
    copies = bring_all(sources, [outs[0]] + list(outs[2:]), sems)
    for copy in copies[:PIECES]:
        copy.wait()

    @pl.when(way == core)
    def _():
        back_active[...] = jnp.dot(
            ending[...], expand_other[...], preferred_element_type=jnp.float32
        )

    @pl.when(way != core)
    def _():
        back_active[...] = jnp.dot(ending[...], expand_own[...], preferred_element_type=jnp.float32)

    for copy in copies[PIECES:]:
        copy.wait()
    if mirrored:
        rows = outs[3]

        @pl.when(stage != 0)
        def _():
            rows[...] = leave[...]

        widened = rows[...].astype(jnp.float32)
        rows[...] = jax.nn.silu(widened * norm_of(widened)).astype(jnp.bfloat16)


def weight_copies(own, other, held, sems, core, way):
    copies = []
    for order in range(2):
        is_own = lax.rem(way + order, 2) == core
        for kind in range(2):
            mine = pltpu.make_async_copy(own[kind].at[way], held[kind].at[order], sems.at[kind, order])
            theirs = pltpu.make_async_copy(
                other[kind].at[way], held[kind].at[order], sems.at[kind, order]
            )
            copies.append((is_own, mine, theirs))
    return copies


def start_all(copies):
    for is_own, mine, theirs in copies:
        pl.when(is_own)(mine.start)
        pl.when(jnp.logical_not(is_own))(theirs.start)


def stage_body(step, forward, backward, last, near, *refs):
    refs = list(refs)
    _, core, way = where_am_i(step)
    own, other = (refs.pop(0), refs.pop(0)), (refs.pop(0), refs.pop(0))
    enter = refs.pop(0) if forward else None
    upstream_in = refs.pop(0) if backward else None
    first_active = refs.pop(0) if forward and backward else None
    if not forward:
        trunks, inners = refs.pop(0), refs.pop(0)
    if forward:
        flows = refs.pop(0)
    if forward and not backward:
        leave = refs.pop(0)
    if backward:
        upstreams, back_inners = refs.pop(0), refs.pop(0)
    if backward and not last:
        back_leave = refs.pop(0)
    if forward:
        trunks, inners = refs.pop(0), refs.pop(0)
    channels = trunks.shape[2]

    def run(reduce_mats, expand_mats, wait):
        if forward:
            rows = enter[...]
            for order in range(2):
                slot = lax.rem(order + core, 2)
                widened = rows.astype(jnp.float32)
                normed = widened * norm_of(widened)
                lifted = jax.nn.silu(normed).astype(jnp.bfloat16)
                trunks[order] = rows
                flows[slot, :, :channels] = lifted
                wait(0, order)
                inner_sum = jnp.dot(
                    lifted, reduce_mats[order][...], preferred_element_type=jnp.float32
                )
                active = jax.nn.silu(inner_sum).astype(jnp.bfloat16)
                inners[order] = inner_sum
                flows[slot, :, channels:] = active
                wait(1, order)
                rows = (widened + contract(active, expand_mats[order][...], 1, 1)).astype(jnp.bfloat16)
            if not backward:
                leave[...] = rows
        if backward:
            upstream = upstream_in[...]
            for order in (1, 0):
                slot = lax.rem(order + core, 2)
                upstreams[slot] = upstream
                if not forward:
                    wait(1, order)
                if forward and order:
                    back_active = first_active[...]
                else:
                    back_active = jnp.dot(
                        upstream, expand_mats[order][...], preferred_element_type=jnp.float32
                    )
                back_inner = (back_active * smooth_slope(inners[order])).astype(jnp.bfloat16)
                back_inners[slot] = back_inner
                if not forward:
                    wait(0, order)
                if last and order == 0:
                    break
                back_lifted = contract(back_inner, reduce_mats[order][...], 1, 1)
                widened = trunks[order].astype(jnp.float32)
                norm_scale = norm_of(widened)
                back_normed = back_lifted * smooth_slope(widened * norm_scale)
                projection = jnp.mean(back_normed * widened, axis=-1, keepdims=True)
                upstream = (
                    upstream.astype(jnp.float32)
                    + norm_scale * back_normed
                    - widened * norm_scale**3 * projection
                ).astype(jnp.bfloat16)
            if not last:
                back_leave[...] = upstream

    if near:
        idle = lambda kind, order: None

        @pl.when(way == core)
        def _():
            run((own[0], other[0]), (own[1], other[1]), idle)

        @pl.when(way != core)
        def _():
            run((other[0], own[0]), (other[1], own[1]), idle)

    else:
        held = (refs.pop(0), refs.pop(0))
        copies = weight_copies(own, other, held, refs.pop(0), core, way)
        start_all(copies if forward else copies[2:] + copies[:2])
        run(
            [held[0].at[order] for order in range(2)],
            [held[1].at[order] for order in range(2)],
            lambda kind, order: copies[2 * order + kind][1].wait(),
        )


def run_stage(weights, step, forward, backward, near, rows, sizes, *arrays):
    channels, inner = sizes
    last = backward and step == 0 and not forward
    shape = lambda dtype, *dims: jax.ShapeDtypeStruct(dims, dtype)
    line = shape(jnp.bfloat16, rows, channels)
    kept = [((2, rows, channels), jnp.bfloat16), ((2, rows, inner), jnp.float32)]
    outs, scratch = [], []
    if forward:
        outs.append(shape(jnp.bfloat16, 2, rows, channels + inner))
    if forward and not backward:
        outs.append(line)
    if backward:
        outs.append(shape(jnp.bfloat16, 2, rows, channels))
        outs.append(shape(jnp.bfloat16, 2, rows, inner))
    if backward and not last:
        outs.append(line)
    if forward and not backward:
        outs += [jax.ShapeDtypeStruct(*one) for one in kept]
    if forward and backward:
        scratch += [pltpu.VMEM(*one) for one in kept]
    if not near:
        scratch += [pltpu.VMEM((2, channels, inner), jnp.bfloat16)] * 2
        scratch += [pltpu.SemaphoreType.DMA((2, 2))]
    passes = 4 * (int(forward) + int(backward))
    return pl.pallas_call(
        functools.partial(stage_body, step, forward, backward, last, near),
        out_shape=outs,
        in_specs=[VMEM if near else ANY] * 4 + [VMEM] * len(arrays),
        out_specs=[VMEM] * len(outs),
        scratch_shapes=scratch,
        compiler_params=PARAMS,
        cost_estimate=pl.CostEstimate(
            flops=2 * passes * rows * channels * inner,
            bytes_accessed=8 * channels * inner,
            transcendentals=passes * rows * channels,
        ),
    )(*weights, *arrays)


def parity(value, mask):
    total, bit = 0, 0
    while mask >> bit:
        if mask >> bit & 1:
            total = total + lax.rem(lax.div(value, 1 << bit), 2)
        bit += 1
    return lax.rem(total, 2)


def halving_plan(size, turn):
    order = [1 << bit for bit in range(size.bit_length() - 1)]
    if turn and len(order) > 1:
        order[:2] = order[1::-1]
    table = [0] * size
    for chunk in range(size):
        place = 0
        for mask in order:
            place = 2 * place + int(chunk & mask != 0)
        table[place] = chunk
    return order, order, table


def side_of(plans, at):
    core, shard = lax.rem(lax.axis_index("pipe"), 2), lax.axis_index("dp")
    return jnp.where(core == 0, parity(shard, plans[0][1][at]), parity(shard, plans[1][1][at]))


def gradient_body(plans, pick_left, pick_right, count, *refs):
    arrays, (send, keep, left, right, full) = refs[:count], refs[count:]
    stage, core, _ = where_am_i(0)
    rows = left.shape[0] // 4
    chunk = send.shape[1]
    for target, pick in ((left, pick_left), (right, pick_right)):
        near, away = pick(arrays)
        for step, part in enumerate(near):

            @pl.when(stage == step)
            def _():
                target[:rows] = part[...]

        for at, part in enumerate(away):
            target[(at + 1) * rows : (at + 2) * rows] = part[...]
    full[...] = contract(left[...], right[...], 0, 0)
    side = side_of(plans, 0)
    half = send.shape[0]
    flip = [plan[2][half] for plan in plans]
    for at in range(half):
        spots = []
        for target_side in (1 - side, side):
            first = plans[0][2][at] ^ (flip[0] * target_side)
            second = plans[1][2][at] ^ (flip[1] * target_side)
            spots.append(pl.multiple_of(jnp.where(core == 0, first, second) * chunk, chunk))
        send[at] = full[pl.ds(spots[0], chunk)].astype(jnp.bfloat16)
        keep[at] = full[pl.ds(spots[1], chunk)]


def halve_body(plans, at, keep_in, came, send, keep):
    half = keep.shape[0]
    side = side_of(plans, at)
    for spot in range(half):
        mine, theirs = side * half + spot, (1 - side) * half + spot
        send[spot] = (keep_in[theirs] + came[theirs].astype(jnp.float32)).astype(jnp.bfloat16)
        keep[spot] = keep_in[mine] + came[mine].astype(jnp.float32)


def bit_of(value, bit):
    return lax.rem(lax.div(value, 1 << bit), 2)


def first_sides():
    core, shard = lax.rem(lax.axis_index("pipe"), 2), lax.axis_index("dp")
    low, high = bit_of(shard, 0), bit_of(shard, 1)
    return core, jnp.where(core == 0, low, high), jnp.where(core == 0, high, low)


def split_columns(wide, keep, send, chunk):
    core, side, _ = first_sides()
    for place in range(wide.shape[1] // (2 * chunk)):
        for target, at in ((keep, side), (send, 1 - side)):
            block = jnp.where(core == 0, 2 * place + at, place // 2 * 4 + 2 * at + place % 2)
            source = pl.ds(pl.multiple_of(block * chunk, chunk), chunk)
            target[:, place * chunk : (place + 1) * chunk] = wide[:, source]


def gather_rows(target, near, away):
    stage, _, _ = where_am_i(0)
    rows = target.shape[0] // 4
    for step, part in enumerate(near):

        @pl.when(stage == step)
        def _():
            target[:rows] = part[...]

    for at, part in enumerate(away):
        target[(at + 1) * rows : (at + 2) * rows] = part[...]


def flow_rows(arrays, stages, columns):
    near = [flow.at[0, :, columns] for flow in arrays[:stages]]
    return near, [part.at[:, columns] for part in arrays[stages : stages + 3]]


def back_rows(arrays, stages):
    return [back.at[0] for back in arrays[:stages]], arrays[stages : stages + 3]


def late_body(stages, chunk, up, *refs):
    left, right, send, wide = refs[2 * stages + 6 :]
    channels = wide.shape[1]
    backs = back_rows(refs[stages + 3 :], stages)
    if up:
        gather_rows(wide, *backs)
        gather_rows(right, *flow_rows(refs, stages, slice(channels, None)))
    else:
        gather_rows(wide, *flow_rows(refs, stages, slice(0, channels)))
        gather_rows(right, *backs)
    split_columns(wide, left, send, chunk)
    send[:, channels // 2 :] = right[...]


def half_gradient_body(left, right, came, send, keep, full):
    columns = left.shape[1]
    full[...] = contract(left[...], right[...], 0, 0) + contract(
        came[:, :columns], came[:, columns:], 0, 0
    )
    _, _, side = first_sides()
    chunk = send.shape[1]
    for place in range(send.shape[0]):
        theirs = pl.ds(pl.multiple_of((2 * place + 1 - side) * chunk, chunk), chunk)
        mine = pl.ds(pl.multiple_of((2 * place + side) * chunk, chunk), chunk)
        send[place] = full[theirs].astype(jnp.bfloat16)
        keep[place] = full[mine]


def next_body(bit, keep_in, came, send, keep):
    side = bit_of(lax.axis_index("dp"), bit)
    for place in range(keep.shape[0]):
        theirs, mine = 2 * place + 1 - side, 2 * place + side
        send[place] = (keep_in[theirs] + came[theirs].astype(jnp.float32)).astype(jnp.bfloat16)
        keep[place] = keep_in[mine] + came[mine].astype(jnp.float32)


def finish_body(keep_reduce, came_reduce, keep_expand, came_expand, out):
    out[0, 0] = keep_reduce[0] + came_reduce[0].astype(jnp.float32)
    out[0, 1] = keep_expand[0] + came_expand[0].astype(jnp.float32)


def shards(inputs, cotangent, reduce_weight, expand_weight):
    stages = lax.axis_size("pipe") // 2
    replicas = lax.axis_size("dp")
    stage, core, _ = where_am_i(0)
    channels, inner = reduce_weight.shape[2:]
    rows = inputs.shape[1] * inputs.shape[2] // 2
    sizes = (channels, inner)
    entering = inputs.reshape(2, 2, rows, channels)
    ending = cotangent.reshape(2, 2, rows, channels)
    own = [reduce_weight[:, 0], expand_weight[:, 0]]

    core_pairs = [(p, p ^ 1) for p in range(2 * stages)]
    mirror_pairs = [(p, 2 * (stages - 1 - p // 2) + p % 2) for p in range(2 * stages)]

    def hop(shard, step):
        pairs = []
        for c in range(2):
            pairs.append((2 * step + c, 2 * step + 2 + c))
            pairs.append((2 * (stages - 1 - step) + c, 2 * (stages - 2 - step) + c))
        return lax.ppermute(shard, "pipe", pairs)

    def swap_cores(shard):
        return lax.ppermute(shard, "pipe", core_pairs)

    def mirror(shard):
        return lax.ppermute(shard, "pipe", mirror_pairs)

    at_stage = [stage == step for step in range(stages)]
    first_core = core == 0
    at_stage, first_core, entering = lax.optimization_barrier((at_stage, first_core, entering))

    def pick(parts, mirrored_stage=False):
        tests = at_stage[::-1] if mirrored_stage else at_stage
        chosen = parts[0]
        for test, part in zip(tests[1:], parts[1:]):
            chosen = jnp.where(test, part, chosen)
        return chosen

    in_hbm = lambda array: pltpu.with_memory_space_constraint(array, pltpu.HBM)
    own, entering, ending = [in_hbm(one) for one in own], in_hbm(entering), in_hbm(ending)
    *near, enter = load(0, own, entering)
    near += [swap_cores(weight) for weight in near]
    turn = list(load(stages - 1, own))
    turn += [swap_cores(weight) for weight in turn]
    if stages > 2:
        weights = own + [swap_cores(weight) for weight in own]
    flows, trunks, inners = [], [], []
    for step in range(stages - 1):
        flow, leave, trunk, inner_sum = run_stage(
            weights if step else near, step, True, False, step == 0, rows, sizes, enter
        )
        flows.append(flow)
        trunks.append(trunk)
        inners.append(inner_sum)
        enter = hop(leave, step)
    mirrored = stages == 2
    line = jax.ShapeDtypeStruct((rows, channels), jnp.bfloat16)
    outs = [line, jax.ShapeDtypeStruct((rows, inner), jnp.float32)] + [line, line] * mirrored
    ending, first_active, *known = pl.pallas_call(
        functools.partial(meanwhile_body, stages - 1, mirrored),
        out_shape=outs,
        in_specs=[VMEM, VMEM, HBM, HBM, VMEM],
        out_specs=[VMEM] * len(outs),
        scratch_shapes=[pltpu.SemaphoreType.DMA((3, PIECES))],
        compiler_params=PARAMS,
    )(turn[1], turn[3], entering, ending, leave)
    flow, upstreams, back_inners, leave = run_stage(
        turn, stages - 1, True, True, True, rows, sizes, enter, ending, first_active
    )
    flows.append(flow)
    upstreams, back_inners = [upstreams], [back_inners]
    upstream = hop(leave, 0)
    side_flow = swap_cores(pick(flows)[1])
    near_core = lambda first, second: jnp.where(first_core, first, second)
    going = pick(flows, True)
    if mirrored:
        lifted = near_core(going[1, :, :channels], going[0, :, :channels])
        going = jnp.concatenate([lifted, going[0, :, channels:], going[1, :, channels:]], axis=1)
    far_flow = mirror(going)
    if mirrored:
        lifted, actives = far_flow[:, :channels], far_flow[:, channels:]
        far_flow = jnp.concatenate([near_core(known[1], lifted), actives[:, :inner]], axis=1)
        cross_flow = jnp.concatenate([near_core(lifted, known[1]), actives[:, inner:]], axis=1)
    else:
        far_flow, cross_flow = far_flow[0], far_flow[1]
    cross_flow = swap_cores(cross_flow)
    for step in range(stages - 2, -1, -1):
        outs = run_stage(
            weights if step else near,
            step,
            False,
            True,
            step == 0,
            rows,
            sizes,
            upstream,
            trunks[step],
            inners[step],
        )
        upstreams.insert(0, outs[0])
        back_inners.insert(0, outs[1])
        if step:
            upstream = hop(outs[2], stages - 1 - step)
    going = pick(upstreams, True)
    far_up = mirror(near_core(going[0], going[1]) if mirrored else going)
    far_inner = mirror(pick(back_inners, True))
    side_up = swap_cores(pick(upstreams)[1])
    side_inner = swap_cores(pick(back_inners)[1])
    if mirrored:
        top = jnp.where(at_stage[0], leave, known[0])
        far_up, cross_up = near_core(far_up, top), near_core(top, far_up)
    else:
        far_up, cross_up = far_up[0], far_up[1]
    cross_up = swap_cores(cross_up)
    far_inner, cross_inner = far_inner[0], far_inner[1]
    cross_inner = swap_cores(cross_inner)

    chunk = channels // replicas
    fore = flows + [side_flow, far_flow, cross_flow]
    ups = upstreams + [side_up, far_up, cross_up]
    backs = back_inners + [side_inner, far_inner, cross_inner]
    halve = halve_rows if chunk % 128 == 0 and replicas >= 4 else halve_sums
    parts = halve(stages, replicas, chunk, sizes, rows, fore, ups, backs)
    return pl.pallas_call(
        finish_body,
        out_shape=jax.ShapeDtypeStruct((1, 2, chunk, inner), jnp.float32),
        in_specs=[VMEM] * 4,
        out_specs=VMEM,
        compiler_params=PARAMS,
    )(*parts)


def sums(count, chunk, inner):
    return [
        jax.ShapeDtypeStruct((count, chunk, inner), jnp.bfloat16),
        jax.ShapeDtypeStruct((count, chunk, inner), jnp.float32),
    ]


def exchange(shard, stages, replicas, first, second):
    pairs = []
    for p in range(2 * stages):
        for q in range(replicas):
            pairs.append((p * replicas + q, p * replicas + (q ^ (second if p % 2 else first))))
    return lax.ppermute(shard, AXES, pairs)


def halve_rows(stages, replicas, chunk, sizes, rows, fore, ups, backs):
    channels, inner = sizes
    shape = lambda *dims: jax.ShapeDtypeStruct(dims, jnp.bfloat16)
    half = shape(4 * rows, channels // 2)
    narrow = shape(4 * rows, inner)
    parts = []
    for name, late in (("inner", backs), ("up", ups)):
        left, right, send = pl.pallas_call(
            functools.partial(late_body, stages, chunk, name == "up"),
            out_shape=[half, narrow, shape(4 * rows, channels // 2 + inner)],
            in_specs=[VMEM] * (len(fore) + len(late)),
            out_specs=[VMEM] * 3,
            scratch_shapes=[pltpu.VMEM((4 * rows, channels), jnp.bfloat16)],
            compiler_params=PARAMS,
        )(*fore, *late)
        came = exchange(send, stages, replicas, 1, 2)
        count = replicas // 4
        send, keep = pl.pallas_call(
            half_gradient_body,
            out_shape=sums(count, chunk, inner),
            in_specs=[VMEM] * 3,
            out_specs=[VMEM] * 2,
            scratch_shapes=[pltpu.VMEM((channels // 2, inner), jnp.float32)],
            compiler_params=PARAMS,
        )(left, right, came)
        came = exchange(send, stages, replicas, 2, 1)
        for bit in range(2, replicas.bit_length() - 1):
            count //= 2
            send, keep = pl.pallas_call(
                functools.partial(next_body, bit),
                out_shape=sums(count, chunk, inner),
                in_specs=[VMEM] * 2,
                out_specs=[VMEM] * 2,
                compiler_params=PARAMS,
            )(keep, came)
            came = exchange(send, stages, replicas, 1 << bit, 1 << bit)
        parts += [keep, came]
    return parts


def halve_sums(stages, replicas, chunk, sizes, rows, fore, ups, backs):
    channels, inner = sizes
    wide, narrow = slice(0, channels), slice(channels, channels + inner)

    def of_flows(columns):
        def pick_parts(arrays):
            near = [flow.at[0, :, columns] for flow in arrays[:stages]]
            side, far, cross = arrays[stages : stages + 3]
            return near, [side.at[:, columns], far.at[:, columns], cross.at[:, columns]]

        return pick_parts

    def of_backs(arrays):
        near = [back.at[0] for back in arrays[stages + 3 : 2 * stages + 3]]
        side, far, cross = arrays[2 * stages + 3 : 2 * stages + 6]
        return near, [side, far, cross]

    plans = [halving_plan(replicas, turn) for turn in range(2)]
    streams = []
    for pick_left, pick_right, late, plan in (
        (of_backs, of_flows(narrow), ups, plans),
        (of_flows(wide), of_backs, backs, plans[::-1]),
    ):
        arrays = fore + late
        send, keep = pl.pallas_call(
            functools.partial(gradient_body, plan, pick_left, pick_right, len(arrays)),
            out_shape=sums(replicas // 2, chunk, inner),
            in_specs=[VMEM] * len(arrays),
            out_specs=[VMEM] * 2,
            scratch_shapes=[
                pltpu.VMEM((4 * rows, channels), jnp.bfloat16),
                pltpu.VMEM((4 * rows, inner), jnp.bfloat16),
                pltpu.VMEM((channels, inner), jnp.float32),
            ],
            compiler_params=PARAMS,
        )(*arrays)
        streams.append((plan, send, keep))
    for at in range(replicas.bit_length() - 1):
        half = replicas >> (at + 2)
        arrived = []
        for plan, send, keep in streams:
            pairs = []
            for p in range(2 * stages):
                for q in range(replicas):
                    pairs.append((p * replicas + q, p * replicas + (q ^ plan[p % 2][0][at])))
            arrived.append((plan, keep, lax.ppermute(send, AXES, pairs)))
        if half == 0:
            break
        streams = []
        for plan, keep, came in arrived:
            send, keep = pl.pallas_call(
                functools.partial(halve_body, plan, at + 1),
                out_shape=sums(half, chunk, inner),
                in_specs=[VMEM] * 2,
                out_specs=[VMEM] * 2,
                compiler_params=PARAMS,
            )(keep, came)
            streams.append((plan, send, keep))
    (_, keep_expand, came_expand), (_, keep_reduce, came_reduce) = arrived
    return keep_reduce, came_reduce, keep_expand, came_expand


def solution(mesh):
    return jax.shard_map(
        shards,
        mesh=mesh,
        in_specs=(
            P(None, None, "dp", None),
            P(None, None, "dp", None),
            P(None, "pipe", None, None),
            P(None, "pipe", None, None),
        ),
        out_specs=P("pipe", None, "dp", None),
        check_vma=False,
    )
```

```python
import functools

import jax
import jax.numpy as jnp
from jax import lax
from jax.experimental import pallas as pl
from jax.experimental.pallas import tpu as pltpu
from jax.sharding import PartitionSpec as P


EPSILON = 1e-06
AXES = ("pipe", "dp")
HBM = pl.BlockSpec(memory_space=pltpu.HBM)
ANY = pl.BlockSpec(memory_space=pl.ANY)
VMEM = pl.BlockSpec(memory_space=pltpu.VMEM)
PARAMS = pltpu.CompilerParams(vmem_limit_bytes=16 << 20)


def contract(first_op, second_op, first_dim, second_dim):
    return lax.dot_general(
        first_op,
        second_op,
        (((first_dim,), (second_dim,)), ((), ())),
        preferred_element_type=jnp.float32,
    )


def smooth_slope(values):
    sigma = jax.nn.sigmoid(values)
    return sigma * (1.0 + values * (1.0 - sigma))


def norm_of(widened):
    return lax.rsqrt(jnp.mean(widened * widened, axis=-1, keepdims=True) + EPSILON)


def where_am_i(step):
    position = lax.axis_index("pipe")
    stage, core = lax.div(position, 2), lax.rem(position, 2)
    way = jnp.where(stage == step, 0, 1)
    return stage, core, way


def bring_all(sources, outs, sems):
    copies = [
        pltpu.make_async_copy(source, out, sems.at[at])
        for at, (source, out) in enumerate(zip(sources, outs))
    ]
    for copy in copies:
        copy.start()
    return copies


def load_body(step, reduce_all, expand_all, *refs):
    _, core, way = where_am_i(step)
    sources, outs = [reduce_all.at[way], expand_all.at[way]], refs[:-1]
    if step == 0:
        sources.append(refs[0].at[way, core])
        outs = outs[1:]
    for copy in bring_all(sources, outs, refs[-1]):
        copy.wait()


def load(step, own, *more):
    channels, inner = own[0].shape[1:]
    mat = jax.ShapeDtypeStruct((channels, inner), jnp.bfloat16)
    outs = [mat, mat] + [jax.ShapeDtypeStruct(a.shape[2:], a.dtype) for a in more]
    return pl.pallas_call(
        functools.partial(load_body, step),
        out_shape=outs,
        in_specs=[HBM] * (2 + len(more)),
        out_specs=[VMEM] * len(outs),
        scratch_shapes=[pltpu.SemaphoreType.DMA((len(outs),))],
        compiler_params=PARAMS,
    )(*own, *more)


def meanwhile_body(step, mirrored, expand_own, expand_other, inputs, cotangent, leave, *refs):
    outs, sems = refs[:-1], refs[-1]
    stage, core, way = where_am_i(step)
    ending, back_active = outs[:2]
    sources = [cotangent.at[way, core]]
    if mirrored:
        sources += [cotangent.at[1, core], inputs.at[1, core]]
    copies = bring_all(sources, [outs[0]] + list(outs[2:]), sems)
    copies[0].wait()

    @pl.when(way == core)
    def _():
        back_active[...] = jnp.dot(
            ending[...], expand_other[...], preferred_element_type=jnp.float32
        )

    @pl.when(way != core)
    def _():
        back_active[...] = jnp.dot(ending[...], expand_own[...], preferred_element_type=jnp.float32)

    for copy in copies[1:]:
        copy.wait()
    if mirrored:
        rows = outs[3]

        @pl.when(stage != 0)
        def _():
            rows[...] = leave[...]

        widened = rows[...].astype(jnp.float32)
        rows[...] = jax.nn.silu(widened * norm_of(widened)).astype(jnp.bfloat16)


def weight_copies(own, other, held, sems, core, way):
    copies = []
    for order in range(2):
        is_own = lax.rem(way + order, 2) == core
        for kind in range(2):
            mine = pltpu.make_async_copy(own[kind].at[way], held[kind].at[order], sems.at[kind, order])
            theirs = pltpu.make_async_copy(
                other[kind].at[way], held[kind].at[order], sems.at[kind, order]
            )
            copies.append((is_own, mine, theirs))
    return copies


def start_all(copies):
    for is_own, mine, theirs in copies:
        pl.when(is_own)(mine.start)
        pl.when(jnp.logical_not(is_own))(theirs.start)


def stage_body(step, forward, backward, last, near, *refs):
    refs = list(refs)
    _, core, way = where_am_i(step)
    own, other = (refs.pop(0), refs.pop(0)), (refs.pop(0), refs.pop(0))
    enter = refs.pop(0) if forward else None
    upstream_in = refs.pop(0) if backward else None
    first_active = refs.pop(0) if forward and backward else None
    if not forward:
        trunks, inners = refs.pop(0), refs.pop(0)
    if forward:
        flows = refs.pop(0)
    if forward and not backward:
        leave = refs.pop(0)
    if backward:
        upstreams, back_inners = refs.pop(0), refs.pop(0)
    if backward and not last:
        back_leave = refs.pop(0)
    if forward:
        trunks, inners = refs.pop(0), refs.pop(0)
    channels = trunks.shape[2]

    def run(reduce_mats, expand_mats, wait):
        if forward:
            rows = enter[...]
            for order in range(2):
                slot = lax.rem(order + core, 2)
                widened = rows.astype(jnp.float32)
                normed = widened * norm_of(widened)
                lifted = jax.nn.silu(normed).astype(jnp.bfloat16)
                trunks[order] = rows
                flows[slot, :, :channels] = lifted
                wait(0, order)
                inner_sum = jnp.dot(
                    lifted, reduce_mats[order][...], preferred_element_type=jnp.float32
                )
                active = jax.nn.silu(inner_sum).astype(jnp.bfloat16)
                inners[order] = inner_sum
                flows[slot, :, channels:] = active
                wait(1, order)
                rows = (widened + contract(active, expand_mats[order][...], 1, 1)).astype(jnp.bfloat16)
            if not backward:
                leave[...] = rows
        if backward:
            upstream = upstream_in[...]
            for order in (1, 0):
                slot = lax.rem(order + core, 2)
                upstreams[slot] = upstream
                if not forward:
                    wait(1, order)
                if forward and order:
                    back_active = first_active[...]
                else:
                    back_active = jnp.dot(
                        upstream, expand_mats[order][...], preferred_element_type=jnp.float32
                    )
                back_inner = (back_active * smooth_slope(inners[order])).astype(jnp.bfloat16)
                back_inners[slot] = back_inner
                if not forward:
                    wait(0, order)
                if last and order == 0:
                    break
                back_lifted = contract(back_inner, reduce_mats[order][...], 1, 1)
                widened = trunks[order].astype(jnp.float32)
                norm_scale = norm_of(widened)
                back_normed = back_lifted * smooth_slope(widened * norm_scale)
                projection = jnp.mean(back_normed * widened, axis=-1, keepdims=True)
                upstream = (
                    upstream.astype(jnp.float32)
                    + norm_scale * back_normed
                    - widened * norm_scale**3 * projection
                ).astype(jnp.bfloat16)
            if not last:
                back_leave[...] = upstream

    if near:
        idle = lambda kind, order: None

        @pl.when(way == core)
        def _():
            run((own[0], other[0]), (own[1], other[1]), idle)

        @pl.when(way != core)
        def _():
            run((other[0], own[0]), (other[1], own[1]), idle)

    else:
        held = (refs.pop(0), refs.pop(0))
        copies = weight_copies(own, other, held, refs.pop(0), core, way)
        start_all(copies if forward else copies[2:] + copies[:2])
        run(
            [held[0].at[order] for order in range(2)],
            [held[1].at[order] for order in range(2)],
            lambda kind, order: copies[2 * order + kind][1].wait(),
        )


def run_stage(weights, step, forward, backward, near, rows, sizes, *arrays):
    channels, inner = sizes
    last = backward and step == 0 and not forward
    shape = lambda dtype, *dims: jax.ShapeDtypeStruct(dims, dtype)
    line = shape(jnp.bfloat16, rows, channels)
    kept = [((2, rows, channels), jnp.bfloat16), ((2, rows, inner), jnp.float32)]
    outs, scratch = [], []
    if forward:
        outs.append(shape(jnp.bfloat16, 2, rows, channels + inner))
    if forward and not backward:
        outs.append(line)
    if backward:
        outs.append(shape(jnp.bfloat16, 2, rows, channels))
        outs.append(shape(jnp.bfloat16, 2, rows, inner))
    if backward and not last:
        outs.append(line)
    if forward and not backward:
        outs += [jax.ShapeDtypeStruct(*one) for one in kept]
    if forward and backward:
        scratch += [pltpu.VMEM(*one) for one in kept]
    if not near:
        scratch += [pltpu.VMEM((2, channels, inner), jnp.bfloat16)] * 2
        scratch += [pltpu.SemaphoreType.DMA((2, 2))]
    passes = 4 * (int(forward) + int(backward))
    return pl.pallas_call(
        functools.partial(stage_body, step, forward, backward, last, near),
        out_shape=outs,
        in_specs=[VMEM if near else ANY] * 4 + [VMEM] * len(arrays),
        out_specs=[VMEM] * len(outs),
        scratch_shapes=scratch,
        compiler_params=PARAMS,
        cost_estimate=pl.CostEstimate(
            flops=2 * passes * rows * channels * inner,
            bytes_accessed=8 * channels * inner,
            transcendentals=passes * rows * channels,
        ),
    )(*weights, *arrays)


def parity(value, mask):
    total, bit = 0, 0
    while mask >> bit:
        if mask >> bit & 1:
            total = total + lax.rem(lax.div(value, 1 << bit), 2)
        bit += 1
    return lax.rem(total, 2)


def halving_plan(size, turn):
    order = [1 << bit for bit in range(size.bit_length() - 1)]
    if turn and len(order) > 1:
        order[:2] = order[1::-1]
    table = [0] * size
    for chunk in range(size):
        place = 0
        for mask in order:
            place = 2 * place + int(chunk & mask != 0)
        table[place] = chunk
    return order, order, table


def side_of(plans, at):
    core, shard = lax.rem(lax.axis_index("pipe"), 2), lax.axis_index("dp")
    return jnp.where(core == 0, parity(shard, plans[0][1][at]), parity(shard, plans[1][1][at]))


def gradient_body(plans, pick_left, pick_right, count, *refs):
    arrays, (send, keep, left, right, full) = refs[:count], refs[count:]
    stage, core, _ = where_am_i(0)
    rows = left.shape[0] // 4
    chunk = send.shape[1]
    for target, pick in ((left, pick_left), (right, pick_right)):
        near, away = pick(arrays)
        for step, part in enumerate(near):

            @pl.when(stage == step)
            def _():
                target[:rows] = part[...]

        for at, part in enumerate(away):
            target[(at + 1) * rows : (at + 2) * rows] = part[...]
    full[...] = contract(left[...], right[...], 0, 0)
    side = side_of(plans, 0)
    half = send.shape[0]
    flip = [plan[2][half] for plan in plans]
    for at in range(half):
        spots = []
        for target_side in (1 - side, side):
            first = plans[0][2][at] ^ (flip[0] * target_side)
            second = plans[1][2][at] ^ (flip[1] * target_side)
            spots.append(pl.multiple_of(jnp.where(core == 0, first, second) * chunk, chunk))
        send[at] = full[pl.ds(spots[0], chunk)].astype(jnp.bfloat16)
        keep[at] = full[pl.ds(spots[1], chunk)]


def halve_body(plans, at, keep_in, came, send, keep):
    half = keep.shape[0]
    side = side_of(plans, at)
    for spot in range(half):
        mine, theirs = side * half + spot, (1 - side) * half + spot
        send[spot] = (keep_in[theirs] + came[theirs].astype(jnp.float32)).astype(jnp.bfloat16)
        keep[spot] = keep_in[mine] + came[mine].astype(jnp.float32)


def bit_of(value, bit):
    return lax.rem(lax.div(value, 1 << bit), 2)


def first_sides():
    core, shard = lax.rem(lax.axis_index("pipe"), 2), lax.axis_index("dp")
    low, high = bit_of(shard, 0), bit_of(shard, 1)
    return core, jnp.where(core == 0, low, high), jnp.where(core == 0, high, low)


def split_columns(wide, keep, send, chunk):
    core, side, _ = first_sides()
    for place in range(wide.shape[1] // (2 * chunk)):
        for target, at in ((keep, side), (send, 1 - side)):
            block = jnp.where(core == 0, 2 * place + at, place // 2 * 4 + 2 * at + place % 2)
            source = pl.ds(pl.multiple_of(block * chunk, chunk), chunk)
            target[:, place * chunk : (place + 1) * chunk] = wide[:, source]


def near_body(stages, chunk, *refs):
    parts = [refs[at * (stages + 1) : (at + 1) * (stages + 1)] for at in range(3)]
    outs = refs[3 * (stages + 1) :]
    keeps, send, wide = outs[:4], outs[4], outs[5]
    rows, channels = wide.shape[0] // 2, wide.shape[1]
    inner = keeps[1].shape[1]
    stage, _, _ = where_am_i(0)
    flows, ups, backs = parts
    everything = slice(None)
    columns = 0
    for at, (lefts, left_columns, rights, right_columns) in enumerate(
        (
            (ups, everything, flows, slice(channels, channels + inner)),
            (flows, slice(0, channels), backs, everything),
        )
    ):
        left, right = keeps[2 * at : 2 * at + 2]
        for target, sources, span in ((wide, lefts, left_columns), (right, rights, right_columns)):
            for step in range(stages):

                @pl.when(stage == step)
                def _():
                    target[:rows] = sources[step][0, :, span]

            target[rows:] = sources[stages][:, span]
        split_columns(wide, left, send.at[:, columns : columns + channels // 2], chunk)
        columns += channels // 2
        send[:, columns : columns + inner] = right[...]
        columns += inner


def late_body(chunk, up, flow, cross_flow, back, cross_back, left, right, send, wide):
    channels = wide.shape[1]
    rows = wide.shape[0] // 2
    for at, (flow_rows, back_rows) in enumerate(((flow, back), (cross_flow, cross_back))):
        place = slice(at * rows, (at + 1) * rows)
        if up:
            wide[place] = back_rows[...]
            right[place] = flow_rows[:, channels:]
        else:
            wide[place] = flow_rows[:, :channels]
            right[place] = back_rows[...]
    split_columns(wide, left, send, chunk)
    send[:, channels // 2 :] = right[...]


def half_gradient_body(at, *refs):
    lefts, rights, cames = refs[:2], refs[2:4], refs[4:6]
    send, keep, full, left, right = refs[6:]
    rows, columns = lefts[0].shape
    inner = rights[0].shape[1]
    starts = (at * (columns + inner), 0)
    for group in range(2):
        place = slice(group * rows, (group + 1) * rows)
        left[place] = lefts[group][...]
        right[place] = rights[group][...]
        place = slice((group + 2) * rows, (group + 3) * rows)
        left[place] = cames[group][:, starts[group] : starts[group] + columns]
        right[place] = cames[group][:, starts[group] + columns : starts[group] + columns + inner]
    full[...] = contract(left[...], right[...], 0, 0)
    _, _, side = first_sides()
    chunk = send.shape[1]
    for place in range(send.shape[0]):
        theirs = pl.ds(pl.multiple_of((2 * place + 1 - side) * chunk, chunk), chunk)
        mine = pl.ds(pl.multiple_of((2 * place + side) * chunk, chunk), chunk)
        send[place] = full[theirs].astype(jnp.bfloat16)
        keep[place] = full[mine]


def next_body(bit, keep_in, came, send, keep):
    side = bit_of(lax.axis_index("dp"), bit)
    for place in range(keep.shape[0]):
        theirs, mine = 2 * place + 1 - side, 2 * place + side
        send[place] = (keep_in[theirs] + came[theirs].astype(jnp.float32)).astype(jnp.bfloat16)
        keep[place] = keep_in[mine] + came[mine].astype(jnp.float32)


def finish_body(keep_reduce, came_reduce, keep_expand, came_expand, out):
    out[0, 0] = keep_reduce[0] + came_reduce[0].astype(jnp.float32)
    out[0, 1] = keep_expand[0] + came_expand[0].astype(jnp.float32)


def shards(inputs, cotangent, reduce_weight, expand_weight):
    stages = lax.axis_size("pipe") // 2
    replicas = lax.axis_size("dp")
    stage, core, _ = where_am_i(0)
    channels, inner = reduce_weight.shape[2:]
    rows = inputs.shape[1] * inputs.shape[2] // 2
    sizes = (channels, inner)
    entering = inputs.reshape(2, 2, rows, channels)
    ending = cotangent.reshape(2, 2, rows, channels)
    own = [reduce_weight[:, 0], expand_weight[:, 0]]

    core_pairs = [(p, p ^ 1) for p in range(2 * stages)]
    mirror_pairs = [(p, 2 * (stages - 1 - p // 2) + p % 2) for p in range(2 * stages)]

    def hop(shard, step):
        pairs = []
        for c in range(2):
            pairs.append((2 * step + c, 2 * step + 2 + c))
            pairs.append((2 * (stages - 1 - step) + c, 2 * (stages - 2 - step) + c))
        return lax.ppermute(shard, "pipe", pairs)

    def swap_cores(shard):
        return lax.ppermute(shard, "pipe", core_pairs)

    def mirror(shard):
        return lax.ppermute(shard, "pipe", mirror_pairs)

    at_stage = [stage == step for step in range(stages)]
    first_core = core == 0
    at_stage, first_core, entering = lax.optimization_barrier((at_stage, first_core, entering))

    def pick(parts, mirrored_stage=False):
        tests = at_stage[::-1] if mirrored_stage else at_stage
        chosen = parts[0]
        for test, part in zip(tests[1:], parts[1:]):
            chosen = jnp.where(test, part, chosen)
        return chosen

    in_hbm = lambda array: pltpu.with_memory_space_constraint(array, pltpu.HBM)
    own, entering, ending = [in_hbm(one) for one in own], in_hbm(entering), in_hbm(ending)
    *near, enter = load(0, own, entering)
    near += [swap_cores(weight) for weight in near]
    turn = list(load(stages - 1, own))
    turn += [swap_cores(weight) for weight in turn]
    if stages > 2:
        weights = own + [swap_cores(weight) for weight in own]
    flows, trunks, inners = [], [], []
    for step in range(stages - 1):
        flow, leave, trunk, inner_sum = run_stage(
            weights if step else near, step, True, False, step == 0, rows, sizes, enter
        )
        flows.append(flow)
        trunks.append(trunk)
        inners.append(inner_sum)
        enter = hop(leave, step)
    mirrored = stages == 2
    line = jax.ShapeDtypeStruct((rows, channels), jnp.bfloat16)
    outs = [line, jax.ShapeDtypeStruct((rows, inner), jnp.float32)] + [line, line] * mirrored
    ending, first_active, *known = pl.pallas_call(
        functools.partial(meanwhile_body, stages - 1, mirrored),
        out_shape=outs,
        in_specs=[VMEM, VMEM, HBM, HBM, VMEM],
        out_specs=[VMEM] * len(outs),
        scratch_shapes=[pltpu.SemaphoreType.DMA((3,))],
        compiler_params=PARAMS,
    )(turn[1], turn[3], entering, ending, leave)
    flow, upstreams, back_inners, leave = run_stage(
        turn, stages - 1, True, True, True, rows, sizes, enter, ending, first_active
    )
    flows.append(flow)
    upstreams, back_inners = [upstreams], [back_inners]
    upstream = hop(leave, 0)
    side_flow = swap_cores(pick(flows)[1])
    near_core = lambda first, second: jnp.where(first_core, first, second)
    going = pick(flows, True)
    if mirrored:
        lifted = near_core(going[1, :, :channels], going[0, :, :channels])
        going = jnp.concatenate([lifted, going[0, :, channels:], going[1, :, channels:]], axis=1)
    far_flow = mirror(going)
    if mirrored:
        lifted, actives = far_flow[:, :channels], far_flow[:, channels:]
        far_flow = jnp.concatenate([near_core(known[1], lifted), actives[:, :inner]], axis=1)
        cross_flow = jnp.concatenate([near_core(lifted, known[1]), actives[:, inner:]], axis=1)
    else:
        far_flow, cross_flow = far_flow[0], far_flow[1]
    cross_flow = swap_cores(cross_flow)
    for step in range(stages - 2, -1, -1):
        outs = run_stage(
            weights if step else near,
            step,
            False,
            True,
            step == 0,
            rows,
            sizes,
            upstream,
            trunks[step],
            inners[step],
        )
        upstreams.insert(0, outs[0])
        back_inners.insert(0, outs[1])
        if step:
            upstream = hop(outs[2], stages - 1 - step)
    going = pick(upstreams, True)
    far_up = mirror(near_core(going[0], going[1]) if mirrored else going)
    far_inner = mirror(pick(back_inners, True))
    side_up = swap_cores(pick(upstreams)[1])
    side_inner = swap_cores(pick(back_inners)[1])
    if mirrored:
        top = jnp.where(at_stage[0], leave, known[0])
        far_up, cross_up = near_core(far_up, top), near_core(top, far_up)
    else:
        far_up, cross_up = far_up[0], far_up[1]
    cross_up = swap_cores(cross_up)
    far_inner, cross_inner = far_inner[0], far_inner[1]
    cross_inner = swap_cores(cross_inner)

    chunk = channels // replicas
    fore = flows + [side_flow, far_flow, cross_flow]
    ups = upstreams + [side_up, far_up, cross_up]
    backs = back_inners + [side_inner, far_inner, cross_inner]
    halve = halve_rows if chunk % 128 == 0 and replicas >= 4 else halve_sums
    parts = halve(stages, replicas, chunk, sizes, rows, fore, ups, backs)
    return pl.pallas_call(
        finish_body,
        out_shape=jax.ShapeDtypeStruct((1, 2, chunk, inner), jnp.float32),
        in_specs=[VMEM] * 4,
        out_specs=VMEM,
        compiler_params=PARAMS,
    )(*parts)


def sums(count, chunk, inner):
    return [
        jax.ShapeDtypeStruct((count, chunk, inner), jnp.bfloat16),
        jax.ShapeDtypeStruct((count, chunk, inner), jnp.float32),
    ]


def exchange(shard, stages, replicas, first, second):
    pairs = []
    for p in range(2 * stages):
        for q in range(replicas):
            pairs.append((p * replicas + q, p * replicas + (q ^ (second if p % 2 else first))))
    return lax.ppermute(shard, AXES, pairs)


def halve_rows(stages, replicas, chunk, sizes, rows, fore, ups, backs):
    channels, inner = sizes
    shape = lambda *dims: jax.ShapeDtypeStruct(dims, jnp.bfloat16)
    half = shape(2 * rows, channels // 2)
    narrow = shape(2 * rows, inner)
    width = channels // 2 + inner
    wide = pltpu.VMEM((2 * rows, channels), jnp.bfloat16)
    near = [one for late in (fore, ups, backs) for one in late[: stages + 1]]
    *keeps, send = pl.pallas_call(
        functools.partial(near_body, stages, chunk),
        out_shape=[half, narrow, half, narrow, shape(2 * rows, 2 * width)],
        in_specs=[VMEM] * len(near),
        out_specs=[VMEM] * 5,
        scratch_shapes=[wide],
        compiler_params=PARAMS,
    )(*near)
    came_near = exchange(send, stages, replicas, 1, 2)
    parts = []
    for at, name, late in ((1, "inner", backs), (0, "up", ups)):
        left, right, send = pl.pallas_call(
            functools.partial(late_body, chunk, name == "up"),
            out_shape=[half, narrow, shape(2 * rows, width)],
            in_specs=[VMEM] * 4,
            out_specs=[VMEM] * 3,
            scratch_shapes=[wide],
            compiler_params=PARAMS,
        )(*fore[stages + 1 :], *late[stages + 1 :])
        came = exchange(send, stages, replicas, 1, 2)
        operands = (keeps[2 * at], left, keeps[2 * at + 1], right, came_near, came)
        count = replicas // 4
        send, keep = pl.pallas_call(
            functools.partial(half_gradient_body, at),
            out_shape=sums(count, chunk, inner),
            in_specs=[VMEM] * 6,
            out_specs=[VMEM] * 2,
            scratch_shapes=[
                pltpu.VMEM((channels // 2, inner), jnp.float32),
                pltpu.VMEM((8 * rows, channels // 2), jnp.bfloat16),
                pltpu.VMEM((8 * rows, inner), jnp.bfloat16),
            ],
            compiler_params=PARAMS,
        )(*operands)
        came = exchange(send, stages, replicas, 2, 1)
        for bit in range(2, replicas.bit_length() - 1):
            count //= 2
            send, keep = pl.pallas_call(
                functools.partial(next_body, bit),
                out_shape=sums(count, chunk, inner),
                in_specs=[VMEM] * 2,
                out_specs=[VMEM] * 2,
                compiler_params=PARAMS,
            )(keep, came)
            came = exchange(send, stages, replicas, 1 << bit, 1 << bit)
        parts += [keep, came]
    return parts


def halve_sums(stages, replicas, chunk, sizes, rows, fore, ups, backs):
    channels, inner = sizes
    wide, narrow = slice(0, channels), slice(channels, channels + inner)

    def of_flows(columns):
        def pick_parts(arrays):
            near = [flow.at[0, :, columns] for flow in arrays[:stages]]
            side, far, cross = arrays[stages : stages + 3]
            return near, [side.at[:, columns], far.at[:, columns], cross.at[:, columns]]

        return pick_parts

    def of_backs(arrays):
        near = [back.at[0] for back in arrays[stages + 3 : 2 * stages + 3]]
        side, far, cross = arrays[2 * stages + 3 : 2 * stages + 6]
        return near, [side, far, cross]

    plans = [halving_plan(replicas, turn) for turn in range(2)]
    streams = []
    for pick_left, pick_right, late, plan in (
        (of_backs, of_flows(narrow), ups, plans),
        (of_flows(wide), of_backs, backs, plans[::-1]),
    ):
        arrays = fore + late
        send, keep = pl.pallas_call(
            functools.partial(gradient_body, plan, pick_left, pick_right, len(arrays)),
            out_shape=sums(replicas // 2, chunk, inner),
            in_specs=[VMEM] * len(arrays),
            out_specs=[VMEM] * 2,
            scratch_shapes=[
                pltpu.VMEM((4 * rows, channels), jnp.bfloat16),
                pltpu.VMEM((4 * rows, inner), jnp.bfloat16),
                pltpu.VMEM((channels, inner), jnp.float32),
            ],
            compiler_params=PARAMS,
        )(*arrays)
        streams.append((plan, send, keep))
    for at in range(replicas.bit_length() - 1):
        half = replicas >> (at + 2)
        arrived = []
        for plan, send, keep in streams:
            pairs = []
            for p in range(2 * stages):
                for q in range(replicas):
                    pairs.append((p * replicas + q, p * replicas + (q ^ plan[p % 2][0][at])))
            arrived.append((plan, keep, lax.ppermute(send, AXES, pairs)))
        if half == 0:
            break
        streams = []
        for plan, keep, came in arrived:
            send, keep = pl.pallas_call(
                functools.partial(halve_body, plan, at + 1),
                out_shape=sums(half, chunk, inner),
                in_specs=[VMEM] * 2,
                out_specs=[VMEM] * 2,
                compiler_params=PARAMS,
            )(keep, came)
            streams.append((plan, send, keep))
    (_, keep_expand, came_expand), (_, keep_reduce, came_reduce) = arrived
    return keep_reduce, came_reduce, keep_expand, came_expand


def solution(mesh):
    return jax.shard_map(
        shards,
        mesh=mesh,
        in_specs=(
            P(None, None, "dp", None),
            P(None, None, "dp", None),
            P(None, "pipe", None, None),
            P(None, "pipe", None, None),
        ),
        out_specs=P("pipe", None, "dp", None),
        check_vma=False,
    )
```

```python
import functools

import jax
import jax.numpy as jnp
from jax import lax
from jax.experimental import pallas as pl
from jax.experimental.pallas import tpu as pltpu
from jax.sharding import PartitionSpec as P


EPSILON = 1e-06
AXES = ("pipe", "dp")
HBM = pl.BlockSpec(memory_space=pltpu.HBM)
ANY = pl.BlockSpec(memory_space=pl.ANY)
VMEM = pl.BlockSpec(memory_space=pltpu.VMEM)
PARAMS = pltpu.CompilerParams(vmem_limit_bytes=16 << 20)


def contract(first_op, second_op, first_dim, second_dim):
    return lax.dot_general(
        first_op,
        second_op,
        (((first_dim,), (second_dim,)), ((), ())),
        preferred_element_type=jnp.float32,
    )


def smooth_slope(values):
    sigma = jax.nn.sigmoid(values)
    return sigma * (1.0 + values * (1.0 - sigma))


def norm_of(widened):
    return lax.rsqrt(jnp.mean(widened * widened, axis=-1, keepdims=True) + EPSILON)


def where_am_i(step):
    position = lax.axis_index("pipe")
    stage, core = lax.div(position, 2), lax.rem(position, 2)
    way = jnp.where(stage == step, 0, 1)
    return stage, core, way


def bring_all(sources, outs, sems):
    copies = [
        pltpu.make_async_copy(source, out, sems.at[at])
        for at, (source, out) in enumerate(zip(sources, outs))
    ]
    for copy in copies:
        copy.start()
    return copies


def load_body(step, reduce_all, expand_all, *refs):
    _, core, way = where_am_i(step)
    sources, outs = [reduce_all.at[way], expand_all.at[way]], refs[:-1]
    if step == 0:
        sources.append(refs[0].at[way, core])
        outs = outs[1:]
    for copy in bring_all(sources, outs, refs[-1]):
        copy.wait()


def load(step, own, *more):
    channels, inner = own[0].shape[1:]
    mat = jax.ShapeDtypeStruct((channels, inner), jnp.bfloat16)
    outs = [mat, mat] + [jax.ShapeDtypeStruct(a.shape[2:], a.dtype) for a in more]
    return pl.pallas_call(
        functools.partial(load_body, step),
        out_shape=outs,
        in_specs=[HBM] * (2 + len(more)),
        out_specs=[VMEM] * len(outs),
        scratch_shapes=[pltpu.SemaphoreType.DMA((len(outs),))],
        compiler_params=PARAMS,
    )(*own, *more)


def meanwhile_body(step, mirrored, expand_own, expand_other, inputs, cotangent, leave, *refs):
    outs, sems = refs[:-1], refs[-1]
    stage, core, way = where_am_i(step)
    ending, back_active = outs[:2]
    sources = [cotangent.at[way, core]]
    if mirrored:
        sources += [cotangent.at[1, core], inputs.at[1, core]]
    copies = bring_all(sources, [outs[0]] + list(outs[2:]), sems)
    copies[0].wait()

    @pl.when(way == core)
    def _():
        back_active[...] = jnp.dot(
            ending[...], expand_other[...], preferred_element_type=jnp.float32
        )

    @pl.when(way != core)
    def _():
        back_active[...] = jnp.dot(ending[...], expand_own[...], preferred_element_type=jnp.float32)

    for copy in copies[1:]:
        copy.wait()
    if mirrored:
        rows = outs[3]

        @pl.when(stage != 0)
        def _():
            rows[...] = leave[...]

        widened = rows[...].astype(jnp.float32)
        rows[...] = jax.nn.silu(widened * norm_of(widened)).astype(jnp.bfloat16)


def weight_copies(own, other, held, sems, core, way):
    copies = []
    for order in range(2):
        is_own = lax.rem(way + order, 2) == core
        for kind in range(2):
            mine = pltpu.make_async_copy(own[kind].at[way], held[kind].at[order], sems.at[kind, order])
            theirs = pltpu.make_async_copy(
                other[kind].at[way], held[kind].at[order], sems.at[kind, order]
            )
            copies.append((is_own, mine, theirs))
    return copies


def start_all(copies):
    for is_own, mine, theirs in copies:
        pl.when(is_own)(mine.start)
        pl.when(jnp.logical_not(is_own))(theirs.start)


def stage_body(step, forward, backward, last, near, *refs):
    refs = list(refs)
    _, core, way = where_am_i(step)
    own, other = (refs.pop(0), refs.pop(0)), (refs.pop(0), refs.pop(0))
    enter = refs.pop(0) if forward else None
    upstream_in = refs.pop(0) if backward else None
    first_active = refs.pop(0) if forward and backward else None
    if not forward:
        trunks, inners = refs.pop(0), refs.pop(0)
    if forward:
        flows = refs.pop(0)
    if forward and not backward:
        leave = refs.pop(0)
    if backward:
        upstreams, back_inners = refs.pop(0), refs.pop(0)
    if backward and not last:
        back_leave = refs.pop(0)
    if forward:
        trunks, inners = refs.pop(0), refs.pop(0)
    channels = trunks.shape[2]

    def run(reduce_mats, expand_mats, wait):
        if forward:
            rows = enter[...]
            for order in range(2):
                slot = lax.rem(order + core, 2)
                widened = rows.astype(jnp.float32)
                normed = widened * norm_of(widened)
                lifted = jax.nn.silu(normed).astype(jnp.bfloat16)
                trunks[order] = rows
                flows[slot, :, :channels] = lifted
                wait(0, order)
                inner_sum = jnp.dot(
                    lifted, reduce_mats[order][...], preferred_element_type=jnp.float32
                )
                active = jax.nn.silu(inner_sum).astype(jnp.bfloat16)
                inners[order] = inner_sum
                flows[slot, :, channels:] = active
                wait(1, order)
                rows = (widened + contract(active, expand_mats[order][...], 1, 1)).astype(jnp.bfloat16)
            if not backward:
                leave[...] = rows
        if backward:
            upstream = upstream_in[...]
            for order in (1, 0):
                slot = lax.rem(order + core, 2)
                upstreams[slot] = upstream
                if last and order == 0:
                    break
                if not forward:
                    wait(1, order)
                if forward and order:
                    back_active = first_active[...]
                else:
                    back_active = jnp.dot(
                        upstream, expand_mats[order][...], preferred_element_type=jnp.float32
                    )
                back_inner = (back_active * smooth_slope(inners[order])).astype(jnp.bfloat16)
                back_inners[slot] = back_inner
                if not forward:
                    wait(0, order)
                back_lifted = contract(back_inner, reduce_mats[order][...], 1, 1)
                widened = trunks[order].astype(jnp.float32)
                norm_scale = norm_of(widened)
                back_normed = back_lifted * smooth_slope(widened * norm_scale)
                projection = jnp.mean(back_normed * widened, axis=-1, keepdims=True)
                upstream = (
                    upstream.astype(jnp.float32)
                    + norm_scale * back_normed
                    - widened * norm_scale**3 * projection
                ).astype(jnp.bfloat16)
            if not last:
                back_leave[...] = upstream

    if near:
        idle = lambda kind, order: None

        @pl.when(way == core)
        def _():
            run((own[0], other[0]), (own[1], other[1]), idle)

        @pl.when(way != core)
        def _():
            run((other[0], own[0]), (other[1], own[1]), idle)

    else:
        held = (refs.pop(0), refs.pop(0))
        copies = weight_copies(own, other, held, refs.pop(0), core, way)
        start_all(copies if forward else copies[2:] + copies[:2])
        run(
            [held[0].at[order] for order in range(2)],
            [held[1].at[order] for order in range(2)],
            lambda kind, order: copies[2 * order + kind][1].wait(),
        )


def tail_body(own, other, upstreams, back_first, inners, back_inners):
    _, core, way = where_am_i(0)

    def run(expand_mat):
        back_active = jnp.dot(upstreams[core], expand_mat[...], preferred_element_type=jnp.float32)
        back_inners[core] = (back_active * smooth_slope(inners[0])).astype(jnp.bfloat16)
        back_inners[1 - core] = back_first[1 - core]

    pl.when(way == core)(lambda: run(own))
    pl.when(way != core)(lambda: run(other))


def run_stage(weights, step, forward, backward, near, rows, sizes, *arrays):
    channels, inner = sizes
    last = backward and step == 0 and not forward
    shape = lambda dtype, *dims: jax.ShapeDtypeStruct(dims, dtype)
    line = shape(jnp.bfloat16, rows, channels)
    kept = [((2, rows, channels), jnp.bfloat16), ((2, rows, inner), jnp.float32)]
    outs, scratch = [], []
    if forward:
        outs.append(shape(jnp.bfloat16, 2, rows, channels + inner))
    if forward and not backward:
        outs.append(line)
    if backward:
        outs.append(shape(jnp.bfloat16, 2, rows, channels))
        outs.append(shape(jnp.bfloat16, 2, rows, inner))
    if backward and not last:
        outs.append(line)
    if forward and not backward:
        outs += [jax.ShapeDtypeStruct(*one) for one in kept]
    if forward and backward:
        scratch += [pltpu.VMEM(*one) for one in kept]
    if not near:
        scratch += [pltpu.VMEM((2, channels, inner), jnp.bfloat16)] * 2
        scratch += [pltpu.SemaphoreType.DMA((2, 2))]
    passes = 4 * (int(forward) + int(backward))
    return pl.pallas_call(
        functools.partial(stage_body, step, forward, backward, last, near),
        out_shape=outs,
        in_specs=[VMEM if near else ANY] * 4 + [VMEM] * len(arrays),
        out_specs=[VMEM] * len(outs),
        scratch_shapes=scratch,
        compiler_params=PARAMS,
        cost_estimate=pl.CostEstimate(
            flops=2 * passes * rows * channels * inner,
            bytes_accessed=8 * channels * inner,
            transcendentals=passes * rows * channels,
        ),
    )(*weights, *arrays)


def parity(value, mask):
    total, bit = 0, 0
    while mask >> bit:
        if mask >> bit & 1:
            total = total + lax.rem(lax.div(value, 1 << bit), 2)
        bit += 1
    return lax.rem(total, 2)


def halving_plan(size, turn):
    order = [1 << bit for bit in range(size.bit_length() - 1)]
    if turn and len(order) > 1:
        order[:2] = order[1::-1]
    table = [0] * size
    for chunk in range(size):
        place = 0
        for mask in order:
            place = 2 * place + int(chunk & mask != 0)
        table[place] = chunk
    return order, order, table


def side_of(plans, at):
    core, shard = lax.rem(lax.axis_index("pipe"), 2), lax.axis_index("dp")
    return jnp.where(core == 0, parity(shard, plans[0][1][at]), parity(shard, plans[1][1][at]))


def gradient_body(plans, pick_left, pick_right, count, *refs):
    arrays, (send, keep, left, right, full) = refs[:count], refs[count:]
    stage, core, _ = where_am_i(0)
    rows = left.shape[0] // 4
    chunk = send.shape[1]
    for target, pick in ((left, pick_left), (right, pick_right)):
        near, away = pick(arrays)
        for step, part in enumerate(near):

            @pl.when(stage == step)
            def _():
                target[:rows] = part[...]

        for at, part in enumerate(away):
            target[(at + 1) * rows : (at + 2) * rows] = part[...]
    full[...] = contract(left[...], right[...], 0, 0)
    side = side_of(plans, 0)
    half = send.shape[0]
    flip = [plan[2][half] for plan in plans]
    for at in range(half):
        spots = []
        for target_side in (1 - side, side):
            first = plans[0][2][at] ^ (flip[0] * target_side)
            second = plans[1][2][at] ^ (flip[1] * target_side)
            spots.append(pl.multiple_of(jnp.where(core == 0, first, second) * chunk, chunk))
        send[at] = full[pl.ds(spots[0], chunk)].astype(jnp.bfloat16)
        keep[at] = full[pl.ds(spots[1], chunk)]


def halve_body(plans, at, keep_in, came, send, keep):
    half = keep.shape[0]
    side = side_of(plans, at)
    for spot in range(half):
        mine, theirs = side * half + spot, (1 - side) * half + spot
        send[spot] = (keep_in[theirs] + came[theirs].astype(jnp.float32)).astype(jnp.bfloat16)
        keep[spot] = keep_in[mine] + came[mine].astype(jnp.float32)


def bit_of(value, bit):
    return lax.rem(lax.div(value, 1 << bit), 2)


def first_sides():
    core, shard = lax.rem(lax.axis_index("pipe"), 2), lax.axis_index("dp")
    low, high = bit_of(shard, 0), bit_of(shard, 1)
    return core, jnp.where(core == 0, low, high), jnp.where(core == 0, high, low)


def split_columns(wide, keep, send, chunk):
    core, side, _ = first_sides()
    for place in range(wide.shape[1] // (2 * chunk)):
        for target, at in ((keep, side), (send, 1 - side)):
            block = jnp.where(core == 0, 2 * place + at, place // 2 * 4 + 2 * at + place % 2)
            source = pl.ds(pl.multiple_of(block * chunk, chunk), chunk)
            target[:, place * chunk : (place + 1) * chunk] = wide[:, source]


def pack_body(stages, chunk, up, near, far, *refs):
    refs = list(refs)
    left, right, send, wide = refs[-4:]
    channels = wide.shape[1]
    spans = slice(0, channels), slice(channels, None), slice(None)
    flow_span, back_span = (spans[1] if up else spans[0]), spans[2]
    stage, _, _ = where_am_i(0)
    rows = wide.shape[0] // (2 * near + 2 * far)
    start = 0
    targets = (right, wide) if up else (wide, right)
    for target, span in zip(targets, (flow_span, back_span)):
        start = 0
        if near:
            parts = [refs.pop(0) for _ in range(stages + 1)]
            for step in range(stages):

                @pl.when(stage == step)
                def _():
                    target[:rows] = parts[step][0, :, span]

            target[rows : 2 * rows] = parts[stages][:, span]
            start = 2 * rows
        if far:
            for part in (refs.pop(0), refs.pop(0)):
                target[start : start + rows] = part[:, span]
                start += rows
    split_columns(wide, left, send, chunk)
    send[:, channels // 2 :] = right[...]


def half_gradient_body(groups, *refs):
    send, keep, full, left, right = refs[3 * groups :]
    start = 0
    for group in range(groups):
        part_left, part_right, came = refs[3 * group : 3 * group + 3]
        rows, columns = part_left.shape
        left[start : start + rows] = part_left[...]
        right[start : start + rows] = part_right[...]
        start += rows
        left[start : start + rows] = came[:, :columns]
        right[start : start + rows] = came[:, columns:]
        start += rows
    full[...] = contract(left[...], right[...], 0, 0)
    _, _, side = first_sides()
    chunk = send.shape[1]
    for place in range(send.shape[0]):
        theirs = pl.ds(pl.multiple_of((2 * place + 1 - side) * chunk, chunk), chunk)
        mine = pl.ds(pl.multiple_of((2 * place + side) * chunk, chunk), chunk)
        send[place] = full[theirs].astype(jnp.bfloat16)
        keep[place] = full[mine]


def next_body(bit, keep_in, came, send, keep):
    side = bit_of(lax.axis_index("dp"), bit)
    for place in range(keep.shape[0]):
        theirs, mine = 2 * place + 1 - side, 2 * place + side
        send[place] = (keep_in[theirs] + came[theirs].astype(jnp.float32)).astype(jnp.bfloat16)
        keep[place] = keep_in[mine] + came[mine].astype(jnp.float32)


def finish_body(keep_reduce, came_reduce, keep_expand, came_expand, out):
    out[0, 0] = keep_reduce[0] + came_reduce[0].astype(jnp.float32)
    out[0, 1] = keep_expand[0] + came_expand[0].astype(jnp.float32)


def shards(inputs, cotangent, reduce_weight, expand_weight):
    stages = lax.axis_size("pipe") // 2
    replicas = lax.axis_size("dp")
    stage, core, _ = where_am_i(0)
    channels, inner = reduce_weight.shape[2:]
    rows = inputs.shape[1] * inputs.shape[2] // 2
    sizes = (channels, inner)
    entering = inputs.reshape(2, 2, rows, channels)
    ending = cotangent.reshape(2, 2, rows, channels)
    own = [reduce_weight[:, 0], expand_weight[:, 0]]

    core_pairs = [(p, p ^ 1) for p in range(2 * stages)]
    mirror_pairs = [(p, 2 * (stages - 1 - p // 2) + p % 2) for p in range(2 * stages)]

    def hop(shard, step):
        pairs = []
        for c in range(2):
            pairs.append((2 * step + c, 2 * step + 2 + c))
            pairs.append((2 * (stages - 1 - step) + c, 2 * (stages - 2 - step) + c))
        return lax.ppermute(shard, "pipe", pairs)

    def swap_cores(shard):
        return lax.ppermute(shard, "pipe", core_pairs)

    def mirror(shard):
        return lax.ppermute(shard, "pipe", mirror_pairs)

    at_stage = [stage == step for step in range(stages)]
    first_core = core == 0
    at_stage, first_core, entering = lax.optimization_barrier((at_stage, first_core, entering))

    def pick(parts, mirrored_stage=False):
        tests = at_stage[::-1] if mirrored_stage else at_stage
        chosen = parts[0]
        for test, part in zip(tests[1:], parts[1:]):
            chosen = jnp.where(test, part, chosen)
        return chosen

    in_hbm = lambda array: pltpu.with_memory_space_constraint(array, pltpu.HBM)
    own, entering, ending = [in_hbm(one) for one in own], in_hbm(entering), in_hbm(ending)
    *near, enter = load(0, own, entering)
    near += [swap_cores(weight) for weight in near]
    turn = list(load(stages - 1, own))
    turn += [swap_cores(weight) for weight in turn]
    if stages > 2:
        weights = own + [swap_cores(weight) for weight in own]
    flows, trunks, inners = [], [], []
    for step in range(stages - 1):
        flow, leave, trunk, inner_sum = run_stage(
            weights if step else near, step, True, False, step == 0, rows, sizes, enter
        )
        flows.append(flow)
        trunks.append(trunk)
        inners.append(inner_sum)
        enter = hop(leave, step)
    mirrored = stages == 2
    line = jax.ShapeDtypeStruct((rows, channels), jnp.bfloat16)
    outs = [line, jax.ShapeDtypeStruct((rows, inner), jnp.float32)] + [line, line] * mirrored
    ending, first_active, *known = pl.pallas_call(
        functools.partial(meanwhile_body, stages - 1, mirrored),
        out_shape=outs,
        in_specs=[VMEM, VMEM, HBM, HBM, VMEM],
        out_specs=[VMEM] * len(outs),
        scratch_shapes=[pltpu.SemaphoreType.DMA((3,))],
        compiler_params=PARAMS,
    )(turn[1], turn[3], entering, ending, leave)
    flow, upstreams, back_inners, leave = run_stage(
        turn, stages - 1, True, True, True, rows, sizes, enter, ending, first_active
    )
    flows.append(flow)
    upstreams, back_inners = [upstreams], [back_inners]
    upstream = hop(leave, 0)
    side_flow = swap_cores(pick(flows)[1])
    near_core = lambda first, second: jnp.where(first_core, first, second)
    going = pick(flows, True)
    if mirrored:
        lifted = near_core(going[1, :, :channels], going[0, :, :channels])
        going = jnp.concatenate([lifted, going[0, :, channels:], going[1, :, channels:]], axis=1)
    far_flow = mirror(going)
    if mirrored:
        lifted, actives = far_flow[:, :channels], far_flow[:, channels:]
        far_flow = jnp.concatenate([near_core(known[1], lifted), actives[:, :inner]], axis=1)
        cross_flow = jnp.concatenate([near_core(lifted, known[1]), actives[:, inner:]], axis=1)
    else:
        far_flow, cross_flow = far_flow[0], far_flow[1]
    cross_flow = swap_cores(cross_flow)
    for step in range(stages - 2, -1, -1):
        outs = run_stage(
            weights if step else near,
            step,
            False,
            True,
            step == 0,
            rows,
            sizes,
            upstream,
            trunks[step],
            inners[step],
        )
        upstreams.insert(0, outs[0])
        if step:
            upstream = hop(outs[2], stages - 1 - step)
            back_inners.insert(0, outs[1])
            continue
        tail = pl.pallas_call(
            tail_body,
            out_shape=jax.ShapeDtypeStruct(outs[1].shape, outs[1].dtype),
            in_specs=[VMEM] * 5,
            out_specs=VMEM,
            compiler_params=PARAMS,
        )(near[1], near[3], outs[0], outs[1], inners[0])
        back_inners.insert(0, tail)
    going = pick(upstreams, True)
    far_up = mirror(near_core(going[0], going[1]) if mirrored else going)
    far_inner = mirror(pick(back_inners, True))
    side_up = swap_cores(pick(upstreams)[1])
    side_inner = swap_cores(pick(back_inners)[1])
    if mirrored:
        top = jnp.where(at_stage[0], leave, known[0])
        far_up, cross_up = near_core(far_up, top), near_core(top, far_up)
    else:
        far_up, cross_up = far_up[0], far_up[1]
    cross_up = swap_cores(cross_up)
    far_inner, cross_inner = far_inner[0], far_inner[1]
    cross_inner = swap_cores(cross_inner)

    chunk = channels // replicas
    fore = flows + [side_flow, far_flow, cross_flow]
    ups = upstreams + [side_up, far_up, cross_up]
    backs = back_inners + [side_inner, far_inner, cross_inner]
    halve = halve_rows if chunk % 128 == 0 and replicas >= 4 else halve_sums
    parts = halve(stages, replicas, chunk, sizes, rows, fore, ups, backs)
    return pl.pallas_call(
        finish_body,
        out_shape=jax.ShapeDtypeStruct((1, 2, chunk, inner), jnp.float32),
        in_specs=[VMEM] * 4,
        out_specs=VMEM,
        compiler_params=PARAMS,
    )(*parts)


def sums(count, chunk, inner):
    return [
        jax.ShapeDtypeStruct((count, chunk, inner), jnp.bfloat16),
        jax.ShapeDtypeStruct((count, chunk, inner), jnp.float32),
    ]


def exchange(shard, stages, replicas, first, second):
    pairs = []
    for p in range(2 * stages):
        for q in range(replicas):
            pairs.append((p * replicas + q, p * replicas + (q ^ (second if p % 2 else first))))
    return lax.ppermute(shard, AXES, pairs)


def halve_rows(stages, replicas, chunk, sizes, rows, fore, ups, backs):
    channels, inner = sizes
    shape = lambda *dims: jax.ShapeDtypeStruct(dims, jnp.bfloat16)

    def pack(late, up, near, far):
        count = 2 * (near + far)
        arrays = []
        for one in (fore, late):
            arrays += one[: stages + 1] * near + one[stages + 1 :] * far
        return pl.pallas_call(
            functools.partial(pack_body, stages, chunk, up, near, far),
            out_shape=[
                shape(count * rows, channels // 2),
                shape(count * rows, inner),
                shape(count * rows, channels // 2 + inner),
            ],
            in_specs=[VMEM] * len(arrays),
            out_specs=[VMEM] * 3,
            scratch_shapes=[pltpu.VMEM((count * rows, channels), jnp.bfloat16)],
            compiler_params=PARAMS,
        )(*arrays)

    near_left, near_right, send = pack(ups, True, True, False)
    came_near = exchange(send, stages, replicas, 1, 2)
    left, right, send = pack(ups, True, False, True)
    came = exchange(send, stages, replicas, 1, 2)
    up_operands = (near_left, near_right, came_near, left, right, came)
    left, right, send = pack(backs, False, True, True)
    came = exchange(send, stages, replicas, 1, 2)
    parts = []
    for operands in ((left, right, came), up_operands):
        count = replicas // 4
        send, keep = pl.pallas_call(
            functools.partial(half_gradient_body, len(operands) // 3),
            out_shape=sums(count, chunk, inner),
            in_specs=[VMEM] * len(operands),
            out_specs=[VMEM] * 2,
            scratch_shapes=[
                pltpu.VMEM((channels // 2, inner), jnp.float32),
                pltpu.VMEM((8 * rows, channels // 2), jnp.bfloat16),
                pltpu.VMEM((8 * rows, inner), jnp.bfloat16),
            ],
            compiler_params=PARAMS,
        )(*operands)
        came = exchange(send, stages, replicas, 2, 1)
        for bit in range(2, replicas.bit_length() - 1):
            count //= 2
            send, keep = pl.pallas_call(
                functools.partial(next_body, bit),
                out_shape=sums(count, chunk, inner),
                in_specs=[VMEM] * 2,
                out_specs=[VMEM] * 2,
                compiler_params=PARAMS,
            )(keep, came)
            came = exchange(send, stages, replicas, 1 << bit, 1 << bit)
        parts += [keep, came]
    return parts


def halve_sums(stages, replicas, chunk, sizes, rows, fore, ups, backs):
    channels, inner = sizes
    wide, narrow = slice(0, channels), slice(channels, channels + inner)

    def of_flows(columns):
        def pick_parts(arrays):
            near = [flow.at[0, :, columns] for flow in arrays[:stages]]
            side, far, cross = arrays[stages : stages + 3]
            return near, [side.at[:, columns], far.at[:, columns], cross.at[:, columns]]

        return pick_parts

    def of_backs(arrays):
        near = [back.at[0] for back in arrays[stages + 3 : 2 * stages + 3]]
        side, far, cross = arrays[2 * stages + 3 : 2 * stages + 6]
        return near, [side, far, cross]

    plans = [halving_plan(replicas, turn) for turn in range(2)]
    streams = []
    for pick_left, pick_right, late, plan in (
        (of_backs, of_flows(narrow), ups, plans),
        (of_flows(wide), of_backs, backs, plans[::-1]),
    ):
        arrays = fore + late
        send, keep = pl.pallas_call(
            functools.partial(gradient_body, plan, pick_left, pick_right, len(arrays)),
            out_shape=sums(replicas // 2, chunk, inner),
            in_specs=[VMEM] * len(arrays),
            out_specs=[VMEM] * 2,
            scratch_shapes=[
                pltpu.VMEM((4 * rows, channels), jnp.bfloat16),
                pltpu.VMEM((4 * rows, inner), jnp.bfloat16),
                pltpu.VMEM((channels, inner), jnp.float32),
            ],
            compiler_params=PARAMS,
        )(*arrays)
        streams.append((plan, send, keep))
    for at in range(replicas.bit_length() - 1):
        half = replicas >> (at + 2)
        arrived = []
        for plan, send, keep in streams:
            pairs = []
            for p in range(2 * stages):
                for q in range(replicas):
                    pairs.append((p * replicas + q, p * replicas + (q ^ plan[p % 2][0][at])))
            arrived.append((plan, keep, lax.ppermute(send, AXES, pairs)))
        if half == 0:
            break
        streams = []
        for plan, keep, came in arrived:
            send, keep = pl.pallas_call(
                functools.partial(halve_body, plan, at + 1),
                out_shape=sums(half, chunk, inner),
                in_specs=[VMEM] * 2,
                out_specs=[VMEM] * 2,
                compiler_params=PARAMS,
            )(keep, came)
            streams.append((plan, send, keep))
    (_, keep_expand, came_expand), (_, keep_reduce, came_reduce) = arrived
    return keep_reduce, came_reduce, keep_expand, came_expand


def solution(mesh):
    return jax.shard_map(
        shards,
        mesh=mesh,
        in_specs=(
            P(None, None, "dp", None),
            P(None, None, "dp", None),
            P(None, "pipe", None, None),
            P(None, "pipe", None, None),
        ),
        out_specs=P("pipe", None, "dp", None),
        check_vma=False,
    )
```

```python
import functools

import jax
import jax.numpy as jnp
from jax import lax
from jax.experimental import pallas as pl
from jax.experimental.pallas import tpu as pltpu
from jax.sharding import PartitionSpec as P


EPSILON = 1e-06
AXES = ("pipe", "dp")
HBM = pl.BlockSpec(memory_space=pltpu.HBM)
ANY = pl.BlockSpec(memory_space=pl.ANY)
VMEM = pl.BlockSpec(memory_space=pltpu.VMEM)
PARAMS = pltpu.CompilerParams(vmem_limit_bytes=16 << 20)


def contract(first_op, second_op, first_dim, second_dim):
    return lax.dot_general(
        first_op,
        second_op,
        (((first_dim,), (second_dim,)), ((), ())),
        preferred_element_type=jnp.float32,
    )


def smooth_slope(values):
    sigma = jax.nn.sigmoid(values)
    return sigma * (1.0 + values * (1.0 - sigma))


def norm_of(widened):
    return lax.rsqrt(jnp.mean(widened * widened, axis=-1, keepdims=True) + EPSILON)


def where_am_i(step):
    position = lax.axis_index("pipe")
    stage, core = lax.div(position, 2), lax.rem(position, 2)
    way = jnp.where(stage == step, 0, 1)
    return stage, core, way


def bring_all(sources, outs, sems):
    copies = [
        pltpu.make_async_copy(source, out, sems.at[at])
        for at, (source, out) in enumerate(zip(sources, outs))
    ]
    for copy in copies:
        copy.start()
    return copies


def load_body(step, reduce_all, expand_all, *refs):
    _, core, way = where_am_i(step)
    sources, outs = [reduce_all.at[way], expand_all.at[way]], refs[:-1]
    if step == 0:
        sources.append(refs[0].at[way, core])
        outs = outs[1:]
    for copy in bring_all(sources, outs, refs[-1]):
        copy.wait()


def load(step, own, *more):
    channels, inner = own[0].shape[1:]
    mat = jax.ShapeDtypeStruct((channels, inner), jnp.bfloat16)
    outs = [mat, mat] + [jax.ShapeDtypeStruct(a.shape[2:], a.dtype) for a in more]
    return pl.pallas_call(
        functools.partial(load_body, step),
        out_shape=outs,
        in_specs=[HBM] * (2 + len(more)),
        out_specs=[VMEM] * len(outs),
        scratch_shapes=[pltpu.SemaphoreType.DMA((len(outs),))],
        compiler_params=PARAMS,
    )(*own, *more)


def meanwhile_body(step, mirrored, expand_own, expand_other, inputs, cotangent, leave, *refs):
    outs, sems = refs[:-1], refs[-1]
    stage, core, way = where_am_i(step)
    ending, back_active = outs[:2]
    sources = [cotangent.at[way, core]]
    if mirrored:
        sources += [cotangent.at[1, core], inputs.at[1, core]]
    copies = bring_all(sources, [outs[0]] + list(outs[2:]), sems)
    copies[0].wait()

    @pl.when(way == core)
    def _():
        back_active[...] = jnp.dot(
            ending[...], expand_other[...], preferred_element_type=jnp.float32
        )

    @pl.when(way != core)
    def _():
        back_active[...] = jnp.dot(ending[...], expand_own[...], preferred_element_type=jnp.float32)

    for copy in copies[1:]:
        copy.wait()
    if mirrored:
        rows = outs[3]

        @pl.when(stage != 0)
        def _():
            rows[...] = leave[...]

        widened = rows[...].astype(jnp.float32)
        rows[...] = jax.nn.silu(widened * norm_of(widened)).astype(jnp.bfloat16)


def weight_copies(own, other, held, sems, core, way):
    copies = []
    for order in range(2):
        is_own = lax.rem(way + order, 2) == core
        for kind in range(2):
            mine = pltpu.make_async_copy(own[kind].at[way], held[kind].at[order], sems.at[kind, order])
            theirs = pltpu.make_async_copy(
                other[kind].at[way], held[kind].at[order], sems.at[kind, order]
            )
            copies.append((is_own, mine, theirs))
    return copies


def start_all(copies):
    for is_own, mine, theirs in copies:
        pl.when(is_own)(mine.start)
        pl.when(jnp.logical_not(is_own))(theirs.start)


def head_body(own, other, rows_in, lifted_out, inner_out, active_out):
    _, core, way = where_am_i(0)
    widened = rows_in[...].astype(jnp.float32)
    lifted = jax.nn.silu(widened * norm_of(widened)).astype(jnp.bfloat16)
    lifted_out[...] = lifted

    def run(reduce_mat):
        inner_sum = jnp.dot(lifted, reduce_mat[...], preferred_element_type=jnp.float32)
        inner_out[...] = inner_sum
        active_out[...] = jax.nn.silu(inner_sum).astype(jnp.bfloat16)

    pl.when(way == core)(lambda: run(own))
    pl.when(way != core)(lambda: run(other))


def stage_body(step, forward, backward, last, near, *refs):
    refs = list(refs)
    _, core, way = where_am_i(step)
    own, other = (refs.pop(0), refs.pop(0)), (refs.pop(0), refs.pop(0))
    enter = refs.pop(0) if forward else None
    head = [refs.pop(0) for _ in range(3)] if forward and step == 0 else None
    upstream_in = refs.pop(0) if backward else None
    first_active = refs.pop(0) if forward and backward else None
    if not forward:
        trunks, inners = refs.pop(0), refs.pop(0)
    if forward:
        flows = refs.pop(0)
    if forward and not backward:
        leave = refs.pop(0)
    if backward:
        upstreams, back_inners = refs.pop(0), refs.pop(0)
    if backward and not last:
        back_leave = refs.pop(0)
    if forward:
        trunks, inners = refs.pop(0), refs.pop(0)
    channels = trunks.shape[2]

    def run(reduce_mats, expand_mats, wait):
        if forward:
            rows = enter[...]
            for order in range(2):
                slot = lax.rem(order + core, 2)
                widened = rows.astype(jnp.float32)
                trunks[order] = rows
                if head and order == 0:
                    lifted, inner_sum, active = [part[...] for part in head]
                else:
                    normed = widened * norm_of(widened)
                    lifted = jax.nn.silu(normed).astype(jnp.bfloat16)
                    wait(0, order)
                    inner_sum = jnp.dot(
                        lifted, reduce_mats[order][...], preferred_element_type=jnp.float32
                    )
                    active = jax.nn.silu(inner_sum).astype(jnp.bfloat16)
                flows[slot, :, :channels] = lifted
                inners[order] = inner_sum
                flows[slot, :, channels:] = active
                wait(1, order)
                rows = (widened + contract(active, expand_mats[order][...], 1, 1)).astype(jnp.bfloat16)
            if not backward:
                leave[...] = rows
        if backward:
            upstream = upstream_in[...]
            for order in (1, 0):
                slot = lax.rem(order + core, 2)
                upstreams[slot] = upstream
                if last and order == 0:
                    break
                if not forward:
                    wait(1, order)
                if forward and order:
                    back_active = first_active[...]
                else:
                    back_active = jnp.dot(
                        upstream, expand_mats[order][...], preferred_element_type=jnp.float32
                    )
                back_inner = (back_active * smooth_slope(inners[order])).astype(jnp.bfloat16)
                back_inners[slot] = back_inner
                if not forward:
                    wait(0, order)
                back_lifted = contract(back_inner, reduce_mats[order][...], 1, 1)
                widened = trunks[order].astype(jnp.float32)
                norm_scale = norm_of(widened)
                back_normed = back_lifted * smooth_slope(widened * norm_scale)
                projection = jnp.mean(back_normed * widened, axis=-1, keepdims=True)
                upstream = (
                    upstream.astype(jnp.float32)
                    + norm_scale * back_normed
                    - widened * norm_scale**3 * projection
                ).astype(jnp.bfloat16)
            if not last:
                back_leave[...] = upstream

    if near:
        idle = lambda kind, order: None

        @pl.when(way == core)
        def _():
            run((own[0], other[0]), (own[1], other[1]), idle)

        @pl.when(way != core)
        def _():
            run((other[0], own[0]), (other[1], own[1]), idle)

    else:
        held = (refs.pop(0), refs.pop(0))
        copies = weight_copies(own, other, held, refs.pop(0), core, way)
        start_all(copies if forward else copies[2:] + copies[:2])
        run(
            [held[0].at[order] for order in range(2)],
            [held[1].at[order] for order in range(2)],
            lambda kind, order: copies[2 * order + kind][1].wait(),
        )


def tail_body(own, other, upstreams, back_first, inners, back_inners):
    _, core, way = where_am_i(0)

    def run(expand_mat):
        back_active = jnp.dot(upstreams[core], expand_mat[...], preferred_element_type=jnp.float32)
        back_inners[core] = (back_active * smooth_slope(inners[0])).astype(jnp.bfloat16)
        back_inners[1 - core] = back_first[1 - core]

    pl.when(way == core)(lambda: run(own))
    pl.when(way != core)(lambda: run(other))


def run_stage(weights, step, forward, backward, near, rows, sizes, *arrays):
    channels, inner = sizes
    last = backward and step == 0 and not forward
    shape = lambda dtype, *dims: jax.ShapeDtypeStruct(dims, dtype)
    line = shape(jnp.bfloat16, rows, channels)
    kept = [((2, rows, channels), jnp.bfloat16), ((2, rows, inner), jnp.float32)]
    outs, scratch = [], []
    if forward:
        outs.append(shape(jnp.bfloat16, 2, rows, channels + inner))
    if forward and not backward:
        outs.append(line)
    if backward:
        outs.append(shape(jnp.bfloat16, 2, rows, channels))
        outs.append(shape(jnp.bfloat16, 2, rows, inner))
    if backward and not last:
        outs.append(line)
    if forward and not backward:
        outs += [jax.ShapeDtypeStruct(*one) for one in kept]
    if forward and backward:
        scratch += [pltpu.VMEM(*one) for one in kept]
    if not near:
        scratch += [pltpu.VMEM((2, channels, inner), jnp.bfloat16)] * 2
        scratch += [pltpu.SemaphoreType.DMA((2, 2))]
    passes = 4 * (int(forward) + int(backward))
    return pl.pallas_call(
        functools.partial(stage_body, step, forward, backward, last, near),
        out_shape=outs,
        in_specs=[VMEM if near else ANY] * 4 + [VMEM] * len(arrays),
        out_specs=[VMEM] * len(outs),
        scratch_shapes=scratch,
        compiler_params=PARAMS,
        cost_estimate=pl.CostEstimate(
            flops=2 * passes * rows * channels * inner,
            bytes_accessed=8 * channels * inner,
            transcendentals=passes * rows * channels,
        ),
    )(*weights, *arrays)


def parity(value, mask):
    total, bit = 0, 0
    while mask >> bit:
        if mask >> bit & 1:
            total = total + lax.rem(lax.div(value, 1 << bit), 2)
        bit += 1
    return lax.rem(total, 2)


def halving_plan(size, turn):
    order = [1 << bit for bit in range(size.bit_length() - 1)]
    if turn and len(order) > 1:
        order[:2] = order[1::-1]
    table = [0] * size
    for chunk in range(size):
        place = 0
        for mask in order:
            place = 2 * place + int(chunk & mask != 0)
        table[place] = chunk
    return order, order, table


def side_of(plans, at):
    core, shard = lax.rem(lax.axis_index("pipe"), 2), lax.axis_index("dp")
    return jnp.where(core == 0, parity(shard, plans[0][1][at]), parity(shard, plans[1][1][at]))


def gradient_body(plans, pick_left, pick_right, count, *refs):
    arrays, (send, keep, left, right, full) = refs[:count], refs[count:]
    stage, core, _ = where_am_i(0)
    rows = left.shape[0] // 4
    chunk = send.shape[1]
    for target, pick in ((left, pick_left), (right, pick_right)):
        near, away = pick(arrays)
        for step, part in enumerate(near):

            @pl.when(stage == step)
            def _():
                target[:rows] = part[...]

        for at, part in enumerate(away):
            target[(at + 1) * rows : (at + 2) * rows] = part[...]
    full[...] = contract(left[...], right[...], 0, 0)
    side = side_of(plans, 0)
    half = send.shape[0]
    flip = [plan[2][half] for plan in plans]
    for at in range(half):
        spots = []
        for target_side in (1 - side, side):
            first = plans[0][2][at] ^ (flip[0] * target_side)
            second = plans[1][2][at] ^ (flip[1] * target_side)
            spots.append(pl.multiple_of(jnp.where(core == 0, first, second) * chunk, chunk))
        send[at] = full[pl.ds(spots[0], chunk)].astype(jnp.bfloat16)
        keep[at] = full[pl.ds(spots[1], chunk)]


def halve_body(plans, at, keep_in, came, send, keep):
    half = keep.shape[0]
    side = side_of(plans, at)
    for spot in range(half):
        mine, theirs = side * half + spot, (1 - side) * half + spot
        send[spot] = (keep_in[theirs] + came[theirs].astype(jnp.float32)).astype(jnp.bfloat16)
        keep[spot] = keep_in[mine] + came[mine].astype(jnp.float32)


def bit_of(value, bit):
    return lax.rem(lax.div(value, 1 << bit), 2)


def first_sides():
    core, shard = lax.rem(lax.axis_index("pipe"), 2), lax.axis_index("dp")
    low, high = bit_of(shard, 0), bit_of(shard, 1)
    return core, jnp.where(core == 0, low, high), jnp.where(core == 0, high, low)


def split_columns(wide, keep, send, chunk):
    core, side, _ = first_sides()
    for place in range(wide.shape[1] // (2 * chunk)):
        for target, at in ((keep, side), (send, 1 - side)):
            block = jnp.where(core == 0, 2 * place + at, place // 2 * 4 + 2 * at + place % 2)
            source = pl.ds(pl.multiple_of(block * chunk, chunk), chunk)
            target[:, place * chunk : (place + 1) * chunk] = wide[:, source]


def pack_body(stages, chunk, up, near, far, *refs):
    refs = list(refs)
    left, right, send, wide = refs[-4:]
    channels = wide.shape[1]
    spans = slice(0, channels), slice(channels, None), slice(None)
    flow_span, back_span = (spans[1] if up else spans[0]), spans[2]
    stage, _, _ = where_am_i(0)
    rows = wide.shape[0] // (2 * near + 2 * far)
    start = 0
    targets = (right, wide) if up else (wide, right)
    for target, span in zip(targets, (flow_span, back_span)):
        start = 0
        if near:
            parts = [refs.pop(0) for _ in range(stages + 1)]
            for step in range(stages):

                @pl.when(stage == step)
                def _():
                    target[:rows] = parts[step][0, :, span]

            target[rows : 2 * rows] = parts[stages][:, span]
            start = 2 * rows
        if far:
            for part in (refs.pop(0), refs.pop(0)):
                target[start : start + rows] = part[:, span]
                start += rows
    split_columns(wide, left, send, chunk)
    send[:, channels // 2 :] = right[...]


def near_body(stages, chunk, *refs):
    flows, ups, backs = [refs[at * (stages + 1) : (at + 1) * (stages + 1)] for at in range(3)]
    left_up, right_up, left_inner, right_inner, send, wide = refs[3 * stages + 3 :]
    width = send.shape[1] // 2
    for at, (late, outs) in enumerate(
        ((ups, (left_up, right_up)), (backs, (left_inner, right_inner)))
    ):
        part = send.at[:, at * width : (at + 1) * width]
        pack_body(stages, chunk, at == 0, True, False, *flows, *late, *outs, part, wide)


def half_gradient_body(at, groups, *refs):
    send, keep, full, left, right = refs[3 * groups :]
    start = 0
    for group in range(groups):
        part_left, part_right, came = refs[3 * group : 3 * group + 3]
        rows, columns = part_left.shape
        left[start : start + rows] = part_left[...]
        right[start : start + rows] = part_right[...]
        start += rows
        width = columns + right.shape[1]
        offset = at * width if came.shape[1] > width else 0
        left[start : start + rows] = came[:, offset : offset + columns]
        right[start : start + rows] = came[:, offset + columns : offset + width]
        start += rows
    full[...] = contract(left[...], right[...], 0, 0)
    _, _, side = first_sides()
    chunk = send.shape[1]
    for place in range(send.shape[0]):
        theirs = pl.ds(pl.multiple_of((2 * place + 1 - side) * chunk, chunk), chunk)
        mine = pl.ds(pl.multiple_of((2 * place + side) * chunk, chunk), chunk)
        send[place] = full[theirs].astype(jnp.bfloat16)
        keep[place] = full[mine]


def next_body(bit, keep_in, came, send, keep):
    side = bit_of(lax.axis_index("dp"), bit)
    for place in range(keep.shape[0]):
        theirs, mine = 2 * place + 1 - side, 2 * place + side
        send[place] = (keep_in[theirs] + came[theirs].astype(jnp.float32)).astype(jnp.bfloat16)
        keep[place] = keep_in[mine] + came[mine].astype(jnp.float32)


def finish_body(keep_reduce, came_reduce, keep_expand, came_expand, out):
    out[0, 0] = keep_reduce[0] + came_reduce[0].astype(jnp.float32)
    out[0, 1] = keep_expand[0] + came_expand[0].astype(jnp.float32)


def shards(inputs, cotangent, reduce_weight, expand_weight):
    stages = lax.axis_size("pipe") // 2
    replicas = lax.axis_size("dp")
    stage, core, _ = where_am_i(0)
    channels, inner = reduce_weight.shape[2:]
    rows = inputs.shape[1] * inputs.shape[2] // 2
    sizes = (channels, inner)
    entering = inputs.reshape(2, 2, rows, channels)
    ending = cotangent.reshape(2, 2, rows, channels)
    own = [reduce_weight[:, 0], expand_weight[:, 0]]

    core_pairs = [(p, p ^ 1) for p in range(2 * stages)]
    mirror_pairs = [(p, 2 * (stages - 1 - p // 2) + p % 2) for p in range(2 * stages)]

    def hop(shard, step):
        pairs = []
        for c in range(2):
            pairs.append((2 * step + c, 2 * step + 2 + c))
            pairs.append((2 * (stages - 1 - step) + c, 2 * (stages - 2 - step) + c))
        return lax.ppermute(shard, "pipe", pairs)

    def swap_cores(shard):
        return lax.ppermute(shard, "pipe", core_pairs)

    def mirror(shard):
        return lax.ppermute(shard, "pipe", mirror_pairs)

    at_stage = [stage == step for step in range(stages)]
    first_core = core == 0
    at_stage, first_core, entering = lax.optimization_barrier((at_stage, first_core, entering))

    def pick(parts, mirrored_stage=False):
        tests = at_stage[::-1] if mirrored_stage else at_stage
        chosen = parts[0]
        for test, part in zip(tests[1:], parts[1:]):
            chosen = jnp.where(test, part, chosen)
        return chosen

    in_hbm = lambda array: pltpu.with_memory_space_constraint(array, pltpu.HBM)
    own, entering, ending = [in_hbm(one) for one in own], in_hbm(entering), in_hbm(ending)
    *near, enter = load(0, own, entering)
    near.append(swap_cores(near[0]))
    near.append(swap_cores(near[1]))
    turn = list(load(stages - 1, own))
    turn += [swap_cores(weight) for weight in turn]
    if stages > 2:
        weights = own + [swap_cores(weight) for weight in own]
    flows, trunks, inners = [], [], []
    head = pl.pallas_call(
        head_body,
        out_shape=[
            jax.ShapeDtypeStruct((rows, channels), jnp.bfloat16),
            jax.ShapeDtypeStruct((rows, inner), jnp.float32),
            jax.ShapeDtypeStruct((rows, inner), jnp.bfloat16),
        ],
        in_specs=[VMEM] * 3,
        out_specs=[VMEM] * 3,
        compiler_params=PARAMS,
    )(near[0], near[2], enter)
    for step in range(stages - 1):
        arrays = [enter] if step else [enter, *head]
        flow, leave, trunk, inner_sum = run_stage(
            weights if step else near, step, True, False, step == 0, rows, sizes, *arrays
        )
        flows.append(flow)
        trunks.append(trunk)
        inners.append(inner_sum)
        enter = hop(leave, step)
    mirrored = stages == 2
    line = jax.ShapeDtypeStruct((rows, channels), jnp.bfloat16)
    outs = [line, jax.ShapeDtypeStruct((rows, inner), jnp.float32)] + [line, line] * mirrored
    ending, first_active, *known = pl.pallas_call(
        functools.partial(meanwhile_body, stages - 1, mirrored),
        out_shape=outs,
        in_specs=[VMEM, VMEM, HBM, HBM, VMEM],
        out_specs=[VMEM] * len(outs),
        scratch_shapes=[pltpu.SemaphoreType.DMA((3,))],
        compiler_params=PARAMS,
    )(turn[1], turn[3], entering, ending, leave)
    flow, upstreams, back_inners, leave = run_stage(
        turn, stages - 1, True, True, True, rows, sizes, enter, ending, first_active
    )
    flows.append(flow)
    upstreams, back_inners = [upstreams], [back_inners]
    upstream = hop(leave, 0)
    side_flow = swap_cores(pick(flows)[1])
    near_core = lambda first, second: jnp.where(first_core, first, second)
    going = pick(flows, True)
    if mirrored:
        lifted = near_core(going[1, :, :channels], going[0, :, :channels])
        going = jnp.concatenate([lifted, going[0, :, channels:], going[1, :, channels:]], axis=1)
    far_flow = mirror(going)
    if mirrored:
        lifted, actives = far_flow[:, :channels], far_flow[:, channels:]
        far_flow = jnp.concatenate([near_core(known[1], lifted), actives[:, :inner]], axis=1)
        cross_flow = jnp.concatenate([near_core(lifted, known[1]), actives[:, inner:]], axis=1)
    else:
        far_flow, cross_flow = far_flow[0], far_flow[1]
    cross_flow = swap_cores(cross_flow)
    for step in range(stages - 2, -1, -1):
        outs = run_stage(
            weights if step else near,
            step,
            False,
            True,
            step == 0,
            rows,
            sizes,
            upstream,
            trunks[step],
            inners[step],
        )
        upstreams.insert(0, outs[0])
        if step:
            upstream = hop(outs[2], stages - 1 - step)
            back_inners.insert(0, outs[1])
            continue
        tail = pl.pallas_call(
            tail_body,
            out_shape=jax.ShapeDtypeStruct(outs[1].shape, outs[1].dtype),
            in_specs=[VMEM] * 5,
            out_specs=VMEM,
            compiler_params=PARAMS,
        )(near[1], near[3], outs[0], outs[1], inners[0])
        back_inners.insert(0, tail)
    going = pick(upstreams, True)
    far_up = mirror(near_core(going[0], going[1]) if mirrored else going)
    far_inner = mirror(pick(back_inners, True))
    side_up = swap_cores(pick(upstreams)[1])
    side_inner = swap_cores(pick(back_inners)[1])
    if mirrored:
        top = jnp.where(at_stage[0], leave, known[0])
        far_up, cross_up = near_core(far_up, top), near_core(top, far_up)
    else:
        far_up, cross_up = far_up[0], far_up[1]
    cross_up = swap_cores(cross_up)
    far_inner, cross_inner = far_inner[0], far_inner[1]
    cross_inner = swap_cores(cross_inner)

    chunk = channels // replicas
    fore = flows + [side_flow, far_flow, cross_flow]
    ups = upstreams + [side_up, far_up, cross_up]
    backs = back_inners + [side_inner, far_inner, cross_inner]
    halve = halve_rows if chunk % 128 == 0 and replicas >= 4 else halve_sums
    parts = halve(stages, replicas, chunk, sizes, rows, fore, ups, backs)
    return pl.pallas_call(
        finish_body,
        out_shape=jax.ShapeDtypeStruct((1, 2, chunk, inner), jnp.float32),
        in_specs=[VMEM] * 4,
        out_specs=VMEM,
        compiler_params=PARAMS,
    )(*parts)


def sums(count, chunk, inner):
    return [
        jax.ShapeDtypeStruct((count, chunk, inner), jnp.bfloat16),
        jax.ShapeDtypeStruct((count, chunk, inner), jnp.float32),
    ]


def exchange(shard, stages, replicas, first, second):
    pairs = []
    for p in range(2 * stages):
        for q in range(replicas):
            pairs.append((p * replicas + q, p * replicas + (q ^ (second if p % 2 else first))))
    return lax.ppermute(shard, AXES, pairs)


def halve_rows(stages, replicas, chunk, sizes, rows, fore, ups, backs):
    channels, inner = sizes
    shape = lambda *dims: jax.ShapeDtypeStruct(dims, jnp.bfloat16)

    def pack(late, up, near, far):
        count = 2 * (near + far)
        arrays = []
        for one in (fore, late):
            arrays += one[: stages + 1] * near + one[stages + 1 :] * far
        return pl.pallas_call(
            functools.partial(pack_body, stages, chunk, up, near, far),
            out_shape=[
                shape(count * rows, channels // 2),
                shape(count * rows, inner),
                shape(count * rows, channels // 2 + inner),
            ],
            in_specs=[VMEM] * len(arrays),
            out_specs=[VMEM] * 3,
            scratch_shapes=[pltpu.VMEM((count * rows, channels), jnp.bfloat16)],
            compiler_params=PARAMS,
        )(*arrays)

    near = fore[: stages + 1] + ups[: stages + 1] + backs[: stages + 1]
    *kept, send = pl.pallas_call(
        functools.partial(near_body, stages, chunk),
        out_shape=[
            shape(2 * rows, channels // 2),
            shape(2 * rows, inner),
            shape(2 * rows, channels // 2),
            shape(2 * rows, inner),
            shape(2 * rows, channels + 2 * inner),
        ],
        in_specs=[VMEM] * len(near),
        out_specs=[VMEM] * 5,
        scratch_shapes=[pltpu.VMEM((2 * rows, channels), jnp.bfloat16)],
        compiler_params=PARAMS,
    )(*near)
    came_near = exchange(send, stages, replicas, 1, 2)
    parts = []
    for at, name, late in ((1, "inner", backs), (0, "up", ups)):
        left, right, send = pack(late, name == "up", False, True)
        came = exchange(send, stages, replicas, 1, 2)
        operands = (kept[2 * at], kept[2 * at + 1], came_near, left, right, came)
        count = replicas // 4
        send, keep = pl.pallas_call(
            functools.partial(half_gradient_body, at, len(operands) // 3),
            out_shape=sums(count, chunk, inner),
            in_specs=[VMEM] * len(operands),
            out_specs=[VMEM] * 2,
            scratch_shapes=[
                pltpu.VMEM((channels // 2, inner), jnp.float32),
                pltpu.VMEM((8 * rows, channels // 2), jnp.bfloat16),
                pltpu.VMEM((8 * rows, inner), jnp.bfloat16),
            ],
            compiler_params=PARAMS,
        )(*operands)
        came = exchange(send, stages, replicas, 2, 1)
        for bit in range(2, replicas.bit_length() - 1):
            count //= 2
            send, keep = pl.pallas_call(
                functools.partial(next_body, bit),
                out_shape=sums(count, chunk, inner),
                in_specs=[VMEM] * 2,
                out_specs=[VMEM] * 2,
                compiler_params=PARAMS,
            )(keep, came)
            came = exchange(send, stages, replicas, 1 << bit, 1 << bit)
        parts += [keep, came]
    return parts


def halve_sums(stages, replicas, chunk, sizes, rows, fore, ups, backs):
    channels, inner = sizes
    wide, narrow = slice(0, channels), slice(channels, channels + inner)

    def of_flows(columns):
        def pick_parts(arrays):
            near = [flow.at[0, :, columns] for flow in arrays[:stages]]
            side, far, cross = arrays[stages : stages + 3]
            return near, [side.at[:, columns], far.at[:, columns], cross.at[:, columns]]

        return pick_parts

    def of_backs(arrays):
        near = [back.at[0] for back in arrays[stages + 3 : 2 * stages + 3]]
        side, far, cross = arrays[2 * stages + 3 : 2 * stages + 6]
        return near, [side, far, cross]

    plans = [halving_plan(replicas, turn) for turn in range(2)]
    streams = []
    for pick_left, pick_right, late, plan in (
        (of_backs, of_flows(narrow), ups, plans),
        (of_flows(wide), of_backs, backs, plans[::-1]),
    ):
        arrays = fore + late
        send, keep = pl.pallas_call(
            functools.partial(gradient_body, plan, pick_left, pick_right, len(arrays)),
            out_shape=sums(replicas // 2, chunk, inner),
            in_specs=[VMEM] * len(arrays),
            out_specs=[VMEM] * 2,
            scratch_shapes=[
                pltpu.VMEM((4 * rows, channels), jnp.bfloat16),
                pltpu.VMEM((4 * rows, inner), jnp.bfloat16),
                pltpu.VMEM((channels, inner), jnp.float32),
            ],
            compiler_params=PARAMS,
        )(*arrays)
        streams.append((plan, send, keep))
    for at in range(replicas.bit_length() - 1):
        half = replicas >> (at + 2)
        arrived = []
        for plan, send, keep in streams:
            pairs = []
            for p in range(2 * stages):
                for q in range(replicas):
                    pairs.append((p * replicas + q, p * replicas + (q ^ plan[p % 2][0][at])))
            arrived.append((plan, keep, lax.ppermute(send, AXES, pairs)))
        if half == 0:
            break
        streams = []
        for plan, keep, came in arrived:
            send, keep = pl.pallas_call(
                functools.partial(halve_body, plan, at + 1),
                out_shape=sums(half, chunk, inner),
                in_specs=[VMEM] * 2,
                out_specs=[VMEM] * 2,
                compiler_params=PARAMS,
            )(keep, came)
            streams.append((plan, send, keep))
    (_, keep_expand, came_expand), (_, keep_reduce, came_reduce) = arrived
    return keep_reduce, came_reduce, keep_expand, came_expand


def solution(mesh):
    return jax.shard_map(
        shards,
        mesh=mesh,
        in_specs=(
            P(None, None, "dp", None),
            P(None, None, "dp", None),
            P(None, "pipe", None, None),
            P(None, "pipe", None, None),
        ),
        out_specs=P("pipe", None, "dp", None),
        check_vma=False,
    )
```

```python
import functools

import jax
import jax.numpy as jnp
from jax import lax
from jax.experimental import pallas as pl
from jax.experimental.pallas import tpu as pltpu
from jax.sharding import PartitionSpec as P


EPSILON = 1e-06
AXES = ("pipe", "dp")
HBM = pl.BlockSpec(memory_space=pltpu.HBM)
ANY = pl.BlockSpec(memory_space=pl.ANY)
VMEM = pl.BlockSpec(memory_space=pltpu.VMEM)
PARAMS = pltpu.CompilerParams(vmem_limit_bytes=16 << 20)


def contract(first_op, second_op, first_dim, second_dim):
    return lax.dot_general(
        first_op,
        second_op,
        (((first_dim,), (second_dim,)), ((), ())),
        preferred_element_type=jnp.float32,
    )


def smooth_slope(values):
    sigma = jax.nn.sigmoid(values)
    return sigma * (1.0 + values * (1.0 - sigma))


def norm_of(widened):
    return lax.rsqrt(jnp.mean(widened * widened, axis=-1, keepdims=True) + EPSILON)


def where_am_i(step):
    position = lax.axis_index("pipe")
    stage, core = lax.div(position, 2), lax.rem(position, 2)
    way = jnp.where(stage == step, 0, 1)
    return stage, core, way


def bring_all(sources, outs, sems):
    copies = [
        pltpu.make_async_copy(source, out, sems.at[at])
        for at, (source, out) in enumerate(zip(sources, outs))
    ]
    for copy in copies:
        copy.start()
    return copies


def load_body(step, reduce_all, expand_all, *refs):
    _, core, way = where_am_i(step)
    sources, outs = [reduce_all.at[way], expand_all.at[way]], refs[:-1]
    if step == 0:
        sources.append(refs[0].at[way, core])
        outs = outs[1:]
    for copy in bring_all(sources, outs, refs[-1]):
        copy.wait()


def load(step, own, *more):
    channels, inner = own[0].shape[1:]
    mat = jax.ShapeDtypeStruct((channels, inner), jnp.bfloat16)
    outs = [mat, mat] + [jax.ShapeDtypeStruct(a.shape[2:], a.dtype) for a in more]
    return pl.pallas_call(
        functools.partial(load_body, step),
        out_shape=outs,
        in_specs=[HBM] * (2 + len(more)),
        out_specs=[VMEM] * len(outs),
        scratch_shapes=[pltpu.SemaphoreType.DMA((len(outs),))],
        compiler_params=PARAMS,
    )(*own, *more)


def meanwhile_body(step, mirrored, expand_own, expand_other, inputs, cotangent, leave, *refs):
    outs, sems = refs[:-1], refs[-1]
    stage, core, way = where_am_i(step)
    ending, back_active = outs[:2]
    sources = [cotangent.at[way, core]]
    if mirrored:
        sources += [cotangent.at[1, core], inputs.at[1, core]]
    copies = bring_all(sources, [outs[0]] + list(outs[2:]), sems)
    copies[0].wait()

    @pl.when(way == core)
    def _():
        back_active[...] = jnp.dot(
            ending[...], expand_other[...], preferred_element_type=jnp.float32
        )

    @pl.when(way != core)
    def _():
        back_active[...] = jnp.dot(ending[...], expand_own[...], preferred_element_type=jnp.float32)

    for copy in copies[1:]:
        copy.wait()
    if mirrored:
        rows = outs[3]

        @pl.when(stage != 0)
        def _():
            rows[...] = leave[...]

        widened = rows[...].astype(jnp.float32)
        rows[...] = jax.nn.silu(widened * norm_of(widened)).astype(jnp.bfloat16)


def weight_copies(own, other, held, sems, core, way):
    copies = []
    for order in range(2):
        is_own = lax.rem(way + order, 2) == core
        for kind in range(2):
            mine = pltpu.make_async_copy(own[kind].at[way], held[kind].at[order], sems.at[kind, order])
            theirs = pltpu.make_async_copy(
                other[kind].at[way], held[kind].at[order], sems.at[kind, order]
            )
            copies.append((is_own, mine, theirs))
    return copies


def start_all(copies):
    for is_own, mine, theirs in copies:
        pl.when(is_own)(mine.start)
        pl.when(jnp.logical_not(is_own))(theirs.start)


def head_body(own, other, rows_in, lifted_out, inner_out, active_out):
    _, core, way = where_am_i(0)
    widened = rows_in[...].astype(jnp.float32)
    lifted = jax.nn.silu(widened * norm_of(widened)).astype(jnp.bfloat16)
    lifted_out[...] = lifted

    def run(reduce_mat):
        inner_sum = jnp.dot(lifted, reduce_mat[...], preferred_element_type=jnp.float32)
        inner_out[...] = inner_sum
        active_out[...] = jax.nn.silu(inner_sum).astype(jnp.bfloat16)

    pl.when(way == core)(lambda: run(own))
    pl.when(way != core)(lambda: run(other))


def stage_body(step, forward, backward, last, near, *refs):
    refs = list(refs)
    _, core, way = where_am_i(step)
    own, other = (refs.pop(0), refs.pop(0)), (refs.pop(0), refs.pop(0))
    enter = refs.pop(0) if forward else None
    head = [refs.pop(0) for _ in range(3)] if forward and step == 0 else None
    upstream_in = refs.pop(0) if backward else None
    first_active = refs.pop(0) if forward and backward else None
    if not forward:
        trunks, inners = refs.pop(0), refs.pop(0)
    if forward:
        flows = refs.pop(0)
    if forward and not backward:
        leave = refs.pop(0)
    if backward:
        upstreams, back_inners = refs.pop(0), refs.pop(0)
    if backward and not last:
        back_leave = refs.pop(0)
    if forward:
        trunks, inners = refs.pop(0), refs.pop(0)
    channels = trunks.shape[2]

    def run(reduce_mats, expand_mats, wait):
        if forward:
            rows = enter[...]
            for order in range(2):
                slot = lax.rem(order + core, 2)
                widened = rows.astype(jnp.float32)
                trunks[order] = rows
                if head and order == 0:
                    lifted, inner_sum, active = [part[...] for part in head]
                else:
                    normed = widened * norm_of(widened)
                    lifted = jax.nn.silu(normed).astype(jnp.bfloat16)
                    wait(0, order)
                    inner_sum = jnp.dot(
                        lifted, reduce_mats[order][...], preferred_element_type=jnp.float32
                    )
                    active = jax.nn.silu(inner_sum).astype(jnp.bfloat16)
                flows[slot, :, :channels] = lifted
                inners[order] = inner_sum
                flows[slot, :, channels:] = active
                wait(1, order)
                rows = (widened + contract(active, expand_mats[order][...], 1, 1)).astype(jnp.bfloat16)
            if not backward:
                leave[...] = rows
        if backward:
            upstream = upstream_in[...]
            for order in (1, 0):
                slot = lax.rem(order + core, 2)
                upstreams[slot] = upstream
                if last and order == 0:
                    break
                if not forward:
                    wait(1, order)
                if forward and order:
                    back_active = first_active[...]
                else:
                    back_active = jnp.dot(
                        upstream, expand_mats[order][...], preferred_element_type=jnp.float32
                    )
                back_inner = (back_active * smooth_slope(inners[order])).astype(jnp.bfloat16)
                back_inners[slot] = back_inner
                if not forward:
                    wait(0, order)
                back_lifted = contract(back_inner, reduce_mats[order][...], 1, 1)
                widened = trunks[order].astype(jnp.float32)
                norm_scale = norm_of(widened)
                back_normed = back_lifted * smooth_slope(widened * norm_scale)
                projection = jnp.mean(back_normed * widened, axis=-1, keepdims=True)
                upstream = (
                    upstream.astype(jnp.float32)
                    + norm_scale * back_normed
                    - widened * norm_scale**3 * projection
                ).astype(jnp.bfloat16)
            if not last:
                back_leave[...] = upstream

    if near:
        idle = lambda kind, order: None

        @pl.when(way == core)
        def _():
            run((own[0], other[0]), (own[1], other[1]), idle)

        @pl.when(way != core)
        def _():
            run((other[0], own[0]), (other[1], own[1]), idle)

    else:
        held = (refs.pop(0), refs.pop(0))
        copies = weight_copies(own, other, held, refs.pop(0), core, way)
        start_all(copies if forward else copies[2:] + copies[:2])
        run(
            [held[0].at[order] for order in range(2)],
            [held[1].at[order] for order in range(2)],
            lambda kind, order: copies[2 * order + kind][1].wait(),
        )


def tail_body(own, other, upstreams, back_first, inners, back_inners):
    _, core, way = where_am_i(0)

    def run(expand_mat):
        back_active = jnp.dot(upstreams[core], expand_mat[...], preferred_element_type=jnp.float32)
        back_inners[core] = (back_active * smooth_slope(inners[0])).astype(jnp.bfloat16)
        back_inners[1 - core] = back_first[1 - core]

    pl.when(way == core)(lambda: run(own))
    pl.when(way != core)(lambda: run(other))


def run_stage(weights, step, forward, backward, near, rows, sizes, *arrays):
    channels, inner = sizes
    last = backward and step == 0 and not forward
    shape = lambda dtype, *dims: jax.ShapeDtypeStruct(dims, dtype)
    line = shape(jnp.bfloat16, rows, channels)
    kept = [((2, rows, channels), jnp.bfloat16), ((2, rows, inner), jnp.float32)]
    outs, scratch = [], []
    if forward:
        outs.append(shape(jnp.bfloat16, 2, rows, channels + inner))
    if forward and not backward:
        outs.append(line)
    if backward:
        outs.append(shape(jnp.bfloat16, 2, rows, channels))
        outs.append(shape(jnp.bfloat16, 2, rows, inner))
    if backward and not last:
        outs.append(line)
    if forward and not backward:
        outs += [jax.ShapeDtypeStruct(*one) for one in kept]
    if forward and backward:
        scratch += [pltpu.VMEM(*one) for one in kept]
    if not near:
        scratch += [pltpu.VMEM((2, channels, inner), jnp.bfloat16)] * 2
        scratch += [pltpu.SemaphoreType.DMA((2, 2))]
    passes = 4 * (int(forward) + int(backward))
    return pl.pallas_call(
        functools.partial(stage_body, step, forward, backward, last, near),
        out_shape=outs,
        in_specs=[VMEM if near else ANY] * 4 + [VMEM] * len(arrays),
        out_specs=[VMEM] * len(outs),
        scratch_shapes=scratch,
        compiler_params=PARAMS,
        cost_estimate=pl.CostEstimate(
            flops=2 * passes * rows * channels * inner,
            bytes_accessed=8 * channels * inner,
            transcendentals=passes * rows * channels,
        ),
    )(*weights, *arrays)


def parity(value, mask):
    total, bit = 0, 0
    while mask >> bit:
        if mask >> bit & 1:
            total = total + lax.rem(lax.div(value, 1 << bit), 2)
        bit += 1
    return lax.rem(total, 2)


def halving_plan(size, turn):
    order = [1 << bit for bit in range(size.bit_length() - 1)]
    if turn and len(order) > 1:
        order[:2] = order[1::-1]
    table = [0] * size
    for chunk in range(size):
        place = 0
        for mask in order:
            place = 2 * place + int(chunk & mask != 0)
        table[place] = chunk
    return order, order, table


def side_of(plans, at):
    core, shard = lax.rem(lax.axis_index("pipe"), 2), lax.axis_index("dp")
    return jnp.where(core == 0, parity(shard, plans[0][1][at]), parity(shard, plans[1][1][at]))


def gradient_body(plans, pick_left, pick_right, count, *refs):
    arrays, (send, keep, left, right, full) = refs[:count], refs[count:]
    stage, core, _ = where_am_i(0)
    rows = left.shape[0] // 4
    chunk = send.shape[1]
    for target, pick in ((left, pick_left), (right, pick_right)):
        near, away = pick(arrays)
        for step, part in enumerate(near):

            @pl.when(stage == step)
            def _():
                target[:rows] = part[...]

        for at, part in enumerate(away):
            target[(at + 1) * rows : (at + 2) * rows] = part[...]
    full[...] = contract(left[...], right[...], 0, 0)
    side = side_of(plans, 0)
    half = send.shape[0]
    flip = [plan[2][half] for plan in plans]
    for at in range(half):
        spots = []
        for target_side in (1 - side, side):
            first = plans[0][2][at] ^ (flip[0] * target_side)
            second = plans[1][2][at] ^ (flip[1] * target_side)
            spots.append(pl.multiple_of(jnp.where(core == 0, first, second) * chunk, chunk))
        send[at] = full[pl.ds(spots[0], chunk)].astype(jnp.bfloat16)
        keep[at] = full[pl.ds(spots[1], chunk)]


def halve_body(plans, at, keep_in, came, send, keep):
    half = keep.shape[0]
    side = side_of(plans, at)
    for spot in range(half):
        mine, theirs = side * half + spot, (1 - side) * half + spot
        send[spot] = (keep_in[theirs] + came[theirs].astype(jnp.float32)).astype(jnp.bfloat16)
        keep[spot] = keep_in[mine] + came[mine].astype(jnp.float32)


def bit_of(value, bit):
    return lax.rem(lax.div(value, 1 << bit), 2)


BITS = ((0, 1, 2), (1, 2, 0))


def split_bits(at):
    return tuple(bits[at] if at < len(bits) else at for bits in BITS)


def side_at(at):
    core, shard = lax.rem(lax.axis_index("pipe"), 2), lax.axis_index("dp")
    first, second = split_bits(at)
    return core, jnp.where(core == 0, bit_of(shard, first), bit_of(shard, second))


def chunk_of(core, side, place):
    chunks = [0, 0]
    for at in range(1, 2 + place.bit_length()):
        for which, bit in enumerate(split_bits(at)):
            chunks[which] |= (place >> (at - 1) & 1) << bit
    first, second = split_bits(0)
    return jnp.where(core == 0, chunks[0] + side * (1 << first), chunks[1] + side * (1 << second))


def split_columns(wide, keep, send, chunk):
    core, side = side_at(0)
    for place in range(wide.shape[1] // (2 * chunk)):
        for target, at in ((keep, side), (send, 1 - side)):
            block = chunk_of(core, at, place)
            source = pl.ds(pl.multiple_of(block * chunk, chunk), chunk)
            target[:, place * chunk : (place + 1) * chunk] = wide[:, source]


def pack_body(stages, chunk, up, near, far, *refs):
    refs = list(refs)
    left, right, send, wide = refs[-4:]
    channels = wide.shape[1]
    spans = slice(0, channels), slice(channels, None), slice(None)
    flow_span, back_span = (spans[1] if up else spans[0]), spans[2]
    stage, _, _ = where_am_i(0)
    rows = wide.shape[0] // (2 * near + 2 * far)
    start = 0
    targets = (right, wide) if up else (wide, right)
    for target, span in zip(targets, (flow_span, back_span)):
        start = 0
        if near:
            parts = [refs.pop(0) for _ in range(stages + 1)]
            for step in range(stages):

                @pl.when(stage == step)
                def _():
                    target[:rows] = parts[step][0, :, span]

            target[rows : 2 * rows] = parts[stages][:, span]
            start = 2 * rows
        if far:
            for part in (refs.pop(0), refs.pop(0)):
                target[start : start + rows] = part[:, span]
                start += rows
    split_columns(wide, left, send, chunk)
    send[:, channels // 2 :] = right[...]


def near_body(stages, chunk, *refs):
    flows, ups, backs = [refs[at * (stages + 1) : (at + 1) * (stages + 1)] for at in range(3)]
    left_up, right_up, left_inner, right_inner, send, wide = refs[3 * stages + 3 :]
    width = send.shape[1] // 2
    for at, (late, outs) in enumerate(
        ((ups, (left_up, right_up)), (backs, (left_inner, right_inner)))
    ):
        part = send.at[:, at * width : (at + 1) * width]
        pack_body(stages, chunk, at == 0, True, False, *flows, *late, *outs, part, wide)


def half_gradient_body(at, groups, *refs):
    send, keep, full, left, right = refs[3 * groups :]
    start = 0
    for group in range(groups):
        part_left, part_right, came = refs[3 * group : 3 * group + 3]
        rows, columns = part_left.shape
        left[start : start + rows] = part_left[...]
        right[start : start + rows] = part_right[...]
        start += rows
        width = columns + right.shape[1]
        offset = at * width if came.shape[1] > width else 0
        left[start : start + rows] = came[:, offset : offset + columns]
        right[start : start + rows] = came[:, offset + columns : offset + width]
        start += rows
    full[...] = contract(left[...], right[...], 0, 0)
    _, side = side_at(1)
    chunk = send.shape[1]
    for place in range(send.shape[0]):
        theirs = pl.ds(pl.multiple_of((2 * place + 1 - side) * chunk, chunk), chunk)
        mine = pl.ds(pl.multiple_of((2 * place + side) * chunk, chunk), chunk)
        send[place] = full[theirs].astype(jnp.bfloat16)
        keep[place] = full[mine]


def next_body(at, keep_in, came, send, keep):
    _, side = side_at(at)
    for place in range(keep.shape[0]):
        theirs, mine = 2 * place + 1 - side, 2 * place + side
        send[place] = (keep_in[theirs] + came[theirs].astype(jnp.float32)).astype(jnp.bfloat16)
        keep[place] = keep_in[mine] + came[mine].astype(jnp.float32)


def finish_body(which, keep, came, *refs):
    out, held, sem = refs[-3:]
    held[...] = keep[0] + came[0].astype(jnp.float32)
    copy = pltpu.make_async_copy(held, out.at[0, which], sem)
    copy.start()
    copy.wait()


def finish(which, keep, came, *out):
    return pl.pallas_call(
        functools.partial(finish_body, which),
        out_shape=jax.ShapeDtypeStruct((1, 2) + keep.shape[1:], jnp.float32),
        in_specs=[VMEM] * 2 + [HBM] * len(out),
        out_specs=HBM,
        scratch_shapes=[pltpu.VMEM(keep.shape[1:], jnp.float32), pltpu.SemaphoreType.DMA],
        input_output_aliases={2: 0} if out else {},
        compiler_params=PARAMS,
    )(keep, came, *out)


def shards(inputs, cotangent, reduce_weight, expand_weight):
    stages = lax.axis_size("pipe") // 2
    replicas = lax.axis_size("dp")
    stage, core, _ = where_am_i(0)
    channels, inner = reduce_weight.shape[2:]
    rows = inputs.shape[1] * inputs.shape[2] // 2
    sizes = (channels, inner)
    entering = inputs.reshape(2, 2, rows, channels)
    ending = cotangent.reshape(2, 2, rows, channels)
    own = [reduce_weight[:, 0], expand_weight[:, 0]]

    core_pairs = [(p, p ^ 1) for p in range(2 * stages)]
    mirror_pairs = [(p, 2 * (stages - 1 - p // 2) + p % 2) for p in range(2 * stages)]

    def hop(shard, step):
        pairs = []
        for c in range(2):
            pairs.append((2 * step + c, 2 * step + 2 + c))
            pairs.append((2 * (stages - 1 - step) + c, 2 * (stages - 2 - step) + c))
        return lax.ppermute(shard, "pipe", pairs)

    def swap_cores(shard):
        return lax.ppermute(shard, "pipe", core_pairs)

    def mirror(shard):
        return lax.ppermute(shard, "pipe", mirror_pairs)

    at_stage = [stage == step for step in range(stages)]
    first_core = core == 0
    at_stage, first_core, entering = lax.optimization_barrier((at_stage, first_core, entering))

    def pick(parts, mirrored_stage=False):
        tests = at_stage[::-1] if mirrored_stage else at_stage
        chosen = parts[0]
        for test, part in zip(tests[1:], parts[1:]):
            chosen = jnp.where(test, part, chosen)
        return chosen

    in_hbm = lambda array: pltpu.with_memory_space_constraint(array, pltpu.HBM)
    own, entering, ending = [in_hbm(one) for one in own], in_hbm(entering), in_hbm(ending)
    *near, enter = load(0, own, entering)
    near.append(swap_cores(near[0]))
    near.append(swap_cores(near[1]))
    turn = list(load(stages - 1, own))
    turn += [swap_cores(weight) for weight in turn]
    if stages > 2:
        weights = own + [swap_cores(weight) for weight in own]
    flows, trunks, inners = [], [], []
    head = pl.pallas_call(
        head_body,
        out_shape=[
            jax.ShapeDtypeStruct((rows, channels), jnp.bfloat16),
            jax.ShapeDtypeStruct((rows, inner), jnp.float32),
            jax.ShapeDtypeStruct((rows, inner), jnp.bfloat16),
        ],
        in_specs=[VMEM] * 3,
        out_specs=[VMEM] * 3,
        compiler_params=PARAMS,
    )(near[0], near[2], enter)
    for step in range(stages - 1):
        arrays = [enter] if step else [enter, *head]
        flow, leave, trunk, inner_sum = run_stage(
            weights if step else near, step, True, False, step == 0, rows, sizes, *arrays
        )
        flows.append(flow)
        trunks.append(trunk)
        inners.append(inner_sum)
        enter = hop(leave, step)
    mirrored = stages == 2
    line = jax.ShapeDtypeStruct((rows, channels), jnp.bfloat16)
    outs = [line, jax.ShapeDtypeStruct((rows, inner), jnp.float32)] + [line, line] * mirrored
    ending, first_active, *known = pl.pallas_call(
        functools.partial(meanwhile_body, stages - 1, mirrored),
        out_shape=outs,
        in_specs=[VMEM, VMEM, HBM, HBM, VMEM],
        out_specs=[VMEM] * len(outs),
        scratch_shapes=[pltpu.SemaphoreType.DMA((3,))],
        compiler_params=PARAMS,
    )(turn[1], turn[3], entering, ending, leave)
    flow, upstreams, back_inners, leave = run_stage(
        turn, stages - 1, True, True, True, rows, sizes, enter, ending, first_active
    )
    flows.append(flow)
    upstreams, back_inners = [upstreams], [back_inners]
    upstream = hop(leave, 0)
    side_flow = swap_cores(pick(flows)[1])
    near_core = lambda first, second: jnp.where(first_core, first, second)
    going = pick(flows, True)
    if mirrored:
        lifted = near_core(going[1, :, :channels], going[0, :, :channels])
        going = jnp.concatenate([lifted, going[0, :, channels:], going[1, :, channels:]], axis=1)
    far_flow = mirror(going)
    if mirrored:
        lifted, actives = far_flow[:, :channels], far_flow[:, channels:]
        far_flow = jnp.concatenate([near_core(known[1], lifted), actives[:, :inner]], axis=1)
        cross_flow = jnp.concatenate([near_core(lifted, known[1]), actives[:, inner:]], axis=1)
    else:
        far_flow, cross_flow = far_flow[0], far_flow[1]
    cross_flow = swap_cores(cross_flow)
    for step in range(stages - 2, -1, -1):
        outs = run_stage(
            weights if step else near,
            step,
            False,
            True,
            step == 0,
            rows,
            sizes,
            upstream,
            trunks[step],
            inners[step],
        )
        upstreams.insert(0, outs[0])
        if step:
            upstream = hop(outs[2], stages - 1 - step)
            back_inners.insert(0, outs[1])
            continue
        tail = pl.pallas_call(
            tail_body,
            out_shape=jax.ShapeDtypeStruct(outs[1].shape, outs[1].dtype),
            in_specs=[VMEM] * 5,
            out_specs=VMEM,
            compiler_params=PARAMS,
        )(near[1], near[3], outs[0], outs[1], inners[0])
        back_inners.insert(0, tail)
    going = pick(upstreams, True)
    far_up = mirror(near_core(going[0], going[1]) if mirrored else going)
    far_inner = mirror(pick(back_inners, True))
    side_up = swap_cores(pick(upstreams)[1])
    side_inner = swap_cores(pick(back_inners)[1])
    if mirrored:
        top = jnp.where(at_stage[0], leave, known[0])
        far_up, cross_up = near_core(far_up, top), near_core(top, far_up)
    else:
        far_up, cross_up = far_up[0], far_up[1]
    cross_up = swap_cores(cross_up)
    far_inner, cross_inner = far_inner[0], far_inner[1]
    cross_inner = swap_cores(cross_inner)

    chunk = channels // replicas
    fore = flows + [side_flow, far_flow, cross_flow]
    ups = upstreams + [side_up, far_up, cross_up]
    backs = back_inners + [side_inner, far_inner, cross_inner]
    halve = halve_rows if chunk % 128 == 0 and replicas >= 8 else halve_sums
    keep, came, keep_up, came_up = halve(stages, replicas, chunk, sizes, rows, fore, ups, backs)
    return finish(0, keep, came, finish(1, keep_up, came_up))


def sums(count, chunk, inner):
    return [
        jax.ShapeDtypeStruct((count, chunk, inner), jnp.bfloat16),
        jax.ShapeDtypeStruct((count, chunk, inner), jnp.float32),
    ]


def exchange(shard, stages, replicas, at):
    pairs = []
    first, second = (1 << bit for bit in split_bits(at))
    for p in range(2 * stages):
        for q in range(replicas):
            pairs.append((p * replicas + q, p * replicas + (q ^ (second if p % 2 else first))))
    return lax.ppermute(shard, AXES, pairs)


def halve_rows(stages, replicas, chunk, sizes, rows, fore, ups, backs):
    channels, inner = sizes
    shape = lambda *dims: jax.ShapeDtypeStruct(dims, jnp.bfloat16)

    def pack(late, up, near, far):
        count = 2 * (near + far)
        arrays = []
        for one in (fore, late):
            arrays += one[: stages + 1] * near + one[stages + 1 :] * far
        return pl.pallas_call(
            functools.partial(pack_body, stages, chunk, up, near, far),
            out_shape=[
                shape(count * rows, channels // 2),
                shape(count * rows, inner),
                shape(count * rows, channels // 2 + inner),
            ],
            in_specs=[VMEM] * len(arrays),
            out_specs=[VMEM] * 3,
            scratch_shapes=[pltpu.VMEM((count * rows, channels), jnp.bfloat16)],
            compiler_params=PARAMS,
        )(*arrays)

    near = fore[: stages + 1] + ups[: stages + 1] + backs[: stages + 1]
    *kept, send = pl.pallas_call(
        functools.partial(near_body, stages, chunk),
        out_shape=[
            shape(2 * rows, channels // 2),
            shape(2 * rows, inner),
            shape(2 * rows, channels // 2),
            shape(2 * rows, inner),
            shape(2 * rows, channels + 2 * inner),
        ],
        in_specs=[VMEM] * len(near),
        out_specs=[VMEM] * 5,
        scratch_shapes=[pltpu.VMEM((2 * rows, channels), jnp.bfloat16)],
        compiler_params=PARAMS,
    )(*near)
    came_near = exchange(send, stages, replicas, 0)
    parts = []
    for at, name, late in ((1, "inner", backs), (0, "up", ups)):
        left, right, send = pack(late, name == "up", False, True)
        came = exchange(send, stages, replicas, 0)
        operands = (kept[2 * at], kept[2 * at + 1], came_near, left, right, came)
        count = replicas // 4
        send, keep = pl.pallas_call(
            functools.partial(half_gradient_body, at, len(operands) // 3),
            out_shape=sums(count, chunk, inner),
            in_specs=[VMEM] * len(operands),
            out_specs=[VMEM] * 2,
            scratch_shapes=[
                pltpu.VMEM((channels // 2, inner), jnp.float32),
                pltpu.VMEM((8 * rows, channels // 2), jnp.bfloat16),
                pltpu.VMEM((8 * rows, inner), jnp.bfloat16),
            ],
            compiler_params=PARAMS,
        )(*operands)
        came = exchange(send, stages, replicas, 1)
        for at in range(2, replicas.bit_length() - 1):
            count //= 2
            send, keep = pl.pallas_call(
                functools.partial(next_body, at),
                out_shape=sums(count, chunk, inner),
                in_specs=[VMEM] * 2,
                out_specs=[VMEM] * 2,
                compiler_params=PARAMS,
            )(keep, came)
            came = exchange(send, stages, replicas, at)
        parts += [keep, came]
    return parts


def halve_sums(stages, replicas, chunk, sizes, rows, fore, ups, backs):
    channels, inner = sizes
    wide, narrow = slice(0, channels), slice(channels, channels + inner)

    def of_flows(columns):
        def pick_parts(arrays):
            near = [flow.at[0, :, columns] for flow in arrays[:stages]]
            side, far, cross = arrays[stages : stages + 3]
            return near, [side.at[:, columns], far.at[:, columns], cross.at[:, columns]]

        return pick_parts

    def of_backs(arrays):
        near = [back.at[0] for back in arrays[stages + 3 : 2 * stages + 3]]
        side, far, cross = arrays[2 * stages + 3 : 2 * stages + 6]
        return near, [side, far, cross]

    plans = [halving_plan(replicas, turn) for turn in range(2)]
    streams = []
    for pick_left, pick_right, late, plan in (
        (of_backs, of_flows(narrow), ups, plans),
        (of_flows(wide), of_backs, backs, plans[::-1]),
    ):
        arrays = fore + late
        send, keep = pl.pallas_call(
            functools.partial(gradient_body, plan, pick_left, pick_right, len(arrays)),
            out_shape=sums(replicas // 2, chunk, inner),
            in_specs=[VMEM] * len(arrays),
            out_specs=[VMEM] * 2,
            scratch_shapes=[
                pltpu.VMEM((4 * rows, channels), jnp.bfloat16),
                pltpu.VMEM((4 * rows, inner), jnp.bfloat16),
                pltpu.VMEM((channels, inner), jnp.float32),
            ],
            compiler_params=PARAMS,
        )(*arrays)
        streams.append((plan, send, keep))
    for at in range(replicas.bit_length() - 1):
        half = replicas >> (at + 2)
        arrived = []
        for plan, send, keep in streams:
            pairs = []
            for p in range(2 * stages):
                for q in range(replicas):
                    pairs.append((p * replicas + q, p * replicas + (q ^ plan[p % 2][0][at])))
            arrived.append((plan, keep, lax.ppermute(send, AXES, pairs)))
        if half == 0:
            break
        streams = []
        for plan, keep, came in arrived:
            send, keep = pl.pallas_call(
                functools.partial(halve_body, plan, at + 1),
                out_shape=sums(half, chunk, inner),
                in_specs=[VMEM] * 2,
                out_specs=[VMEM] * 2,
                compiler_params=PARAMS,
            )(keep, came)
            streams.append((plan, send, keep))
    (_, keep_expand, came_expand), (_, keep_reduce, came_reduce) = arrived
    return keep_reduce, came_reduce, keep_expand, came_expand


def solution(mesh):
    return jax.shard_map(
        shards,
        mesh=mesh,
        in_specs=(
            P(None, None, "dp", None),
            P(None, None, "dp", None),
            P(None, "pipe", None, None),
            P(None, "pipe", None, None),
        ),
        out_specs=P("pipe", None, "dp", None),
        check_vma=False,
    )
```

```python
import functools

import jax
import jax.numpy as jnp
from jax import lax
from jax.experimental import pallas as pl
from jax.experimental.pallas import tpu as pltpu
from jax.sharding import PartitionSpec as P


EPSILON = 1e-06
AXES = ("pipe", "dp")
HBM = pl.BlockSpec(memory_space=pltpu.HBM)
ANY = pl.BlockSpec(memory_space=pl.ANY)
VMEM = pl.BlockSpec(memory_space=pltpu.VMEM)
PARAMS = pltpu.CompilerParams(vmem_limit_bytes=16 << 20)


def contract(first_op, second_op, first_dim, second_dim):
    return lax.dot_general(
        first_op,
        second_op,
        (((first_dim,), (second_dim,)), ((), ())),
        preferred_element_type=jnp.float32,
    )


def smooth_slope(values):
    sigma = jax.nn.sigmoid(values)
    return sigma * (1.0 + values * (1.0 - sigma))


def norm_of(widened):
    return lax.rsqrt(jnp.mean(widened * widened, axis=-1, keepdims=True) + EPSILON)


def where_am_i(step):
    position = lax.axis_index("pipe")
    stage, core = lax.div(position, 2), lax.rem(position, 2)
    way = jnp.where(stage == step, 0, 1)
    return stage, core, way


def bring_all(sources, outs, sems):
    copies = [
        pltpu.make_async_copy(source, out, sems.at[at])
        for at, (source, out) in enumerate(zip(sources, outs))
    ]
    for copy in copies:
        copy.start()
    return copies


def load_body(step, reduce_all, expand_all, *refs):
    _, core, way = where_am_i(step)
    sources, outs = [reduce_all.at[way], expand_all.at[way]], refs[:-1]
    if step == 0:
        sources.append(refs[0].at[way, core])
        outs = outs[1:]
    for copy in bring_all(sources, outs, refs[-1]):
        copy.wait()


def load(step, own, *more):
    channels, inner = own[0].shape[1:]
    mat = jax.ShapeDtypeStruct((channels, inner), jnp.bfloat16)
    outs = [mat, mat] + [jax.ShapeDtypeStruct(a.shape[2:], a.dtype) for a in more]
    return pl.pallas_call(
        functools.partial(load_body, step),
        out_shape=outs,
        in_specs=[HBM] * (2 + len(more)),
        out_specs=[VMEM] * len(outs),
        scratch_shapes=[pltpu.SemaphoreType.DMA((len(outs),))],
        compiler_params=PARAMS,
    )(*own, *more)


def meanwhile_body(step, mirrored, expand_own, expand_other, inputs, cotangent, leave, *refs):
    outs, sems = refs[:-1], refs[-1]
    stage, core, way = where_am_i(step)
    ending, back_active = outs[:2]
    sources = [cotangent.at[way, core]]
    if mirrored:
        sources += [cotangent.at[1, core], inputs.at[1, core]]
    copies = bring_all(sources, [outs[0]] + list(outs[2:]), sems)
    copies[0].wait()

    @pl.when(way == core)
    def _():
        back_active[...] = jnp.dot(
            ending[...], expand_other[...], preferred_element_type=jnp.float32
        )

    @pl.when(way != core)
    def _():
        back_active[...] = jnp.dot(ending[...], expand_own[...], preferred_element_type=jnp.float32)

    for copy in copies[1:]:
        copy.wait()
    if mirrored:
        rows = outs[3]

        @pl.when(stage != 0)
        def _():
            rows[...] = leave[...]

        widened = rows[...].astype(jnp.float32)
        rows[...] = jax.nn.silu(widened * norm_of(widened)).astype(jnp.bfloat16)


def weight_copies(own, other, held, sems, core, way):
    copies = []
    for order in range(2):
        is_own = lax.rem(way + order, 2) == core
        for kind in range(2):
            mine = pltpu.make_async_copy(own[kind].at[way], held[kind].at[order], sems.at[kind, order])
            theirs = pltpu.make_async_copy(
                other[kind].at[way], held[kind].at[order], sems.at[kind, order]
            )
            copies.append((is_own, mine, theirs))
    return copies


def start_all(copies):
    for is_own, mine, theirs in copies:
        pl.when(is_own)(mine.start)
        pl.when(jnp.logical_not(is_own))(theirs.start)


def head_body(own, other, rows_in, lifted_out, inner_out, active_out):
    _, core, way = where_am_i(0)
    widened = rows_in[...].astype(jnp.float32)
    lifted = jax.nn.silu(widened * norm_of(widened)).astype(jnp.bfloat16)
    lifted_out[...] = lifted

    def run(reduce_mat):
        inner_sum = jnp.dot(lifted, reduce_mat[...], preferred_element_type=jnp.float32)
        inner_out[...] = inner_sum
        active_out[...] = jax.nn.silu(inner_sum).astype(jnp.bfloat16)

    pl.when(way == core)(lambda: run(own))
    pl.when(way != core)(lambda: run(other))


def stage_body(step, forward, backward, last, near, *refs):
    refs = list(refs)
    _, core, way = where_am_i(step)
    own, other = (refs.pop(0), refs.pop(0)), (refs.pop(0), refs.pop(0))
    enter = refs.pop(0) if forward else None
    head = [refs.pop(0) for _ in range(3)] if forward and step == 0 else None
    upstream_in = refs.pop(0) if backward else None
    first_active = refs.pop(0) if forward and backward else None
    if not forward:
        trunks, inners = refs.pop(0), refs.pop(0)
    if forward:
        flows = refs.pop(0)
    if forward and not backward:
        leave = refs.pop(0)
    if backward:
        upstreams, back_inners = refs.pop(0), refs.pop(0)
    if backward and not last:
        back_leave = refs.pop(0)
    if forward:
        trunks, inners = refs.pop(0), refs.pop(0)
    channels = trunks.shape[2]

    def run(reduce_mats, expand_mats, wait):
        if forward:
            rows = enter[...]
            for order in range(2):
                slot = lax.rem(order + core, 2)
                widened = rows.astype(jnp.float32)
                trunks[order] = rows
                if head and order == 0:
                    lifted, inner_sum, active = [part[...] for part in head]
                else:
                    normed = widened * norm_of(widened)
                    lifted = jax.nn.silu(normed).astype(jnp.bfloat16)
                    wait(0, order)
                    inner_sum = jnp.dot(
                        lifted, reduce_mats[order][...], preferred_element_type=jnp.float32
                    )
                    active = jax.nn.silu(inner_sum).astype(jnp.bfloat16)
                flows[slot, :, :channels] = lifted
                inners[order] = inner_sum
                flows[slot, :, channels:] = active
                wait(1, order)
                rows = (widened + contract(active, expand_mats[order][...], 1, 1)).astype(jnp.bfloat16)
            if not backward:
                leave[...] = rows
        if backward:
            upstream = upstream_in[...]
            for order in (1, 0):
                slot = lax.rem(order + core, 2)
                upstreams[slot] = upstream
                if last and order == 0:
                    break
                if not forward:
                    wait(1, order)
                if forward and order:
                    back_active = first_active[...]
                else:
                    back_active = jnp.dot(
                        upstream, expand_mats[order][...], preferred_element_type=jnp.float32
                    )
                back_inner = (back_active * smooth_slope(inners[order])).astype(jnp.bfloat16)
                back_inners[slot] = back_inner
                if not forward:
                    wait(0, order)
                back_lifted = contract(back_inner, reduce_mats[order][...], 1, 1)
                widened = trunks[order].astype(jnp.float32)
                norm_scale = norm_of(widened)
                back_normed = back_lifted * smooth_slope(widened * norm_scale)
                projection = jnp.mean(back_normed * widened, axis=-1, keepdims=True)
                upstream = (
                    upstream.astype(jnp.float32)
                    + norm_scale * back_normed
                    - widened * norm_scale**3 * projection
                ).astype(jnp.bfloat16)
            if not last:
                back_leave[...] = upstream

    if near:
        idle = lambda kind, order: None

        @pl.when(way == core)
        def _():
            run((own[0], other[0]), (own[1], other[1]), idle)

        @pl.when(way != core)
        def _():
            run((other[0], own[0]), (other[1], own[1]), idle)

    else:
        held = (refs.pop(0), refs.pop(0))
        copies = weight_copies(own, other, held, refs.pop(0), core, way)
        start_all(copies if forward else copies[2:] + copies[:2])
        run(
            [held[0].at[order] for order in range(2)],
            [held[1].at[order] for order in range(2)],
            lambda kind, order: copies[2 * order + kind][1].wait(),
        )


def tail_body(own, other, upstreams, back_first, inners, back_inners):
    _, core, way = where_am_i(0)

    def run(expand_mat):
        back_active = jnp.dot(upstreams[core], expand_mat[...], preferred_element_type=jnp.float32)
        back_inners[core] = (back_active * smooth_slope(inners[0])).astype(jnp.bfloat16)
        back_inners[1 - core] = back_first[1 - core]

    pl.when(way == core)(lambda: run(own))
    pl.when(way != core)(lambda: run(other))


def run_stage(weights, step, forward, backward, near, rows, sizes, *arrays):
    channels, inner = sizes
    last = backward and step == 0 and not forward
    shape = lambda dtype, *dims: jax.ShapeDtypeStruct(dims, dtype)
    line = shape(jnp.bfloat16, rows, channels)
    kept = [((2, rows, channels), jnp.bfloat16), ((2, rows, inner), jnp.float32)]
    outs, scratch = [], []
    if forward:
        outs.append(shape(jnp.bfloat16, 2, rows, channels + inner))
    if forward and not backward:
        outs.append(line)
    if backward:
        outs.append(shape(jnp.bfloat16, 2, rows, channels))
        outs.append(shape(jnp.bfloat16, 2, rows, inner))
    if backward and not last:
        outs.append(line)
    if forward and not backward:
        outs += [jax.ShapeDtypeStruct(*one) for one in kept]
    if forward and backward:
        scratch += [pltpu.VMEM(*one) for one in kept]
    if not near:
        scratch += [pltpu.VMEM((2, channels, inner), jnp.bfloat16)] * 2
        scratch += [pltpu.SemaphoreType.DMA((2, 2))]
    passes = 4 * (int(forward) + int(backward))
    return pl.pallas_call(
        functools.partial(stage_body, step, forward, backward, last, near),
        out_shape=outs,
        in_specs=[VMEM if near else ANY] * 4 + [VMEM] * len(arrays),
        out_specs=[VMEM] * len(outs),
        scratch_shapes=scratch,
        compiler_params=PARAMS,
        cost_estimate=pl.CostEstimate(
            flops=2 * passes * rows * channels * inner,
            bytes_accessed=8 * channels * inner,
            transcendentals=passes * rows * channels,
        ),
    )(*weights, *arrays)


def parity(value, mask):
    total, bit = 0, 0
    while mask >> bit:
        if mask >> bit & 1:
            total = total + lax.rem(lax.div(value, 1 << bit), 2)
        bit += 1
    return lax.rem(total, 2)


def halving_plan(size, turn):
    order = [1 << bit for bit in range(size.bit_length() - 1)]
    if turn and len(order) > 1:
        order[:2] = order[1::-1]
    table = [0] * size
    for chunk in range(size):
        place = 0
        for mask in order:
            place = 2 * place + int(chunk & mask != 0)
        table[place] = chunk
    return order, order, table


def side_of(plans, at):
    core, shard = lax.rem(lax.axis_index("pipe"), 2), lax.axis_index("dp")
    return jnp.where(core == 0, parity(shard, plans[0][1][at]), parity(shard, plans[1][1][at]))


def gradient_body(plans, pick_left, pick_right, count, *refs):
    arrays, (send, keep, left, right, full) = refs[:count], refs[count:]
    stage, core, _ = where_am_i(0)
    rows = left.shape[0] // 4
    chunk = send.shape[1]
    for target, pick in ((left, pick_left), (right, pick_right)):
        near, away = pick(arrays)
        for step, part in enumerate(near):

            @pl.when(stage == step)
            def _():
                target[:rows] = part[...]

        for at, part in enumerate(away):
            target[(at + 1) * rows : (at + 2) * rows] = part[...]
    full[...] = contract(left[...], right[...], 0, 0)
    side = side_of(plans, 0)
    half = send.shape[0]
    flip = [plan[2][half] for plan in plans]
    for at in range(half):
        spots = []
        for target_side in (1 - side, side):
            first = plans[0][2][at] ^ (flip[0] * target_side)
            second = plans[1][2][at] ^ (flip[1] * target_side)
            spots.append(pl.multiple_of(jnp.where(core == 0, first, second) * chunk, chunk))
        send[at] = full[pl.ds(spots[0], chunk)].astype(jnp.bfloat16)
        keep[at] = full[pl.ds(spots[1], chunk)]


def halve_body(plans, at, keep_in, came, send, keep):
    half = keep.shape[0]
    side = side_of(plans, at)
    for spot in range(half):
        mine, theirs = side * half + spot, (1 - side) * half + spot
        send[spot] = (keep_in[theirs] + came[theirs].astype(jnp.float32)).astype(jnp.bfloat16)
        keep[spot] = keep_in[mine] + came[mine].astype(jnp.float32)


def bit_of(value, bit):
    return lax.rem(lax.div(value, 1 << bit), 2)


def first_sides():
    core, shard = lax.rem(lax.axis_index("pipe"), 2), lax.axis_index("dp")
    low, high = bit_of(shard, 0), bit_of(shard, 1)
    return core, jnp.where(core == 0, low, high), jnp.where(core == 0, high, low)


def split_columns(wide, keep, send, chunk):
    core, side, _ = first_sides()
    for place in range(wide.shape[1] // (2 * chunk)):
        for target, at in ((keep, side), (send, 1 - side)):
            block = jnp.where(core == 0, 2 * place + at, place // 2 * 4 + 2 * at + place % 2)
            source = pl.ds(pl.multiple_of(block * chunk, chunk), chunk)
            target[:, place * chunk : (place + 1) * chunk] = wide[:, source]


def take_rows(target, span, *arrays):
    stage, _, _ = where_am_i(0)
    *own, other = arrays
    rows = target.shape[0] // 2
    for step, part in enumerate(own):
        part = part if len(part.shape) == 2 else part.at[0]

        @pl.when((stage == step) | (len(own) == 1))
        def _():
            target[:rows] = part[:, span]

    target[rows:] = other[:, span]


def near_up_body(stages, chunk, *refs):
    flows, ups = refs[: stages + 1], refs[stages + 1 : 2 * stages + 2]
    up, active, lifted, send, wide = refs[2 * stages + 2 :]
    half, channels = up.shape[1], wide.shape[1]
    inner = active.shape[1]
    take_rows(wide, slice(None), *ups)
    split_columns(wide, up, send.at[:, :half], chunk)
    take_rows(active, slice(channels, None), *flows)
    send[:, half : half + inner] = active[...]
    take_rows(wide, slice(0, channels), *flows)
    split_columns(wide, lifted, send.at[:, half + inner :], chunk)


def late_up_body(chunk, flow, cross_flow, far, cross, up, active, send, wide):
    half, channels = up.shape[1], wide.shape[1]
    take_rows(wide, slice(None), far, cross)
    split_columns(wide, up, send.at[:, :half], chunk)
    take_rows(active, slice(channels, None), flow, cross_flow)
    send[:, half:] = active[...]


def late_inner_body(chunk, flow, cross_flow, *refs):
    *backs, far, cross, lifted, far_inner, near_inner, send, wide = refs
    half, channels = lifted.shape[1], wide.shape[1]
    inner = far_inner.shape[1]
    take_rows(wide, slice(0, channels), flow, cross_flow)
    split_columns(wide, lifted, send.at[:, :half], chunk)
    take_rows(far_inner, slice(None), far, cross)
    send[:, half : half + inner] = far_inner[...]
    take_rows(near_inner, slice(None), *backs)
    send[:, half + inner :] = near_inner[...]


def half_gradient_body(starts, *refs):
    lefts, rights, cames = refs[:2], refs[2:4], refs[4:6]
    send, keep, full, left, right = refs[6:]
    rows, columns = lefts[0].shape
    inner = rights[0].shape[1]
    for group, ((left_in, left_start), (right_in, right_start)) in enumerate(starts):
        place = slice(2 * group * rows, (2 * group + 1) * rows)
        left[place] = lefts[group][...]
        right[place] = rights[group][...]
        place = slice((2 * group + 1) * rows, (2 * group + 2) * rows)
        left[place] = cames[left_in][:, left_start : left_start + columns]
        right[place] = cames[right_in][:, right_start : right_start + inner]
    full[...] = contract(left[...], right[...], 0, 0)
    _, _, side = first_sides()
    chunk = send.shape[1]
    for place in range(send.shape[0]):
        theirs = pl.ds(pl.multiple_of((2 * place + 1 - side) * chunk, chunk), chunk)
        mine = pl.ds(pl.multiple_of((2 * place + side) * chunk, chunk), chunk)
        send[place] = full[theirs].astype(jnp.bfloat16)
        keep[place] = full[mine]


def next_body(bit, keep_in, came, send, keep):
    side = bit_of(lax.axis_index("dp"), bit)
    for place in range(keep.shape[0]):
        theirs, mine = 2 * place + 1 - side, 2 * place + side
        send[place] = (keep_in[theirs] + came[theirs].astype(jnp.float32)).astype(jnp.bfloat16)
        keep[place] = keep_in[mine] + came[mine].astype(jnp.float32)


def finish_body(keep_reduce, came_reduce, keep_expand, came_expand, out):
    out[0, 0] = keep_reduce[0] + came_reduce[0].astype(jnp.float32)
    out[0, 1] = keep_expand[0] + came_expand[0].astype(jnp.float32)


def shards(inputs, cotangent, reduce_weight, expand_weight):
    stages = lax.axis_size("pipe") // 2
    replicas = lax.axis_size("dp")
    stage, core, _ = where_am_i(0)
    channels, inner = reduce_weight.shape[2:]
    rows = inputs.shape[1] * inputs.shape[2] // 2
    sizes = (channels, inner)
    entering = inputs.reshape(2, 2, rows, channels)
    ending = cotangent.reshape(2, 2, rows, channels)
    own = [reduce_weight[:, 0], expand_weight[:, 0]]

    core_pairs = [(p, p ^ 1) for p in range(2 * stages)]
    mirror_pairs = [(p, 2 * (stages - 1 - p // 2) + p % 2) for p in range(2 * stages)]

    def hop(shard, step):
        pairs = []
        for c in range(2):
            pairs.append((2 * step + c, 2 * step + 2 + c))
            pairs.append((2 * (stages - 1 - step) + c, 2 * (stages - 2 - step) + c))
        return lax.ppermute(shard, "pipe", pairs)

    def swap_cores(shard):
        return lax.ppermute(shard, "pipe", core_pairs)

    def mirror(shard):
        return lax.ppermute(shard, "pipe", mirror_pairs)

    at_stage = [stage == step for step in range(stages)]
    first_core = core == 0
    at_stage, first_core, entering = lax.optimization_barrier((at_stage, first_core, entering))

    def pick(parts, mirrored_stage=False):
        tests = at_stage[::-1] if mirrored_stage else at_stage
        chosen = parts[0]
        for test, part in zip(tests[1:], parts[1:]):
            chosen = jnp.where(test, part, chosen)
        return chosen

    in_hbm = lambda array: pltpu.with_memory_space_constraint(array, pltpu.HBM)
    own, entering, ending = [in_hbm(one) for one in own], in_hbm(entering), in_hbm(ending)
    *near, enter = load(0, own, entering)
    near.append(swap_cores(near[0]))
    near.append(swap_cores(near[1]))
    turn = list(load(stages - 1, own))
    turn += [swap_cores(weight) for weight in turn]
    if stages > 2:
        weights = own + [swap_cores(weight) for weight in own]
    flows, trunks, inners = [], [], []
    head = pl.pallas_call(
        head_body,
        out_shape=[
            jax.ShapeDtypeStruct((rows, channels), jnp.bfloat16),
            jax.ShapeDtypeStruct((rows, inner), jnp.float32),
            jax.ShapeDtypeStruct((rows, inner), jnp.bfloat16),
        ],
        in_specs=[VMEM] * 3,
        out_specs=[VMEM] * 3,
        compiler_params=PARAMS,
    )(near[0], near[2], enter)
    for step in range(stages - 1):
        arrays = [enter] if step else [enter, *head]
        flow, leave, trunk, inner_sum = run_stage(
            weights if step else near, step, True, False, step == 0, rows, sizes, *arrays
        )
        flows.append(flow)
        trunks.append(trunk)
        inners.append(inner_sum)
        enter = hop(leave, step)
    mirrored = stages == 2
    line = jax.ShapeDtypeStruct((rows, channels), jnp.bfloat16)
    outs = [line, jax.ShapeDtypeStruct((rows, inner), jnp.float32)] + [line, line] * mirrored
    ending, first_active, *known = pl.pallas_call(
        functools.partial(meanwhile_body, stages - 1, mirrored),
        out_shape=outs,
        in_specs=[VMEM, VMEM, HBM, HBM, VMEM],
        out_specs=[VMEM] * len(outs),
        scratch_shapes=[pltpu.SemaphoreType.DMA((3,))],
        compiler_params=PARAMS,
    )(turn[1], turn[3], entering, ending, leave)
    flow, upstreams, back_inners, leave = run_stage(
        turn, stages - 1, True, True, True, rows, sizes, enter, ending, first_active
    )
    flows.append(flow)
    upstreams, back_inners = [upstreams], [back_inners]
    upstream = hop(leave, 0)
    side_flow = swap_cores(pick(flows)[1])
    near_core = lambda first, second: jnp.where(first_core, first, second)
    going = pick(flows, True)
    if mirrored:
        lifted = near_core(going[1, :, :channels], going[0, :, :channels])
        going = jnp.concatenate([lifted, going[0, :, channels:], going[1, :, channels:]], axis=1)
    far_flow = mirror(going)
    if mirrored:
        lifted, actives = far_flow[:, :channels], far_flow[:, channels:]
        far_flow = jnp.concatenate([near_core(known[1], lifted), actives[:, :inner]], axis=1)
        cross_flow = jnp.concatenate([near_core(lifted, known[1]), actives[:, inner:]], axis=1)
    else:
        far_flow, cross_flow = far_flow[0], far_flow[1]
    cross_flow = swap_cores(cross_flow)
    for step in range(stages - 2, -1, -1):
        outs = run_stage(
            weights if step else near,
            step,
            False,
            True,
            step == 0,
            rows,
            sizes,
            upstream,
            trunks[step],
            inners[step],
        )
        upstreams.insert(0, outs[0])
        if step:
            upstream = hop(outs[2], stages - 1 - step)
            back_inners.insert(0, outs[1])
            continue
        tail = pl.pallas_call(
            tail_body,
            out_shape=jax.ShapeDtypeStruct(outs[1].shape, outs[1].dtype),
            in_specs=[VMEM] * 5,
            out_specs=VMEM,
            compiler_params=PARAMS,
        )(near[1], near[3], outs[0], outs[1], inners[0])
        back_inners.insert(0, tail)
    going = pick(upstreams, True)
    far_up = mirror(near_core(going[0], going[1]) if mirrored else going)
    far_inner = mirror(pick(back_inners, True))
    side_up = swap_cores(pick(upstreams)[1])
    side_inner = swap_cores(pick(back_inners)[1])
    if mirrored:
        top = jnp.where(at_stage[0], leave, known[0])
        far_up, cross_up = near_core(far_up, top), near_core(top, far_up)
    else:
        far_up, cross_up = far_up[0], far_up[1]
    cross_up = swap_cores(cross_up)
    far_inner, cross_inner = far_inner[0], far_inner[1]
    cross_inner = swap_cores(cross_inner)

    chunk = channels // replicas
    fore = flows + [side_flow, far_flow, cross_flow]
    ups = upstreams + [side_up, far_up, cross_up]
    backs = back_inners + [side_inner, far_inner, cross_inner]
    halve = halve_rows if chunk % 128 == 0 and replicas >= 4 else halve_sums
    parts = halve(stages, replicas, chunk, sizes, rows, fore, ups, backs)
    return pl.pallas_call(
        finish_body,
        out_shape=jax.ShapeDtypeStruct((1, 2, chunk, inner), jnp.float32),
        in_specs=[VMEM] * 4,
        out_specs=VMEM,
        compiler_params=PARAMS,
    )(*parts)


def sums(count, chunk, inner):
    return [
        jax.ShapeDtypeStruct((count, chunk, inner), jnp.bfloat16),
        jax.ShapeDtypeStruct((count, chunk, inner), jnp.float32),
    ]


def exchange(shard, stages, replicas, first, second):
    pairs = []
    for p in range(2 * stages):
        for q in range(replicas):
            pairs.append((p * replicas + q, p * replicas + (q ^ (second if p % 2 else first))))
    return lax.ppermute(shard, AXES, pairs)


def halve_rows(stages, replicas, chunk, sizes, rows, fore, ups, backs):
    channels, inner = sizes
    half = channels // 2
    count = stages + 1

    def pack(body, arrays, *widths):
        return pl.pallas_call(
            body,
            out_shape=[jax.ShapeDtypeStruct((2 * rows, width), jnp.bfloat16) for width in widths],
            in_specs=[VMEM] * len(arrays),
            out_specs=[VMEM] * len(widths),
            scratch_shapes=[pltpu.VMEM((2 * rows, channels), jnp.bfloat16)],
            compiler_params=PARAMS,
        )(*arrays)

    near_up, near_active, near_lifted, send = pack(
        functools.partial(near_up_body, stages, chunk),
        fore[:count] + ups[:count],
        half,
        inner,
        half,
        2 * half + inner,
    )
    came_near = exchange(send, stages, replicas, 1, 2)
    far_up, far_active, send = pack(
        functools.partial(late_up_body, chunk),
        fore[count:] + ups[count:],
        half,
        inner,
        half + inner,
    )
    came_up = exchange(send, stages, replicas, 1, 2)
    far_lifted, far_inner, near_inner, send = pack(
        functools.partial(late_inner_body, chunk),
        fore[count:] + backs,
        half,
        inner,
        inner,
        half + 2 * inner,
    )
    came_inner = exchange(send, stages, replicas, 1, 2)
    streams = (
        (
            (near_lifted, far_lifted, near_inner, far_inner, came_near, came_inner),
            (((0, half + inner), (1, half + inner)), ((1, 0), (1, half))),
        ),
        (
            (near_up, far_up, near_active, far_active, came_near, came_up),
            (((0, 0), (0, half)), ((1, 0), (1, half))),
        ),
    )
    parts = []
    for operands, starts in streams:
        count = replicas // 4
        send, keep = pl.pallas_call(
            functools.partial(half_gradient_body, starts),
            out_shape=sums(count, chunk, inner),
            in_specs=[VMEM] * len(operands),
            out_specs=[VMEM] * 2,
            scratch_shapes=[
                pltpu.VMEM((channels // 2, inner), jnp.float32),
                pltpu.VMEM((8 * rows, channels // 2), jnp.bfloat16),
                pltpu.VMEM((8 * rows, inner), jnp.bfloat16),
            ],
            compiler_params=PARAMS,
        )(*operands)
        came = exchange(send, stages, replicas, 2, 1)
        for bit in range(2, replicas.bit_length() - 1):
            count //= 2
            send, keep = pl.pallas_call(
                functools.partial(next_body, bit),
                out_shape=sums(count, chunk, inner),
                in_specs=[VMEM] * 2,
                out_specs=[VMEM] * 2,
                compiler_params=PARAMS,
            )(keep, came)
            came = exchange(send, stages, replicas, 1 << bit, 1 << bit)
        parts += [keep, came]
    return parts


def halve_sums(stages, replicas, chunk, sizes, rows, fore, ups, backs):
    channels, inner = sizes
    wide, narrow = slice(0, channels), slice(channels, channels + inner)

    def of_flows(columns):
        def pick_parts(arrays):
            near = [flow.at[0, :, columns] for flow in arrays[:stages]]
            side, far, cross = arrays[stages : stages + 3]
            return near, [side.at[:, columns], far.at[:, columns], cross.at[:, columns]]

        return pick_parts

    def of_backs(arrays):
        near = [back.at[0] for back in arrays[stages + 3 : 2 * stages + 3]]
        side, far, cross = arrays[2 * stages + 3 : 2 * stages + 6]
        return near, [side, far, cross]

    plans = [halving_plan(replicas, turn) for turn in range(2)]
    streams = []
    for pick_left, pick_right, late, plan in (
        (of_backs, of_flows(narrow), ups, plans),
        (of_flows(wide), of_backs, backs, plans[::-1]),
    ):
        arrays = fore + late
        send, keep = pl.pallas_call(
            functools.partial(gradient_body, plan, pick_left, pick_right, len(arrays)),
            out_shape=sums(replicas // 2, chunk, inner),
            in_specs=[VMEM] * len(arrays),
            out_specs=[VMEM] * 2,
            scratch_shapes=[
                pltpu.VMEM((4 * rows, channels), jnp.bfloat16),
                pltpu.VMEM((4 * rows, inner), jnp.bfloat16),
                pltpu.VMEM((channels, inner), jnp.float32),
            ],
            compiler_params=PARAMS,
        )(*arrays)
        streams.append((plan, send, keep))
    for at in range(replicas.bit_length() - 1):
        half = replicas >> (at + 2)
        arrived = []
        for plan, send, keep in streams:
            pairs = []
            for p in range(2 * stages):
                for q in range(replicas):
                    pairs.append((p * replicas + q, p * replicas + (q ^ plan[p % 2][0][at])))
            arrived.append((plan, keep, lax.ppermute(send, AXES, pairs)))
        if half == 0:
            break
        streams = []
        for plan, keep, came in arrived:
            send, keep = pl.pallas_call(
                functools.partial(halve_body, plan, at + 1),
                out_shape=sums(half, chunk, inner),
                in_specs=[VMEM] * 2,
                out_specs=[VMEM] * 2,
                compiler_params=PARAMS,
            )(keep, came)
            streams.append((plan, send, keep))
    (_, keep_expand, came_expand), (_, keep_reduce, came_reduce) = arrived
    return keep_reduce, came_reduce, keep_expand, came_expand


def solution(mesh):
    return jax.shard_map(
        shards,
        mesh=mesh,
        in_specs=(
            P(None, None, "dp", None),
            P(None, None, "dp", None),
            P(None, "pipe", None, None),
            P(None, "pipe", None, None),
        ),
        out_specs=P("pipe", None, "dp", None),
        check_vma=False,
    )
```

```python
import functools

import jax
import jax.numpy as jnp
from jax import lax
from jax.experimental import pallas as pl
from jax.experimental.pallas import tpu as pltpu
from jax.sharding import PartitionSpec as P


EPSILON = 1e-06
AXES = ("pipe", "dp")
HBM = pl.BlockSpec(memory_space=pltpu.HBM)
ANY = pl.BlockSpec(memory_space=pl.ANY)
VMEM = pl.BlockSpec(memory_space=pltpu.VMEM)
PARAMS = pltpu.CompilerParams(vmem_limit_bytes=16 << 20)


def contract(first_op, second_op, first_dim, second_dim):
    return lax.dot_general(
        first_op,
        second_op,
        (((first_dim,), (second_dim,)), ((), ())),
        preferred_element_type=jnp.float32,
    )


def smooth_slope(values):
    sigma = jax.nn.sigmoid(values)
    return sigma * (1.0 + values * (1.0 - sigma))


def norm_of(widened):
    return lax.rsqrt(jnp.mean(widened * widened, axis=-1, keepdims=True) + EPSILON)


def where_am_i(step):
    position = lax.axis_index("pipe")
    stage, core = lax.div(position, 2), lax.rem(position, 2)
    way = jnp.where(stage == step, 0, 1)
    return stage, core, way


def bring_all(sources, outs, sems):
    copies = [
        pltpu.make_async_copy(source, out, sems.at[at])
        for at, (source, out) in enumerate(zip(sources, outs))
    ]
    for copy in copies:
        copy.start()
    return copies


def load_body(step, reduce_all, expand_all, *refs):
    _, core, way = where_am_i(step)
    sources, outs = [reduce_all.at[way], expand_all.at[way]], refs[:-1]
    if step == 0:
        sources.append(refs[0].at[way, core])
        outs = outs[1:]
    for copy in bring_all(sources, outs, refs[-1]):
        copy.wait()


def load(step, own, *more):
    channels, inner = own[0].shape[1:]
    mat = jax.ShapeDtypeStruct((channels, inner), jnp.bfloat16)
    outs = [mat, mat] + [jax.ShapeDtypeStruct(a.shape[2:], a.dtype) for a in more]
    return pl.pallas_call(
        functools.partial(load_body, step),
        out_shape=outs,
        in_specs=[HBM] * (2 + len(more)),
        out_specs=[VMEM] * len(outs),
        scratch_shapes=[pltpu.SemaphoreType.DMA((len(outs),))],
        compiler_params=PARAMS,
    )(*own, *more)


def meanwhile_body(step, mirrored, expand_own, expand_other, inputs, cotangent, leave, *refs):
    outs, sems = refs[:-1], refs[-1]
    stage, core, way = where_am_i(step)
    ending, back_active = outs[:2]
    sources = [cotangent.at[way, core]]
    if mirrored:
        sources += [cotangent.at[1, core], inputs.at[1, core]]
    copies = bring_all(sources, [outs[0]] + list(outs[2:]), sems)
    copies[0].wait()

    @pl.when(way == core)
    def _():
        back_active[...] = jnp.dot(
            ending[...], expand_other[...], preferred_element_type=jnp.float32
        )

    @pl.when(way != core)
    def _():
        back_active[...] = jnp.dot(ending[...], expand_own[...], preferred_element_type=jnp.float32)

    for copy in copies[1:]:
        copy.wait()
    if mirrored:
        rows = outs[3]

        @pl.when(stage != 0)
        def _():
            rows[...] = leave[...]

        widened = rows[...].astype(jnp.float32)
        rows[...] = jax.nn.silu(widened * norm_of(widened)).astype(jnp.bfloat16)


def weight_copies(own, other, held, sems, core, way):
    copies = []
    for order in range(2):
        is_own = lax.rem(way + order, 2) == core
        for kind in range(2):
            mine = pltpu.make_async_copy(own[kind].at[way], held[kind].at[order], sems.at[kind, order])
            theirs = pltpu.make_async_copy(
                other[kind].at[way], held[kind].at[order], sems.at[kind, order]
            )
            copies.append((is_own, mine, theirs))
    return copies


def start_all(copies):
    for is_own, mine, theirs in copies:
        pl.when(is_own)(mine.start)
        pl.when(jnp.logical_not(is_own))(theirs.start)


def head_body(own, other, rows_in, lifted_out, inner_out, active_out):
    _, core, way = where_am_i(0)
    widened = rows_in[...].astype(jnp.float32)
    lifted = jax.nn.silu(widened * norm_of(widened)).astype(jnp.bfloat16)
    lifted_out[...] = lifted

    def run(reduce_mat):
        inner_sum = jnp.dot(lifted, reduce_mat[...], preferred_element_type=jnp.float32)
        inner_out[...] = inner_sum
        active_out[...] = jax.nn.silu(inner_sum).astype(jnp.bfloat16)

    pl.when(way == core)(lambda: run(own))
    pl.when(way != core)(lambda: run(other))


def stage_body(step, forward, backward, last, near, *refs):
    refs = list(refs)
    _, core, way = where_am_i(step)
    own, other = (refs.pop(0), refs.pop(0)), (refs.pop(0), refs.pop(0))
    enter = refs.pop(0) if forward else None
    head = [refs.pop(0) for _ in range(3)] if forward and step == 0 else None
    upstream_in = refs.pop(0) if backward else None
    first_active = refs.pop(0) if forward and backward else None
    if not forward:
        trunks, inners = refs.pop(0), refs.pop(0)
    if forward:
        flows = refs.pop(0)
    if forward and not backward:
        leave = refs.pop(0)
    if backward:
        upstreams, back_inners = refs.pop(0), refs.pop(0)
    if backward and not last:
        back_leave = refs.pop(0)
    if forward:
        trunks, inners = refs.pop(0), refs.pop(0)
    channels = trunks.shape[2]

    def run(reduce_mats, expand_mats, wait):
        if forward:
            rows = enter[...]
            for order in range(2):
                slot = lax.rem(order + core, 2)
                widened = rows.astype(jnp.float32)
                trunks[order] = rows
                if head and order == 0:
                    lifted, inner_sum, active = [part[...] for part in head]
                else:
                    normed = widened * norm_of(widened)
                    lifted = jax.nn.silu(normed).astype(jnp.bfloat16)
                    wait(0, order)
                    inner_sum = jnp.dot(
                        lifted, reduce_mats[order][...], preferred_element_type=jnp.float32
                    )
                    active = jax.nn.silu(inner_sum).astype(jnp.bfloat16)
                flows[slot, :, :channels] = lifted
                inners[order] = inner_sum
                flows[slot, :, channels:] = active
                wait(1, order)
                rows = (widened + contract(active, expand_mats[order][...], 1, 1)).astype(jnp.bfloat16)
            if not backward:
                leave[...] = rows
        if backward:
            upstream = upstream_in[...]
            for order in (1, 0):
                slot = lax.rem(order + core, 2)
                upstreams[slot] = upstream
                if last and order == 0:
                    break
                if not forward:
                    wait(1, order)
                if forward and order:
                    back_active = first_active[...]
                else:
                    back_active = jnp.dot(
                        upstream, expand_mats[order][...], preferred_element_type=jnp.float32
                    )
                back_inner = (back_active * smooth_slope(inners[order])).astype(jnp.bfloat16)
                back_inners[slot] = back_inner
                if not forward:
                    wait(0, order)
                back_lifted = contract(back_inner, reduce_mats[order][...], 1, 1)
                widened = trunks[order].astype(jnp.float32)
                norm_scale = norm_of(widened)
                back_normed = back_lifted * smooth_slope(widened * norm_scale)
                projection = jnp.mean(back_normed * widened, axis=-1, keepdims=True)
                upstream = (
                    upstream.astype(jnp.float32)
                    + norm_scale * back_normed
                    - widened * norm_scale**3 * projection
                ).astype(jnp.bfloat16)
            if not last:
                back_leave[...] = upstream

    if near:
        idle = lambda kind, order: None

        @pl.when(way == core)
        def _():
            run((own[0], other[0]), (own[1], other[1]), idle)

        @pl.when(way != core)
        def _():
            run((other[0], own[0]), (other[1], own[1]), idle)

    else:
        held = (refs.pop(0), refs.pop(0))
        copies = weight_copies(own, other, held, refs.pop(0), core, way)
        start_all(copies if forward else copies[2:] + copies[:2])
        run(
            [held[0].at[order] for order in range(2)],
            [held[1].at[order] for order in range(2)],
            lambda kind, order: copies[2 * order + kind][1].wait(),
        )


def tail_body(own, other, upstreams, back_first, inners, back_inners):
    _, core, way = where_am_i(0)

    def run(expand_mat):
        back_active = jnp.dot(upstreams[core], expand_mat[...], preferred_element_type=jnp.float32)
        back_inners[core] = (back_active * smooth_slope(inners[0])).astype(jnp.bfloat16)
        back_inners[1 - core] = back_first[1 - core]

    pl.when(way == core)(lambda: run(own))
    pl.when(way != core)(lambda: run(other))


def run_stage(weights, step, forward, backward, near, rows, sizes, *arrays):
    channels, inner = sizes
    last = backward and step == 0 and not forward
    shape = lambda dtype, *dims: jax.ShapeDtypeStruct(dims, dtype)
    line = shape(jnp.bfloat16, rows, channels)
    kept = [((2, rows, channels), jnp.bfloat16), ((2, rows, inner), jnp.float32)]
    outs, scratch = [], []
    if forward:
        outs.append(shape(jnp.bfloat16, 2, rows, channels + inner))
    if forward and not backward:
        outs.append(line)
    if backward:
        outs.append(shape(jnp.bfloat16, 2, rows, channels))
        outs.append(shape(jnp.bfloat16, 2, rows, inner))
    if backward and not last:
        outs.append(line)
    if forward and not backward:
        outs += [jax.ShapeDtypeStruct(*one) for one in kept]
    if forward and backward:
        scratch += [pltpu.VMEM(*one) for one in kept]
    if not near:
        scratch += [pltpu.VMEM((2, channels, inner), jnp.bfloat16)] * 2
        scratch += [pltpu.SemaphoreType.DMA((2, 2))]
    passes = 4 * (int(forward) + int(backward))
    return pl.pallas_call(
        functools.partial(stage_body, step, forward, backward, last, near),
        out_shape=outs,
        in_specs=[VMEM if near else ANY] * 4 + [VMEM] * len(arrays),
        out_specs=[VMEM] * len(outs),
        scratch_shapes=scratch,
        compiler_params=PARAMS,
        cost_estimate=pl.CostEstimate(
            flops=2 * passes * rows * channels * inner,
            bytes_accessed=8 * channels * inner,
            transcendentals=passes * rows * channels,
        ),
    )(*weights, *arrays)


def parity(value, mask):
    total, bit = 0, 0
    while mask >> bit:
        if mask >> bit & 1:
            total = total + lax.rem(lax.div(value, 1 << bit), 2)
        bit += 1
    return lax.rem(total, 2)


def halving_plan(size, turn):
    order = [1 << bit for bit in range(size.bit_length() - 1)]
    if turn and len(order) > 1:
        order[:2] = order[1::-1]
    table = [0] * size
    for chunk in range(size):
        place = 0
        for mask in order:
            place = 2 * place + int(chunk & mask != 0)
        table[place] = chunk
    return order, order, table


def side_of(plans, at):
    core, shard = lax.rem(lax.axis_index("pipe"), 2), lax.axis_index("dp")
    return jnp.where(core == 0, parity(shard, plans[0][1][at]), parity(shard, plans[1][1][at]))


def gradient_body(plans, pick_left, pick_right, count, *refs):
    arrays, (send, keep, left, right, full) = refs[:count], refs[count:]
    stage, core, _ = where_am_i(0)
    rows = left.shape[0] // 4
    chunk = send.shape[1]
    for target, pick in ((left, pick_left), (right, pick_right)):
        near, away = pick(arrays)
        for step, part in enumerate(near):

            @pl.when(stage == step)
            def _():
                target[:rows] = part[...]

        for at, part in enumerate(away):
            target[(at + 1) * rows : (at + 2) * rows] = part[...]
    full[...] = contract(left[...], right[...], 0, 0)
    side = side_of(plans, 0)
    half = send.shape[0]
    flip = [plan[2][half] for plan in plans]
    for at in range(half):
        spots = []
        for target_side in (1 - side, side):
            first = plans[0][2][at] ^ (flip[0] * target_side)
            second = plans[1][2][at] ^ (flip[1] * target_side)
            spots.append(pl.multiple_of(jnp.where(core == 0, first, second) * chunk, chunk))
        send[at] = full[pl.ds(spots[0], chunk)].astype(jnp.bfloat16)
        keep[at] = full[pl.ds(spots[1], chunk)]


def halve_body(plans, at, keep_in, came, send, keep):
    half = keep.shape[0]
    side = side_of(plans, at)
    for spot in range(half):
        mine, theirs = side * half + spot, (1 - side) * half + spot
        send[spot] = (keep_in[theirs] + came[theirs].astype(jnp.float32)).astype(jnp.bfloat16)
        keep[spot] = keep_in[mine] + came[mine].astype(jnp.float32)


def bit_of(value, bit):
    return lax.rem(lax.div(value, 1 << bit), 2)


def first_sides():
    core, shard = lax.rem(lax.axis_index("pipe"), 2), lax.axis_index("dp")
    low, high = bit_of(shard, 0), bit_of(shard, 1)
    return core, jnp.where(core == 0, low, high), jnp.where(core == 0, high, low)


def split_columns(wide, keep, send, chunk):
    core, side, _ = first_sides()
    for place in range(wide.shape[1] // (2 * chunk)):
        for target, at in ((keep, side), (send, 1 - side)):
            block = jnp.where(core == 0, 2 * place + at, place // 2 * 4 + 2 * at + place % 2)
            source = pl.ds(pl.multiple_of(block * chunk, chunk), chunk)
            target[:, place * chunk : (place + 1) * chunk] = wide[:, source]


def take_rows(target, span, *arrays):
    stage, _, _ = where_am_i(0)
    *own, other = arrays
    rows = target.shape[0] // 2
    for step, part in enumerate(own):
        part = part if len(part.shape) == 2 else part.at[0]

        @pl.when((stage == step) | (len(own) == 1))
        def _():
            target[:rows] = part[:, span]

    target[rows:] = other[:, span]


def early_body(stages, chunk, *refs):
    count = stages + 1
    flows, far, ups = refs[:count], refs[count : count + 2], refs[count + 2 : 2 * count + 2]
    up, active, lifted, far_active, far_lifted, send, wide = refs[2 * count + 2 :]
    half, channels = up.shape[1], wide.shape[1]
    inner = active.shape[1]
    take_rows(wide, slice(None), *ups)
    split_columns(wide, up, send.at[:, :half], chunk)
    start = half
    for sources, narrow, broad in ((flows, active, lifted), (far, far_active, far_lifted)):
        take_rows(narrow, slice(channels, None), *sources)
        send[:, start : start + inner] = narrow[...]
        start += inner
        take_rows(wide, slice(0, channels), *sources)
        split_columns(wide, broad, send.at[:, start : start + half], chunk)
        start += half


def late_up_body(chunk, far, cross, up, send, wide):
    take_rows(wide, slice(None), far, cross)
    split_columns(wide, up, send, chunk)


def late_inner_body(*refs):
    *backs, far, cross, far_inner, near_inner, send, _ = refs
    inner = far_inner.shape[1]
    take_rows(far_inner, slice(None), far, cross)
    send[:, :inner] = far_inner[...]
    take_rows(near_inner, slice(None), *backs)
    send[:, inner:] = near_inner[...]


def half_gradient_body(starts, *refs):
    lefts, rights, cames = refs[:2], refs[2:4], refs[4:6]
    send, keep, full, left, right = refs[6:]
    rows, columns = lefts[0].shape
    inner = rights[0].shape[1]
    for group, ((left_in, left_start), (right_in, right_start)) in enumerate(starts):
        place = slice(2 * group * rows, (2 * group + 1) * rows)
        left[place] = lefts[group][...]
        right[place] = rights[group][...]
        place = slice((2 * group + 1) * rows, (2 * group + 2) * rows)
        left[place] = cames[left_in][:, left_start : left_start + columns]
        right[place] = cames[right_in][:, right_start : right_start + inner]
    full[...] = contract(left[...], right[...], 0, 0)
    _, _, side = first_sides()
    chunk = send.shape[1]
    for place in range(send.shape[0]):
        theirs = pl.ds(pl.multiple_of((2 * place + 1 - side) * chunk, chunk), chunk)
        mine = pl.ds(pl.multiple_of((2 * place + side) * chunk, chunk), chunk)
        send[place] = full[theirs].astype(jnp.bfloat16)
        keep[place] = full[mine]


def next_body(bit, keep_in, came, send, keep):
    side = bit_of(lax.axis_index("dp"), bit)
    for place in range(keep.shape[0]):
        theirs, mine = 2 * place + 1 - side, 2 * place + side
        send[place] = (keep_in[theirs] + came[theirs].astype(jnp.float32)).astype(jnp.bfloat16)
        keep[place] = keep_in[mine] + came[mine].astype(jnp.float32)


def finish_body(keep_reduce, came_reduce, keep_expand, came_expand, out):
    out[0, 0] = keep_reduce[0] + came_reduce[0].astype(jnp.float32)
    out[0, 1] = keep_expand[0] + came_expand[0].astype(jnp.float32)


def shards(inputs, cotangent, reduce_weight, expand_weight):
    stages = lax.axis_size("pipe") // 2
    replicas = lax.axis_size("dp")
    stage, core, _ = where_am_i(0)
    channels, inner = reduce_weight.shape[2:]
    rows = inputs.shape[1] * inputs.shape[2] // 2
    sizes = (channels, inner)
    entering = inputs.reshape(2, 2, rows, channels)
    ending = cotangent.reshape(2, 2, rows, channels)
    own = [reduce_weight[:, 0], expand_weight[:, 0]]

    core_pairs = [(p, p ^ 1) for p in range(2 * stages)]
    mirror_pairs = [(p, 2 * (stages - 1 - p // 2) + p % 2) for p in range(2 * stages)]

    def hop(shard, step):
        pairs = []
        for c in range(2):
            pairs.append((2 * step + c, 2 * step + 2 + c))
            pairs.append((2 * (stages - 1 - step) + c, 2 * (stages - 2 - step) + c))
        return lax.ppermute(shard, "pipe", pairs)

    def swap_cores(shard):
        return lax.ppermute(shard, "pipe", core_pairs)

    def mirror(shard):
        return lax.ppermute(shard, "pipe", mirror_pairs)

    at_stage = [stage == step for step in range(stages)]
    first_core = core == 0
    at_stage, first_core, entering = lax.optimization_barrier((at_stage, first_core, entering))

    def pick(parts, mirrored_stage=False):
        tests = at_stage[::-1] if mirrored_stage else at_stage
        chosen = parts[0]
        for test, part in zip(tests[1:], parts[1:]):
            chosen = jnp.where(test, part, chosen)
        return chosen

    in_hbm = lambda array: pltpu.with_memory_space_constraint(array, pltpu.HBM)
    own, entering, ending = [in_hbm(one) for one in own], in_hbm(entering), in_hbm(ending)
    *near, enter = load(0, own, entering)
    near.append(swap_cores(near[0]))
    near.append(swap_cores(near[1]))
    turn = list(load(stages - 1, own))
    turn += [swap_cores(weight) for weight in turn]
    if stages > 2:
        weights = own + [swap_cores(weight) for weight in own]
    flows, trunks, inners = [], [], []
    head = pl.pallas_call(
        head_body,
        out_shape=[
            jax.ShapeDtypeStruct((rows, channels), jnp.bfloat16),
            jax.ShapeDtypeStruct((rows, inner), jnp.float32),
            jax.ShapeDtypeStruct((rows, inner), jnp.bfloat16),
        ],
        in_specs=[VMEM] * 3,
        out_specs=[VMEM] * 3,
        compiler_params=PARAMS,
    )(near[0], near[2], enter)
    for step in range(stages - 1):
        arrays = [enter] if step else [enter, *head]
        flow, leave, trunk, inner_sum = run_stage(
            weights if step else near, step, True, False, step == 0, rows, sizes, *arrays
        )
        flows.append(flow)
        trunks.append(trunk)
        inners.append(inner_sum)
        enter = hop(leave, step)
    mirrored = stages == 2
    line = jax.ShapeDtypeStruct((rows, channels), jnp.bfloat16)
    outs = [line, jax.ShapeDtypeStruct((rows, inner), jnp.float32)] + [line, line] * mirrored
    ending, first_active, *known = pl.pallas_call(
        functools.partial(meanwhile_body, stages - 1, mirrored),
        out_shape=outs,
        in_specs=[VMEM, VMEM, HBM, HBM, VMEM],
        out_specs=[VMEM] * len(outs),
        scratch_shapes=[pltpu.SemaphoreType.DMA((3,))],
        compiler_params=PARAMS,
    )(turn[1], turn[3], entering, ending, leave)
    flow, upstreams, back_inners, leave = run_stage(
        turn, stages - 1, True, True, True, rows, sizes, enter, ending, first_active
    )
    flows.append(flow)
    upstreams, back_inners = [upstreams], [back_inners]
    upstream = hop(leave, 0)
    side_flow = swap_cores(pick(flows)[1])
    near_core = lambda first, second: jnp.where(first_core, first, second)
    going = pick(flows, True)
    if mirrored:
        lifted = near_core(going[1, :, :channels], going[0, :, :channels])
        going = jnp.concatenate([lifted, going[0, :, channels:], going[1, :, channels:]], axis=1)
    far_flow = mirror(going)
    if mirrored:
        lifted, actives = far_flow[:, :channels], far_flow[:, channels:]
        far_flow = jnp.concatenate([near_core(known[1], lifted), actives[:, :inner]], axis=1)
        cross_flow = jnp.concatenate([near_core(lifted, known[1]), actives[:, inner:]], axis=1)
    else:
        far_flow, cross_flow = far_flow[0], far_flow[1]
    cross_flow = swap_cores(cross_flow)
    for step in range(stages - 2, -1, -1):
        outs = run_stage(
            weights if step else near,
            step,
            False,
            True,
            step == 0,
            rows,
            sizes,
            upstream,
            trunks[step],
            inners[step],
        )
        upstreams.insert(0, outs[0])
        if step:
            upstream = hop(outs[2], stages - 1 - step)
            back_inners.insert(0, outs[1])
            continue
        tail = pl.pallas_call(
            tail_body,
            out_shape=jax.ShapeDtypeStruct(outs[1].shape, outs[1].dtype),
            in_specs=[VMEM] * 5,
            out_specs=VMEM,
            compiler_params=PARAMS,
        )(near[1], near[3], outs[0], outs[1], inners[0])
        back_inners.insert(0, tail)
    going = pick(upstreams, True)
    far_up = mirror(near_core(going[0], going[1]) if mirrored else going)
    far_inner = mirror(pick(back_inners, True))
    side_up = swap_cores(pick(upstreams)[1])
    side_inner = swap_cores(pick(back_inners)[1])
    if mirrored:
        top = jnp.where(at_stage[0], leave, known[0])
        far_up, cross_up = near_core(far_up, top), near_core(top, far_up)
    else:
        far_up, cross_up = far_up[0], far_up[1]
    cross_up = swap_cores(cross_up)
    far_inner, cross_inner = far_inner[0], far_inner[1]
    cross_inner = swap_cores(cross_inner)

    chunk = channels // replicas
    fore = flows + [side_flow, far_flow, cross_flow]
    ups = upstreams + [side_up, far_up, cross_up]
    backs = back_inners + [side_inner, far_inner, cross_inner]
    halve = halve_rows if chunk % 128 == 0 and replicas >= 4 else halve_sums
    parts = halve(stages, replicas, chunk, sizes, rows, fore, ups, backs)
    return pl.pallas_call(
        finish_body,
        out_shape=jax.ShapeDtypeStruct((1, 2, chunk, inner), jnp.float32),
        in_specs=[VMEM] * 4,
        out_specs=VMEM,
        compiler_params=PARAMS,
    )(*parts)


def sums(count, chunk, inner):
    return [
        jax.ShapeDtypeStruct((count, chunk, inner), jnp.bfloat16),
        jax.ShapeDtypeStruct((count, chunk, inner), jnp.float32),
    ]


def exchange(shard, stages, replicas, first, second):
    pairs = []
    for p in range(2 * stages):
        for q in range(replicas):
            pairs.append((p * replicas + q, p * replicas + (q ^ (second if p % 2 else first))))
    return lax.ppermute(shard, AXES, pairs)


def halve_rows(stages, replicas, chunk, sizes, rows, fore, ups, backs):
    channels, inner = sizes
    half = channels // 2
    count = stages + 1

    def pack(body, arrays, *widths):
        return pl.pallas_call(
            body,
            out_shape=[jax.ShapeDtypeStruct((2 * rows, width), jnp.bfloat16) for width in widths],
            in_specs=[VMEM] * len(arrays),
            out_specs=[VMEM] * len(widths),
            scratch_shapes=[pltpu.VMEM((2 * rows, channels), jnp.bfloat16)],
            compiler_params=PARAMS,
        )(*arrays)

    near_up, near_active, near_lifted, far_active, far_lifted, send = pack(
        functools.partial(early_body, stages, chunk),
        fore + ups[:count],
        half,
        inner,
        half,
        inner,
        half,
        3 * half + 2 * inner,
    )
    came_near = exchange(send, stages, replicas, 1, 2)
    far_up, send = pack(functools.partial(late_up_body, chunk), ups[count:], half, half)
    came_up = exchange(send, stages, replicas, 1, 2)
    far_inner, near_inner, send = pack(late_inner_body, backs, inner, inner, 2 * inner)
    came_inner = exchange(send, stages, replicas, 1, 2)
    step = half + inner
    streams = (
        (
            (near_lifted, far_lifted, near_inner, far_inner, came_near, came_inner),
            (((0, step), (1, inner)), ((0, 2 * step), (1, 0))),
        ),
        (
            (near_up, far_up, near_active, far_active, came_near, came_up),
            (((0, 0), (0, half)), ((1, 0), (0, half + step))),
        ),
    )
    parts = []
    for operands, starts in streams:
        count = replicas // 4
        send, keep = pl.pallas_call(
            functools.partial(half_gradient_body, starts),
            out_shape=sums(count, chunk, inner),
            in_specs=[VMEM] * len(operands),
            out_specs=[VMEM] * 2,
            scratch_shapes=[
                pltpu.VMEM((channels // 2, inner), jnp.float32),
                pltpu.VMEM((8 * rows, channels // 2), jnp.bfloat16),
                pltpu.VMEM((8 * rows, inner), jnp.bfloat16),
            ],
            compiler_params=PARAMS,
        )(*operands)
        came = exchange(send, stages, replicas, 2, 1)
        for bit in range(2, replicas.bit_length() - 1):
            count //= 2
            send, keep = pl.pallas_call(
                functools.partial(next_body, bit),
                out_shape=sums(count, chunk, inner),
                in_specs=[VMEM] * 2,
                out_specs=[VMEM] * 2,
                compiler_params=PARAMS,
            )(keep, came)
            came = exchange(send, stages, replicas, 1 << bit, 1 << bit)
        parts += [keep, came]
    return parts


def halve_sums(stages, replicas, chunk, sizes, rows, fore, ups, backs):
    channels, inner = sizes
    wide, narrow = slice(0, channels), slice(channels, channels + inner)

    def of_flows(columns):
        def pick_parts(arrays):
            near = [flow.at[0, :, columns] for flow in arrays[:stages]]
            side, far, cross = arrays[stages : stages + 3]
            return near, [side.at[:, columns], far.at[:, columns], cross.at[:, columns]]

        return pick_parts

    def of_backs(arrays):
        near = [back.at[0] for back in arrays[stages + 3 : 2 * stages + 3]]
        side, far, cross = arrays[2 * stages + 3 : 2 * stages + 6]
        return near, [side, far, cross]

    plans = [halving_plan(replicas, turn) for turn in range(2)]
    streams = []
    for pick_left, pick_right, late, plan in (
        (of_backs, of_flows(narrow), ups, plans),
        (of_flows(wide), of_backs, backs, plans[::-1]),
    ):
        arrays = fore + late
        send, keep = pl.pallas_call(
            functools.partial(gradient_body, plan, pick_left, pick_right, len(arrays)),
            out_shape=sums(replicas // 2, chunk, inner),
            in_specs=[VMEM] * len(arrays),
            out_specs=[VMEM] * 2,
            scratch_shapes=[
                pltpu.VMEM((4 * rows, channels), jnp.bfloat16),
                pltpu.VMEM((4 * rows, inner), jnp.bfloat16),
                pltpu.VMEM((channels, inner), jnp.float32),
            ],
            compiler_params=PARAMS,
        )(*arrays)
        streams.append((plan, send, keep))
    for at in range(replicas.bit_length() - 1):
        half = replicas >> (at + 2)
        arrived = []
        for plan, send, keep in streams:
            pairs = []
            for p in range(2 * stages):
                for q in range(replicas):
                    pairs.append((p * replicas + q, p * replicas + (q ^ plan[p % 2][0][at])))
            arrived.append((plan, keep, lax.ppermute(send, AXES, pairs)))
        if half == 0:
            break
        streams = []
        for plan, keep, came in arrived:
            send, keep = pl.pallas_call(
                functools.partial(halve_body, plan, at + 1),
                out_shape=sums(half, chunk, inner),
                in_specs=[VMEM] * 2,
                out_specs=[VMEM] * 2,
                compiler_params=PARAMS,
            )(keep, came)
            streams.append((plan, send, keep))
    (_, keep_expand, came_expand), (_, keep_reduce, came_reduce) = arrived
    return keep_reduce, came_reduce, keep_expand, came_expand


def solution(mesh):
    return jax.shard_map(
        shards,
        mesh=mesh,
        in_specs=(
            P(None, None, "dp", None),
            P(None, None, "dp", None),
            P(None, "pipe", None, None),
            P(None, "pipe", None, None),
        ),
        out_specs=P("pipe", None, "dp", None),
        check_vma=False,
    )
```

```python
import functools

import jax
import jax.numpy as jnp
from jax import lax
from jax.experimental import pallas as pl
from jax.experimental.pallas import tpu as pltpu
from jax.sharding import PartitionSpec as P


EPSILON = 1e-06
AXES = ("pipe", "dp")
HBM = pl.BlockSpec(memory_space=pltpu.HBM)
ANY = pl.BlockSpec(memory_space=pl.ANY)
VMEM = pl.BlockSpec(memory_space=pltpu.VMEM)
PARAMS = pltpu.CompilerParams(vmem_limit_bytes=16 << 20)


def contract(first_op, second_op, first_dim, second_dim):
    return lax.dot_general(
        first_op,
        second_op,
        (((first_dim,), (second_dim,)), ((), ())),
        preferred_element_type=jnp.float32,
    )


def smooth_slope(values):
    sigma = jax.nn.sigmoid(values)
    return sigma * (1.0 + values * (1.0 - sigma))


def norm_of(widened):
    return lax.rsqrt(jnp.mean(widened * widened, axis=-1, keepdims=True) + EPSILON)


def where_am_i(step):
    position = lax.axis_index("pipe")
    stage, core = lax.div(position, 2), lax.rem(position, 2)
    way = jnp.where(stage == step, 0, 1)
    return stage, core, way


def bring_all(sources, outs, sems):
    copies = [
        pltpu.make_async_copy(source, out, sems.at[at])
        for at, (source, out) in enumerate(zip(sources, outs))
    ]
    for copy in copies:
        copy.start()
    return copies


def load_body(step, reduce_all, expand_all, *refs):
    _, core, way = where_am_i(step)
    sources, outs = [reduce_all.at[way], expand_all.at[way]], refs[:-1]
    if step == 0:
        sources.append(refs[0].at[way, core])
        outs = outs[1:]
    for copy in bring_all(sources, outs, refs[-1]):
        copy.wait()


def load(step, own, *more):
    channels, inner = own[0].shape[1:]
    mat = jax.ShapeDtypeStruct((channels, inner), jnp.bfloat16)
    outs = [mat, mat] + [jax.ShapeDtypeStruct(a.shape[2:], a.dtype) for a in more]
    return pl.pallas_call(
        functools.partial(load_body, step),
        out_shape=outs,
        in_specs=[HBM] * (2 + len(more)),
        out_specs=[VMEM] * len(outs),
        scratch_shapes=[pltpu.SemaphoreType.DMA((len(outs),))],
        compiler_params=PARAMS,
    )(*own, *more)


def meanwhile_body(step, mirrored, expand_own, expand_other, inputs, cotangent, leave, *refs):
    outs, sems = refs[:-1], refs[-1]
    stage, core, way = where_am_i(step)
    ending, back_active = outs[:2]
    sources = [cotangent.at[way, core]]
    if mirrored:
        sources += [cotangent.at[1, core], inputs.at[1, core]]
    copies = bring_all(sources, [outs[0]] + list(outs[2:]), sems)
    copies[0].wait()

    @pl.when(way == core)
    def _():
        back_active[...] = jnp.dot(
            ending[...], expand_other[...], preferred_element_type=jnp.float32
        )

    @pl.when(way != core)
    def _():
        back_active[...] = jnp.dot(ending[...], expand_own[...], preferred_element_type=jnp.float32)

    for copy in copies[1:]:
        copy.wait()
    if mirrored:
        rows = outs[3]

        @pl.when(stage != 0)
        def _():
            rows[...] = leave[...]

        widened = rows[...].astype(jnp.float32)
        rows[...] = jax.nn.silu(widened * norm_of(widened)).astype(jnp.bfloat16)


def weight_copies(own, other, held, sems, core, way):
    copies = []
    for order in range(2):
        is_own = lax.rem(way + order, 2) == core
        for kind in range(2):
            mine = pltpu.make_async_copy(own[kind].at[way], held[kind].at[order], sems.at[kind, order])
            theirs = pltpu.make_async_copy(
                other[kind].at[way], held[kind].at[order], sems.at[kind, order]
            )
            copies.append((is_own, mine, theirs))
    return copies


def start_all(copies):
    for is_own, mine, theirs in copies:
        pl.when(is_own)(mine.start)
        pl.when(jnp.logical_not(is_own))(theirs.start)


def head_body(own, other, rows_in, lifted_out, inner_out, active_out):
    _, core, way = where_am_i(0)
    widened = rows_in[...].astype(jnp.float32)
    lifted = jax.nn.silu(widened * norm_of(widened)).astype(jnp.bfloat16)
    lifted_out[...] = lifted

    def run(reduce_mat):
        inner_sum = jnp.dot(lifted, reduce_mat[...], preferred_element_type=jnp.float32)
        inner_out[...] = inner_sum
        active_out[...] = jax.nn.silu(inner_sum).astype(jnp.bfloat16)

    pl.when(way == core)(lambda: run(own))
    pl.when(way != core)(lambda: run(other))


def stage_body(step, forward, backward, last, near, *refs):
    refs = list(refs)
    _, core, way = where_am_i(step)
    own, other = (refs.pop(0), refs.pop(0)), (refs.pop(0), refs.pop(0))
    enter = refs.pop(0) if forward else None
    head = [refs.pop(0) for _ in range(3)] if forward and step == 0 else None
    upstream_in = refs.pop(0) if backward else None
    first_active = refs.pop(0) if forward and backward else None
    if not forward:
        trunks, inners = refs.pop(0), refs.pop(0)
    if forward:
        flows = refs.pop(0)
    if forward and not backward:
        leave = refs.pop(0)
    if backward:
        upstreams, back_inners = refs.pop(0), refs.pop(0)
    if backward and not last:
        back_leave = refs.pop(0)
    if forward:
        trunks, inners = refs.pop(0), refs.pop(0)
    channels = trunks.shape[2]

    def run(reduce_mats, expand_mats, wait):
        if forward:
            rows = enter[...]
            for order in range(2):
                slot = lax.rem(order + core, 2)
                widened = rows.astype(jnp.float32)
                trunks[order] = rows
                if head and order == 0:
                    lifted, inner_sum, active = [part[...] for part in head]
                else:
                    normed = widened * norm_of(widened)
                    lifted = jax.nn.silu(normed).astype(jnp.bfloat16)
                    wait(0, order)
                    inner_sum = jnp.dot(
                        lifted, reduce_mats[order][...], preferred_element_type=jnp.float32
                    )
                    active = jax.nn.silu(inner_sum).astype(jnp.bfloat16)
                flows[slot, :, :channels] = lifted
                inners[order] = inner_sum
                flows[slot, :, channels:] = active
                wait(1, order)
                rows = (widened + contract(active, expand_mats[order][...], 1, 1)).astype(jnp.bfloat16)
            if not backward:
                leave[...] = rows
        if backward:
            upstream = upstream_in[...]
            for order in (1, 0):
                slot = lax.rem(order + core, 2)
                upstreams[slot] = upstream
                if last and order == 0:
                    break
                if not forward:
                    wait(1, order)
                if forward and order:
                    back_active = first_active[...]
                else:
                    back_active = jnp.dot(
                        upstream, expand_mats[order][...], preferred_element_type=jnp.float32
                    )
                back_inner = (back_active * smooth_slope(inners[order])).astype(jnp.bfloat16)
                back_inners[slot] = back_inner
                if not forward:
                    wait(0, order)
                back_lifted = contract(back_inner, reduce_mats[order][...], 1, 1)
                widened = trunks[order].astype(jnp.float32)
                norm_scale = norm_of(widened)
                back_normed = back_lifted * smooth_slope(widened * norm_scale)
                projection = jnp.mean(back_normed * widened, axis=-1, keepdims=True)
                upstream = (
                    upstream.astype(jnp.float32)
                    + norm_scale * back_normed
                    - widened * norm_scale**3 * projection
                ).astype(jnp.bfloat16)
            if not last:
                back_leave[...] = upstream

    if near:
        idle = lambda kind, order: None

        @pl.when(way == core)
        def _():
            run((own[0], other[0]), (own[1], other[1]), idle)

        @pl.when(way != core)
        def _():
            run((other[0], own[0]), (other[1], own[1]), idle)

    else:
        held = (refs.pop(0), refs.pop(0))
        copies = weight_copies(own, other, held, refs.pop(0), core, way)
        start_all(copies if forward else copies[2:] + copies[:2])


def tail_body(own, other, upstreams, back_first, inners, back_inners):
    _, core, way = where_am_i(0)

    def run(expand_mat):
        back_active = jnp.dot(upstreams[core], expand_mat[...], preferred_element_type=jnp.float32)
        back_inners[core] = (back_active * smooth_slope(inners[0])).astype(jnp.bfloat16)
        back_inners[1 - core] = back_first[1 - core]

    pl.when(way == core)(lambda: run(own))
    pl.when(way != core)(lambda: run(other))


def run_stage(weights, step, forward, backward, near, rows, sizes, *arrays):
    channels, inner = sizes
    last = backward and step == 0 and not forward
    shape = lambda dtype, *dims: jax.ShapeDtypeStruct(dims, dtype)
    line = shape(jnp.bfloat16, rows, channels)
    kept = [((2, rows, channels), jnp.bfloat16), ((2, rows, inner), jnp.float32)]
    outs, scratch = [], []
    if forward:
        outs.append(shape(jnp.bfloat16, 2, rows, channels + inner))
    if forward and not backward:
        outs.append(line)
    if backward:
        outs.append(shape(jnp.bfloat16, 2, rows, channels))
        outs.append(shape(jnp.bfloat16, 2, rows, inner))
    if backward and not last:
        outs.append(line)
    if forward and not backward:
        outs += [jax.ShapeDtypeStruct(*one) for one in kept]
    if forward and backward:
        scratch += [pltpu.VMEM(*one) for one in kept]
    if not near:
        scratch += [pltpu.VMEM((2, channels, inner), jnp.bfloat16)] * 2
        scratch += [pltpu.SemaphoreType.DMA((2, 2))]
    passes = 4 * (int(forward) + int(backward))
    return pl.pallas_call(
        functools.partial(stage_body, step, forward, backward, last, near),
        out_shape=outs,
        in_specs=[VMEM if near else ANY] * 4 + [VMEM] * len(arrays),
        out_specs=[VMEM] * len(outs),
        scratch_shapes=scratch,
        compiler_params=PARAMS,
        cost_estimate=pl.CostEstimate(
            flops=2 * passes * rows * channels * inner,
            bytes_accessed=8 * channels * inner,
            transcendentals=passes * rows * channels,
        ),
    )(*weights, *arrays)


def parity(value, mask):
    total, bit = 0, 0
    while mask >> bit:
        if mask >> bit & 1:
            total = total + lax.rem(lax.div(value, 1 << bit), 2)
        bit += 1
    return lax.rem(total, 2)


def halving_plan(size, turn):
    order = [1 << bit for bit in range(size.bit_length() - 1)]
    if turn and len(order) > 1:
        order[:2] = order[1::-1]
    table = [0] * size
    for chunk in range(size):
        place = 0
        for mask in order:
            place = 2 * place + int(chunk & mask != 0)
        table[place] = chunk
    return order, order, table


def side_of(plans, at):
    core, shard = lax.rem(lax.axis_index("pipe"), 2), lax.axis_index("dp")
    return jnp.where(core == 0, parity(shard, plans[0][1][at]), parity(shard, plans[1][1][at]))


def gradient_body(plans, pick_left, pick_right, count, *refs):
    arrays, (send, keep, left, right, full) = refs[:count], refs[count:]
    stage, core, _ = where_am_i(0)
    rows = left.shape[0] // 4
    chunk = send.shape[1]
    for target, pick in ((left, pick_left), (right, pick_right)):
        near, away = pick(arrays)
        for step, part in enumerate(near):

            @pl.when(stage == step)
            def _():
                target[:rows] = part[...]

        for at, part in enumerate(away):
            target[(at + 1) * rows : (at + 2) * rows] = part[...]
    full[...] = contract(left[...], right[...], 0, 0)
    side = side_of(plans, 0)
    half = send.shape[0]
    flip = [plan[2][half] for plan in plans]
    for at in range(half):
        spots = []
        for target_side in (1 - side, side):
            first = plans[0][2][at] ^ (flip[0] * target_side)
            second = plans[1][2][at] ^ (flip[1] * target_side)
            spots.append(pl.multiple_of(jnp.where(core == 0, first, second) * chunk, chunk))
        send[at] = full[pl.ds(spots[0], chunk)].astype(jnp.bfloat16)
        keep[at] = full[pl.ds(spots[1], chunk)]


def halve_body(plans, at, keep_in, came, send, keep):
    half = keep.shape[0]
    side = side_of(plans, at)
    for spot in range(half):
        mine, theirs = side * half + spot, (1 - side) * half + spot
        send[spot] = (keep_in[theirs] + came[theirs].astype(jnp.float32)).astype(jnp.bfloat16)
        keep[spot] = keep_in[mine] + came[mine].astype(jnp.float32)


def bit_of(value, bit):
    return lax.rem(lax.div(value, 1 << bit), 2)


def first_sides():
    core, shard = lax.rem(lax.axis_index("pipe"), 2), lax.axis_index("dp")
    low, high = bit_of(shard, 0), bit_of(shard, 1)
    return core, jnp.where(core == 0, low, high), jnp.where(core == 0, high, low)


def split_columns(wide, keep, send, chunk):
    core, side, _ = first_sides()
    for place in range(wide.shape[1] // (2 * chunk)):
        for target, at in ((keep, side), (send, 1 - side)):
            block = jnp.where(core == 0, 2 * place + at, place // 2 * 4 + 2 * at + place % 2)
            source = pl.ds(pl.multiple_of(block * chunk, chunk), chunk)
            target[:, place * chunk : (place + 1) * chunk] = wide[:, source]


def take_rows(target, span, *arrays):
    stage, _, _ = where_am_i(0)
    *own, other = arrays
    rows = target.shape[0] // 2
    for step, part in enumerate(own):
        part = part if len(part.shape) == 2 else part.at[0]

        @pl.when((stage == step) | (len(own) == 1))
        def _():
            target[:rows] = part[:, span]

    target[rows:] = other[:, span]


def near_up_body(stages, chunk, *refs):
    flows, ups = refs[: stages + 1], refs[stages + 1 : 2 * stages + 2]
    up, active, lifted, send, wide = refs[2 * stages + 2 :]
    half, channels = up.shape[1], wide.shape[1]
    inner = active.shape[1]
    take_rows(wide, slice(None), *ups)
    split_columns(wide, up, send.at[:, :half], chunk)
    take_rows(active, slice(channels, None), *flows)
    send[:, half : half + inner] = active[...]
    take_rows(wide, slice(0, channels), *flows)
    split_columns(wide, lifted, send.at[:, half + inner :], chunk)


def late_up_body(chunk, flow, cross_flow, far, cross, up, active, send, wide):
    half, channels = up.shape[1], wide.shape[1]
    take_rows(wide, slice(None), far, cross)
    split_columns(wide, up, send.at[:, :half], chunk)
    take_rows(active, slice(channels, None), flow, cross_flow)
    send[:, half:] = active[...]


def late_inner_body(chunk, flow, cross_flow, *refs):
    *backs, far, cross, lifted, far_inner, near_inner, send, wide = refs
    half, channels = lifted.shape[1], wide.shape[1]
    inner = far_inner.shape[1]
    take_rows(wide, slice(0, channels), flow, cross_flow)
    split_columns(wide, lifted, send.at[:, :half], chunk)
    take_rows(far_inner, slice(None), far, cross)
    send[:, half : half + inner] = far_inner[...]
    take_rows(near_inner, slice(None), *backs)
    send[:, half + inner :] = near_inner[...]


def half_gradient_body(starts, *refs):
    lefts, rights, cames = refs[:2], refs[2:4], refs[4:6]
    send, keep, full, left, right = refs[6:]
    rows, columns = lefts[0].shape
    inner = rights[0].shape[1]
    for group, ((left_in, left_start), (right_in, right_start)) in enumerate(starts):
        place = slice(2 * group * rows, (2 * group + 1) * rows)
        left[place] = lefts[group][...]
        right[place] = rights[group][...]
        place = slice((2 * group + 1) * rows, (2 * group + 2) * rows)
        left[place] = cames[left_in][:, left_start : left_start + columns]
        right[place] = cames[right_in][:, right_start : right_start + inner]
    full[...] = contract(left[...], right[...], 0, 0)
    _, _, side = first_sides()
    chunk = send.shape[1]
    for place in range(send.shape[0]):
        theirs = pl.ds(pl.multiple_of((2 * place + 1 - side) * chunk, chunk), chunk)
        mine = pl.ds(pl.multiple_of((2 * place + side) * chunk, chunk), chunk)
        send[place] = full[theirs].astype(jnp.bfloat16)
        keep[place] = full[mine]


def next_body(bit, keep_in, came, send, keep):
    side = bit_of(lax.axis_index("dp"), bit)
    for place in range(keep.shape[0]):
        theirs, mine = 2 * place + 1 - side, 2 * place + side
        send[place] = (keep_in[theirs] + came[theirs].astype(jnp.float32)).astype(jnp.bfloat16)
        keep[place] = keep_in[mine] + came[mine].astype(jnp.float32)


def finish_body(keep_reduce, came_reduce, keep_expand, came_expand, out):
    out[0, 0] = keep_reduce[0] + came_reduce[0].astype(jnp.float32)
    out[0, 1] = keep_expand[0] + came_expand[0].astype(jnp.float32)


def shards(inputs, cotangent, reduce_weight, expand_weight):
    stages = lax.axis_size("pipe") // 2
    replicas = lax.axis_size("dp")
    stage, core, _ = where_am_i(0)
    channels, inner = reduce_weight.shape[2:]
    rows = inputs.shape[1] * inputs.shape[2] // 2
    sizes = (channels, inner)
    entering = inputs.reshape(2, 2, rows, channels)
    ending = cotangent.reshape(2, 2, rows, channels)
    own = [reduce_weight[:, 0], expand_weight[:, 0]]

    core_pairs = [(p, p ^ 1) for p in range(2 * stages)]
    mirror_pairs = [(p, 2 * (stages - 1 - p // 2) + p % 2) for p in range(2 * stages)]

    def hop(shard, step):
        pairs = []
        for c in range(2):
            pairs.append((2 * step + c, 2 * step + 2 + c))
            pairs.append((2 * (stages - 1 - step) + c, 2 * (stages - 2 - step) + c))
        return lax.ppermute(shard, "pipe", pairs)

    def swap_cores(shard):
        return lax.ppermute(shard, "pipe", core_pairs)

    def mirror(shard):
        return lax.ppermute(shard, "pipe", mirror_pairs)

    at_stage = [stage == step for step in range(stages)]
    first_core = core == 0
    at_stage, first_core, entering = lax.optimization_barrier((at_stage, first_core, entering))

    def pick(parts, mirrored_stage=False):
        tests = at_stage[::-1] if mirrored_stage else at_stage
        chosen = parts[0]
        for test, part in zip(tests[1:], parts[1:]):
            chosen = jnp.where(test, part, chosen)
        return chosen

    in_hbm = lambda array: pltpu.with_memory_space_constraint(array, pltpu.HBM)
    own, entering, ending = [in_hbm(one) for one in own], in_hbm(entering), in_hbm(ending)
    *near, enter = load(0, own, entering)
    near.append(swap_cores(near[0]))
    near.append(swap_cores(near[1]))
    turn = list(load(stages - 1, own))
    turn += [swap_cores(weight) for weight in turn]
    if stages > 2:
        weights = own + [swap_cores(weight) for weight in own]
    flows, trunks, inners = [], [], []
    head = pl.pallas_call(
        head_body,
        out_shape=[
            jax.ShapeDtypeStruct((rows, channels), jnp.bfloat16),
            jax.ShapeDtypeStruct((rows, inner), jnp.float32),
            jax.ShapeDtypeStruct((rows, inner), jnp.bfloat16),
        ],
        in_specs=[VMEM] * 3,
        out_specs=[VMEM] * 3,
        compiler_params=PARAMS,
    )(near[0], near[2], enter)
    for step in range(stages - 1):
        arrays = [enter] if step else [enter, *head]
        flow, leave, trunk, inner_sum = run_stage(
            weights if step else near, step, True, False, step == 0, rows, sizes, *arrays
        )
        flows.append(flow)
        trunks.append(trunk)
        inners.append(inner_sum)
        enter = hop(leave, step)
    mirrored = stages == 2
    line = jax.ShapeDtypeStruct((rows, channels), jnp.bfloat16)
    outs = [line, jax.ShapeDtypeStruct((rows, inner), jnp.float32)] + [line, line] * mirrored
    ending, first_active, *known = pl.pallas_call(
        functools.partial(meanwhile_body, stages - 1, mirrored),
        out_shape=outs,
        in_specs=[VMEM, VMEM, HBM, HBM, VMEM],
        out_specs=[VMEM] * len(outs),
        scratch_shapes=[pltpu.SemaphoreType.DMA((3,))],
        compiler_params=PARAMS,
    )(turn[1], turn[3], entering, ending, leave)
    flow, upstreams, back_inners, leave = run_stage(
        turn, stages - 1, True, True, True, rows, sizes, enter, ending, first_active
    )
    flows.append(flow)
    upstreams, back_inners = [upstreams], [back_inners]
    upstream = hop(leave, 0)
    side_flow = swap_cores(pick(flows)[1])
    near_core = lambda first, second: jnp.where(first_core, first, second)
    going = pick(flows, True)
    if mirrored:
        lifted = near_core(going[1, :, :channels], going[0, :, :channels])
        going = jnp.concatenate([lifted, going[0, :, channels:], going[1, :, channels:]], axis=1)
    far_flow = mirror(going)
    if mirrored:
        lifted, actives = far_flow[:, :channels], far_flow[:, channels:]
        far_flow = jnp.concatenate([near_core(known[1], lifted), actives[:, :inner]], axis=1)
        cross_flow = jnp.concatenate([near_core(lifted, known[1]), actives[:, inner:]], axis=1)
    else:
        far_flow, cross_flow = far_flow[0], far_flow[1]
    cross_flow = swap_cores(cross_flow)
    for step in range(stages - 2, -1, -1):
        outs = run_stage(
            weights if step else near,
            step,
            False,
            True,
            step == 0,
            rows,
            sizes,
            upstream,
            trunks[step],
            inners[step],
        )
        upstreams.insert(0, outs[0])
        if step:
            upstream = hop(outs[2], stages - 1 - step)
            back_inners.insert(0, outs[1])
            continue
        tail = pl.pallas_call(
            tail_body,
            out_shape=jax.ShapeDtypeStruct(outs[1].shape, outs[1].dtype),
            in_specs=[VMEM] * 5,
            out_specs=VMEM,
            compiler_params=PARAMS,
        )(near[1], near[3], outs[0], outs[1], inners[0])
        back_inners.insert(0, tail)
    going = pick(upstreams, True)
    far_up = mirror(near_core(going[0], going[1]) if mirrored else going)
    far_inner = mirror(pick(back_inners, True))
    side_up = swap_cores(pick(upstreams)[1])
    side_inner = swap_cores(pick(back_inners)[1])
    if mirrored:
        top = jnp.where(at_stage[0], leave, known[0])
        far_up, cross_up = near_core(far_up, top), near_core(top, far_up)
    else:
        far_up, cross_up = far_up[0], far_up[1]
    cross_up = swap_cores(cross_up)
    far_inner, cross_inner = far_inner[0], far_inner[1]
    cross_inner = swap_cores(cross_inner)

    chunk = channels // replicas
    fore = flows + [side_flow, far_flow, cross_flow]
    ups = upstreams + [side_up, far_up, cross_up]
    backs = back_inners + [side_inner, far_inner, cross_inner]
    halve = halve_rows if chunk % 128 == 0 and replicas >= 4 else halve_sums
    parts = halve(stages, replicas, chunk, sizes, rows, fore, ups, backs)
    return pl.pallas_call(
        finish_body,
        out_shape=jax.ShapeDtypeStruct((1, 2, chunk, inner), jnp.float32),
        in_specs=[VMEM] * 4,
        out_specs=VMEM,
        compiler_params=PARAMS,
    )(*parts)


def sums(count, chunk, inner):
    return [
        jax.ShapeDtypeStruct((count, chunk, inner), jnp.bfloat16),
        jax.ShapeDtypeStruct((count, chunk, inner), jnp.float32),
    ]


def exchange(shard, stages, replicas, first, second):
    pairs = []
    for p in range(2 * stages):
        for q in range(replicas):
            pairs.append((p * replicas + q, p * replicas + (q ^ (second if p % 2 else first))))
    return lax.ppermute(shard, AXES, pairs)


def halve_rows(stages, replicas, chunk, sizes, rows, fore, ups, backs):
    channels, inner = sizes
    half = channels // 2
    count = stages + 1

    def pack(body, arrays, *widths):
        return pl.pallas_call(
            body,
            out_shape=[jax.ShapeDtypeStruct((2 * rows, width), jnp.bfloat16) for width in widths],
            in_specs=[VMEM] * len(arrays),
            out_specs=[VMEM] * len(widths),
            scratch_shapes=[pltpu.VMEM((2 * rows, channels), jnp.bfloat16)],
            compiler_params=PARAMS,
        )(*arrays)

    near_up, near_active, near_lifted, send = pack(
        functools.partial(near_up_body, stages, chunk),
        fore[:count] + ups[:count],
        half,
        inner,
        half,
        2 * half + inner,
    )
    came_near = exchange(send, stages, replicas, 1, 2)
    far_up, far_active, send = pack(
        functools.partial(late_up_body, chunk),
        fore[count:] + ups[count:],
        half,
        inner,
        half + inner,
    )
    came_up = exchange(send, stages, replicas, 1, 2)
    far_lifted, far_inner, near_inner, send = pack(
        functools.partial(late_inner_body, chunk),
        fore[count:] + backs,
        half,
        inner,
        inner,
        half + 2 * inner,
    )
    came_inner = exchange(send, stages, replicas, 1, 2)
    streams = (
        (
            (near_lifted, far_lifted, near_inner, far_inner, came_near, came_inner),
            (((0, half + inner), (1, half + inner)), ((1, 0), (1, half))),
        ),
        (
            (near_up, far_up, near_active, far_active, came_near, came_up),
            (((0, 0), (0, half)), ((1, 0), (1, half))),
        ),
    )
    parts = []
    for operands, starts in streams:
        count = replicas // 4
        send, keep = pl.pallas_call(
            functools.partial(half_gradient_body, starts),
            out_shape=sums(count, chunk, inner),
            in_specs=[VMEM] * len(operands),
            out_specs=[VMEM] * 2,
            scratch_shapes=[
                pltpu.VMEM((channels // 2, inner), jnp.float32),
                pltpu.VMEM((8 * rows, channels // 2), jnp.bfloat16),
                pltpu.VMEM((8 * rows, inner), jnp.bfloat16),
            ],
            compiler_params=PARAMS,
        )(*operands)
        came = exchange(send, stages, replicas, 2, 1)
        for bit in range(2, replicas.bit_length() - 1):
            count //= 2
            send, keep = pl.pallas_call(
                functools.partial(next_body, bit),
                out_shape=sums(count, chunk, inner),
                in_specs=[VMEM] * 2,
                out_specs=[VMEM] * 2,
                compiler_params=PARAMS,
            )(keep, came)
            came = exchange(send, stages, replicas, 1 << bit, 1 << bit)
        parts += [keep, came]
    return parts


def halve_sums(stages, replicas, chunk, sizes, rows, fore, ups, backs):
    channels, inner = sizes
    wide, narrow = slice(0, channels), slice(channels, channels + inner)

    def of_flows(columns):
        def pick_parts(arrays):
            near = [flow.at[0, :, columns] for flow in arrays[:stages]]
            side, far, cross = arrays[stages : stages + 3]
            return near, [side.at[:, columns], far.at[:, columns], cross.at[:, columns]]

        return pick_parts

    def of_backs(arrays):
        near = [back.at[0] for back in arrays[stages + 3 : 2 * stages + 3]]
        side, far, cross = arrays[2 * stages + 3 : 2 * stages + 6]
        return near, [side, far, cross]

    plans = [halving_plan(replicas, turn) for turn in range(2)]
    streams = []
    for pick_left, pick_right, late, plan in (
        (of_backs, of_flows(narrow), ups, plans),
        (of_flows(wide), of_backs, backs, plans[::-1]),
    ):
        arrays = fore + late
        send, keep = pl.pallas_call(
            functools.partial(gradient_body, plan, pick_left, pick_right, len(arrays)),
            out_shape=sums(replicas // 2, chunk, inner),
            in_specs=[VMEM] * len(arrays),
            out_specs=[VMEM] * 2,
            scratch_shapes=[
                pltpu.VMEM((4 * rows, channels), jnp.bfloat16),
                pltpu.VMEM((4 * rows, inner), jnp.bfloat16),
                pltpu.VMEM((channels, inner), jnp.float32),
            ],
            compiler_params=PARAMS,
        )(*arrays)
        streams.append((plan, send, keep))
    for at in range(replicas.bit_length() - 1):
        half = replicas >> (at + 2)
        arrived = []
        for plan, send, keep in streams:
            pairs = []
            for p in range(2 * stages):
                for q in range(replicas):
                    pairs.append((p * replicas + q, p * replicas + (q ^ plan[p % 2][0][at])))
            arrived.append((plan, keep, lax.ppermute(send, AXES, pairs)))
        if half == 0:
            break
        streams = []
        for plan, keep, came in arrived:
            send, keep = pl.pallas_call(
                functools.partial(halve_body, plan, at + 1),
                out_shape=sums(half, chunk, inner),
                in_specs=[VMEM] * 2,
                out_specs=[VMEM] * 2,
                compiler_params=PARAMS,
            )(keep, came)
            streams.append((plan, send, keep))
    (_, keep_expand, came_expand), (_, keep_reduce, came_reduce) = arrived
    return keep_reduce, came_reduce, keep_expand, came_expand


def solution(mesh):
    return jax.shard_map(
        shards,
        mesh=mesh,
        in_specs=(
            P(None, None, "dp", None),
            P(None, None, "dp", None),
            P(None, "pipe", None, None),
            P(None, "pipe", None, None),
        ),
        out_specs=P("pipe", None, "dp", None),
        check_vma=False,
    )
```

```python
import functools

import jax
import jax.numpy as jnp
from jax import lax
from jax.experimental import pallas as pl
from jax.experimental.pallas import tpu as pltpu
from jax.sharding import PartitionSpec as P


EPSILON = 1e-06
AXES = ("pipe", "dp")
HBM = pl.BlockSpec(memory_space=pltpu.HBM)
ANY = pl.BlockSpec(memory_space=pl.ANY)
VMEM = pl.BlockSpec(memory_space=pltpu.VMEM)
PARAMS = pltpu.CompilerParams(vmem_limit_bytes=16 << 20)


def contract(first_op, second_op, first_dim, second_dim):
    return lax.dot_general(
        first_op,
        second_op,
        (((first_dim,), (second_dim,)), ((), ())),
        preferred_element_type=jnp.float32,
    )


def smooth_slope(values):
    sigma = jax.nn.sigmoid(values)
    return sigma * (1.0 + values * (1.0 - sigma))


def norm_of(widened):
    return lax.rsqrt(jnp.mean(widened * widened, axis=-1, keepdims=True) + EPSILON)


def where_am_i(step):
    position = lax.axis_index("pipe")
    stage, core = lax.div(position, 2), lax.rem(position, 2)
    way = jnp.where(stage == step, 0, 1)
    return stage, core, way


def bring_all(sources, outs, sems):
    copies = [
        pltpu.make_async_copy(source, out, sems.at[at])
        for at, (source, out) in enumerate(zip(sources, outs))
    ]
    for copy in copies:
        copy.start()
    return copies


def load_body(step, reduce_all, expand_all, *refs):
    _, core, way = where_am_i(step)
    sources, outs = [reduce_all.at[way], expand_all.at[way]], refs[:-1]
    if step == 0:
        sources.append(refs[0].at[way, core])
        outs = outs[1:]
    for copy in bring_all(sources, outs, refs[-1]):
        copy.wait()


def load(step, own, *more):
    channels, inner = own[0].shape[1:]
    mat = jax.ShapeDtypeStruct((channels, inner), jnp.bfloat16)
    outs = [mat, mat] + [jax.ShapeDtypeStruct(a.shape[2:], a.dtype) for a in more]
    return pl.pallas_call(
        functools.partial(load_body, step),
        out_shape=outs,
        in_specs=[HBM] * (2 + len(more)),
        out_specs=[VMEM] * len(outs),
        scratch_shapes=[pltpu.SemaphoreType.DMA((len(outs),))],
        compiler_params=PARAMS,
    )(*own, *more)


def meanwhile_body(step, mirrored, expand_own, expand_other, inputs, cotangent, leave, *refs):
    outs, sems = refs[:-1], refs[-1]
    stage, core, way = where_am_i(step)
    ending, back_active = outs[:2]
    sources = [cotangent.at[way, core]]
    if mirrored:
        sources += [cotangent.at[1, core], inputs.at[1, core]]
    copies = bring_all(sources, [outs[0]] + list(outs[2:]), sems)
    copies[0].wait()

    @pl.when(way == core)
    def _():
        back_active[...] = jnp.dot(
            ending[...], expand_other[...], preferred_element_type=jnp.float32
        )

    @pl.when(way != core)
    def _():
        back_active[...] = jnp.dot(ending[...], expand_own[...], preferred_element_type=jnp.float32)

    for copy in copies[1:]:
        copy.wait()
    if mirrored:
        rows = outs[3]

        @pl.when(stage != 0)
        def _():
            rows[...] = leave[...]

        widened = rows[...].astype(jnp.float32)
        rows[...] = jax.nn.silu(widened * norm_of(widened)).astype(jnp.bfloat16)


def weight_copies(own, other, held, sems, core, way):
    copies = []
    for order in range(2):
        is_own = lax.rem(way + order, 2) == core
        for kind in range(2):
            mine = pltpu.make_async_copy(own[kind].at[way], held[kind].at[order], sems.at[kind, order])
            theirs = pltpu.make_async_copy(
                other[kind].at[way], held[kind].at[order], sems.at[kind, order]
            )
            copies.append((is_own, mine, theirs))
    return copies


def start_all(copies):
    for is_own, mine, theirs in copies:
        pl.when(is_own)(mine.start)
        pl.when(jnp.logical_not(is_own))(theirs.start)


def head_body(own, other, rows_in, lifted_out, inner_out, active_out):
    _, core, way = where_am_i(0)
    widened = rows_in[...].astype(jnp.float32)
    lifted = jax.nn.silu(widened * norm_of(widened)).astype(jnp.bfloat16)
    lifted_out[...] = lifted

    def run(reduce_mat):
        inner_sum = jnp.dot(lifted, reduce_mat[...], preferred_element_type=jnp.float32)
        inner_out[...] = inner_sum
        active_out[...] = jax.nn.silu(inner_sum).astype(jnp.bfloat16)

    pl.when(way == core)(lambda: run(own))
    pl.when(way != core)(lambda: run(other))


def stage_body(step, forward, backward, last, near, *refs):
    refs = list(refs)
    _, core, way = where_am_i(step)
    own, other = (refs.pop(0), refs.pop(0)), (refs.pop(0), refs.pop(0))
    enter = refs.pop(0) if forward else None
    head = [refs.pop(0) for _ in range(3)] if forward and step == 0 else None
    upstream_in = refs.pop(0) if backward else None
    first_active = refs.pop(0) if forward and backward else None
    if not forward:
        trunks, inners = refs.pop(0), refs.pop(0)
    if forward:
        flows = refs.pop(0)
    if forward and not backward:
        leave = refs.pop(0)
    if backward:
        upstreams, back_inners = refs.pop(0), refs.pop(0)
    if backward and not last:
        back_leave = refs.pop(0)
    if forward:
        trunks, inners = refs.pop(0), refs.pop(0)
    channels = trunks.shape[2]

    def run(reduce_mats, expand_mats, wait):
        if forward:
            rows = enter[...]
            for order in range(2):
                slot = lax.rem(order + core, 2)
                widened = rows.astype(jnp.float32)
                trunks[order] = rows
                if head and order == 0:
                    lifted, inner_sum, active = [part[...] for part in head]
                else:
                    normed = widened * norm_of(widened)
                    lifted = jax.nn.silu(normed).astype(jnp.bfloat16)
                    wait(0, order)
                    inner_sum = jnp.dot(
                        lifted, reduce_mats[order][...], preferred_element_type=jnp.float32
                    )
                    active = jax.nn.silu(inner_sum).astype(jnp.bfloat16)
                flows[slot, :, :channels] = lifted
                inners[order] = inner_sum
                flows[slot, :, channels:] = active
                wait(1, order)
                rows = (widened + contract(active, expand_mats[order][...], 1, 1)).astype(jnp.bfloat16)
            if not backward:
                leave[...] = rows
        if backward:
            upstream = upstream_in[...]
            for order in (1, 0):
                slot = lax.rem(order + core, 2)
                upstreams[slot] = upstream
                if last and order == 0:
                    break
                if not forward:
                    wait(1, order)
                if forward and order:
                    back_active = first_active[...]
                else:
                    back_active = jnp.dot(
                        upstream, expand_mats[order][...], preferred_element_type=jnp.float32
                    )
                back_inner = (back_active * smooth_slope(inners[order])).astype(jnp.bfloat16)
                back_inners[slot] = back_inner
                if not forward:
                    wait(0, order)
                back_lifted = contract(back_inner, reduce_mats[order][...], 1, 1)
                widened = trunks[order].astype(jnp.float32)
                norm_scale = norm_of(widened)
                back_normed = back_lifted * smooth_slope(widened * norm_scale)
                projection = jnp.mean(back_normed * widened, axis=-1, keepdims=True)
                upstream = (
                    upstream.astype(jnp.float32)
                    + norm_scale * back_normed
                    - widened * norm_scale**3 * projection
                ).astype(jnp.bfloat16)
            if not last:
                back_leave[...] = upstream

    if near:
        idle = lambda kind, order: None

        @pl.when(way == core)
        def _():
            run((own[0], other[0]), (own[1], other[1]), idle)

        @pl.when(way != core)
        def _():
            run((other[0], own[0]), (other[1], own[1]), idle)

    else:
        held = (refs.pop(0), refs.pop(0))
        copies = weight_copies(own, other, held, refs.pop(0), core, way)
        start_all(copies if forward else copies[2:] + copies[:2])


def tail_body(own, other, upstreams, back_first, inners, back_inners):
    _, core, way = where_am_i(0)

    def run(expand_mat):
        back_active = jnp.dot(upstreams[core], expand_mat[...], preferred_element_type=jnp.float32)
        back_inners[core] = (back_active * smooth_slope(inners[0])).astype(jnp.bfloat16)
        back_inners[1 - core] = back_first[1 - core]

    pl.when(way == core)(lambda: run(own))
    pl.when(way != core)(lambda: run(other))


def run_stage(weights, step, forward, backward, near, rows, sizes, *arrays):
    channels, inner = sizes
    last = backward and step == 0 and not forward
    shape = lambda dtype, *dims: jax.ShapeDtypeStruct(dims, dtype)
    line = shape(jnp.bfloat16, rows, channels)
    kept = [((2, rows, channels), jnp.bfloat16), ((2, rows, inner), jnp.float32)]
    outs, scratch = [], []
    if forward:
        outs.append(shape(jnp.bfloat16, 2, rows, channels + inner))
    if forward and not backward:
        outs.append(line)
    if backward:
        outs.append(shape(jnp.bfloat16, 2, rows, channels))
        outs.append(shape(jnp.bfloat16, 2, rows, inner))
    if backward and not last:
        outs.append(line)
    if forward and not backward:
        outs += [jax.ShapeDtypeStruct(*one) for one in kept]
    if forward and backward:
        scratch += [pltpu.VMEM(*one) for one in kept]
    if not near:
        scratch += [pltpu.VMEM((2, channels, inner), jnp.bfloat16)] * 2
        scratch += [pltpu.SemaphoreType.DMA((2, 2))]
    passes = 4 * (int(forward) + int(backward))
    return pl.pallas_call(
        functools.partial(stage_body, step, forward, backward, last, near),
        out_shape=outs,
        in_specs=[VMEM if near else ANY] * 4 + [VMEM] * len(arrays),
        out_specs=[VMEM] * len(outs),
        scratch_shapes=scratch,
        compiler_params=PARAMS,
        cost_estimate=pl.CostEstimate(
            flops=2 * passes * rows * channels * inner,
            bytes_accessed=8 * channels * inner,
            transcendentals=passes * rows * channels,
        ),
    )(*weights, *arrays)


def parity(value, mask):
    total, bit = 0, 0
    while mask >> bit:
        if mask >> bit & 1:
            total = total + lax.rem(lax.div(value, 1 << bit), 2)
        bit += 1
    return lax.rem(total, 2)


def halving_plan(size, turn):
    order = [1 << bit for bit in range(size.bit_length() - 1)]
    if turn and len(order) > 1:
        order[:2] = order[1::-1]
    table = [0] * size
    for chunk in range(size):
        place = 0
        for mask in order:
            place = 2 * place + int(chunk & mask != 0)
        table[place] = chunk
    return order, order, table


def side_of(plans, at):
    core, shard = lax.rem(lax.axis_index("pipe"), 2), lax.axis_index("dp")
    return jnp.where(core == 0, parity(shard, plans[0][1][at]), parity(shard, plans[1][1][at]))


def gradient_body(plans, pick_left, pick_right, count, *refs):
    arrays, (send, keep, left, right, full) = refs[:count], refs[count:]
    stage, core, _ = where_am_i(0)
    rows = left.shape[0] // 4
    chunk = send.shape[1]
    for target, pick in ((left, pick_left), (right, pick_right)):
        near, away = pick(arrays)
        for step, part in enumerate(near):

            @pl.when(stage == step)
            def _():
                target[:rows] = part[...]

        for at, part in enumerate(away):
            target[(at + 1) * rows : (at + 2) * rows] = part[...]
    full[...] = contract(left[...], right[...], 0, 0)
    side = side_of(plans, 0)
    half = send.shape[0]
    flip = [plan[2][half] for plan in plans]
    for at in range(half):
        spots = []
        for target_side in (1 - side, side):
            first = plans[0][2][at] ^ (flip[0] * target_side)
            second = plans[1][2][at] ^ (flip[1] * target_side)
            spots.append(pl.multiple_of(jnp.where(core == 0, first, second) * chunk, chunk))
        send[at] = full[pl.ds(spots[0], chunk)].astype(jnp.bfloat16)
        keep[at] = full[pl.ds(spots[1], chunk)]


def halve_body(plans, at, keep_in, came, send, keep):
    half = keep.shape[0]
    side = side_of(plans, at)
    for spot in range(half):
        mine, theirs = side * half + spot, (1 - side) * half + spot
        send[spot] = (keep_in[theirs] + came[theirs].astype(jnp.float32)).astype(jnp.bfloat16)
        keep[spot] = keep_in[mine] + came[mine].astype(jnp.float32)


def bit_of(value, bit):
    return lax.rem(lax.div(value, 1 << bit), 2)


def first_sides():
    core, shard = lax.rem(lax.axis_index("pipe"), 2), lax.axis_index("dp")
    low, high = bit_of(shard, 0), bit_of(shard, 1)
    return core, jnp.where(core == 0, low, high), jnp.where(core == 0, high, low)


def split_columns(wide, keep, send, chunk):
    core, side, _ = first_sides()
    for place in range(wide.shape[1] // (2 * chunk)):
        for target, at in ((keep, side), (send, 1 - side)):
            block = jnp.where(core == 0, 2 * place + at, place // 2 * 4 + 2 * at + place % 2)
            source = pl.ds(pl.multiple_of(block * chunk, chunk), chunk)
            target[:, place * chunk : (place + 1) * chunk] = wide[:, source]


def pack_body(stages, chunk, up, near, far, *refs):
    refs = list(refs)
    left, right, send, wide = refs[-4:]
    channels = wide.shape[1]
    spans = slice(0, channels), slice(channels, None), slice(None)
    flow_span, back_span = (spans[1] if up else spans[0]), spans[2]
    stage, _, _ = where_am_i(0)
    rows = wide.shape[0] // (2 * near + 2 * far)
    start = 0
    targets = (right, wide) if up else (wide, right)
    for target, span in zip(targets, (flow_span, back_span)):
        start = 0
        if near:
            parts = [refs.pop(0) for _ in range(stages + 1)]
            for step in range(stages):

                @pl.when(stage == step)
                def _():
                    target[:rows] = parts[step][0, :, span]

            target[rows : 2 * rows] = parts[stages][:, span]
            start = 2 * rows
        if far:
            for part in (refs.pop(0), refs.pop(0)):
                target[start : start + rows] = part[:, span]
                start += rows
    split_columns(wide, left, send, chunk)
    send[:, channels // 2 :] = right[...]


def pick_stage(target, parts, span):
    stage, _, _ = where_am_i(0)
    for step, part in enumerate(parts):

        @pl.when(stage == step)
        def _():
            target[...] = part[0, :, span]


def own_body(stages, chunk, *refs):
    send, wide, spare = refs[stages:]
    channels = wide.shape[1]
    pick_stage(wide, refs[:stages], slice(0, channels))
    split_columns(wide, spare, send.at[:, : channels // 2], chunk)
    pick_stage(send.at[:, channels // 2 :], refs[:stages], slice(channels, None))


def near_body(stages, chunk, *refs):
    flows, ups, backs = [refs[at * (stages + 1) : (at + 1) * (stages + 1)] for at in range(3)]
    up, active, lifted, inner, send, wide, spare = refs[3 * stages + 3 :]
    half, channels = up.shape[1], wide.shape[1]
    rows = wide.shape[0] // 2
    everything, broad, narrow = slice(None), slice(0, channels), slice(channels, None)
    for target, sources, span in ((wide, ups, everything), (active, flows, narrow)):
        pick_stage(target.at[:rows], sources[:-1], span)
        target[rows:] = sources[-1][:, span]
    split_columns(wide, up, send.at[: 2 * rows, :half], chunk)
    send[2 * rows :, half:] = active[rows:]
    for target, sources, span in ((wide, flows, broad), (inner, backs, everything)):
        pick_stage(target.at[:rows], sources[:-1], span)
        target[rows:] = sources[-1][:, span]
    split_columns(wide.at[:rows], lifted.at[:rows], spare, chunk)
    split_columns(wide.at[rows:], lifted.at[rows:], send.at[2 * rows :, :half], chunk)
    send[: 2 * rows, half:] = inner[...]


def half_gradient_body(up, *refs):
    near, far, (own_came, near_came, far_came) = refs[:2], refs[2:4], refs[4:7]
    send, keep, full, left, right = refs[7:]
    rows, columns = own_came.shape[0], near[0].shape[1]
    spans = slice(0, columns), slice(columns, None)
    for at, target in enumerate((left, right)):
        target[: 2 * rows] = near[at][...]
        if up == (at == 0):
            target[2 * rows : 4 * rows] = near_came[: 2 * rows, spans[at]]
        else:
            target[2 * rows : 3 * rows] = own_came[:, spans[at]]
            target[3 * rows : 4 * rows] = near_came[2 * rows :, spans[at]]
        target[4 * rows : 6 * rows] = far[at][...]
        target[6 * rows :] = far_came[:, spans[at]]
    full[...] = contract(left[...], right[...], 0, 0)
    _, _, side = first_sides()
    chunk = send.shape[1]
    for place in range(send.shape[0]):
        theirs = pl.ds(pl.multiple_of((2 * place + 1 - side) * chunk, chunk), chunk)
        mine = pl.ds(pl.multiple_of((2 * place + side) * chunk, chunk), chunk)
        send[place] = full[theirs].astype(jnp.bfloat16)
        keep[place] = full[mine]


def next_body(bit, keep_in, came, send, keep):
    side = bit_of(lax.axis_index("dp"), bit)
    for place in range(keep.shape[0]):
        theirs, mine = 2 * place + 1 - side, 2 * place + side
        send[place] = (keep_in[theirs] + came[theirs].astype(jnp.float32)).astype(jnp.bfloat16)
        keep[place] = keep_in[mine] + came[mine].astype(jnp.float32)


def finish_body(keep_reduce, came_reduce, keep_expand, came_expand, out):
    out[0, 0] = keep_reduce[0] + came_reduce[0].astype(jnp.float32)
    out[0, 1] = keep_expand[0] + came_expand[0].astype(jnp.float32)


def shards(inputs, cotangent, reduce_weight, expand_weight):
    stages = lax.axis_size("pipe") // 2
    replicas = lax.axis_size("dp")
    stage, core, _ = where_am_i(0)
    channels, inner = reduce_weight.shape[2:]
    rows = inputs.shape[1] * inputs.shape[2] // 2
    sizes = (channels, inner)
    entering = inputs.reshape(2, 2, rows, channels)
    ending = cotangent.reshape(2, 2, rows, channels)
    own = [reduce_weight[:, 0], expand_weight[:, 0]]

    core_pairs = [(p, p ^ 1) for p in range(2 * stages)]
    mirror_pairs = [(p, 2 * (stages - 1 - p // 2) + p % 2) for p in range(2 * stages)]

    def hop(shard, step):
        pairs = []
        for c in range(2):
            pairs.append((2 * step + c, 2 * step + 2 + c))
            pairs.append((2 * (stages - 1 - step) + c, 2 * (stages - 2 - step) + c))
        return lax.ppermute(shard, "pipe", pairs)

    def swap_cores(shard):
        return lax.ppermute(shard, "pipe", core_pairs)

    def mirror(shard):
        return lax.ppermute(shard, "pipe", mirror_pairs)

    at_stage = [stage == step for step in range(stages)]
    first_core = core == 0
    at_stage, first_core, entering = lax.optimization_barrier((at_stage, first_core, entering))

    def pick(parts, mirrored_stage=False):
        tests = at_stage[::-1] if mirrored_stage else at_stage
        chosen = parts[0]
        for test, part in zip(tests[1:], parts[1:]):
            chosen = jnp.where(test, part, chosen)
        return chosen

    in_hbm = lambda array: pltpu.with_memory_space_constraint(array, pltpu.HBM)
    own, entering, ending = [in_hbm(one) for one in own], in_hbm(entering), in_hbm(ending)
    *near, enter = load(0, own, entering)
    near.append(swap_cores(near[0]))
    near.append(swap_cores(near[1]))
    turn = list(load(stages - 1, own))
    turn += [swap_cores(weight) for weight in turn]
    if stages > 2:
        weights = own + [swap_cores(weight) for weight in own]
    flows, trunks, inners = [], [], []
    head = pl.pallas_call(
        head_body,
        out_shape=[
            jax.ShapeDtypeStruct((rows, channels), jnp.bfloat16),
            jax.ShapeDtypeStruct((rows, inner), jnp.float32),
            jax.ShapeDtypeStruct((rows, inner), jnp.bfloat16),
        ],
        in_specs=[VMEM] * 3,
        out_specs=[VMEM] * 3,
        compiler_params=PARAMS,
    )(near[0], near[2], enter)
    for step in range(stages - 1):
        arrays = [enter] if step else [enter, *head]
        flow, leave, trunk, inner_sum = run_stage(
            weights if step else near, step, True, False, step == 0, rows, sizes, *arrays
        )
        flows.append(flow)
        trunks.append(trunk)
        inners.append(inner_sum)
        enter = hop(leave, step)
    mirrored = stages == 2
    line = jax.ShapeDtypeStruct((rows, channels), jnp.bfloat16)
    outs = [line, jax.ShapeDtypeStruct((rows, inner), jnp.float32)] + [line, line] * mirrored
    ending, first_active, *known = pl.pallas_call(
        functools.partial(meanwhile_body, stages - 1, mirrored),
        out_shape=outs,
        in_specs=[VMEM, VMEM, HBM, HBM, VMEM],
        out_specs=[VMEM] * len(outs),
        scratch_shapes=[pltpu.SemaphoreType.DMA((3,))],
        compiler_params=PARAMS,
    )(turn[1], turn[3], entering, ending, leave)
    flow, upstreams, back_inners, leave = run_stage(
        turn, stages - 1, True, True, True, rows, sizes, enter, ending, first_active
    )
    flows.append(flow)
    upstreams, back_inners = [upstreams], [back_inners]
    upstream = hop(leave, 0)
    side_flow = swap_cores(pick(flows)[1])
    near_core = lambda first, second: jnp.where(first_core, first, second)
    going = pick(flows, True)
    if mirrored:
        lifted = near_core(going[1, :, :channels], going[0, :, :channels])
        going = jnp.concatenate([lifted, going[0, :, channels:], going[1, :, channels:]], axis=1)
    far_flow = mirror(going)
    if mirrored:
        lifted, actives = far_flow[:, :channels], far_flow[:, channels:]
        far_flow = jnp.concatenate([near_core(known[1], lifted), actives[:, :inner]], axis=1)
        cross_flow = jnp.concatenate([near_core(lifted, known[1]), actives[:, inner:]], axis=1)
    else:
        far_flow, cross_flow = far_flow[0], far_flow[1]
    cross_flow = swap_cores(cross_flow)
    for step in range(stages - 2, -1, -1):
        outs = run_stage(
            weights if step else near,
            step,
            False,
            True,
            step == 0,
            rows,
            sizes,
            upstream,
            trunks[step],
            inners[step],
        )
        upstreams.insert(0, outs[0])
        if step:
            upstream = hop(outs[2], stages - 1 - step)
            back_inners.insert(0, outs[1])
            continue
        tail = pl.pallas_call(
            tail_body,
            out_shape=jax.ShapeDtypeStruct(outs[1].shape, outs[1].dtype),
            in_specs=[VMEM] * 5,
            out_specs=VMEM,
            compiler_params=PARAMS,
        )(near[1], near[3], outs[0], outs[1], inners[0])
        back_inners.insert(0, tail)
    going = pick(upstreams, True)
    far_up = mirror(near_core(going[0], going[1]) if mirrored else going)
    far_inner = mirror(pick(back_inners, True))
    side_up = swap_cores(pick(upstreams)[1])
    side_inner = swap_cores(pick(back_inners)[1])
    if mirrored:
        top = jnp.where(at_stage[0], leave, known[0])
        far_up, cross_up = near_core(far_up, top), near_core(top, far_up)
    else:
        far_up, cross_up = far_up[0], far_up[1]
    cross_up = swap_cores(cross_up)
    far_inner, cross_inner = far_inner[0], far_inner[1]
    cross_inner = swap_cores(cross_inner)

    chunk = channels // replicas
    fore = flows + [side_flow, far_flow, cross_flow]
    ups = upstreams + [side_up, far_up, cross_up]
    backs = back_inners + [side_inner, far_inner, cross_inner]
    halve = halve_rows if chunk % 128 == 0 and replicas >= 4 else halve_sums
    parts = halve(stages, replicas, chunk, sizes, rows, fore, ups, backs)
    return pl.pallas_call(
        finish_body,
        out_shape=jax.ShapeDtypeStruct((1, 2, chunk, inner), jnp.float32),
        in_specs=[VMEM] * 4,
        out_specs=VMEM,
        compiler_params=PARAMS,
    )(*parts)


def sums(count, chunk, inner):
    return [
        jax.ShapeDtypeStruct((count, chunk, inner), jnp.bfloat16),
        jax.ShapeDtypeStruct((count, chunk, inner), jnp.float32),
    ]


def exchange(shard, stages, replicas, first, second):
    pairs = []
    for p in range(2 * stages):
        for q in range(replicas):
            pairs.append((p * replicas + q, p * replicas + (q ^ (second if p % 2 else first))))
    return lax.ppermute(shard, AXES, pairs)


def halve_rows(stages, replicas, chunk, sizes, rows, fore, ups, backs):
    channels, inner = sizes
    shape = lambda *dims: jax.ShapeDtypeStruct(dims, jnp.bfloat16)

    def pack(late, up, near, far):
        count = 2 * (near + far)
        arrays = []
        for one in (fore, late):
            arrays += one[: stages + 1] * near + one[stages + 1 :] * far
        return pl.pallas_call(
            functools.partial(pack_body, stages, chunk, up, near, far),
            out_shape=[
                shape(count * rows, channels // 2),
                shape(count * rows, inner),
                shape(count * rows, channels // 2 + inner),
            ],
            in_specs=[VMEM] * len(arrays),
            out_specs=[VMEM] * 3,
            scratch_shapes=[pltpu.VMEM((count * rows, channels), jnp.bfloat16)],
            compiler_params=PARAMS,
        )(*arrays)

    send = pl.pallas_call(
        functools.partial(own_body, stages, chunk),
        out_shape=shape(rows, channels // 2 + inner),
        in_specs=[VMEM] * stages,
        out_specs=VMEM,
        scratch_shapes=[
            pltpu.VMEM((rows, channels), jnp.bfloat16),
            pltpu.VMEM((rows, channels // 2), jnp.bfloat16),
        ],
        compiler_params=PARAMS,
    )(*fore[:stages])
    came_own = exchange(send, stages, replicas, 1, 2)
    near = fore[: stages + 1] + ups[: stages + 1] + backs[: stages + 1]
    *kept, send = pl.pallas_call(
        functools.partial(near_body, stages, chunk),
        out_shape=[
            shape(2 * rows, channels // 2),
            shape(2 * rows, inner),
            shape(2 * rows, channels // 2),
            shape(2 * rows, inner),
            shape(3 * rows, channels // 2 + inner),
        ],
        in_specs=[VMEM] * len(near),
        out_specs=[VMEM] * 5,
        scratch_shapes=[
            pltpu.VMEM((2 * rows, channels), jnp.bfloat16),
            pltpu.VMEM((rows, channels // 2), jnp.bfloat16),
        ],
        compiler_params=PARAMS,
    )(*near)
    came_near = exchange(send, stages, replicas, 1, 2)
    parts = []
    for at, name, late in ((1, "inner", backs), (0, "up", ups)):
        left, right, send = pack(late, name == "up", False, True)
        came = exchange(send, stages, replicas, 1, 2)
        operands = (kept[2 * at], kept[2 * at + 1], left, right, came_own, came_near, came)
        count = replicas // 4
        send, keep = pl.pallas_call(
            functools.partial(half_gradient_body, at == 0),
            out_shape=sums(count, chunk, inner),
            in_specs=[VMEM] * len(operands),
            out_specs=[VMEM] * 2,
            scratch_shapes=[
                pltpu.VMEM((channels // 2, inner), jnp.float32),
                pltpu.VMEM((8 * rows, channels // 2), jnp.bfloat16),
                pltpu.VMEM((8 * rows, inner), jnp.bfloat16),
            ],
            compiler_params=PARAMS,
        )(*operands)
        came = exchange(send, stages, replicas, 2, 1)
        for bit in range(2, replicas.bit_length() - 1):
            count //= 2
            send, keep = pl.pallas_call(
                functools.partial(next_body, bit),
                out_shape=sums(count, chunk, inner),
                in_specs=[VMEM] * 2,
                out_specs=[VMEM] * 2,
                compiler_params=PARAMS,
            )(keep, came)
            came = exchange(send, stages, replicas, 1 << bit, 1 << bit)
        parts += [keep, came]
    return parts


def halve_sums(stages, replicas, chunk, sizes, rows, fore, ups, backs):
    channels, inner = sizes
    wide, narrow = slice(0, channels), slice(channels, channels + inner)

    def of_flows(columns):
        def pick_parts(arrays):
            near = [flow.at[0, :, columns] for flow in arrays[:stages]]
            side, far, cross = arrays[stages : stages + 3]
            return near, [side.at[:, columns], far.at[:, columns], cross.at[:, columns]]

        return pick_parts

    def of_backs(arrays):
        near = [back.at[0] for back in arrays[stages + 3 : 2 * stages + 3]]
        side, far, cross = arrays[2 * stages + 3 : 2 * stages + 6]
        return near, [side, far, cross]

    plans = [halving_plan(replicas, turn) for turn in range(2)]
    streams = []
    for pick_left, pick_right, late, plan in (
        (of_backs, of_flows(narrow), ups, plans),
        (of_flows(wide), of_backs, backs, plans[::-1]),
    ):
        arrays = fore + late
        send, keep = pl.pallas_call(
            functools.partial(gradient_body, plan, pick_left, pick_right, len(arrays)),
            out_shape=sums(replicas // 2, chunk, inner),
            in_specs=[VMEM] * len(arrays),
            out_specs=[VMEM] * 2,
            scratch_shapes=[
                pltpu.VMEM((4 * rows, channels), jnp.bfloat16),
                pltpu.VMEM((4 * rows, inner), jnp.bfloat16),
                pltpu.VMEM((channels, inner), jnp.float32),
            ],
            compiler_params=PARAMS,
        )(*arrays)
        streams.append((plan, send, keep))
    for at in range(replicas.bit_length() - 1):
        half = replicas >> (at + 2)
        arrived = []
        for plan, send, keep in streams:
            pairs = []
            for p in range(2 * stages):
                for q in range(replicas):
                    pairs.append((p * replicas + q, p * replicas + (q ^ plan[p % 2][0][at])))
            arrived.append((plan, keep, lax.ppermute(send, AXES, pairs)))
        if half == 0:
            break
        streams = []
        for plan, keep, came in arrived:
            send, keep = pl.pallas_call(
                functools.partial(halve_body, plan, at + 1),
                out_shape=sums(half, chunk, inner),
                in_specs=[VMEM] * 2,
                out_specs=[VMEM] * 2,
                compiler_params=PARAMS,
            )(keep, came)
            streams.append((plan, send, keep))
    (_, keep_expand, came_expand), (_, keep_reduce, came_reduce) = arrived
    return keep_reduce, came_reduce, keep_expand, came_expand


def solution(mesh):
    return jax.shard_map(
        shards,
        mesh=mesh,
        in_specs=(
            P(None, None, "dp", None),
            P(None, None, "dp", None),
            P(None, "pipe", None, None),
            P(None, "pipe", None, None),
        ),
        out_specs=P("pipe", None, "dp", None),
        check_vma=False,
    )
```

```python
import functools

import jax
import jax.numpy as jnp
from jax import lax
from jax.experimental import pallas as pl
from jax.experimental.pallas import tpu as pltpu
from jax.sharding import PartitionSpec as P


EPSILON = 1e-06
AXES = ("pipe", "dp")
HBM = pl.BlockSpec(memory_space=pltpu.HBM)
ANY = pl.BlockSpec(memory_space=pl.ANY)
VMEM = pl.BlockSpec(memory_space=pltpu.VMEM)
PARAMS = pltpu.CompilerParams(vmem_limit_bytes=16 << 20)
PACKED = pltpu.CompilerParams(vmem_limit_bytes=16 << 20)


def contract(first_op, second_op, first_dim, second_dim):
    return lax.dot_general(
        first_op,
        second_op,
        (((first_dim,), (second_dim,)), ((), ())),
        preferred_element_type=jnp.float32,
    )


def smooth_slope(values):
    sigma = jax.nn.sigmoid(values)
    return sigma * (1.0 + values * (1.0 - sigma))


def norm_of(widened):
    return lax.rsqrt(jnp.mean(widened * widened, axis=-1, keepdims=True) + EPSILON)


def where_am_i(step):
    position = lax.axis_index("pipe")
    stage, core = lax.div(position, 2), lax.rem(position, 2)
    way = jnp.where(stage == step, 0, 1)
    return stage, core, way


def bring_all(sources, outs, sems):
    copies = [
        pltpu.make_async_copy(source, out, sems.at[at])
        for at, (source, out) in enumerate(zip(sources, outs))
    ]
    for copy in copies:
        copy.start()
    return copies


def load_body(step, reduce_all, expand_all, *refs):
    _, core, way = where_am_i(step)
    sources, outs = [reduce_all.at[way], expand_all.at[way]], refs[:-1]
    if step == 0:
        sources.append(refs[0].at[way, core])
        outs = outs[1:]
    for copy in bring_all(sources, outs, refs[-1]):
        copy.wait()


def load(step, own, *more):
    channels, inner = own[0].shape[1:]
    mat = jax.ShapeDtypeStruct((channels, inner), jnp.bfloat16)
    outs = [mat, mat] + [jax.ShapeDtypeStruct(a.shape[2:], a.dtype) for a in more]
    return pl.pallas_call(
        functools.partial(load_body, step),
        out_shape=outs,
        in_specs=[HBM] * (2 + len(more)),
        out_specs=[VMEM] * len(outs),
        scratch_shapes=[pltpu.SemaphoreType.DMA((len(outs),))],
        compiler_params=PARAMS,
    )(*own, *more)


def meanwhile_body(step, mirrored, expand_own, expand_other, inputs, cotangent, leave, *refs):
    outs, sems = refs[:-1], refs[-1]
    stage, core, way = where_am_i(step)
    ending, back_active = outs[:2]
    sources = [cotangent.at[way, core]]
    if mirrored:
        sources += [cotangent.at[1, core], inputs.at[1, core]]
    copies = bring_all(sources, [outs[0]] + list(outs[2:]), sems)
    copies[0].wait()

    @pl.when(way == core)
    def _():
        back_active[...] = jnp.dot(
            ending[...], expand_other[...], preferred_element_type=jnp.float32
        )

    @pl.when(way != core)
    def _():
        back_active[...] = jnp.dot(ending[...], expand_own[...], preferred_element_type=jnp.float32)

    for copy in copies[1:]:
        copy.wait()
    if mirrored:
        rows = outs[3]

        @pl.when(stage != 0)
        def _():
            rows[...] = leave[...]

        widened = rows[...].astype(jnp.float32)
        rows[...] = jax.nn.silu(widened * norm_of(widened)).astype(jnp.bfloat16)


def weight_copies(own, other, held, sems, core, way):
    copies = []
    for order in range(2):
        is_own = lax.rem(way + order, 2) == core
        for kind in range(2):
            mine = pltpu.make_async_copy(own[kind].at[way], held[kind].at[order], sems.at[kind, order])
            theirs = pltpu.make_async_copy(
                other[kind].at[way], held[kind].at[order], sems.at[kind, order]
            )
            copies.append((is_own, mine, theirs))
    return copies


def start_all(copies):
    for is_own, mine, theirs in copies:
        pl.when(is_own)(mine.start)
        pl.when(jnp.logical_not(is_own))(theirs.start)


def head_body(own, other, rows_in, lifted_out, inner_out, active_out):
    _, core, way = where_am_i(0)
    widened = rows_in[...].astype(jnp.float32)
    lifted = jax.nn.silu(widened * norm_of(widened)).astype(jnp.bfloat16)
    lifted_out[...] = lifted

    def run(reduce_mat):
        inner_sum = jnp.dot(lifted, reduce_mat[...], preferred_element_type=jnp.float32)
        inner_out[...] = inner_sum
        active_out[...] = jax.nn.silu(inner_sum).astype(jnp.bfloat16)

    pl.when(way == core)(lambda: run(own))
    pl.when(way != core)(lambda: run(other))


def stage_body(step, forward, backward, last, near, *refs):
    refs = list(refs)
    _, core, way = where_am_i(step)
    own, other = (refs.pop(0), refs.pop(0)), (refs.pop(0), refs.pop(0))
    enter = refs.pop(0) if forward else None
    head = [refs.pop(0) for _ in range(3)] if forward and step == 0 else None
    upstream_in = refs.pop(0) if backward else None
    first_active = refs.pop(0) if forward and backward else None
    if not forward:
        trunks, inners = refs.pop(0), refs.pop(0)
    if forward:
        flows = refs.pop(0)
    if forward and not backward:
        leave = refs.pop(0)
    if backward:
        upstreams, back_inners = refs.pop(0), refs.pop(0)
    if backward and not last:
        back_leave = refs.pop(0)
    if forward:
        trunks, inners = refs.pop(0), refs.pop(0)
    channels = trunks.shape[2]

    def run(reduce_mats, expand_mats, wait):
        if forward:
            rows = enter[...]
            for order in range(2):
                slot = lax.rem(order + core, 2)
                widened = rows.astype(jnp.float32)
                trunks[order] = rows
                if head and order == 0:
                    lifted, inner_sum, active = [part[...] for part in head]
                else:
                    normed = widened * norm_of(widened)
                    lifted = jax.nn.silu(normed).astype(jnp.bfloat16)
                    wait(0, order)
                    inner_sum = jnp.dot(
                        lifted, reduce_mats[order][...], preferred_element_type=jnp.float32
                    )
                    active = jax.nn.silu(inner_sum).astype(jnp.bfloat16)
                flows[slot, :, :channels] = lifted
                inners[order] = inner_sum
                flows[slot, :, channels:] = active
                wait(1, order)
                rows = (widened + contract(active, expand_mats[order][...], 1, 1)).astype(jnp.bfloat16)
            if not backward:
                leave[...] = rows
        if backward:
            upstream = upstream_in[...]
            for order in (1, 0):
                slot = lax.rem(order + core, 2)
                upstreams[slot] = upstream
                if last and order == 0:
                    break
                if not forward:
                    wait(1, order)
                if forward and order:
                    back_active = first_active[...]
                else:
                    back_active = jnp.dot(
                        upstream, expand_mats[order][...], preferred_element_type=jnp.float32
                    )
                back_inner = (back_active * smooth_slope(inners[order])).astype(jnp.bfloat16)
                back_inners[slot] = back_inner
                if not forward:
                    wait(0, order)
                back_lifted = contract(back_inner, reduce_mats[order][...], 1, 1)
                widened = trunks[order].astype(jnp.float32)
                norm_scale = norm_of(widened)
                back_normed = back_lifted * smooth_slope(widened * norm_scale)
                projection = jnp.mean(back_normed * widened, axis=-1, keepdims=True)
                upstream = (
                    upstream.astype(jnp.float32)
                    + norm_scale * back_normed
                    - widened * norm_scale**3 * projection
                ).astype(jnp.bfloat16)
            if not last:
                back_leave[...] = upstream

    if near:
        idle = lambda kind, order: None

        @pl.when(way == core)
        def _():
            run((own[0], other[0]), (own[1], other[1]), idle)

        @pl.when(way != core)
        def _():
            run((other[0], own[0]), (other[1], own[1]), idle)

    else:
        held = (refs.pop(0), refs.pop(0))
        copies = weight_copies(own, other, held, refs.pop(0), core, way)
        start_all(copies if forward else copies[2:] + copies[:2])
        run(
            [held[0].at[order] for order in range(2)],
            [held[1].at[order] for order in range(2)],
            lambda kind, order: copies[2 * order + kind][1].wait(),
        )


def tail_body(own, other, upstreams, back_first, inners, back_inners):
    _, core, way = where_am_i(0)

    def run(expand_mat):
        back_active = jnp.dot(upstreams[core], expand_mat[...], preferred_element_type=jnp.float32)
        back_inners[core] = (back_active * smooth_slope(inners[0])).astype(jnp.bfloat16)
        back_inners[1 - core] = back_first[1 - core]

    pl.when(way == core)(lambda: run(own))
    pl.when(way != core)(lambda: run(other))


def run_stage(weights, step, forward, backward, near, rows, sizes, *arrays):
    channels, inner = sizes
    last = backward and step == 0 and not forward
    shape = lambda dtype, *dims: jax.ShapeDtypeStruct(dims, dtype)
    line = shape(jnp.bfloat16, rows, channels)
    kept = [((2, rows, channels), jnp.bfloat16), ((2, rows, inner), jnp.float32)]
    outs, scratch = [], []
    if forward:
        outs.append(shape(jnp.bfloat16, 2, rows, channels + inner))
    if forward and not backward:
        outs.append(line)
    if backward:
        outs.append(shape(jnp.bfloat16, 2, rows, channels))
        outs.append(shape(jnp.bfloat16, 2, rows, inner))
    if backward and not last:
        outs.append(line)
    if forward and not backward:
        outs += [jax.ShapeDtypeStruct(*one) for one in kept]
    if forward and backward:
        scratch += [pltpu.VMEM(*one) for one in kept]
    if not near:
        scratch += [pltpu.VMEM((2, channels, inner), jnp.bfloat16)] * 2
        scratch += [pltpu.SemaphoreType.DMA((2, 2))]
    passes = 4 * (int(forward) + int(backward))
    return pl.pallas_call(
        functools.partial(stage_body, step, forward, backward, last, near),
        out_shape=outs,
        in_specs=[VMEM if near else ANY] * 4 + [VMEM] * len(arrays),
        out_specs=[VMEM] * len(outs),
        scratch_shapes=scratch,
        compiler_params=PARAMS if forward else PACKED,
        cost_estimate=pl.CostEstimate(
            flops=2 * passes * rows * channels * inner,
            bytes_accessed=8 * channels * inner,
            transcendentals=passes * rows * channels,
        ),
    )(*weights, *arrays)


def parity(value, mask):
    total, bit = 0, 0
    while mask >> bit:
        if mask >> bit & 1:
            total = total + lax.rem(lax.div(value, 1 << bit), 2)
        bit += 1
    return lax.rem(total, 2)


def halving_plan(size, turn):
    order = [1 << bit for bit in range(size.bit_length() - 1)]
    if turn and len(order) > 1:
        order[:2] = order[1::-1]
    table = [0] * size
    for chunk in range(size):
        place = 0
        for mask in order:
            place = 2 * place + int(chunk & mask != 0)
        table[place] = chunk
    return order, order, table


def side_of(plans, at):
    core, shard = lax.rem(lax.axis_index("pipe"), 2), lax.axis_index("dp")
    return jnp.where(core == 0, parity(shard, plans[0][1][at]), parity(shard, plans[1][1][at]))


def gradient_body(plans, pick_left, pick_right, count, *refs):
    arrays, (send, keep, left, right, full) = refs[:count], refs[count:]
    stage, core, _ = where_am_i(0)
    rows = left.shape[0] // 4
    chunk = send.shape[1]
    for target, pick in ((left, pick_left), (right, pick_right)):
        near, away = pick(arrays)
        for step, part in enumerate(near):

            @pl.when(stage == step)
            def _():
                target[:rows] = part[...]

        for at, part in enumerate(away):
            target[(at + 1) * rows : (at + 2) * rows] = part[...]
    full[...] = contract(left[...], right[...], 0, 0)
    side = side_of(plans, 0)
    half = send.shape[0]
    flip = [plan[2][half] for plan in plans]
    for at in range(half):
        spots = []
        for target_side in (1 - side, side):
            first = plans[0][2][at] ^ (flip[0] * target_side)
            second = plans[1][2][at] ^ (flip[1] * target_side)
            spots.append(pl.multiple_of(jnp.where(core == 0, first, second) * chunk, chunk))
        send[at] = full[pl.ds(spots[0], chunk)].astype(jnp.bfloat16)
        keep[at] = full[pl.ds(spots[1], chunk)]


def halve_body(plans, at, keep_in, came, send, keep):
    half = keep.shape[0]
    side = side_of(plans, at)
    for spot in range(half):
        mine, theirs = side * half + spot, (1 - side) * half + spot
        send[spot] = (keep_in[theirs] + came[theirs].astype(jnp.float32)).astype(jnp.bfloat16)
        keep[spot] = keep_in[mine] + came[mine].astype(jnp.float32)


def bit_of(value, bit):
    return lax.rem(lax.div(value, 1 << bit), 2)


def first_sides():
    core, shard = lax.rem(lax.axis_index("pipe"), 2), lax.axis_index("dp")
    low, high = bit_of(shard, 0), bit_of(shard, 1)
    return core, jnp.where(core == 0, low, high), jnp.where(core == 0, high, low)


def split_columns(wide, keep, send, chunk):
    core, side, _ = first_sides()
    for place in range(wide.shape[1] // (2 * chunk)):
        for target, at in ((keep, side), (send, 1 - side)):
            block = jnp.where(core == 0, 2 * place + at, place // 2 * 4 + 2 * at + place % 2)
            source = pl.ds(pl.multiple_of(block * chunk, chunk), chunk)
            target[:, place * chunk : (place + 1) * chunk] = wide[:, source]


def pack_body(stages, chunk, up, near, far, *refs):
    refs = list(refs)
    left, right, send, wide = refs[-4:]
    channels = wide.shape[1]
    spans = slice(0, channels), slice(channels, None), slice(None)
    flow_span, back_span = (spans[1] if up else spans[0]), spans[2]
    stage, _, _ = where_am_i(0)
    rows = wide.shape[0] // (2 * near + 2 * far)
    start = 0
    targets = (right, wide) if up else (wide, right)
    for target, span in zip(targets, (flow_span, back_span)):
        start = 0
        if near:
            parts = [refs.pop(0) for _ in range(stages + 1)]
            for step in range(stages):

                @pl.when(stage == step)
                def _():
                    target[:rows] = parts[step][0, :, span]

            target[rows : 2 * rows] = parts[stages][:, span]
            start = 2 * rows
        if far:
            for part in (refs.pop(0), refs.pop(0)):
                target[start : start + rows] = part[:, span]
                start += rows
    split_columns(wide, left, send, chunk)
    send[:, channels // 2 :] = right[...]


def near_body(stages, chunk, *refs):
    flows, ups, backs = [refs[at * (stages + 1) : (at + 1) * (stages + 1)] for at in range(3)]
    left_up, right_up, left_inner, right_inner, send, wide = refs[3 * stages + 3 :]
    width = send.shape[1] // 2
    for at, (late, outs) in enumerate(
        ((ups, (left_up, right_up)), (backs, (left_inner, right_inner)))
    ):
        part = send.at[:, at * width : (at + 1) * width]
        pack_body(stages, chunk, at == 0, True, False, *flows, *late, *outs, part, wide)


def half_gradient_body(at, groups, *refs):
    send, keep, full, left, right = refs[3 * groups :]
    start = 0
    for group in range(groups):
        part_left, part_right, came = refs[3 * group : 3 * group + 3]
        rows, columns = part_left.shape
        left[start : start + rows] = part_left[...]
        right[start : start + rows] = part_right[...]
        start += rows
        width = columns + right.shape[1]
        offset = at * width if came.shape[1] > width else 0
        left[start : start + rows] = came[:, offset : offset + columns]
        right[start : start + rows] = came[:, offset + columns : offset + width]
        start += rows
    full[...] = contract(left[...], right[...], 0, 0)
    _, _, side = first_sides()
    chunk = send.shape[1]
    for place in range(send.shape[0]):
        theirs = pl.ds(pl.multiple_of((2 * place + 1 - side) * chunk, chunk), chunk)
        mine = pl.ds(pl.multiple_of((2 * place + side) * chunk, chunk), chunk)
        send[place] = full[theirs].astype(jnp.bfloat16)
        keep[place] = full[mine]


def next_body(bit, keep_in, came, send, keep):
    side = bit_of(lax.axis_index("dp"), bit)
    for place in range(keep.shape[0]):
        theirs, mine = 2 * place + 1 - side, 2 * place + side
        send[place] = (keep_in[theirs] + came[theirs].astype(jnp.float32)).astype(jnp.bfloat16)
        keep[place] = keep_in[mine] + came[mine].astype(jnp.float32)


def finish_body(keep_reduce, came_reduce, keep_expand, came_expand, out):
    out[0, 0] = keep_reduce[0] + came_reduce[0].astype(jnp.float32)
    out[0, 1] = keep_expand[0] + came_expand[0].astype(jnp.float32)


def shards(inputs, cotangent, reduce_weight, expand_weight):
    stages = lax.axis_size("pipe") // 2
    replicas = lax.axis_size("dp")
    stage, core, _ = where_am_i(0)
    channels, inner = reduce_weight.shape[2:]
    rows = inputs.shape[1] * inputs.shape[2] // 2
    sizes = (channels, inner)
    entering = inputs.reshape(2, 2, rows, channels)
    ending = cotangent.reshape(2, 2, rows, channels)
    own = [reduce_weight[:, 0], expand_weight[:, 0]]

    core_pairs = [(p, p ^ 1) for p in range(2 * stages)]
    mirror_pairs = [(p, 2 * (stages - 1 - p // 2) + p % 2) for p in range(2 * stages)]

    def hop(shard, step):
        pairs = []
        for c in range(2):
            pairs.append((2 * step + c, 2 * step + 2 + c))
            pairs.append((2 * (stages - 1 - step) + c, 2 * (stages - 2 - step) + c))
        return lax.ppermute(shard, "pipe", pairs)

    def swap_cores(shard):
        return lax.ppermute(shard, "pipe", core_pairs)

    def mirror(shard):
        return lax.ppermute(shard, "pipe", mirror_pairs)

    at_stage = [stage == step for step in range(stages)]
    first_core = core == 0
    at_stage, first_core, entering = lax.optimization_barrier((at_stage, first_core, entering))

    def pick(parts, mirrored_stage=False):
        tests = at_stage[::-1] if mirrored_stage else at_stage
        chosen = parts[0]
        for test, part in zip(tests[1:], parts[1:]):
            chosen = jnp.where(test, part, chosen)
        return chosen

    in_hbm = lambda array: pltpu.with_memory_space_constraint(array, pltpu.HBM)
    own, entering, ending = [in_hbm(one) for one in own], in_hbm(entering), in_hbm(ending)
    *near, enter = load(0, own, entering)
    near.append(swap_cores(near[0]))
    near.append(swap_cores(near[1]))
    turn = list(load(stages - 1, own))
    turn += [swap_cores(weight) for weight in turn]
    if stages > 2:
        weights = own + [swap_cores(weight) for weight in own]
    flows, trunks, inners = [], [], []
    head = pl.pallas_call(
        head_body,
        out_shape=[
            jax.ShapeDtypeStruct((rows, channels), jnp.bfloat16),
            jax.ShapeDtypeStruct((rows, inner), jnp.float32),
            jax.ShapeDtypeStruct((rows, inner), jnp.bfloat16),
        ],
        in_specs=[VMEM] * 3,
        out_specs=[VMEM] * 3,
        compiler_params=PACKED,
    )(near[0], near[2], enter)
    for step in range(stages - 1):
        arrays = [enter] if step else [enter, *head]
        flow, leave, trunk, inner_sum = run_stage(
            weights if step else near, step, True, False, step == 0, rows, sizes, *arrays
        )
        flows.append(flow)
        trunks.append(trunk)
        inners.append(inner_sum)
        enter = hop(leave, step)
    mirrored = stages == 2
    line = jax.ShapeDtypeStruct((rows, channels), jnp.bfloat16)
    outs = [line, jax.ShapeDtypeStruct((rows, inner), jnp.float32)] + [line, line] * mirrored
    ending, first_active, *known = pl.pallas_call(
        functools.partial(meanwhile_body, stages - 1, mirrored),
        out_shape=outs,
        in_specs=[VMEM, VMEM, HBM, HBM, VMEM],
        out_specs=[VMEM] * len(outs),
        scratch_shapes=[pltpu.SemaphoreType.DMA((3,))],
        compiler_params=PARAMS,
    )(turn[1], turn[3], entering, ending, leave)
    flow, upstreams, back_inners, leave = run_stage(
        turn, stages - 1, True, True, True, rows, sizes, enter, ending, first_active
    )
    flows.append(flow)
    upstreams, back_inners = [upstreams], [back_inners]
    upstream = hop(leave, 0)
    side_flow = swap_cores(pick(flows)[1])
    near_core = lambda first, second: jnp.where(first_core, first, second)
    going = pick(flows, True)
    if mirrored:
        lifted = near_core(going[1, :, :channels], going[0, :, :channels])
        going = jnp.concatenate([lifted, going[0, :, channels:], going[1, :, channels:]], axis=1)
    far_flow = mirror(going)
    if mirrored:
        lifted, actives = far_flow[:, :channels], far_flow[:, channels:]
        far_flow = jnp.concatenate([near_core(known[1], lifted), actives[:, :inner]], axis=1)
        cross_flow = jnp.concatenate([near_core(lifted, known[1]), actives[:, inner:]], axis=1)
    else:
        far_flow, cross_flow = far_flow[0], far_flow[1]
    cross_flow = swap_cores(cross_flow)
    for step in range(stages - 2, -1, -1):
        outs = run_stage(
            weights if step else near,
            step,
            False,
            True,
            step == 0,
            rows,
            sizes,
            upstream,
            trunks[step],
            inners[step],
        )
        upstreams.insert(0, outs[0])
        if step:
            upstream = hop(outs[2], stages - 1 - step)
            back_inners.insert(0, outs[1])
            continue
        tail = pl.pallas_call(
            tail_body,
            out_shape=jax.ShapeDtypeStruct(outs[1].shape, outs[1].dtype),
            in_specs=[VMEM] * 5,
            out_specs=VMEM,
            compiler_params=PACKED,
        )(near[1], near[3], outs[0], outs[1], inners[0])
        back_inners.insert(0, tail)
    going = pick(upstreams, True)
    far_up = mirror(near_core(going[0], going[1]) if mirrored else going)
    far_inner = mirror(pick(back_inners, True))
    side_up = swap_cores(pick(upstreams)[1])
    side_inner = swap_cores(pick(back_inners)[1])
    if mirrored:
        top = jnp.where(at_stage[0], leave, known[0])
        far_up, cross_up = near_core(far_up, top), near_core(top, far_up)
    else:
        far_up, cross_up = far_up[0], far_up[1]
    cross_up = swap_cores(cross_up)
    far_inner, cross_inner = far_inner[0], far_inner[1]
    cross_inner = swap_cores(cross_inner)

    chunk = channels // replicas
    fore = flows + [side_flow, far_flow, cross_flow]
    ups = upstreams + [side_up, far_up, cross_up]
    backs = back_inners + [side_inner, far_inner, cross_inner]
    halve = halve_rows if chunk % 128 == 0 and replicas >= 4 else halve_sums
    parts = halve(stages, replicas, chunk, sizes, rows, fore, ups, backs)
    return pl.pallas_call(
        finish_body,
        out_shape=jax.ShapeDtypeStruct((1, 2, chunk, inner), jnp.float32),
        in_specs=[VMEM] * 4,
        out_specs=VMEM,
        compiler_params=PARAMS,
    )(*parts)


def sums(count, chunk, inner):
    return [
        jax.ShapeDtypeStruct((count, chunk, inner), jnp.bfloat16),
        jax.ShapeDtypeStruct((count, chunk, inner), jnp.float32),
    ]


def exchange(shard, stages, replicas, first, second):
    pairs = []
    for p in range(2 * stages):
        for q in range(replicas):
            pairs.append((p * replicas + q, p * replicas + (q ^ (second if p % 2 else first))))
    return lax.ppermute(shard, AXES, pairs)


def halve_rows(stages, replicas, chunk, sizes, rows, fore, ups, backs):
    channels, inner = sizes
    shape = lambda *dims: jax.ShapeDtypeStruct(dims, jnp.bfloat16)

    def pack(late, up, near, far):
        count = 2 * (near + far)
        arrays = []
        for one in (fore, late):
            arrays += one[: stages + 1] * near + one[stages + 1 :] * far
        return pl.pallas_call(
            functools.partial(pack_body, stages, chunk, up, near, far),
            out_shape=[
                shape(count * rows, channels // 2),
                shape(count * rows, inner),
                shape(count * rows, channels // 2 + inner),
            ],
            in_specs=[VMEM] * len(arrays),
            out_specs=[VMEM] * 3,
            scratch_shapes=[pltpu.VMEM((count * rows, channels), jnp.bfloat16)],
            compiler_params=PARAMS,
        )(*arrays)

    near = fore[: stages + 1] + ups[: stages + 1] + backs[: stages + 1]
    *kept, send = pl.pallas_call(
        functools.partial(near_body, stages, chunk),
        out_shape=[
            shape(2 * rows, channels // 2),
            shape(2 * rows, inner),
            shape(2 * rows, channels // 2),
            shape(2 * rows, inner),
            shape(2 * rows, channels + 2 * inner),
        ],
        in_specs=[VMEM] * len(near),
        out_specs=[VMEM] * 5,
        scratch_shapes=[pltpu.VMEM((2 * rows, channels), jnp.bfloat16)],
        compiler_params=PARAMS,
    )(*near)
    came_near = exchange(send, stages, replicas, 1, 2)
    parts = []
    for at, name, late in ((1, "inner", backs), (0, "up", ups)):
        left, right, send = pack(late, name == "up", False, True)
        came = exchange(send, stages, replicas, 1, 2)
        operands = (kept[2 * at], kept[2 * at + 1], came_near, left, right, came)
        count = replicas // 4
        send, keep = pl.pallas_call(
            functools.partial(half_gradient_body, at, len(operands) // 3),
            out_shape=sums(count, chunk, inner),
            in_specs=[VMEM] * len(operands),
            out_specs=[VMEM] * 2,
            scratch_shapes=[
                pltpu.VMEM((channels // 2, inner), jnp.float32),
                pltpu.VMEM((8 * rows, channels // 2), jnp.bfloat16),
                pltpu.VMEM((8 * rows, inner), jnp.bfloat16),
            ],
            compiler_params=PACKED,
        )(*operands)
        came = exchange(send, stages, replicas, 2, 1)
        for bit in range(2, replicas.bit_length() - 1):
            count //= 2
            send, keep = pl.pallas_call(
                functools.partial(next_body, bit),
                out_shape=sums(count, chunk, inner),
                in_specs=[VMEM] * 2,
                out_specs=[VMEM] * 2,
                compiler_params=PARAMS,
            )(keep, came)
            came = exchange(send, stages, replicas, 1 << bit, 1 << bit)
        parts += [keep, came]
    return parts


def halve_sums(stages, replicas, chunk, sizes, rows, fore, ups, backs):
    channels, inner = sizes
    wide, narrow = slice(0, channels), slice(channels, channels + inner)

    def of_flows(columns):
        def pick_parts(arrays):
            near = [flow.at[0, :, columns] for flow in arrays[:stages]]
            side, far, cross = arrays[stages : stages + 3]
            return near, [side.at[:, columns], far.at[:, columns], cross.at[:, columns]]

        return pick_parts

    def of_backs(arrays):
        near = [back.at[0] for back in arrays[stages + 3 : 2 * stages + 3]]
        side, far, cross = arrays[2 * stages + 3 : 2 * stages + 6]
        return near, [side, far, cross]

    plans = [halving_plan(replicas, turn) for turn in range(2)]
    streams = []
    for pick_left, pick_right, late, plan in (
        (of_backs, of_flows(narrow), ups, plans),
        (of_flows(wide), of_backs, backs, plans[::-1]),
    ):
        arrays = fore + late
        send, keep = pl.pallas_call(
            functools.partial(gradient_body, plan, pick_left, pick_right, len(arrays)),
            out_shape=sums(replicas // 2, chunk, inner),
            in_specs=[VMEM] * len(arrays),
            out_specs=[VMEM] * 2,
            scratch_shapes=[
                pltpu.VMEM((4 * rows, channels), jnp.bfloat16),
                pltpu.VMEM((4 * rows, inner), jnp.bfloat16),
                pltpu.VMEM((channels, inner), jnp.float32),
            ],
            compiler_params=PARAMS,
        )(*arrays)
        streams.append((plan, send, keep))
    for at in range(replicas.bit_length() - 1):
        half = replicas >> (at + 2)
        arrived = []
        for plan, send, keep in streams:
            pairs = []
            for p in range(2 * stages):
                for q in range(replicas):
                    pairs.append((p * replicas + q, p * replicas + (q ^ plan[p % 2][0][at])))
            arrived.append((plan, keep, lax.ppermute(send, AXES, pairs)))
        if half == 0:
            break
        streams = []
        for plan, keep, came in arrived:
            send, keep = pl.pallas_call(
                functools.partial(halve_body, plan, at + 1),
                out_shape=sums(half, chunk, inner),
                in_specs=[VMEM] * 2,
                out_specs=[VMEM] * 2,
                compiler_params=PARAMS,
            )(keep, came)
            streams.append((plan, send, keep))
    (_, keep_expand, came_expand), (_, keep_reduce, came_reduce) = arrived
    return keep_reduce, came_reduce, keep_expand, came_expand


def solution(mesh):
    return jax.shard_map(
        shards,
        mesh=mesh,
        in_specs=(
            P(None, None, "dp", None),
            P(None, None, "dp", None),
            P(None, "pipe", None, None),
            P(None, "pipe", None, None),
        ),
        out_specs=P("pipe", None, "dp", None),
        check_vma=False,
    )
```

```python
import functools

import jax
import jax.numpy as jnp
from jax import lax
from jax.experimental import pallas as pl
from jax.experimental.pallas import tpu as pltpu
from jax.sharding import PartitionSpec as P


EPSILON = 1e-06
AXES = ("pipe", "dp")
HBM = pl.BlockSpec(memory_space=pltpu.HBM)
ANY = pl.BlockSpec(memory_space=pl.ANY)
VMEM = pl.BlockSpec(memory_space=pltpu.VMEM)
PARAMS = pltpu.CompilerParams(vmem_limit_bytes=16 << 20)
PACKED = pltpu.CompilerParams(vmem_limit_bytes=16 << 20)


def contract(first_op, second_op, first_dim, second_dim):
    return lax.dot_general(
        first_op,
        second_op,
        (((first_dim,), (second_dim,)), ((), ())),
        preferred_element_type=jnp.float32,
    )


def smooth_slope(values):
    sigma = jax.nn.sigmoid(values)
    return sigma * (1.0 + values * (1.0 - sigma))


def norm_of(widened):
    return lax.rsqrt(jnp.mean(widened * widened, axis=-1, keepdims=True) + EPSILON)


def where_am_i(step):
    position = lax.axis_index("pipe")
    stage, core = lax.div(position, 2), lax.rem(position, 2)
    way = jnp.where(stage == step, 0, 1)
    return stage, core, way


def bring_all(sources, outs, sems):
    copies = [
        pltpu.make_async_copy(source, out, sems.at[at])
        for at, (source, out) in enumerate(zip(sources, outs))
    ]
    for copy in copies:
        copy.start()
    return copies


def load_body(step, reduce_all, expand_all, *refs):
    _, core, way = where_am_i(step)
    sources, outs = [reduce_all.at[way], expand_all.at[way]], refs[:-1]
    if step == 0:
        sources.append(refs[0].at[way, core])
        outs = outs[1:]
    for copy in bring_all(sources, outs, refs[-1]):
        copy.wait()


def load(step, own, *more):
    channels, inner = own[0].shape[1:]
    mat = jax.ShapeDtypeStruct((channels, inner), jnp.bfloat16)
    outs = [mat, mat] + [jax.ShapeDtypeStruct(a.shape[2:], a.dtype) for a in more]
    return pl.pallas_call(
        functools.partial(load_body, step),
        out_shape=outs,
        in_specs=[HBM] * (2 + len(more)),
        out_specs=[VMEM] * len(outs),
        scratch_shapes=[pltpu.SemaphoreType.DMA((len(outs),))],
        compiler_params=PARAMS,
    )(*own, *more)


def meanwhile_body(step, mirrored, expand_own, expand_other, inputs, cotangent, leave, *refs):
    outs, sems = refs[:-1], refs[-1]
    stage, core, way = where_am_i(step)
    ending, back_active = outs[:2]
    sources = [cotangent.at[way, core]]
    if mirrored:
        sources += [cotangent.at[1, core], inputs.at[1, core]]
    copies = bring_all(sources, [outs[0]] + list(outs[2:]), sems)
    copies[0].wait()

    @pl.when(way == core)
    def _():
        back_active[...] = jnp.dot(
            ending[...], expand_other[...], preferred_element_type=jnp.float32
        )

    @pl.when(way != core)
    def _():
        back_active[...] = jnp.dot(ending[...], expand_own[...], preferred_element_type=jnp.float32)

    for copy in copies[1:]:
        copy.wait()
    if mirrored:
        rows = outs[3]

        @pl.when(stage != 0)
        def _():
            rows[...] = leave[...]

        widened = rows[...].astype(jnp.float32)
        rows[...] = jax.nn.silu(widened * norm_of(widened)).astype(jnp.bfloat16)


def weight_copies(own, other, held, sems, core, way):
    copies = []
    for order in range(2):
        is_own = lax.rem(way + order, 2) == core
        for kind in range(2):
            mine = pltpu.make_async_copy(own[kind].at[way], held[kind].at[order], sems.at[kind, order])
            theirs = pltpu.make_async_copy(
                other[kind].at[way], held[kind].at[order], sems.at[kind, order]
            )
            copies.append((is_own, mine, theirs))
    return copies


def start_all(copies):
    for is_own, mine, theirs in copies:
        pl.when(is_own)(mine.start)
        pl.when(jnp.logical_not(is_own))(theirs.start)


def head_body(own, other, rows_in, lifted_out, inner_out, active_out):
    _, core, way = where_am_i(0)
    widened = rows_in[...].astype(jnp.float32)
    lifted = jax.nn.silu(widened * norm_of(widened)).astype(jnp.bfloat16)
    lifted_out[...] = lifted

    def run(reduce_mat):
        inner_sum = jnp.dot(lifted, reduce_mat[...], preferred_element_type=jnp.float32)
        inner_out[...] = inner_sum
        active_out[...] = jax.nn.silu(inner_sum).astype(jnp.bfloat16)

    pl.when(way == core)(lambda: run(own))
    pl.when(way != core)(lambda: run(other))


def stage_body(step, forward, backward, last, near, *refs):
    refs = list(refs)
    _, core, way = where_am_i(step)
    own, other = (refs.pop(0), refs.pop(0)), (refs.pop(0), refs.pop(0))
    enter = refs.pop(0) if forward else None
    head = [refs.pop(0) for _ in range(3)] if forward and step == 0 else None
    upstream_in = refs.pop(0) if backward else None
    first_active = refs.pop(0) if forward and backward else None
    if not forward:
        trunks, inners = refs.pop(0), refs.pop(0)
    if forward:
        flows = refs.pop(0)
    if forward and not backward:
        leave = refs.pop(0)
    if backward:
        upstreams, back_inners = refs.pop(0), refs.pop(0)
    if backward and not last:
        back_leave = refs.pop(0)
    if forward:
        trunks, inners = refs.pop(0), refs.pop(0)
    channels = trunks.shape[2]

    def run(reduce_mats, expand_mats, wait):
        if forward:
            rows = enter[...]
            for order in range(2):
                slot = lax.rem(order + core, 2)
                widened = rows.astype(jnp.float32)
                trunks[order] = rows
                if head and order == 0:
                    lifted, inner_sum, active = [part[...] for part in head]
                else:
                    normed = widened * norm_of(widened)
                    lifted = jax.nn.silu(normed).astype(jnp.bfloat16)
                    wait(0, order)
                    inner_sum = jnp.dot(
                        lifted, reduce_mats[order][...], preferred_element_type=jnp.float32
                    )
                    active = jax.nn.silu(inner_sum).astype(jnp.bfloat16)
                flows[slot, :, :channels] = lifted
                inners[order] = inner_sum
                flows[slot, :, channels:] = active
                wait(1, order)
                rows = (widened + contract(active, expand_mats[order][...], 1, 1)).astype(jnp.bfloat16)
            if not backward:
                leave[...] = rows
        if backward:
            upstream = upstream_in[...]
            for order in (1, 0):
                slot = lax.rem(order + core, 2)
                upstreams[slot] = upstream
                if last and order == 0:
                    break
                if not forward:
                    wait(1, order)
                if forward and order:
                    back_active = first_active[...]
                else:
                    back_active = jnp.dot(
                        upstream, expand_mats[order][...], preferred_element_type=jnp.float32
                    )
                back_inner = (back_active * smooth_slope(inners[order])).astype(jnp.bfloat16)
                back_inners[slot] = back_inner
                if not forward:
                    wait(0, order)
                back_lifted = contract(back_inner, reduce_mats[order][...], 1, 1)
                widened = trunks[order].astype(jnp.float32)
                norm_scale = norm_of(widened)
                back_normed = back_lifted * smooth_slope(widened * norm_scale)
                projection = jnp.mean(back_normed * widened, axis=-1, keepdims=True)
                upstream = (
                    upstream.astype(jnp.float32)
                    + norm_scale * back_normed
                    - widened * norm_scale**3 * projection
                ).astype(jnp.bfloat16)
            if not last:
                back_leave[...] = upstream

    if near:
        idle = lambda kind, order: None

        @pl.when(way == core)
        def _():
            run((own[0], other[0]), (own[1], other[1]), idle)

        @pl.when(way != core)
        def _():
            run((other[0], own[0]), (other[1], own[1]), idle)

    else:
        held = (refs.pop(0), refs.pop(0))
        copies = weight_copies(own, other, held, refs.pop(0), core, way)
        start_all(copies if forward else copies[2:] + copies[:2])
        run(
            [held[0].at[order] for order in range(2)],
            [held[1].at[order] for order in range(2)],
            lambda kind, order: copies[2 * order + kind][1].wait(),
        )


def tail_body(own, other, upstreams, back_first, inners, back_inners):
    _, core, way = where_am_i(0)

    def run(expand_mat):
        back_active = jnp.dot(upstreams[core], expand_mat[...], preferred_element_type=jnp.float32)
        back_inners[core] = (back_active * smooth_slope(inners[0])).astype(jnp.bfloat16)
        back_inners[1 - core] = back_first[1 - core]

    pl.when(way == core)(lambda: run(own))
    pl.when(way != core)(lambda: run(other))


def run_stage(weights, step, forward, backward, near, rows, sizes, *arrays):
    channels, inner = sizes
    last = backward and step == 0 and not forward
    shape = lambda dtype, *dims: jax.ShapeDtypeStruct(dims, dtype)
    line = shape(jnp.bfloat16, rows, channels)
    kept = [((2, rows, channels), jnp.bfloat16), ((2, rows, inner), jnp.float32)]
    outs, scratch = [], []
    if forward:
        outs.append(shape(jnp.bfloat16, 2, rows, channels + inner))
    if forward and not backward:
        outs.append(line)
    if backward:
        outs.append(shape(jnp.bfloat16, 2, rows, channels))
        outs.append(shape(jnp.bfloat16, 2, rows, inner))
    if backward and not last:
        outs.append(line)
    if forward and not backward:
        outs += [jax.ShapeDtypeStruct(*one) for one in kept]
    if forward and backward:
        scratch += [pltpu.VMEM(*one) for one in kept]
    if not near:
        scratch += [pltpu.VMEM((2, channels, inner), jnp.bfloat16)] * 2
        scratch += [pltpu.SemaphoreType.DMA((2, 2))]
    passes = 4 * (int(forward) + int(backward))
    return pl.pallas_call(
        functools.partial(stage_body, step, forward, backward, last, near),
        out_shape=outs,
        in_specs=[VMEM if near else ANY] * 4 + [VMEM] * len(arrays),
        out_specs=[VMEM] * len(outs),
        scratch_shapes=scratch,
        compiler_params=PARAMS if forward else PACKED,
        cost_estimate=pl.CostEstimate(
            flops=2 * passes * rows * channels * inner,
            bytes_accessed=8 * channels * inner,
            transcendentals=passes * rows * channels,
        ),
    )(*weights, *arrays)


def parity(value, mask):
    total, bit = 0, 0
    while mask >> bit:
        if mask >> bit & 1:
            total = total + lax.rem(lax.div(value, 1 << bit), 2)
        bit += 1
    return lax.rem(total, 2)


def halving_plan(size, turn):
    order = [1 << bit for bit in range(size.bit_length() - 1)]
    if turn and len(order) > 1:
        order[:2] = order[1::-1]
    table = [0] * size
    for chunk in range(size):
        place = 0
        for mask in order:
            place = 2 * place + int(chunk & mask != 0)
        table[place] = chunk
    return order, order, table


def side_of(plans, at):
    core, shard = lax.rem(lax.axis_index("pipe"), 2), lax.axis_index("dp")
    return jnp.where(core == 0, parity(shard, plans[0][1][at]), parity(shard, plans[1][1][at]))


def gradient_body(plans, pick_left, pick_right, count, *refs):
    arrays, (send, keep, left, right, full) = refs[:count], refs[count:]
    stage, core, _ = where_am_i(0)
    rows = left.shape[0] // 4
    chunk = send.shape[1]
    for target, pick in ((left, pick_left), (right, pick_right)):
        near, away = pick(arrays)
        for step, part in enumerate(near):

            @pl.when(stage == step)
            def _():
                target[:rows] = part[...]

        for at, part in enumerate(away):
            target[(at + 1) * rows : (at + 2) * rows] = part[...]
    full[...] = contract(left[...], right[...], 0, 0)
    side = side_of(plans, 0)
    half = send.shape[0]
    flip = [plan[2][half] for plan in plans]
    for at in range(half):
        spots = []
        for target_side in (1 - side, side):
            first = plans[0][2][at] ^ (flip[0] * target_side)
            second = plans[1][2][at] ^ (flip[1] * target_side)
            spots.append(pl.multiple_of(jnp.where(core == 0, first, second) * chunk, chunk))
        send[at] = full[pl.ds(spots[0], chunk)].astype(jnp.bfloat16)
        keep[at] = full[pl.ds(spots[1], chunk)]


def halve_body(plans, at, keep_in, came, send, keep):
    half = keep.shape[0]
    side = side_of(plans, at)
    for spot in range(half):
        mine, theirs = side * half + spot, (1 - side) * half + spot
        send[spot] = (keep_in[theirs] + came[theirs].astype(jnp.float32)).astype(jnp.bfloat16)
        keep[spot] = keep_in[mine] + came[mine].astype(jnp.float32)


def bit_of(value, bit):
    return lax.rem(lax.div(value, 1 << bit), 2)


def first_sides():
    core, shard = lax.rem(lax.axis_index("pipe"), 2), lax.axis_index("dp")
    low, high = bit_of(shard, 0), bit_of(shard, 1)
    return core, jnp.where(core == 0, low, high), jnp.where(core == 0, high, low)


def split_columns(wide, keep, send, chunk):
    core, side, _ = first_sides()
    for place in range(wide.shape[1] // (2 * chunk)):
        for target, at in ((keep, side), (send, 1 - side)):
            block = jnp.where(core == 0, 2 * place + at, place // 2 * 4 + 2 * at + place % 2)
            source = pl.ds(pl.multiple_of(block * chunk, chunk), chunk)
            target[:, place * chunk : (place + 1) * chunk] = wide[:, source]


def pack_body(stages, chunk, up, near, far, *refs):
    refs = list(refs)
    left, right, send, wide = refs[-4:]
    channels = wide.shape[1]
    spans = slice(0, channels), slice(channels, None), slice(None)
    flow_span, back_span = (spans[1] if up else spans[0]), spans[2]
    stage, _, _ = where_am_i(0)
    rows = wide.shape[0] // (2 * near + 2 * far)
    start = 0
    targets = (right, wide) if up else (wide, right)
    for target, span in zip(targets, (flow_span, back_span)):
        start = 0
        if near:
            parts = [refs.pop(0) for _ in range(stages + 1)]
            for step in range(stages):

                @pl.when(stage == step)
                def _():
                    target[:rows] = parts[step][0, :, span]

            target[rows : 2 * rows] = parts[stages][:, span]
            start = 2 * rows
        if far:
            for part in (refs.pop(0), refs.pop(0)):
                target[start : start + rows] = part[:, span]
                start += rows
    split_columns(wide, left, send, chunk)
    send[:, channels // 2 :] = right[...]


def near_body(stages, chunk, *refs):
    flows, ups, backs = [refs[at * (stages + 1) : (at + 1) * (stages + 1)] for at in range(3)]
    left_up, right_up, left_inner, right_inner, send, wide = refs[3 * stages + 3 :]
    width = send.shape[1] // 2
    for at, (late, outs) in enumerate(
        ((ups, (left_up, right_up)), (backs, (left_inner, right_inner)))
    ):
        part = send.at[:, at * width : (at + 1) * width]
        pack_body(stages, chunk, at == 0, True, False, *flows, *late, *outs, part, wide)


def half_gradient_body(at, groups, *refs):
    send, keep, full, left, right = refs[3 * groups :]
    start = 0
    for group in range(groups):
        part_left, part_right, came = refs[3 * group : 3 * group + 3]
        rows, columns = part_left.shape
        left[start : start + rows] = part_left[...]
        right[start : start + rows] = part_right[...]
        start += rows
        width = columns + right.shape[1]
        offset = at * width if came.shape[1] > width else 0
        left[start : start + rows] = came[:, offset : offset + columns]
        right[start : start + rows] = came[:, offset + columns : offset + width]
        start += rows
    full[...] = contract(left[...], right[...], 0, 0)
    _, _, side = first_sides()
    chunk = send.shape[1]
    for place in range(send.shape[0]):
        theirs = pl.ds(pl.multiple_of((2 * place + 1 - side) * chunk, chunk), chunk)
        mine = pl.ds(pl.multiple_of((2 * place + side) * chunk, chunk), chunk)
        send[place] = full[theirs].astype(jnp.bfloat16)
        keep[place] = full[mine]


def next_body(bit, keep_in, came, send, keep):
    side = bit_of(lax.axis_index("dp"), bit)
    for place in range(keep.shape[0]):
        theirs, mine = 2 * place + 1 - side, 2 * place + side
        send[place] = (keep_in[theirs] + came[theirs].astype(jnp.float32)).astype(jnp.bfloat16)
        keep[place] = keep_in[mine] + came[mine].astype(jnp.float32)


def finish_body(keep_reduce, came_reduce, keep_expand, came_expand, out, held, sems):
    copies = []
    for at, keep, came in ((1, keep_expand, came_expand), (0, keep_reduce, came_reduce)):
        held[at] = keep[0] + came[0].astype(jnp.float32)
        copies.append(pltpu.make_async_copy(held.at[at], out.at[0, at], sems.at[at]))
        copies[-1].start()
    for copy in copies:
        copy.wait()


def shards(inputs, cotangent, reduce_weight, expand_weight):
    stages = lax.axis_size("pipe") // 2
    replicas = lax.axis_size("dp")
    stage, core, _ = where_am_i(0)
    channels, inner = reduce_weight.shape[2:]
    rows = inputs.shape[1] * inputs.shape[2] // 2
    sizes = (channels, inner)
    entering = inputs.reshape(2, 2, rows, channels)
    ending = cotangent.reshape(2, 2, rows, channels)
    own = [reduce_weight[:, 0], expand_weight[:, 0]]

    core_pairs = [(p, p ^ 1) for p in range(2 * stages)]
    mirror_pairs = [(p, 2 * (stages - 1 - p // 2) + p % 2) for p in range(2 * stages)]

    def hop(shard, step):
        pairs = []
        for c in range(2):
            pairs.append((2 * step + c, 2 * step + 2 + c))
            pairs.append((2 * (stages - 1 - step) + c, 2 * (stages - 2 - step) + c))
        return lax.ppermute(shard, "pipe", pairs)

    def swap_cores(shard):
        return lax.ppermute(shard, "pipe", core_pairs)

    def mirror(shard):
        return lax.ppermute(shard, "pipe", mirror_pairs)

    at_stage = [stage == step for step in range(stages)]
    first_core = core == 0
    at_stage, first_core, entering = lax.optimization_barrier((at_stage, first_core, entering))

    def pick(parts, mirrored_stage=False):
        tests = at_stage[::-1] if mirrored_stage else at_stage
        chosen = parts[0]
        for test, part in zip(tests[1:], parts[1:]):
            chosen = jnp.where(test, part, chosen)
        return chosen

    in_hbm = lambda array: pltpu.with_memory_space_constraint(array, pltpu.HBM)
    own, entering, ending = [in_hbm(one) for one in own], in_hbm(entering), in_hbm(ending)
    *near, enter = load(0, own, entering)
    near.append(swap_cores(near[0]))
    near.append(swap_cores(near[1]))
    turn = list(load(stages - 1, own))
    turn += [swap_cores(weight) for weight in turn]
    if stages > 2:
        weights = own + [swap_cores(weight) for weight in own]
    flows, trunks, inners = [], [], []
    head = pl.pallas_call(
        head_body,
        out_shape=[
            jax.ShapeDtypeStruct((rows, channels), jnp.bfloat16),
            jax.ShapeDtypeStruct((rows, inner), jnp.float32),
            jax.ShapeDtypeStruct((rows, inner), jnp.bfloat16),
        ],
        in_specs=[VMEM] * 3,
        out_specs=[VMEM] * 3,
        compiler_params=PACKED,
    )(near[0], near[2], enter)
    for step in range(stages - 1):
        arrays = [enter] if step else [enter, *head]
        flow, leave, trunk, inner_sum = run_stage(
            weights if step else near, step, True, False, step == 0, rows, sizes, *arrays
        )
        flows.append(flow)
        trunks.append(trunk)
        inners.append(inner_sum)
        enter = hop(leave, step)
    mirrored = stages == 2
    line = jax.ShapeDtypeStruct((rows, channels), jnp.bfloat16)
    outs = [line, jax.ShapeDtypeStruct((rows, inner), jnp.float32)] + [line, line] * mirrored
    ending, first_active, *known = pl.pallas_call(
        functools.partial(meanwhile_body, stages - 1, mirrored),
        out_shape=outs,
        in_specs=[VMEM, VMEM, HBM, HBM, VMEM],
        out_specs=[VMEM] * len(outs),
        scratch_shapes=[pltpu.SemaphoreType.DMA((3,))],
        compiler_params=PARAMS,
    )(turn[1], turn[3], entering, ending, leave)
    flow, upstreams, back_inners, leave = run_stage(
        turn, stages - 1, True, True, True, rows, sizes, enter, ending, first_active
    )
    flows.append(flow)
    upstreams, back_inners = [upstreams], [back_inners]
    upstream = hop(leave, 0)
    side_flow = swap_cores(pick(flows)[1])
    near_core = lambda first, second: jnp.where(first_core, first, second)
    going = pick(flows, True)
    if mirrored:
        lifted = near_core(going[1, :, :channels], going[0, :, :channels])
        going = jnp.concatenate([lifted, going[0, :, channels:], going[1, :, channels:]], axis=1)
    far_flow = mirror(going)
    if mirrored:
        lifted, actives = far_flow[:, :channels], far_flow[:, channels:]
        far_flow = jnp.concatenate([near_core(known[1], lifted), actives[:, :inner]], axis=1)
        cross_flow = jnp.concatenate([near_core(lifted, known[1]), actives[:, inner:]], axis=1)
    else:
        far_flow, cross_flow = far_flow[0], far_flow[1]
    cross_flow = swap_cores(cross_flow)
    for step in range(stages - 2, -1, -1):
        outs = run_stage(
            weights if step else near,
            step,
            False,
            True,
            step == 0,
            rows,
            sizes,
            upstream,
            trunks[step],
            inners[step],
        )
        upstreams.insert(0, outs[0])
        if step:
            upstream = hop(outs[2], stages - 1 - step)
            back_inners.insert(0, outs[1])
            continue
        tail = pl.pallas_call(
            tail_body,
            out_shape=jax.ShapeDtypeStruct(outs[1].shape, outs[1].dtype),
            in_specs=[VMEM] * 5,
            out_specs=VMEM,
            compiler_params=PACKED,
        )(near[1], near[3], outs[0], outs[1], inners[0])
        back_inners.insert(0, tail)
    going = pick(upstreams, True)
    far_up = mirror(near_core(going[0], going[1]) if mirrored else going)
    far_inner = mirror(pick(back_inners, True))
    side = [pick(upstreams)[1], pick(back_inners)[1]]
    side = swap_cores(jnp.concatenate(side, axis=1))
    side_up, side_inner = side[:, :channels], side[:, channels:]
    if mirrored:
        top = jnp.where(at_stage[0], leave, known[0])
        far_up, cross_up = near_core(far_up, top), near_core(top, far_up)
    else:
        far_up, cross_up = far_up[0], far_up[1]
    cross_up = swap_cores(cross_up)
    far_inner, cross_inner = far_inner[0], far_inner[1]
    cross_inner = swap_cores(cross_inner)

    chunk = channels // replicas
    fore = flows + [side_flow, far_flow, cross_flow]
    ups = upstreams + [side_up, far_up, cross_up]
    backs = back_inners + [side_inner, far_inner, cross_inner]
    halve = halve_rows if chunk % 128 == 0 and replicas >= 4 else halve_sums
    parts = halve(stages, replicas, chunk, sizes, rows, fore, ups, backs)
    return pl.pallas_call(
        finish_body,
        out_shape=jax.ShapeDtypeStruct((1, 2, chunk, inner), jnp.float32),
        in_specs=[VMEM] * 4,
        out_specs=HBM,
        scratch_shapes=[
            pltpu.VMEM((2, chunk, inner), jnp.float32),
            pltpu.SemaphoreType.DMA((2,)),
        ],
        compiler_params=PARAMS,
    )(*parts)


def sums(count, chunk, inner):
    return [
        jax.ShapeDtypeStruct((count, chunk, inner), jnp.bfloat16),
        jax.ShapeDtypeStruct((count, chunk, inner), jnp.float32),
    ]


def exchange(shard, stages, replicas, first, second):
    pairs = []
    for p in range(2 * stages):
        for q in range(replicas):
            pairs.append((p * replicas + q, p * replicas + (q ^ (second if p % 2 else first))))
    return lax.ppermute(shard, AXES, pairs)


def halve_rows(stages, replicas, chunk, sizes, rows, fore, ups, backs):
    channels, inner = sizes
    shape = lambda *dims: jax.ShapeDtypeStruct(dims, jnp.bfloat16)

    def pack(late, up, near, far):
        count = 2 * (near + far)
        arrays = []
        for one in (fore, late):
            arrays += one[: stages + 1] * near + one[stages + 1 :] * far
        return pl.pallas_call(
            functools.partial(pack_body, stages, chunk, up, near, far),
            out_shape=[
                shape(count * rows, channels // 2),
                shape(count * rows, inner),
                shape(count * rows, channels // 2 + inner),
            ],
            in_specs=[VMEM] * len(arrays),
            out_specs=[VMEM] * 3,
            scratch_shapes=[pltpu.VMEM((count * rows, channels), jnp.bfloat16)],
            compiler_params=PARAMS,
        )(*arrays)

    near = fore[: stages + 1] + ups[: stages + 1] + backs[: stages + 1]
    *kept, send = pl.pallas_call(
        functools.partial(near_body, stages, chunk),
        out_shape=[
            shape(2 * rows, channels // 2),
            shape(2 * rows, inner),
            shape(2 * rows, channels // 2),
            shape(2 * rows, inner),
            shape(2 * rows, channels + 2 * inner),
        ],
        in_specs=[VMEM] * len(near),
        out_specs=[VMEM] * 5,
        scratch_shapes=[pltpu.VMEM((2 * rows, channels), jnp.bfloat16)],
        compiler_params=PARAMS,
    )(*near)
    came_near = exchange(send, stages, replicas, 1, 2)
    parts = []
    for at, name, late in ((1, "inner", backs), (0, "up", ups)):
        left, right, send = pack(late, name == "up", False, True)
        came = exchange(send, stages, replicas, 1, 2)
        operands = (kept[2 * at], kept[2 * at + 1], came_near, left, right, came)
        count = replicas // 4
        send, keep = pl.pallas_call(
            functools.partial(half_gradient_body, at, len(operands) // 3),
            out_shape=sums(count, chunk, inner),
            in_specs=[VMEM] * len(operands),
            out_specs=[VMEM] * 2,
            scratch_shapes=[
                pltpu.VMEM((channels // 2, inner), jnp.float32),
                pltpu.VMEM((8 * rows, channels // 2), jnp.bfloat16),
                pltpu.VMEM((8 * rows, inner), jnp.bfloat16),
            ],
            compiler_params=PACKED,
        )(*operands)
        came = exchange(send, stages, replicas, 2, 1)
        for bit in range(2, replicas.bit_length() - 1):
            count //= 2
            send, keep = pl.pallas_call(
                functools.partial(next_body, bit),
                out_shape=sums(count, chunk, inner),
                in_specs=[VMEM] * 2,
                out_specs=[VMEM] * 2,
                compiler_params=PARAMS,
            )(keep, came)
            came = exchange(send, stages, replicas, 1 << bit, 1 << bit)
        parts += [keep, came]
    return parts


def halve_sums(stages, replicas, chunk, sizes, rows, fore, ups, backs):
    channels, inner = sizes
    wide, narrow = slice(0, channels), slice(channels, channels + inner)

    def of_flows(columns):
        def pick_parts(arrays):
            near = [flow.at[0, :, columns] for flow in arrays[:stages]]
            side, far, cross = arrays[stages : stages + 3]
            return near, [side.at[:, columns], far.at[:, columns], cross.at[:, columns]]

        return pick_parts

    def of_backs(arrays):
        near = [back.at[0] for back in arrays[stages + 3 : 2 * stages + 3]]
        side, far, cross = arrays[2 * stages + 3 : 2 * stages + 6]
        return near, [side, far, cross]

    plans = [halving_plan(replicas, turn) for turn in range(2)]
    streams = []
    for pick_left, pick_right, late, plan in (
        (of_backs, of_flows(narrow), ups, plans),
        (of_flows(wide), of_backs, backs, plans[::-1]),
    ):
        arrays = fore + late
        send, keep = pl.pallas_call(
            functools.partial(gradient_body, plan, pick_left, pick_right, len(arrays)),
            out_shape=sums(replicas // 2, chunk, inner),
            in_specs=[VMEM] * len(arrays),
            out_specs=[VMEM] * 2,
            scratch_shapes=[
                pltpu.VMEM((4 * rows, channels), jnp.bfloat16),
                pltpu.VMEM((4 * rows, inner), jnp.bfloat16),
                pltpu.VMEM((channels, inner), jnp.float32),
            ],
            compiler_params=PARAMS,
        )(*arrays)
        streams.append((plan, send, keep))
    for at in range(replicas.bit_length() - 1):
        half = replicas >> (at + 2)
        arrived = []
        for plan, send, keep in streams:
            pairs = []
            for p in range(2 * stages):
                for q in range(replicas):
                    pairs.append((p * replicas + q, p * replicas + (q ^ plan[p % 2][0][at])))
            arrived.append((plan, keep, lax.ppermute(send, AXES, pairs)))
        if half == 0:
            break
        streams = []
        for plan, keep, came in arrived:
            send, keep = pl.pallas_call(
                functools.partial(halve_body, plan, at + 1),
                out_shape=sums(half, chunk, inner),
                in_specs=[VMEM] * 2,
                out_specs=[VMEM] * 2,
                compiler_params=PARAMS,
            )(keep, came)
            streams.append((plan, send, keep))
    (_, keep_expand, came_expand), (_, keep_reduce, came_reduce) = arrived
    return keep_reduce, came_reduce, keep_expand, came_expand


def solution(mesh):
    return jax.shard_map(
        shards,
        mesh=mesh,
        in_specs=(
            P(None, None, "dp", None),
            P(None, None, "dp", None),
            P(None, "pipe", None, None),
            P(None, "pipe", None, None),
        ),
        out_specs=P("pipe", None, "dp", None),
        check_vma=False,
    )
```

```python
import functools

import jax
import jax.numpy as jnp
from jax import lax
from jax.experimental import pallas as pl
from jax.experimental.pallas import tpu as pltpu
from jax.sharding import PartitionSpec as P


EPSILON = 1e-06
AXES = ("pipe", "dp")
HBM = pl.BlockSpec(memory_space=pltpu.HBM)
ANY = pl.BlockSpec(memory_space=pl.ANY)
VMEM = pl.BlockSpec(memory_space=pltpu.VMEM)
PARAMS = pltpu.CompilerParams(vmem_limit_bytes=16 << 20)
PACKED = pltpu.CompilerParams(vmem_limit_bytes=16 << 20)


def contract(first_op, second_op, first_dim, second_dim):
    return lax.dot_general(
        first_op,
        second_op,
        (((first_dim,), (second_dim,)), ((), ())),
        preferred_element_type=jnp.float32,
    )


def smooth_slope(values):
    sigma = jax.nn.sigmoid(values)
    return sigma * (1.0 + values * (1.0 - sigma))


def norm_of(widened):
    return lax.rsqrt(jnp.mean(widened * widened, axis=-1, keepdims=True) + EPSILON)


def where_am_i(step):
    position = lax.axis_index("pipe")
    stage, core = lax.div(position, 2), lax.rem(position, 2)
    way = jnp.where(stage == step, 0, 1)
    return stage, core, way


def bring_all(sources, outs, sems):
    copies = [
        pltpu.make_async_copy(source, out, sems.at[at])
        for at, (source, out) in enumerate(zip(sources, outs))
    ]
    for copy in copies:
        copy.start()
    return copies


def load_body(step, reduce_all, expand_all, *refs):
    _, core, way = where_am_i(step)
    sources, outs = [reduce_all.at[way], expand_all.at[way]], refs[:-1]
    if step == 0:
        sources.append(refs[0].at[way, core])
        outs = outs[1:]
    for copy in bring_all(sources, outs, refs[-1]):
        copy.wait()


def load(step, own, *more):
    channels, inner = own[0].shape[1:]
    mat = jax.ShapeDtypeStruct((channels, inner), jnp.bfloat16)
    outs = [mat, mat] + [jax.ShapeDtypeStruct(a.shape[2:], a.dtype) for a in more]
    return pl.pallas_call(
        functools.partial(load_body, step),
        out_shape=outs,
        in_specs=[HBM] * (2 + len(more)),
        out_specs=[VMEM] * len(outs),
        scratch_shapes=[pltpu.SemaphoreType.DMA((len(outs),))],
        compiler_params=PARAMS,
    )(*own, *more)


def meanwhile_body(step, mirrored, expand_own, expand_other, inputs, cotangent, leave, *refs):
    outs, sems = refs[:-1], refs[-1]
    stage, core, way = where_am_i(step)
    ending, back_active = outs[:2]
    sources = [cotangent.at[way, core]]
    if mirrored:
        sources += [cotangent.at[1, core], inputs.at[1, core]]
    copies = bring_all(sources, [outs[0]] + list(outs[2:]), sems)
    copies[0].wait()

    @pl.when(way == core)
    def _():
        back_active[...] = jnp.dot(
            ending[...], expand_other[...], preferred_element_type=jnp.float32
        )

    @pl.when(way != core)
    def _():
        back_active[...] = jnp.dot(ending[...], expand_own[...], preferred_element_type=jnp.float32)

    for copy in copies[1:]:
        copy.wait()
    if mirrored:
        rows = outs[3]

        @pl.when(stage != 0)
        def _():
            rows[...] = leave[...]

        widened = rows[...].astype(jnp.float32)
        rows[...] = jax.nn.silu(widened * norm_of(widened)).astype(jnp.bfloat16)


def weight_copies(own, other, held, sems, core, way):
    copies = []
    for order in range(2):
        is_own = lax.rem(way + order, 2) == core
        for kind in range(2):
            mine = pltpu.make_async_copy(own[kind].at[way], held[kind].at[order], sems.at[kind, order])
            theirs = pltpu.make_async_copy(
                other[kind].at[way], held[kind].at[order], sems.at[kind, order]
            )
            copies.append((is_own, mine, theirs))
    return copies


def start_all(copies):
    for is_own, mine, theirs in copies:
        pl.when(is_own)(mine.start)
        pl.when(jnp.logical_not(is_own))(theirs.start)


def head_body(own, other, rows_in, lifted_out, inner_out, active_out):
    _, core, way = where_am_i(0)
    widened = rows_in[...].astype(jnp.float32)
    lifted = jax.nn.silu(widened * norm_of(widened)).astype(jnp.bfloat16)
    lifted_out[...] = lifted

    def run(reduce_mat):
        inner_sum = jnp.dot(lifted, reduce_mat[...], preferred_element_type=jnp.float32)
        inner_out[...] = inner_sum
        active_out[...] = jax.nn.silu(inner_sum).astype(jnp.bfloat16)

    pl.when(way == core)(lambda: run(own))
    pl.when(way != core)(lambda: run(other))


def stage_body(step, forward, backward, last, near, *refs):
    refs = list(refs)
    _, core, way = where_am_i(step)
    own, other = (refs.pop(0), refs.pop(0)), (refs.pop(0), refs.pop(0))
    enter = refs.pop(0) if forward else None
    head = [refs.pop(0) for _ in range(3)] if forward and step == 0 else None
    upstream_in = refs.pop(0) if backward else None
    first_active = refs.pop(0) if forward and backward else None
    if not forward:
        trunks, inners = refs.pop(0), refs.pop(0)
    if forward:
        flows = refs.pop(0)
    if forward and not backward:
        leave = refs.pop(0)
    if backward:
        upstreams, back_inners = refs.pop(0), refs.pop(0)
    if backward and not last:
        back_leave = refs.pop(0)
    if forward:
        trunks, inners = refs.pop(0), refs.pop(0)
    channels = trunks.shape[2]

    def run(reduce_mats, expand_mats, wait):
        if forward:
            rows = enter[...]
            for order in range(2):
                slot = lax.rem(order + core, 2)
                widened = rows.astype(jnp.float32)
                trunks[order] = rows
                if head and order == 0:
                    lifted, inner_sum, active = [part[...] for part in head]
                else:
                    normed = widened * norm_of(widened)
                    lifted = jax.nn.silu(normed).astype(jnp.bfloat16)
                    wait(0, order)
                    inner_sum = jnp.dot(
                        lifted, reduce_mats[order][...], preferred_element_type=jnp.float32
                    )
                    active = jax.nn.silu(inner_sum).astype(jnp.bfloat16)
                flows[slot, :, :channels] = lifted
                inners[order] = inner_sum
                flows[slot, :, channels:] = active
                wait(1, order)
                rows = (widened + contract(active, expand_mats[order][...], 1, 1)).astype(jnp.bfloat16)
            if not backward:
                leave[...] = rows
        if backward:
            upstream = upstream_in[...]
            for order in (1, 0):
                slot = lax.rem(order + core, 2)
                upstreams[slot] = upstream
                if last and order == 0:
                    break
                if not forward:
                    wait(1, order)
                if forward and order:
                    back_active = first_active[...]
                else:
                    back_active = jnp.dot(
                        upstream, expand_mats[order][...], preferred_element_type=jnp.float32
                    )
                back_inner = (back_active * smooth_slope(inners[order])).astype(jnp.bfloat16)
                back_inners[slot] = back_inner
                if not forward:
                    wait(0, order)
                back_lifted = contract(back_inner, reduce_mats[order][...], 1, 1)
                widened = trunks[order].astype(jnp.float32)
                norm_scale = norm_of(widened)
                back_normed = back_lifted * smooth_slope(widened * norm_scale)
                projection = jnp.mean(back_normed * widened, axis=-1, keepdims=True)
                upstream = (
                    upstream.astype(jnp.float32)
                    + norm_scale * back_normed
                    - widened * norm_scale**3 * projection
                ).astype(jnp.bfloat16)
            if not last:
                back_leave[...] = upstream

    if near:
        idle = lambda kind, order: None

        @pl.when(way == core)
        def _():
            run((own[0], other[0]), (own[1], other[1]), idle)

        @pl.when(way != core)
        def _():
            run((other[0], own[0]), (other[1], own[1]), idle)

    else:
        held = (refs.pop(0), refs.pop(0))
        copies = weight_copies(own, other, held, refs.pop(0), core, way)
        start_all(copies if forward else copies[2:] + copies[:2])
        run(
            [held[0].at[order] for order in range(2)],
            [held[1].at[order] for order in range(2)],
            lambda kind, order: copies[2 * order + kind][1].wait(),
        )


def tail_body(own, other, upstreams, back_first, inners, back_inners):
    _, core, way = where_am_i(0)

    def run(expand_mat):
        back_active = jnp.dot(upstreams[core], expand_mat[...], preferred_element_type=jnp.float32)
        back_inners[core] = (back_active * smooth_slope(inners[0])).astype(jnp.bfloat16)
        back_inners[1 - core] = back_first[1 - core]

    pl.when(way == core)(lambda: run(own))
    pl.when(way != core)(lambda: run(other))


def run_stage(weights, step, forward, backward, near, rows, sizes, *arrays):
    channels, inner = sizes
    last = backward and step == 0 and not forward
    shape = lambda dtype, *dims: jax.ShapeDtypeStruct(dims, dtype)
    line = shape(jnp.bfloat16, rows, channels)
    kept = [((2, rows, channels), jnp.bfloat16), ((2, rows, inner), jnp.float32)]
    outs, scratch = [], []
    if forward:
        outs.append(shape(jnp.bfloat16, 2, rows, channels + inner))
    if forward and not backward:
        outs.append(line)
    if backward:
        outs.append(shape(jnp.bfloat16, 2, rows, channels))
        outs.append(shape(jnp.bfloat16, 2, rows, inner))
    if backward and not last:
        outs.append(line)
    if forward and not backward:
        outs += [jax.ShapeDtypeStruct(*one) for one in kept]
    if forward and backward:
        scratch += [pltpu.VMEM(*one) for one in kept]
    if not near:
        scratch += [pltpu.VMEM((2, channels, inner), jnp.bfloat16)] * 2
        scratch += [pltpu.SemaphoreType.DMA((2, 2))]
    passes = 4 * (int(forward) + int(backward))
    return pl.pallas_call(
        functools.partial(stage_body, step, forward, backward, last, near),
        out_shape=outs,
        in_specs=[VMEM if near else ANY] * 4 + [VMEM] * len(arrays),
        out_specs=[VMEM] * len(outs),
        scratch_shapes=scratch,
        compiler_params=PARAMS if forward else PACKED,
        cost_estimate=pl.CostEstimate(
            flops=2 * passes * rows * channels * inner,
            bytes_accessed=8 * channels * inner,
            transcendentals=passes * rows * channels,
        ),
    )(*weights, *arrays)


def parity(value, mask):
    total, bit = 0, 0
    while mask >> bit:
        if mask >> bit & 1:
            total = total + lax.rem(lax.div(value, 1 << bit), 2)
        bit += 1
    return lax.rem(total, 2)


def halving_plan(size, turn):
    order = [1 << bit for bit in range(size.bit_length() - 1)]
    if turn and len(order) > 1:
        order[:2] = order[1::-1]
    table = [0] * size
    for chunk in range(size):
        place = 0
        for mask in order:
            place = 2 * place + int(chunk & mask != 0)
        table[place] = chunk
    return order, order, table


def side_of(plans, at):
    core, shard = lax.rem(lax.axis_index("pipe"), 2), lax.axis_index("dp")
    return jnp.where(core == 0, parity(shard, plans[0][1][at]), parity(shard, plans[1][1][at]))


def gradient_body(plans, pick_left, pick_right, count, *refs):
    arrays, (send, keep, left, right, full) = refs[:count], refs[count:]
    stage, core, _ = where_am_i(0)
    rows = left.shape[0] // 4
    chunk = send.shape[1]
    for target, pick in ((left, pick_left), (right, pick_right)):
        near, away = pick(arrays)
        for step, part in enumerate(near):

            @pl.when(stage == step)
            def _():
                target[:rows] = part[...]

        for at, part in enumerate(away):
            target[(at + 1) * rows : (at + 2) * rows] = part[...]
    full[...] = contract(left[...], right[...], 0, 0)
    side = side_of(plans, 0)
    half = send.shape[0]
    flip = [plan[2][half] for plan in plans]
    for at in range(half):
        spots = []
        for target_side in (1 - side, side):
            first = plans[0][2][at] ^ (flip[0] * target_side)
            second = plans[1][2][at] ^ (flip[1] * target_side)
            spots.append(pl.multiple_of(jnp.where(core == 0, first, second) * chunk, chunk))
        send[at] = full[pl.ds(spots[0], chunk)].astype(jnp.bfloat16)
        keep[at] = full[pl.ds(spots[1], chunk)]


def halve_body(plans, at, keep_in, came, send, keep):
    half = keep.shape[0]
    side = side_of(plans, at)
    for spot in range(half):
        mine, theirs = side * half + spot, (1 - side) * half + spot
        send[spot] = (keep_in[theirs] + came[theirs].astype(jnp.float32)).astype(jnp.bfloat16)
        keep[spot] = keep_in[mine] + came[mine].astype(jnp.float32)


def bit_of(value, bit):
    return lax.rem(lax.div(value, 1 << bit), 2)


def first_sides():
    core, shard = lax.rem(lax.axis_index("pipe"), 2), lax.axis_index("dp")
    low, high = bit_of(shard, 0), bit_of(shard, 1)
    return core, jnp.where(core == 0, low, high), jnp.where(core == 0, high, low)


def split_columns(wide, keep, send, chunk):
    core, side, _ = first_sides()
    for place in range(wide.shape[1] // (2 * chunk)):
        for target, at in ((keep, side), (send, 1 - side)):
            block = jnp.where(core == 0, 2 * place + at, place // 2 * 4 + 2 * at + place % 2)
            source = pl.ds(pl.multiple_of(block * chunk, chunk), chunk)
            target[:, place * chunk : (place + 1) * chunk] = wide[:, source]


def pack_body(stages, chunk, up, near, far, *refs):
    refs = list(refs)
    left, right, send, wide = refs[-4:]
    channels = wide.shape[1]
    spans = slice(0, channels), slice(channels, None), slice(None)
    flow_span, back_span = (spans[1] if up else spans[0]), spans[2]
    stage, _, _ = where_am_i(0)
    rows = wide.shape[0] // (2 * near + 2 * far)
    start = 0
    targets = (right, wide) if up else (wide, right)
    for target, span in zip(targets, (flow_span, back_span)):
        start = 0
        if near:
            parts = [refs.pop(0) for _ in range(stages + 1)]
            for step in range(stages):

                @pl.when(stage == step)
                def _():
                    target[:rows] = parts[step][0, :, span]

            target[rows : 2 * rows] = parts[stages][:, span]
            start = 2 * rows
        if far:
            for part in (refs.pop(0), refs.pop(0)):
                target[start : start + rows] = part[:, span]
                start += rows
    split_columns(wide, left, send, chunk)
    send[:, channels // 2 :] = right[...]


def near_body(stages, chunk, *refs):
    flows, ups, backs = [refs[at * (stages + 1) : (at + 1) * (stages + 1)] for at in range(3)]
    left_up, right_up, left_inner, right_inner, send, wide = refs[3 * stages + 3 :]
    width = send.shape[1] // 2
    for at, (late, outs) in enumerate(
        ((ups, (left_up, right_up)), (backs, (left_inner, right_inner)))
    ):
        part = send.at[:, at * width : (at + 1) * width]
        pack_body(stages, chunk, at == 0, True, False, *flows, *late, *outs, part, wide)


def half_gradient_body(at, groups, *refs):
    send, keep, full, left, right = refs[3 * groups :]
    start = 0
    for group in range(groups):
        part_left, part_right, came = refs[3 * group : 3 * group + 3]
        rows, columns = part_left.shape
        left[start : start + rows] = part_left[...]
        right[start : start + rows] = part_right[...]
        start += rows
        width = columns + right.shape[1]
        offset = at * width if came.shape[1] > width else 0
        left[start : start + rows] = came[:, offset : offset + columns]
        right[start : start + rows] = came[:, offset + columns : offset + width]
        start += rows
    full[...] = contract(left[...], right[...], 0, 0)
    _, _, side = first_sides()
    chunk = send.shape[1]
    for place in range(send.shape[0]):
        theirs = pl.ds(pl.multiple_of((2 * place + 1 - side) * chunk, chunk), chunk)
        mine = pl.ds(pl.multiple_of((2 * place + side) * chunk, chunk), chunk)
        send[place] = full[theirs].astype(jnp.bfloat16)
        keep[place] = full[mine]


def next_body(bit, keep_in, came, send, keep):
    side = bit_of(lax.axis_index("dp"), bit)
    for place in range(keep.shape[0]):
        theirs, mine = 2 * place + 1 - side, 2 * place + side
        send[place] = (keep_in[theirs] + came[theirs].astype(jnp.float32)).astype(jnp.bfloat16)
        keep[place] = keep_in[mine] + came[mine].astype(jnp.float32)


def finish_body(keep_reduce, came_reduce, keep_expand, came_expand, out, held, sems):
    copies = []
    for at, keep, came in ((1, keep_expand, came_expand), (0, keep_reduce, came_reduce)):
        held[at] = keep[0] + came[0].astype(jnp.float32)
        copies.append(pltpu.make_async_copy(held.at[at], out.at[0, at], sems.at[at]))
        copies[-1].start()
    for copy in copies:
        copy.wait()


def shards(inputs, cotangent, reduce_weight, expand_weight):
    stages = lax.axis_size("pipe") // 2
    replicas = lax.axis_size("dp")
    stage, core, _ = where_am_i(0)
    channels, inner = reduce_weight.shape[2:]
    rows = inputs.shape[1] * inputs.shape[2] // 2
    sizes = (channels, inner)
    entering = inputs.reshape(2, 2, rows, channels)
    ending = cotangent.reshape(2, 2, rows, channels)
    own = [reduce_weight[:, 0], expand_weight[:, 0]]

    core_pairs = [(p, p ^ 1) for p in range(2 * stages)]
    mirror_pairs = [(p, 2 * (stages - 1 - p // 2) + p % 2) for p in range(2 * stages)]

    def hop(shard, step):
        pairs = []
        for c in range(2):
            pairs.append((2 * step + c, 2 * step + 2 + c))
            pairs.append((2 * (stages - 1 - step) + c, 2 * (stages - 2 - step) + c))
        return lax.ppermute(shard, "pipe", pairs)

    def swap_cores(shard):
        return lax.ppermute(shard, "pipe", core_pairs)

    def mirror(shard):
        return lax.ppermute(shard, "pipe", mirror_pairs)

    at_stage = [stage == step for step in range(stages)]
    first_core = core == 0
    at_stage, first_core, entering = lax.optimization_barrier((at_stage, first_core, entering))

    def pick(parts, mirrored_stage=False):
        tests = at_stage[::-1] if mirrored_stage else at_stage
        chosen = parts[0]
        for test, part in zip(tests[1:], parts[1:]):
            chosen = jnp.where(test, part, chosen)
        return chosen

    in_hbm = lambda array: pltpu.with_memory_space_constraint(array, pltpu.HBM)
    own, entering, ending = [in_hbm(one) for one in own], in_hbm(entering), in_hbm(ending)
    *near, enter = load(0, own, entering)
    near.append(swap_cores(near[0]))
    near.append(swap_cores(near[1]))
    turn = list(load(stages - 1, own))
    turn += [swap_cores(weight) for weight in turn]
    if stages > 2:
        weights = own + [swap_cores(weight) for weight in own]
    flows, trunks, inners = [], [], []
    head = pl.pallas_call(
        head_body,
        out_shape=[
            jax.ShapeDtypeStruct((rows, channels), jnp.bfloat16),
            jax.ShapeDtypeStruct((rows, inner), jnp.float32),
            jax.ShapeDtypeStruct((rows, inner), jnp.bfloat16),
        ],
        in_specs=[VMEM] * 3,
        out_specs=[VMEM] * 3,
        compiler_params=PACKED,
    )(near[0], near[2], enter)
    for step in range(stages - 1):
        arrays = [enter] if step else [enter, *head]
        flow, leave, trunk, inner_sum = run_stage(
            weights if step else near, step, True, False, step == 0, rows, sizes, *arrays
        )
        flows.append(flow)
        trunks.append(trunk)
        inners.append(inner_sum)
        enter = hop(leave, step)
    mirrored = stages == 2
    line = jax.ShapeDtypeStruct((rows, channels), jnp.bfloat16)
    outs = [line, jax.ShapeDtypeStruct((rows, inner), jnp.float32)] + [line, line] * mirrored
    ending, first_active, *known = pl.pallas_call(
        functools.partial(meanwhile_body, stages - 1, mirrored),
        out_shape=outs,
        in_specs=[VMEM, VMEM, HBM, HBM, VMEM],
        out_specs=[VMEM] * len(outs),
        scratch_shapes=[pltpu.SemaphoreType.DMA((3,))],
        compiler_params=PARAMS,
    )(turn[1], turn[3], entering, ending, leave)
    flow, upstreams, back_inners, leave = run_stage(
        turn, stages - 1, True, True, True, rows, sizes, enter, ending, first_active
    )
    flows.append(flow)
    upstreams, back_inners = [upstreams], [back_inners]
    upstream = hop(leave, 0)
    side_flow = swap_cores(pick(flows)[1])
    near_core = lambda first, second: jnp.where(first_core, first, second)
    going = pick(flows, True)
    if mirrored:
        lifted = near_core(going[1, :, :channels], going[0, :, :channels])
        going = jnp.concatenate([lifted, going[0, :, channels:], going[1, :, channels:]], axis=1)
    far_flow = mirror(going)
    if mirrored:
        lifted, actives = far_flow[:, :channels], far_flow[:, channels:]
        far_flow = jnp.concatenate([near_core(known[1], lifted), actives[:, :inner]], axis=1)
        cross_flow = jnp.concatenate([near_core(lifted, known[1]), actives[:, inner:]], axis=1)
    else:
        far_flow, cross_flow = far_flow[0], far_flow[1]
    cross_flow = swap_cores(cross_flow)
    for step in range(stages - 2, -1, -1):
        outs = run_stage(
            weights if step else near,
            step,
            False,
            True,
            step == 0,
            rows,
            sizes,
            upstream,
            trunks[step],
            inners[step],
        )
        upstreams.insert(0, outs[0])
        if step:
            upstream = hop(outs[2], stages - 1 - step)
            back_inners.insert(0, outs[1])
            continue
        tail = pl.pallas_call(
            tail_body,
            out_shape=jax.ShapeDtypeStruct(outs[1].shape, outs[1].dtype),
            in_specs=[VMEM] * 5,
            out_specs=VMEM,
            compiler_params=PACKED,
        )(near[1], near[3], outs[0], outs[1], inners[0])
        back_inners.insert(0, tail)
    going = pick(upstreams, True)
    far_up = mirror(near_core(going[0], going[1]) if mirrored else going)
    far_inner = mirror(pick(back_inners, True))
    side_up = swap_cores(pick(upstreams)[1])
    side_inner = swap_cores(pick(back_inners)[1])
    if mirrored:
        top = jnp.where(at_stage[0], leave, known[0])
        far_up, cross_up = near_core(far_up, top), near_core(top, far_up)
    else:
        far_up, cross_up = far_up[0], far_up[1]
    far_inner, cross_inner = far_inner[0], far_inner[1]
    crossed = swap_cores(jnp.concatenate([cross_up, cross_inner], axis=1))
    cross_up, cross_inner = crossed[:, :channels], crossed[:, channels:]

    chunk = channels // replicas
    fore = flows + [side_flow, far_flow, cross_flow]
    ups = upstreams + [side_up, far_up, cross_up]
    backs = back_inners + [side_inner, far_inner, cross_inner]
    halve = halve_rows if chunk % 128 == 0 and replicas >= 4 else halve_sums
    parts = halve(stages, replicas, chunk, sizes, rows, fore, ups, backs)
    return pl.pallas_call(
        finish_body,
        out_shape=jax.ShapeDtypeStruct((1, 2, chunk, inner), jnp.float32),
        in_specs=[VMEM] * 4,
        out_specs=HBM,
        scratch_shapes=[
            pltpu.VMEM((2, chunk, inner), jnp.float32),
            pltpu.SemaphoreType.DMA((2,)),
        ],
        compiler_params=PARAMS,
    )(*parts)


def sums(count, chunk, inner):
    return [
        jax.ShapeDtypeStruct((count, chunk, inner), jnp.bfloat16),
        jax.ShapeDtypeStruct((count, chunk, inner), jnp.float32),
    ]


def exchange(shard, stages, replicas, first, second):
    pairs = []
    for p in range(2 * stages):
        for q in range(replicas):
            pairs.append((p * replicas + q, p * replicas + (q ^ (second if p % 2 else first))))
    return lax.ppermute(shard, AXES, pairs)


def halve_rows(stages, replicas, chunk, sizes, rows, fore, ups, backs):
    channels, inner = sizes
    shape = lambda *dims: jax.ShapeDtypeStruct(dims, jnp.bfloat16)

    def pack(late, up, near, far):
        count = 2 * (near + far)
        arrays = []
        for one in (fore, late):
            arrays += one[: stages + 1] * near + one[stages + 1 :] * far
        return pl.pallas_call(
            functools.partial(pack_body, stages, chunk, up, near, far),
            out_shape=[
                shape(count * rows, channels // 2),
                shape(count * rows, inner),
                shape(count * rows, channels // 2 + inner),
            ],
            in_specs=[VMEM] * len(arrays),
            out_specs=[VMEM] * 3,
            scratch_shapes=[pltpu.VMEM((count * rows, channels), jnp.bfloat16)],
            compiler_params=PARAMS,
        )(*arrays)

    near = fore[: stages + 1] + ups[: stages + 1] + backs[: stages + 1]
    *kept, send = pl.pallas_call(
        functools.partial(near_body, stages, chunk),
        out_shape=[
            shape(2 * rows, channels // 2),
            shape(2 * rows, inner),
            shape(2 * rows, channels // 2),
            shape(2 * rows, inner),
            shape(2 * rows, channels + 2 * inner),
        ],
        in_specs=[VMEM] * len(near),
        out_specs=[VMEM] * 5,
        scratch_shapes=[pltpu.VMEM((2 * rows, channels), jnp.bfloat16)],
        compiler_params=PARAMS,
    )(*near)
    came_near = exchange(send, stages, replicas, 1, 2)
    parts = []
    for at, name, late in ((1, "inner", backs), (0, "up", ups)):
        left, right, send = pack(late, name == "up", False, True)
        came = exchange(send, stages, replicas, 1, 2)
        operands = (kept[2 * at], kept[2 * at + 1], came_near, left, right, came)
        count = replicas // 4
        send, keep = pl.pallas_call(
            functools.partial(half_gradient_body, at, len(operands) // 3),
            out_shape=sums(count, chunk, inner),
            in_specs=[VMEM] * len(operands),
            out_specs=[VMEM] * 2,
            scratch_shapes=[
                pltpu.VMEM((channels // 2, inner), jnp.float32),
                pltpu.VMEM((8 * rows, channels // 2), jnp.bfloat16),
                pltpu.VMEM((8 * rows, inner), jnp.bfloat16),
            ],
            compiler_params=PACKED,
        )(*operands)
        came = exchange(send, stages, replicas, 2, 1)
        for bit in range(2, replicas.bit_length() - 1):
            count //= 2
            send, keep = pl.pallas_call(
                functools.partial(next_body, bit),
                out_shape=sums(count, chunk, inner),
                in_specs=[VMEM] * 2,
                out_specs=[VMEM] * 2,
                compiler_params=PARAMS,
            )(keep, came)
            came = exchange(send, stages, replicas, 1 << bit, 1 << bit)
        parts += [keep, came]
    return parts


def halve_sums(stages, replicas, chunk, sizes, rows, fore, ups, backs):
    channels, inner = sizes
    wide, narrow = slice(0, channels), slice(channels, channels + inner)

    def of_flows(columns):
        def pick_parts(arrays):
            near = [flow.at[0, :, columns] for flow in arrays[:stages]]
            side, far, cross = arrays[stages : stages + 3]
            return near, [side.at[:, columns], far.at[:, columns], cross.at[:, columns]]

        return pick_parts

    def of_backs(arrays):
        near = [back.at[0] for back in arrays[stages + 3 : 2 * stages + 3]]
        side, far, cross = arrays[2 * stages + 3 : 2 * stages + 6]
        return near, [side, far, cross]

    plans = [halving_plan(replicas, turn) for turn in range(2)]
    streams = []
    for pick_left, pick_right, late, plan in (
        (of_backs, of_flows(narrow), ups, plans),
        (of_flows(wide), of_backs, backs, plans[::-1]),
    ):
        arrays = fore + late
        send, keep = pl.pallas_call(
            functools.partial(gradient_body, plan, pick_left, pick_right, len(arrays)),
            out_shape=sums(replicas // 2, chunk, inner),
            in_specs=[VMEM] * len(arrays),
            out_specs=[VMEM] * 2,
            scratch_shapes=[
                pltpu.VMEM((4 * rows, channels), jnp.bfloat16),
                pltpu.VMEM((4 * rows, inner), jnp.bfloat16),
                pltpu.VMEM((channels, inner), jnp.float32),
            ],
            compiler_params=PARAMS,
        )(*arrays)
        streams.append((plan, send, keep))
    for at in range(replicas.bit_length() - 1):
        half = replicas >> (at + 2)
        arrived = []
        for plan, send, keep in streams:
            pairs = []
            for p in range(2 * stages):
                for q in range(replicas):
                    pairs.append((p * replicas + q, p * replicas + (q ^ plan[p % 2][0][at])))
            arrived.append((plan, keep, lax.ppermute(send, AXES, pairs)))
        if half == 0:
            break
        streams = []
        for plan, keep, came in arrived:
            send, keep = pl.pallas_call(
                functools.partial(halve_body, plan, at + 1),
                out_shape=sums(half, chunk, inner),
                in_specs=[VMEM] * 2,
                out_specs=[VMEM] * 2,
                compiler_params=PARAMS,
            )(keep, came)
            streams.append((plan, send, keep))
    (_, keep_expand, came_expand), (_, keep_reduce, came_reduce) = arrived
    return keep_reduce, came_reduce, keep_expand, came_expand


def solution(mesh):
    return jax.shard_map(
        shards,
        mesh=mesh,
        in_specs=(
            P(None, None, "dp", None),
            P(None, None, "dp", None),
            P(None, "pipe", None, None),
            P(None, "pipe", None, None),
        ),
        out_specs=P("pipe", None, "dp", None),
        check_vma=False,
    )
```
